32 devices in a mesh: batch: 8 (over z, y), head: 4 (over x, core).
Axes of the slice: x: 2, y: 2, z: 4, core: 2. Of those that a mesh axis runs over, the one named last changes fastest.
Arguments:
- inputs: bfloat16 [8192, 768], P(('batch', 'head')), may hold values from -6 to 6
- bucket: int32 [16], P('batch'), may hold values from 0 to 1, as said below
- lengths: int32 [16, 4], P('batch'), may hold values from 0 to 512, as said below
- qkv_weight: bfloat16 [768, 2304], P(None, ('batch', 'head')), may hold values from -0.21875 to 0.21875
- query_bias: bfloat16 [768], P(('batch', 'head')), may hold values from -3 to 3
- value_bias: bfloat16 [768], P(('batch', 'head')), may hold values from -3 to 3
- proj_weight: bfloat16 [768, 768], P(None, ('batch', 'head')), may hold values from -1.75 to 1.75
- proj_bias: bfloat16 [768], P(('batch', 'head')), may hold values from -3 to 3
- first_gain: bfloat16 [768], P(('batch', 'head')), may hold values from 0.099609375 to 1.8984375
- first_shift: bfloat16 [768], P(('batch', 'head')), may hold values from -2 to 2
- up_weight: bfloat16 [768, 3072], P(None, ('batch', 'head')), may hold values from -0.21875 to 0.21875
- up_bias: bfloat16 [3072], P(('batch', 'head')), may hold values from -3 to 3
- down_weight: bfloat16 [3072, 768], P(('batch', 'head')), may hold values from -0.109375 to 0.109375
- down_bias: bfloat16 [768], P(('batch', 'head')), may hold values from -3 to 3
- second_gain: bfloat16 [768], P(('batch', 'head')), may hold values from 0.099609375 to 1.8984375
- second_shift: bfloat16 [768], P(('batch', 'head')), may hold values from -2 to 2
- cotangent: bfloat16 [8192, 768], P(('batch', 'head')), may hold values from -6 to 6
Outputs:
- layer_out: bfloat16 [8192, 768], P(('batch', 'head'))
- inputs_grad: bfloat16 [8192, 768], P(('batch', 'head'))
- qkv_grad: float32 [768, 2304], P('batch', 'head')
- qbias_grad: float32 [768], P(('batch', 'head'))
- vbias_grad: float32 [768], P(('batch', 'head'))
- proj_grad: float32 [768, 768], P('head', 'batch')
- pbias_grad: float32 [768], P(('batch', 'head'))
- fgain_grad: float32 [768], P(('batch', 'head'))
- fshift_grad: float32 [768], P(('batch', 'head'))
- up_grad: float32 [768, 3072], P(None, ('batch', 'head'))
- ubias_grad: float32 [3072], P(('batch', 'head'))
- down_grad: float32 [3072, 768], P(('batch', 'head'))
- dbias_grad: float32 [768], P(('batch', 'head'))
- sgain_grad: float32 [768], P(('batch', 'head'))
- sshift_grad: float32 [768], P(('batch', 'head'))
The draws below stay inside these ranges and needn't reach their ends.
Inputs may be any that keep to these rules, and one draw needn't show every extreme that they name: `bucket`: 1 marks a block holding one sequence of up to 512 tokens, 0 a block holding 4 sequences, one in each aligned block of 128 rows. For a block marked 1, entry 0 is its sequence's length, over 128, and the other entries are 0; for a block marked 0, entry u is the length of the sequence starting at row u * 128, 1 to 128; lengths 512 and 128 occur.
All inputs are finite; a program needn't handle non-finite values.
Results may differ from the reference program's by a relative error of at most 0.017.
Values may be sent and summed in bfloat16 or wider, within the bound.
No kernel may reach another device: no remote copies, remote signals or barrier semaphores. Data moves between devices by JAX's collectives and lax.ppermute only.
A program may use at most 128 MiB of HBM per device.

```python
import jax
import jax.numpy as jnp
from jax import lax

D = 768
HEADS = 12
HEAD_DIM = 64
FF = 3072
BIG = 512
SMALL = 128
BLK = 2
UNITS = 4
BLOCKS = 16
TOKENS = 8192
N_BATCH = 8


def draw_both(key):
    groups = BLOCKS // BLK
    shares = jax.random.randint(jax.random.fold_in(key, 101), (groups, 1), 1, 10)
    rolled = jax.random.randint(jax.random.fold_in(key, 102), (groups, BLK), 0, 10)
    bucket = (rolled < shares).astype(jnp.int32).reshape(BLOCKS)
    long_len = jnp.minimum(BIG, jax.random.randint(jax.random.fold_in(key, 103), (BLOCKS, 1), SMALL + 1, BIG + BIG // 2 + 1))
    short_len = jnp.minimum(SMALL, jax.random.randint(jax.random.fold_in(key, 104), (BLOCKS, UNITS), 1, SMALL + SMALL // 2 + 1))
    padding = jnp.zeros((BLOCKS, UNITS - 1), jnp.int32)
    lengths = jnp.where(bucket[:, None] == 1, jnp.concatenate([long_len, padding], 1), short_len)
    return (bucket, lengths.astype(jnp.int32))


def draw_bucket(key, part):
    return draw_both(key)[0]


def draw_lengths(key, part):
    return draw_both(key)[1]


def spiked(values, own_key, source, target, parts, factor):
    owner, partner = [(jnp.arange(values.shape[position]) // (values.shape[position] // parts)).reshape([-1 if axis == position else 1 for axis in range(values.ndim)]) for position in (source, target)]
    chosen = jax.random.permutation(own_key, parts)[partner]
    strong = (owner == chosen) | (owner == (partner + parts // 2) % parts)
    return jnp.where(strong, factor * values, values)


def steps_of(own_key, extent, pieces, low, top_value):
    def one(dim, blocks):
        heights = jax.random.uniform(jax.random.fold_in(jax.random.fold_in(own_key, 6), dim), (blocks,), jnp.float32, low / len(pieces), top_value / len(pieces))
        return jnp.repeat(jnp.exp(heights), extent[dim] // blocks).reshape((-1,) + (1,) * (len(extent) - dim - 1))

    level = one(*pieces[0])
    for cut in pieces[1:]:
        level = level * one(*cut)
    return level


def scatter_about(own_key, dims, width, limit, shards=(), kind=jnp.bfloat16):
    array = jax.random.normal(own_key, dims, jnp.float32) * width
    if len(shards) > 0:
        array = steps_of(own_key, dims, shards, -0.22, 0.18) * array
    return jnp.clip(array, min=-limit, max=limit).astype(kind)


def bell_draw_with(stream_key, dims, width, bound, split, heavy, kind=jnp.bfloat16):
    entries = width * jax.random.normal(stream_key, dims, jnp.float32)
    if split:
        entries = entries * steps_of(stream_key, dims, split, -0.22, 0.18)
    return jnp.clip(spiked(entries, jax.random.fold_in(stream_key, 3), *heavy), -bound, bound).astype(kind)


def setup_inputs(seed: int = 0) -> dict:
    seeds = jax.random.split(jax.random.key(seed), 18)
    inputs = scatter_about(seeds[0], (TOKENS, D), 1.0, 6.0, ((0, 32),))
    bucket = draw_bucket(jax.random.fold_in(seeds[17], 71), 0)
    lengths = draw_lengths(jax.random.fold_in(seeds[17], 71), 0)
    qkv_weight = scatter_about(seeds[3], (D, 3 * D), D ** -0.5, 0.21875, ((1, 32),))
    query_bias = scatter_about(seeds[4], (D,), 0.5, 3.0, ((0, 32),))
    value_bias = scatter_about(seeds[5], (D,), 0.5, 3.0, ((0, 32),))
    proj_weight = scatter_about(seeds[6], (D, D), (D // 64) ** -0.5, 1.75, ((1, 32),))
    proj_bias = scatter_about(seeds[7], (D,), 0.5, 3.0, ((0, 32),))
    first_gain = jnp.clip(1.0 + 0.18 * jax.random.normal(seeds[8], (D,), jnp.float32), 0.099609375, 1.8984375).astype(jnp.bfloat16)
    first_shift = scatter_about(seeds[9], (D,), 0.3, 2.0, ((0, 32),))
    up_weight = scatter_about(seeds[10], (D, FF), D ** -0.5, 0.21875, ((1, 32),))
    up_bias = scatter_about(seeds[11], (FF,), 0.5, 3.0, ((0, 32),))
    down_weight = scatter_about(seeds[12], (FF, D), FF ** -0.5, 0.109375, ((0, 32),))
    down_bias = scatter_about(seeds[13], (D,), 0.5, 3.0, ((0, 32),))
    second_gain = jnp.clip(1.0 + 0.18 * jax.random.normal(seeds[14], (D,), jnp.float32), 0.099609375, 1.8984375).astype(jnp.bfloat16)
    second_shift = scatter_about(seeds[15], (D,), 0.3, 2.0, ((0, 32),))
    cotangent = bell_draw_with(seeds[16], (TOKENS, D), 1.0, 6.0, ((0, 32),), (0, 1, 32, 2.75))
    return dict(inputs=inputs, bucket=bucket, lengths=lengths, qkv_weight=qkv_weight, query_bias=query_bias, value_bias=value_bias, proj_weight=proj_weight, proj_bias=proj_bias, first_gain=first_gain, first_shift=first_shift, up_weight=up_weight, up_bias=up_bias, down_weight=down_weight, down_bias=down_bias, second_gain=second_gain, second_shift=second_shift, cotangent=cotangent)


NORM_EPS = 1e-12
HIGH = lax.Precision.HIGHEST

@jax.custom_vjp
def low(v):
    return lax.optimization_barrier(v.astype(jnp.bfloat16)).astype(jnp.float32)

@jax.custom_vjp
def low_back(v):
    return v

def low_keep(v):
    return (low(v), None)

def low_pass(kept, grad):
    return (grad,)

def back_keep(v):
    return (v, None)

def back_low(kept, grad):
    return (low(grad),)
low.defvjp(low_keep, low_pass)
low_back.defvjp(back_keep, back_low)

def layer_norm(values, gain, shift):
    center = values - lax.optimization_barrier(jnp.mean(values, -1, keepdims=True))
    spread = lax.optimization_barrier(jnp.mean(center * center, -1, keepdims=True))
    return center * lax.rsqrt(spread + NORM_EPS) * gain + shift

def block_masks(bucket, lengths):
    units = jnp.arange(UNITS, dtype=jnp.int32)
    long_live = jnp.clip(lengths[:, :1] - SMALL * units[None, :], 0, SMALL)
    unit_live = jnp.where(bucket[:, None] == 1, long_live, lengths)
    places = jnp.arange(BIG, dtype=jnp.int32)
    unit_of = places // SMALL
    inner = places - unit_of * SMALL
    live_rows = inner[None, :] < jnp.repeat(unit_live, SMALL, axis=1)
    segments = jnp.where(bucket[:, None] == 1, 0, unit_of[None, :])
    return (live_rows, segments)

def attend(packed):
    query, keys, values, live_row, segment = packed
    allowed = (segment[:, None] == segment[None, :]) & live_row[None, :]
    scores = jnp.einsum('qhd,khd->hqk', query, keys, precision=HIGH) * HEAD_DIM ** (-0.5)
    scores = low_back(scores)
    scores = jnp.where(allowed[None], scores, -1e+30)
    highest = lax.optimization_barrier(jnp.max(scores, -1, keepdims=True))
    exp_vals = jnp.exp(scores - highest)
    probs = exp_vals / lax.optimization_barrier(jnp.sum(exp_vals, -1, keepdims=True))
    return jnp.einsum('hqk,khd->qhd', low(probs), values, precision=HIGH)

def forward_group(inputs, params, live_rows, segments):
    qkv_weight, query_bias, value_bias, proj_weight, proj_bias, first_gain, first_shift, up_weight, up_bias, down_weight, down_bias, second_gain, second_shift = params
    row_count = inputs.shape[0]
    projected = jnp.dot(inputs, qkv_weight, precision=HIGH).reshape(row_count, HEADS, 3, HEAD_DIM)
    query = projected[:, :, 0] + query_bias.reshape(HEADS, HEAD_DIM)
    keys = projected[:, :, 1]
    values = projected[:, :, 2] + value_bias.reshape(HEADS, HEAD_DIM)
    query = low_back(low(query)).reshape(BLK, BIG, HEADS, HEAD_DIM)
    keys = low_back(low(keys)).reshape(BLK, BIG, HEADS, HEAD_DIM)
    values = low_back(low(values)).reshape(BLK, BIG, HEADS, HEAD_DIM)
    context = lax.map(jax.checkpoint(attend), (query, keys, values, live_rows, segments))
    context = low_back(low(context.reshape(row_count, D)))
    attn = low_back(jnp.dot(context, proj_weight, precision=HIGH) + proj_bias)
    first = layer_norm(inputs + attn, first_gain, first_shift)
    up_val = low_back(jnp.dot(low(first), up_weight, precision=HIGH) + up_bias)
    hidden = low(jax.nn.gelu(up_val, approximate=False))
    down = low_back(jnp.dot(hidden, down_weight, precision=HIGH) + down_bias)
    return layer_norm(first + down, second_gain, second_shift)

def reference(inputs, bucket, lengths, qkv_weight, query_bias, value_bias, proj_weight, proj_bias, first_gain, first_shift, up_weight, up_bias, down_weight, down_bias, second_gain, second_shift, cotangent):
    params = tuple((item.astype(jnp.float32) for item in (qkv_weight, query_bias, value_bias, proj_weight, proj_bias, first_gain, first_shift, up_weight, up_bias, down_weight, down_bias, second_gain, second_shift)))
    group_rows = BLK * BIG
    in_groups = inputs.astype(jnp.float32).reshape(N_BATCH, group_rows, D)
    cot_groups = cotangent.astype(jnp.float32).reshape(N_BATCH, group_rows, D)
    bucket_groups = bucket.reshape(N_BATCH, BLK)
    length_groups = lengths.reshape(N_BATCH, BLK, UNITS)

    def group_step(totals, item):
        group_in, group_cot, group_bucket, group_lengths = item
        live_rows, segments = block_masks(group_bucket, group_lengths)
        out_cot = group_cot * live_rows.reshape(-1)[:, None].astype(jnp.float32)
        result, pull = jax.vjp(lambda xin, prm: forward_group(xin, prm, live_rows, segments), group_in, params)
        in_grad, param_grads = pull(out_cot)
        totals = tuple((left + right for left, right in zip(totals, param_grads)))
        return (totals, (result.astype(jnp.bfloat16), in_grad.astype(jnp.bfloat16)))
    zero_grads = tuple((jnp.zeros_like(item) for item in params))
    totals, (results, in_grads) = lax.scan(group_step, zero_grads, (in_groups, cot_groups, bucket_groups, length_groups))
    return (results.reshape(-1, D), in_grads.reshape(-1, D), totals[0], totals[1], totals[2], totals[3], totals[4], totals[5], totals[6], totals[7], totals[8], totals[9], totals[10], totals[11], totals[12])
```

```python
import jax
import jax.numpy as jnp
from jax import lax
from jax.experimental import pallas as pl
from jax.experimental.pallas import tpu as pltpu
from jax.sharding import PartitionSpec as P

D = 768
HEADS = 12
HEAD_DIM = 64
FF = 3072
BIG = 512
SMALL = 128
UNITS = 4
NORM_EPS = 1e-12
F32 = jnp.float32
BF16 = jnp.bfloat16

CORE = [(i, i ^ 1) for i in range(4)]
XPAIR = [(i, i ^ 2) for i in range(4)]
YPAIR = [(i, i ^ 1) for i in range(8)]
ZPAIR = [[(i, i ^ (2 * k)) for i in range(8)] for k in range(4)]


def core_swap(v):
    return lax.ppermute(v, "head", CORE)


def x_swap(v):
    return lax.ppermute(v, "head", XPAIR)


def y_swap(v):
    return lax.ppermute(v, "batch", YPAIR)


def z_swap(v, k):
    return lax.ppermute(v, "batch", ZPAIR[k])


def after(value, other):
    return lax.optimization_barrier((value, other))[0]


def nt(a, b, out=F32):
    return lax.dot_general(a, b, (((1,), (1,)), ((), ())), preferred_element_type=F32).astype(out)


def nn(a, b, out=F32):
    return lax.dot_general(a, b, (((1,), (0,)), ((), ())), preferred_element_type=F32).astype(out)


def tn(a, b, out=F32):
    return lax.dot_general(a, b, (((0,), (0,)), ((), ())), preferred_element_type=F32).astype(out)


def gather_plane(shard, direct):
    if not direct:
        whole = lax.all_gather(shard, "batch", axis=0)
        return [whole, x_swap(whole)]
    z = jnp.stack([shard] + [z_swap(shard, k) for k in (1, 2, 3)])
    x = x_swap(z)
    y = y_swap(z)
    return [z, x, y, x_swap(y[:2]), y_swap(x[2:])]


def scatter_plane(parts, direct):
    if not direct:
        total = parts[0].astype(F32) + x_swap(parts[1]).astype(F32)
        return lax.psum_scatter(total, "batch", scatter_dimension=0, tiled=False)
    g0, gx, gy, ga, gb = parts
    ra = x_swap(ga)
    rb = y_swap(gb)
    sy = jnp.concatenate([(gy[:2].astype(F32) + ra.astype(F32)).astype(BF16), gy[2:]])
    sx = jnp.concatenate([gx[:2], (gx[2:].astype(F32) + rb.astype(F32)).astype(BF16)])
    total = g0.astype(F32) + y_swap(sy).astype(F32) + x_swap(sx).astype(F32)
    return total


def finish_z(mine, others):
    return mine + sum(z_swap(others[k - 1].astype(BF16), k).astype(F32) for k in (1, 2, 3))


def order_kernel(rows_q, rows_p, place, *refs):
    sources, (wq, wp, sem) = refs[:10], refs[10:]
    z, y, x, c = place[0], place[1], place[2], place[3]
    copies = []
    for swapped in range(2):
        cc = c if swapped == 0 else 1 - c
        z0, xx, yy, xa, xb = sources[5 * swapped : 5 * swapped + 5]
        p = lax.rem(c + z, 2)
        for kx, ky, pair in ((0, 0, (z0, z0)), (1, 0, (xx, xx)), (0, 1, (yy, yy)), (1, 1, (xa, xb))):
            yi = y + ky - 2 * y * ky
            xi = x + kx - 2 * x * kx
            j = yi * 4 + xi * 2 + cc
            for i in range(2):
                src = pair[i]
                spot = p if pair[0] is not pair[1] else p + 2 * i
                zh = lax.div(z, 2)
                g = zh + i - 2 * zh * i
                copies.append(
                    pltpu.make_async_copy(src.at[spot, pl.ds(0, rows_q)], wq.at[g, j], sem)
                )
            for kz in range(4):
                src = pair[kz // 2]
                spot = kz if pair[0] is pair[1] else kz - 2 * (kz // 2)
                zl, zh = lax.rem(z, 2), lax.div(z, 2)
                k0, k1 = kz % 2, kz // 2
                zi = (zl + k0 - 2 * zl * k0) + 2 * (zh + k1 - 2 * zh * k1)
                copies.append(
                    pltpu.make_async_copy(
                        src.at[spot, pl.ds(rows_q, rows_p)], wp.at[zi * 8 + j], sem
                    )
                )
    for copy in copies:
        copy.start()
    for copy in copies:
        copy.wait()


def order_weights(own, swapped, place, rows_q, rows_p):
    import functools

    return pl.pallas_call(
        functools.partial(order_kernel, rows_q, rows_p),
        out_shape=(
            jax.ShapeDtypeStruct((2, 8, rows_q, D), BF16),
            jax.ShapeDtypeStruct((32, rows_p, D), BF16),
        ),
        grid_spec=pltpu.PrefetchScalarGridSpec(
            num_scalar_prefetch=1,
            grid=(1,),
            in_specs=[pl.BlockSpec(memory_space=pl.ANY)] * 10,
            out_specs=[pl.BlockSpec(memory_space=pl.ANY)] * 2,
            scratch_shapes=[pltpu.SemaphoreType.DMA],
        ),
    )(place, *own, *swapped)


def norm_parts(values):
    center = values - jnp.mean(values, -1, keepdims=True)
    spread = jnp.mean(center * center, -1, keepdims=True)
    scale = lax.rsqrt(spread + NORM_EPS)
    return center * scale, scale


def norm_back(cot, normal, scale, gain):
    w = cot * gain
    return scale * (
        w - jnp.mean(w, -1, keepdims=True) - normal * jnp.mean(w * normal, -1, keepdims=True)
    )


def masks(bucket, lengths, chip_half, c):
    units = jnp.arange(UNITS, dtype=jnp.int32)
    long_live = jnp.clip(lengths[0] - SMALL * units, 0, SMALL)
    unit_live = jnp.where(bucket == 1, long_live, lengths)
    places = jnp.arange(BIG, dtype=jnp.int32)
    unit_of = places // SMALL
    live = (places - unit_of * SMALL) < jnp.repeat(unit_live, SMALL)
    segment = jnp.where(bucket == 1, 0, unit_of)
    live = jnp.where(c == 0, live, jnp.roll(live, BIG // 2))
    segment = jnp.where(c == 0, segment, jnp.roll(segment, BIG // 2))
    return live, segment


def local(
    inputs,
    bucket,
    lengths,
    qkv_weight,
    query_bias,
    value_bias,
    proj_weight,
    proj_bias,
    first_gain,
    first_shift,
    up_weight,
    up_bias,
    down_weight,
    down_bias,
    second_gain,
    second_shift,
    cotangent,
):
    head_count = lax.axis_size("head")
    batch_count = lax.axis_size("batch")
    devices = head_count * batch_count
    direct = batch_count == 8
    b = lax.axis_index("batch")
    h = lax.axis_index("head")
    me = b * head_count + h
    x, c = h // 2, h % 2
    z, y = b // 2, b % 2
    rows = inputs.shape[0]
    wq, wp, wf = 3 * D // devices, D // devices, FF // devices

    vectors = jnp.stack(
        [
            query_bias,
            value_bias,
            proj_bias,
            first_gain,
            first_shift,
            down_bias,
            second_gain,
            second_shift,
        ]
    )
    small = lax.dynamic_update_slice(jnp.zeros((8, D), BF16), vectors, (0, me * wp))
    proj_t = proj_weight.T.reshape(wp, 2, 2, 192).transpose(0, 2, 1, 3).reshape(wp, D)
    a_shard = jnp.concatenate([qkv_weight.T, proj_t, small])
    bias_row = jnp.pad(up_bias[None, :], ((0, 7), (0, D - wf)))
    u_shard = jnp.concatenate([up_weight.T, bias_row])

    other_in = core_swap(inputs)
    group_in = jnp.concatenate([inputs, other_in])

    if direct:
        a_own = gather_plane(a_shard, direct)
        u_shard = after(u_shard, a_own[0])
        u_all = gather_plane(u_shard, direct)
        d_shard = after(down_weight, u_all[0])
        d_all = gather_plane(d_shard, direct)
        a_swapped = [core_swap(v) for v in a_own]
        place = jnp.stack([z, y, x, c]).astype(jnp.int32)
        qkv_w, proj_w = order_weights(a_own, a_swapped, place, wq, wp)
        qkv_w = qkv_w.reshape(2 * 576, D)
        proj_w = proj_w.reshape(D, D)
        small_all = sum(jnp.sum(v[:, wq + wp :].astype(F32), 0) for v in a_own + a_swapped)
    else:
        a_all = lax.all_gather(a_shard, ("batch", "head"), axis=0)
        qkv_all = a_all[:, :wq].reshape(2, 2, 576, D)
        qkv_w = lax.dynamic_index_in_dim(qkv_all, c, 1, keepdims=False).reshape(2 * 576, D)
        proj_w = a_all[:, wq : wq + wp].reshape(D, D)
        small_all = jnp.sum(a_all[:, wq + wp :].astype(F32), 0)
        u_all = gather_plane(u_shard, direct)
        d_all = gather_plane(down_weight, direct)
    qbias, vbias, pbias, fgain, fshift, dbias, sgain, sshift = [small_all[i] for i in range(8)]

    live, segment = masks(
        lax.dynamic_index_in_dim(bucket, x, 0, keepdims=False),
        lax.dynamic_index_in_dim(lengths, x, 0, keepdims=False),
        x,
        c,
    )
    own_live = live[:rows]

    q_own = lax.dynamic_index_in_dim(qbias.reshape(2, 2, 192), c, 1, keepdims=False)
    v_own = lax.dynamic_index_in_dim(vbias.reshape(2, 2, 192), c, 1, keepdims=False)
    bias = jnp.stack(
        [q_own.reshape(6, HEAD_DIM), jnp.zeros((6, HEAD_DIM), F32), v_own.reshape(6, HEAD_DIM)], 1
    ).reshape(-1)
    by_heads = (nt(group_in, qkv_w) + bias).astype(BF16).reshape(2 * rows, 6, 3, HEAD_DIM)
    query, keys, values = by_heads[:, :, 0], by_heads[:, :, 1], by_heads[:, :, 2]
    allowed = (segment[:, None] == segment[None, :]) & live[None, :]
    scale = HEAD_DIM ** (-0.5)
    scores = jnp.einsum("qhd,khd->hqk", query, keys, preferred_element_type=F32) * scale
    scores = jnp.where(allowed[None], scores, -1e30)
    highest = jnp.max(scores, -1, keepdims=True)
    exp_vals = jnp.exp(scores - highest)
    probs = exp_vals / jnp.sum(exp_vals, -1, keepdims=True)
    probs_low = probs.astype(BF16)
    context = jnp.einsum("hqk,khd->qhd", probs_low, values, preferred_element_type=F32)
    context = context.astype(BF16).reshape(2 * rows, 384)
    ctx_in = core_swap(context[rows:])
    ctx_own = context[:rows]
    context_tok = jnp.where(
        c == 0,
        jnp.concatenate([ctx_own, ctx_in], 1),
        jnp.concatenate([ctx_in, ctx_own], 1),
    )
    attn = nt(context_tok, proj_w) + pbias
    first_n, first_r = norm_parts(inputs.astype(F32) + attn)
    first = first_n * fgain + fshift
    first_low = first.astype(BF16)
    first_group = jnp.concatenate([first_low, core_swap(first_low)])

    down_part = 0.0
    kept = []
    for u, d in zip(u_all, d_all):
        n = u.shape[0]
        up_w = u[:, :wf].reshape(n * wf, D)
        up_b = u[:, wf, :wf].reshape(n * wf).astype(F32)
        dn_w = d.reshape(n * wf, D)
        up_val = nt(first_group, up_w) + up_b
        phi = 0.5 * (1.0 + lax.erf(up_val * (2.0**-0.5)))
        hidden = (up_val * phi).astype(BF16)
        slope = (phi + up_val * jnp.exp(-0.5 * up_val * up_val) * 0.3989422804014327).astype(BF16)
        down_part = down_part + nn(hidden, dn_w)
        kept.append((up_w, dn_w, hidden, slope))
    down = down_part[:rows] + core_swap(down_part[rows:]) + dbias
    second_n, second_r = norm_parts(first + down)
    layer_out = (second_n * sgain + sshift).astype(BF16)

    out_cot = cotangent.astype(F32) * own_live[:, None].astype(F32)
    sum_two_cot = norm_back(out_cot, second_n, second_r, sgain)
    sgain_grad = jnp.sum(out_cot * second_n, 0)
    sshift_grad = jnp.sum(out_cot, 0)
    down_cot = sum_two_cot.astype(BF16)
    dbias_grad = jnp.sum(down_cot.astype(F32), 0)
    down_group = jnp.concatenate([down_cot, core_swap(down_cot)])
    ffn_part = 0.0
    up_parts, down_parts, ubias_parts = [], [], []
    for up_w, dn_w, hidden, slope in kept:
        n = up_w.shape[0] // wf
        hidden_cot = nt(down_group, dn_w)
        up_cot = (hidden_cot * slope.astype(F32)).astype(BF16)
        down_parts.append(tn(hidden, down_group, BF16).reshape(n, wf, D))
        up_parts.append(tn(up_cot, first_group, BF16).reshape(n, wf, D))
        ubias_parts.append(jnp.sum(up_cot.astype(F32), 0).reshape(n, wf))
        ffn_part = ffn_part + nn(up_cot, up_w)
    first_cot = sum_two_cot + ffn_part[:rows] + core_swap(ffn_part[rows:])
    sum_one_cot = norm_back(first_cot, first_n, first_r, fgain)
    fgain_grad = jnp.sum(first_cot * first_n, 0)
    fshift_grad = jnp.sum(first_cot, 0)
    attn_cot = sum_one_cot.astype(BF16)
    pbias_grad = jnp.sum(attn_cot.astype(F32), 0)
    attn_group = jnp.concatenate([attn_cot, core_swap(attn_cot)])
    proj_own = lax.dynamic_slice_in_dim(proj_w, c * 384, 384, 1)
    ctx_cot = nn(attn_group, proj_own, BF16).reshape(2 * rows, 6, HEAD_DIM)
    value_cot = jnp.einsum("hqk,qhd->khd", probs_low, ctx_cot, preferred_element_type=F32)
    prob_cot = jnp.einsum("qhd,khd->hqk", ctx_cot, values, preferred_element_type=F32)
    score_cot = (probs * (prob_cot - jnp.sum(probs * prob_cot, -1, keepdims=True))).astype(BF16)
    query_cot = jnp.einsum("hqk,khd->qhd", score_cot, keys, preferred_element_type=F32) * scale
    keys_cot = jnp.einsum("hqk,qhd->khd", score_cot, query, preferred_element_type=F32) * scale
    qkv_cot = jnp.stack([query_cot, keys_cot, value_cot], axis=2).astype(BF16)
    head_sums = jnp.sum(qkv_cot.astype(F32), 0)
    qkv_heads = qkv_cot.reshape(2 * rows, 2 * 576)
    in_part = nn(qkv_heads, qkv_w)
    inputs_grad = (sum_one_cot + in_part[:rows] + core_swap(in_part[rows:])).astype(BF16)

    a_grads = jnp.stack(
        [
            jnp.concatenate(
                [
                    tn(group_in, qkv_heads[:, 576 * g : 576 * g + 576], BF16),
                    tn(attn_group, context[:, 192 * g : 192 * g + 192], BF16),
                ],
                1,
            )
            for g in range(2)
        ]
    )
    wb = D // batch_count
    if direct:
        a_grads = a_grads.reshape(2, 4, 2, wb, D)

        def pick(xi, yi):
            return lax.dynamic_slice(a_grads, (xi, 0, yi, 0, 0), (1, 4, 1, wb, D)).reshape(4, wb, D)

        diag = pick(1 - x, 1 - y)
        a_total = scatter_plane(
            [pick(x, y), pick(1 - x, y), pick(x, 1 - y), diag[:2], diag[2:]], direct
        )
        a_mine = finish_z(
            lax.dynamic_index_in_dim(a_total, z, 0, keepdims=False),
            [lax.dynamic_index_in_dim(a_total, z ^ k, 0, keepdims=False) for k in (1, 2, 3)],
        )
        d_total = scatter_plane(down_parts, direct)
        d_mine = finish_z(d_total[0], d_total[1:])
        u_total = scatter_plane(up_parts, direct)
        u_mine = finish_z(u_total[0], u_total[1:])
    else:
        a_grads = a_grads.reshape(2, batch_count, wb, D)
        a_mine = scatter_plane(
            [
                lax.dynamic_index_in_dim(a_grads, x, 0, keepdims=False),
                lax.dynamic_index_in_dim(a_grads, 1 - x, 0, keepdims=False),
            ],
            direct,
        )
        d_mine = scatter_plane(down_parts, direct)
        u_mine = scatter_plane(up_parts, direct)
    qkv_grad = a_mine[:, :576]
    proj_grad = a_mine[:, 576:].T
    up_grad = u_mine.T
    down_grad = d_mine

    def place_heads(v):
        v = v.reshape(2, 1, 192)
        keep = (jnp.arange(2) == c).astype(F32)[None, :, None]
        return (v * keep).reshape(D)

    sums = jnp.stack(
        [
            place_heads(head_sums[:, 0]),
            place_heads(head_sums[:, 2]),
            pbias_grad,
            fgain_grad,
            fshift_grad,
            dbias_grad,
            sgain_grad,
            sshift_grad,
        ]
    )
    sums = sums.reshape(8, devices, wp).transpose(1, 0, 2).reshape(devices, 8 * wp)
    ubias = jnp.concatenate(ubias_parts)
    k = jnp.arange(batch_count * 2)
    if direct:
        kz = jnp.array([0, 1, 2, 3] * 3 + [0, 1, 2, 3])
        ky = jnp.array([0] * 8 + [1] * 8)
        kx = jnp.array([0] * 4 + [1] * 4 + [0] * 4 + [1] * 4)
        owner = (z ^ kz) * 8 + (y ^ ky) * 4 + (x ^ kx) * 2 + c
    else:
        owner = (k % batch_count) * 4 + (x ^ (k // batch_count)) * 2 + c
    spread = (owner[None, :] == jnp.arange(devices)[:, None]).astype(F32)
    ubias = lax.dot_general(
        spread, ubias, (((1,), (0,)), ((), ())), precision=lax.Precision.HIGHEST
    )
    packed = jnp.concatenate([sums, ubias], 1)
    packed = lax.all_to_all(packed, ("batch", "head"), split_axis=0, concat_axis=0, tiled=True)
    packed = jnp.sum(packed, 0)
    vecs = [packed[i * wp : (i + 1) * wp] for i in range(8)]
    return (
        layer_out,
        inputs_grad,
        qkv_grad,
        vecs[0],
        vecs[1],
        proj_grad,
        vecs[2],
        vecs[3],
        vecs[4],
        up_grad,
        packed[8 * wp :],
        down_grad,
        vecs[5],
        vecs[6],
        vecs[7],
    )


def solution(mesh):
    both = ("batch", "head")
    in_specs = (
        P(both, None),
        P("batch"),
        P("batch", None),
        P(None, both),
        P(both),
        P(both),
        P(None, both),
        P(both),
        P(both),
        P(both),
        P(None, both),
        P(both),
        P(both, None),
        P(both),
        P(both),
        P(both),
        P(both, None),
    )
    out_specs = (
        P(both, None),
        P(both, None),
        P("batch", "head"),
        P(both),
        P(both),
        P("head", "batch"),
        P(both),
        P(both),
        P(both),
        P(None, both),
        P(both),
        P(both, None),
        P(both),
        P(both),
        P(both),
    )
    return jax.shard_map(local, mesh=mesh, in_specs=in_specs, out_specs=out_specs, check_vma=False)
```

```python
import functools

import jax
import jax.numpy as jnp
from jax import lax
from jax.experimental import pallas as pl
from jax.experimental.pallas import tpu as pltpu
from jax.sharding import PartitionSpec as P

D = 768
HEADS = 12
HEAD_DIM = 64
FF = 3072
BIG = 512
SMALL = 128
UNITS = 4
NORM_EPS = 1e-12
F32 = jnp.float32
BF16 = jnp.bfloat16

CORE = [(i, i ^ 1) for i in range(4)]
XPAIR = [(i, i ^ 2) for i in range(4)]
YPAIR = [(i, i ^ 1) for i in range(8)]
ZPAIR = [[(i, i ^ (2 * k)) for i in range(8)] for k in range(4)]


def core_swap(v):
    return lax.ppermute(v, "head", CORE)


def x_swap(v):
    return lax.ppermute(v, "head", XPAIR)


def y_swap(v):
    return lax.ppermute(v, "batch", YPAIR)


def z_swap(v, k):
    return lax.ppermute(v, "batch", ZPAIR[k])


def after(value, other):
    return lax.optimization_barrier((value, other))[0]


def nt(a, b, out=F32):
    return lax.dot_general(a, b, (((1,), (1,)), ((), ())), preferred_element_type=F32).astype(out)


def nn(a, b, out=F32):
    return lax.dot_general(a, b, (((1,), (0,)), ((), ())), preferred_element_type=F32).astype(out)


def tn(a, b, out=F32):
    return lax.dot_general(a, b, (((0,), (0,)), ((), ())), preferred_element_type=F32).astype(out)


def gather_plane(shard, direct):
    if not direct:
        whole = lax.all_gather(shard, "batch", axis=0)
        return [whole, x_swap(whole)]
    z = jnp.stack([shard] + [z_swap(shard, k) for k in (1, 2, 3)])
    x = x_swap(z)
    y = y_swap(z)
    return [z, x, y, x_swap(y[:2]), y_swap(x[2:])]


def scatter_plane(parts, direct):
    if not direct:
        total = parts[0].astype(F32) + x_swap(parts[1]).astype(F32)
        return lax.psum_scatter(total, "batch", scatter_dimension=0, tiled=False)
    g0, gx, gy, ga, gb = parts
    ra = x_swap(ga)
    rb = y_swap(gb)
    sy = jnp.concatenate([(gy[:2].astype(F32) + ra.astype(F32)).astype(BF16), gy[2:]])
    sx = jnp.concatenate([gx[:2], (gx[2:].astype(F32) + rb.astype(F32)).astype(BF16)])
    total = g0.astype(F32) + y_swap(sy).astype(F32) + x_swap(sx).astype(F32)
    return total


def finish_z(mine, others):
    return mine + sum(z_swap(others[k - 1].astype(BF16), k).astype(F32) for k in (1, 2, 3))


def est(flops, moved, trans=0):
    return pl.CostEstimate(flops=int(flops), bytes_accessed=int(moved), transcendentals=int(trans))


def call(kernel, out_shape, operands, scratch=(), cost=None, limit=40):
    vmem = pl.BlockSpec(memory_space=pltpu.VMEM)
    single = not isinstance(out_shape, (tuple, list))
    return pl.pallas_call(
        kernel,
        out_shape=out_shape,
        in_specs=[pl.BlockSpec(memory_space=pltpu.SMEM)] + [vmem] * (len(operands) - 1),
        out_specs=vmem if single else [vmem] * len(out_shape),
        scratch_shapes=list(scratch),
        compiler_params=pltpu.CompilerParams(vmem_limit_bytes=limit << 20),
        cost_estimate=cost,
    )(*operands)


def shape(dims, dtype=BF16):
    return jax.ShapeDtypeStruct(dims, dtype)


def flip(a, bit):
    return a + bit - 2 * a * bit


def order_kernel(rows_q, rows_p, place, *refs):
    sources, (wq, wp, small) = refs[:10], refs[10:]
    z, y, x, c = place[0], place[1], place[2], place[3]
    zl, zh = lax.rem(z, 2), lax.div(z, 2)
    p = flip(c, zl)
    total = jnp.zeros(small.shape, F32)
    for swapped in range(2):
        cc = c if swapped == 0 else 1 - c
        z0, xx, yy, xa, xb = sources[5 * swapped : 5 * swapped + 5]
        for kx, ky, pair in ((0, 0, (z0, z0)), (1, 0, (xx, xx)), (0, 1, (yy, yy)), (1, 1, (xa, xb))):
            j = flip(y, ky) * 4 + flip(x, kx) * 2 + cc
            same = pair[0] is pair[1]
            for i in range(2):
                spot = p + 2 * i if same else p
                wq[flip(zh, i) * 8 + j] = pair[i][spot, 0:rows_q]
            for kz in range(4):
                spot = kz if same else kz % 2
                zi = flip(zl, kz % 2) + 2 * flip(zh, kz // 2)
                src = pair[kz // 2]
                wp[zi * 8 + j] = src[spot, rows_q : rows_q + rows_p]
                total = total + src[spot, rows_q + rows_p :].astype(F32)
    small[...] = total


def order_weights(own, swapped, place, rows_q, rows_p, rows_s):
    return call(
        functools.partial(order_kernel, rows_q, rows_p),
        (
            shape((16, rows_q, D)),
            shape((32, rows_p, D)),
            shape((rows_s, D), F32),
        ),
        (place, *own, *swapped),
        cost=est(1e6, 9e6),
    )


def live_units(meta):
    c, kind = meta[0], meta[1]
    first = meta[2]
    units = []
    for u in range(UNITS):
        far = jnp.clip(first - SMALL * u, 0, SMALL)
        units.append(jnp.where(kind == 1, far, meta[2 + u]))
    return c, kind, units


def place_of(index, c):
    return jnp.bitwise_xor(index, c * (BIG // 2))


def live_of(place, units):
    unit = lax.shift_right_logical(place, 7)
    inner = jnp.bitwise_and(place, SMALL - 1)
    count = jnp.where(
        unit < 2, jnp.where(unit == 0, units[0], units[1]), jnp.where(unit == 2, units[2], units[3])
    )
    return inner < count


def heads_of(row, c):
    parts = []
    for g in range(2):
        lo = row[:, 384 * g : 384 * g + 192]
        hi = row[:, 384 * g + 192 : 384 * g + 384]
        parts.append(jnp.where(c == 0, lo, hi))
    return jnp.concatenate(parts, 1)


def attend_kernel(meta, x0, x1, w, small, q, k, v, ctx0, ctx1, probs, wr, mask):
    c, kind, units = live_units(meta)
    half = x0.shape[0]
    for t in range(3):
        for hd in range(6):
            src = ((hd // 3) * 9 + (hd % 3) * 3 + t) * HEAD_DIM
            dst = (t * 6 + hd) * HEAD_DIM
            wr[dst : dst + HEAD_DIM] = w[src : src + HEAD_DIM]
    biases = (heads_of(small[0:1], c), None, heads_of(small[1:2], c))
    for t, ref in enumerate((q, k, v)):
        for i, xr in enumerate((x0, x1)):
            val = nt(xr[...], wr[384 * t : 384 * t + 384])
            if biases[t] is not None:
                val = val + biases[t]
            ref[half * i : half * i + half] = val.astype(BF16)
    rows = lax.broadcasted_iota(jnp.int32, (BIG, BIG), 0)
    cols = lax.broadcasted_iota(jnp.int32, (BIG, BIG), 1)
    prow, pcol = place_of(rows, c), place_of(cols, c)
    same = jnp.logical_or(
        kind == 1, lax.shift_right_logical(prow, 7) == lax.shift_right_logical(pcol, 7)
    )
    mask[...] = jnp.where(jnp.logical_and(same, live_of(pcol, units)), 0.0, -1e30)
    lane = lax.broadcasted_iota(jnp.int32, (half, 128), 1)
    for pair in range(3):
        lanes = slice(128 * pair, 128 * pair + 128)
        kp, vp = k[:, lanes], v[:, lanes]
        for i, ctx in enumerate((ctx0, ctx1)):
            rws = slice(half * i, half * i + half)
            qp = q[rws, lanes] * jnp.asarray(HEAD_DIM**-0.5, BF16)
            outs = []
            for e in range(2):
                mine = (lane < HEAD_DIM) if e == 0 else (lane >= HEAD_DIM)
                s = nt(jnp.where(mine, qp, jnp.zeros_like(qp)), kp) + mask[rws]
                ex = jnp.exp(s - jnp.max(s, -1, keepdims=True))
                pr = (ex * (1.0 / jnp.sum(ex, -1, keepdims=True))).astype(BF16)
                probs[2 * pair + e, rws] = pr
                outs.append(nn(pr, vp))
            ctx[:, lanes] = jnp.where(lane < HEAD_DIM, outs[0], outs[1]).astype(BF16)


def attend(meta, x0, x1, w, small):
    half = x0.shape[0]
    n = 2 * half
    return call(
        attend_kernel,
        (
            shape((n, 384)),
            shape((n, 384)),
            shape((n, 384)),
            shape((half, 384)),
            shape((half, 384)),
            shape((6, n, n)),
            shape((1152, D)),
        ),
        (meta, x0, x1, w, small),
        scratch=[pltpu.VMEM((n, n), F32)],
        cost=est(2 * n * D * 1152 + 8 * n * n * 384, 9e6, 6 * n * n),
    )


def norm(values):
    center = values - jnp.mean(values, -1, keepdims=True)
    spread = jnp.mean(center * center, -1, keepdims=True)
    scale = lax.rsqrt(spread + NORM_EPS)
    return center * scale, scale


def norm_back(cot, normal, scale, gain):
    w = cot * gain
    return scale * (
        w - jnp.mean(w, -1, keepdims=True) - normal * jnp.mean(w * normal, -1, keepdims=True)
    )


def first_kernel(meta, x, ctx_own, ctx_in, wp, small, first, low, normal, scale):
    c = meta[0]
    mine = pl.multiple_of(c * 384, 128)
    theirs = pl.multiple_of((1 - c) * 384, 128)
    attn = nt(ctx_own[...], wp[:, pl.ds(mine, 384)]) + nt(ctx_in[...], wp[:, pl.ds(theirs, 384)])
    n, r = norm(x[...].astype(F32) + attn + small[2:3])
    out = n * small[3:4] + small[4:5]
    first[...] = out
    low[...] = out.astype(BF16)
    normal[...] = n
    scale[...] = jnp.broadcast_to(r, scale.shape)


def first_norm(meta, x, ctx_own, ctx_in, wp, small):
    n = x.shape[0]
    return call(
        first_kernel,
        (shape((n, D), F32), shape((n, D)), shape((n, D), F32), shape((n, 128), F32)),
        (meta, x, ctx_own, ctx_in, wp, small),
        cost=est(2 * n * D * D, 5e6),
    )


def ffn_kernel(meta, *refs):
    if len(refs) == 11:
        x0, x1, uw, ub, dw, in0, in1, hid, slope, out0, out1 = refs
    else:
        x0, x1, uw, ub, dw, hid, slope, out0, out1 = refs
        in0 = in1 = None
    half = x0.shape[0]
    for i, (xr, before, out) in enumerate(((x0, in0, out0), (x1, in1, out1))):
        rws = slice(half * i, half * i + half)
        up = nt(xr[...], uw[...]) + ub[...]
        phi = 0.5 + 0.5 * lax.erf(up * (2.0**-0.5))
        hd = (up * phi).astype(BF16)
        hid[rws] = hd
        slope[rws] = (phi + up * jnp.exp(-0.5 * up * up) * 0.3989422804014327).astype(BF16)
        part = nn(hd, dw[...])
        out[...] = part if before is None else before[...] + part


def ffn(meta, x0, x1, uw, ub, dw, sums):
    half, width = x0.shape[0], uw.shape[0]
    n = 2 * half
    return call(
        ffn_kernel,
        (shape((n, width)), shape((n, width)), shape((half, D), F32), shape((half, D), F32)),
        (meta, x0, x1, uw, ub, dw, *sums),
        cost=est(4 * n * D * width, 4 * D * width + 5e6, 2 * n * width),
    )


def second_kernel(meta, first, part, got, small, cot, out, sum_two, low, sums):
    c, _, units = live_units(meta)
    n, r = norm(first[...] + (part[...] + got[...] + small[5:6]))
    out[...] = (n * small[6:7] + small[7:8]).astype(BF16)
    index = lax.broadcasted_iota(jnp.int32, (first.shape[0], 1), 0)
    live = live_of(place_of(index, c), units)
    oc = jnp.where(live, cot[...].astype(F32), 0.0)
    st = norm_back(oc, n, r, small[6:7])
    sum_two[...] = st
    lo = st.astype(BF16)
    low[...] = lo
    sums[0:1] = jnp.sum(lo.astype(F32), 0, keepdims=True)
    sums[1:2] = jnp.sum(oc * n, 0, keepdims=True)
    sums[2:3] = jnp.sum(oc, 0, keepdims=True)


def second_norm(meta, first, part, got, small, cot):
    n = first.shape[0]
    return call(
        second_kernel,
        (shape((n, D)), shape((n, D), F32), shape((n, D)), shape((3, D), F32)),
        (meta, first, part, got, small, cot),
        cost=est(40 * n * D, 5e6),
    )


def ffn_back_kernel(meta, *refs):
    if len(refs) == 15:
        d0, d1, x0, x1, uw, dw, hid, slope, in0, in1, dg, ug, ub, out0, out1 = refs
    else:
        d0, d1, x0, x1, uw, dw, hid, slope, dg, ug, ub, out0, out1 = refs
        in0 = in1 = None
    half = x0.shape[0]
    cots = []
    for i, (d, before, out) in enumerate(((d0, in0, out0), (d1, in1, out1))):
        rws = slice(half * i, half * i + half)
        uc = (nt(d[...], dw[...]) * slope[rws].astype(F32)).astype(BF16)
        cots.append(uc)
        part = nn(uc, uw[...])
        out[...] = part if before is None else before[...] + part
    ub[...] = jnp.sum(cots[0].astype(F32), 0, keepdims=True) + jnp.sum(
        cots[1].astype(F32), 0, keepdims=True
    )
    dg[...] = (tn(hid[0:half], d0[...]) + tn(hid[half : 2 * half], d1[...])).astype(BF16)
    ug[...] = (tn(cots[0], x0[...]) + tn(cots[1], x1[...])).astype(BF16)


def ffn_back(meta, d0, d1, x0, x1, uw, dw, hid, slope, sums):
    half, width = x0.shape[0], uw.shape[0]
    return call(
        ffn_back_kernel,
        (
            shape((width, D)),
            shape((width, D)),
            shape((1, width), F32),
            shape((half, D), F32),
            shape((half, D), F32),
        ),
        (meta, d0, d1, x0, x1, uw, dw, hid, slope, *sums),
        cost=est(16 * half * D * width, 8 * D * width + 5e6),
    )


def first_back_kernel(meta, sum_two, part, got, normal, scale, small, sum_one, low, sums):
    fc = sum_two[...] + part[...] + got[...]
    n = normal[...]
    so = norm_back(fc, n, scale[:, 0:1], small[3:4])
    sum_one[...] = so
    lo = so.astype(BF16)
    low[...] = lo
    sums[0:1] = jnp.sum(lo.astype(F32), 0, keepdims=True)
    sums[1:2] = jnp.sum(fc * n, 0, keepdims=True)
    sums[2:3] = jnp.sum(fc, 0, keepdims=True)


def first_back(meta, sum_two, part, got, normal, scale, small):
    n = sum_two.shape[0]
    return call(
        first_back_kernel,
        (shape((n, D), F32), shape((n, D)), shape((3, D), F32)),
        (meta, sum_two, part, got, normal, scale, small),
        cost=est(30 * n * D, 5e6),
    )


def attend_back_kernel(
    meta, a0, a1, x0, x1, wp, wr, q, k, v, ctx0, ctx1, probs, grads, in0, in1, sums, dctx, cots
):
    c = meta[0]
    half = a0.shape[0]
    n = 2 * half
    wpo = wp[:, pl.ds(pl.multiple_of(c * 384, 128), 384)]
    dctx[0:half] = nn(a0[...], wpo).astype(BF16)
    dctx[half:n] = nn(a1[...], wpo).astype(BF16)
    lane = lax.broadcasted_iota(jnp.int32, (n, 128), 1)
    zero = jnp.zeros((n, 128), BF16)
    scale = HEAD_DIM**-0.5
    heads = [[], [], []]
    for pair in range(3):
        lanes = slice(128 * pair, 128 * pair + 128)
        qp, kp, vp, dp = q[:, lanes], k[:, lanes], v[:, lanes], dctx[:, lanes]
        dq = dk = dv = 0.0
        for e in range(2):
            mine = (lane < HEAD_DIM) if e == 0 else (lane >= HEAD_DIM)
            dh, kh, qh = jnp.where(mine, dp, zero), jnp.where(mine, kp, zero), jnp.where(mine, qp, zero)
            pr = probs[2 * pair + e]
            dv = dv + tn(pr, dh)
            pf = pr.astype(F32)
            t = pf * nt(dh, vp)
            ds = (t - pf * jnp.sum(t, -1, keepdims=True)).astype(BF16)
            dq = dq + nn(ds, kh)
            dk = dk + tn(ds, qh)
        for t, val in enumerate((dq * scale, dk * scale, dv)):
            val = val.astype(BF16)
            for e in range(2):
                hd = 2 * pair + e
                g, hh = hd // 3, hd % 3
                at = 640 * g + 192 * t + 64 * hh
                cots[:, at : at + 64] = val[:, 64 * e : 64 * e + 64]
            heads[t].append(val)
    for g in range(2):
        cots[:, 640 * g + 576 : 640 * g + 640] = jnp.zeros((n, 64), BF16)
    parts = [jnp.concatenate(heads[t], 1) for t in range(3)]
    for i, out in enumerate((in0, in1)):
        rws = slice(half * i, half * i + half)
        total = 0.0
        for t in range(3):
            total = total + nn(parts[t][rws], wr[384 * t : 384 * t + 384])
        out[...] = total
    for row, t in ((0, 0), (1, 2)):
        s = jnp.sum(parts[t].astype(F32), 0, keepdims=True)
        for g in range(2):
            sg = s[:, 192 * g : 192 * g + 192]
            sums[row : row + 1, 384 * g : 384 * g + 192] = jnp.where(c == 0, sg, 0.0)
            sums[row : row + 1, 384 * g + 192 : 384 * g + 384] = jnp.where(c == 1, sg, 0.0)
    for d in range(3):
        at = slice(256 * d, 256 * d + 256)
        full = tn(x0[:, at], cots[0:half]) + tn(x1[:, at], cots[half:n])
        pg = tn(a0[:, at], ctx0[...]) + tn(a1[:, at], ctx1[...])
        for g in range(2):
            grads[g, at, 0:576] = full[:, 640 * g : 640 * g + 576].astype(BF16)
            grads[g, at, 576:768] = pg[:, 192 * g : 192 * g + 192].astype(BF16)


def attend_back(meta, a0, a1, x0, x1, wp, wr, q, k, v, ctx0, ctx1, probs):
    half = a0.shape[0]
    n = 2 * half
    return call(
        attend_back_kernel,
        (
            shape((2, D, D)),
            shape((half, D), F32),
            shape((half, D), F32),
            shape((2, D), F32),
        ),
        (meta, a0, a1, x0, x1, wp, wr, q, k, v, ctx0, ctx1, probs),
        scratch=[pltpu.VMEM((n, 384), BF16), pltpu.VMEM((n, 1280), BF16)],
        cost=est(2 * n * D * 3500 + 14 * n * n * 384, 14e6),
        limit=48,
    )


def local(
    inputs,
    bucket,
    lengths,
    qkv_weight,
    query_bias,
    value_bias,
    proj_weight,
    proj_bias,
    first_gain,
    first_shift,
    up_weight,
    up_bias,
    down_weight,
    down_bias,
    second_gain,
    second_shift,
    cotangent,
):
    head_count = lax.axis_size("head")
    batch_count = lax.axis_size("batch")
    devices = head_count * batch_count
    direct = batch_count == 8
    b = lax.axis_index("batch")
    h = lax.axis_index("head")
    me = b * head_count + h
    x, c = h // 2, h % 2
    z, y = b // 2, b % 2
    wq, wp, wf = 3 * D // devices, D // devices, FF // devices

    vectors = jnp.stack(
        [
            query_bias,
            value_bias,
            proj_bias,
            first_gain,
            first_shift,
            down_bias,
            second_gain,
            second_shift,
        ]
    )
    small = lax.dynamic_update_slice(jnp.zeros((16, D), BF16), vectors, (0, me * wp))
    per_row = D // wf
    small = lax.dynamic_update_slice(
        small, up_bias[None, :], (8 + me // per_row, (me % per_row) * wf)
    )
    proj_t = proj_weight.T.reshape(wp, 2, 2, 192).transpose(0, 2, 1, 3).reshape(wp, D)
    a_shard = jnp.concatenate([qkv_weight.T, proj_t, small])
    u_shard = up_weight.T
    other_in = core_swap(inputs)
    meta = jnp.concatenate(
        [
            jnp.stack([c, lax.dynamic_index_in_dim(bucket, x, 0, keepdims=False)]),
            lax.dynamic_index_in_dim(lengths, x, 0, keepdims=False),
        ]
    ).astype(jnp.int32)

    k = jnp.arange(batch_count * 2)
    if direct:
        a_own = gather_plane(a_shard, direct)
        u_shard = after(u_shard, a_own[0])
        u_all = gather_plane(u_shard, direct)
        d_shard = after(down_weight, u_all[0])
        d_all = gather_plane(d_shard, direct)
        a_swapped = [core_swap(v) for v in a_own]
        place = jnp.stack([z, y, x, c]).astype(jnp.int32)
        qkv_w, proj_w, small_all = order_weights(a_own, a_swapped, place, wq, wp, 16)
        qkv_w = qkv_w.reshape(2 * 576, D)
        proj_w = proj_w.reshape(D, D)
        kz = jnp.array([0, 1, 2, 3] * 4)
        ky = jnp.array([0] * 8 + [1] * 8)
        kx = jnp.array([0] * 4 + [1] * 4 + [0] * 4 + [1] * 4)
        owner = (z ^ kz) * 8 + (y ^ ky) * 4 + (x ^ kx) * 2 + c
    else:
        a_all = lax.all_gather(a_shard, ("batch", "head"), axis=0)
        qkv_all = a_all[:, :wq].reshape(2, 2, 576, D)
        qkv_w = lax.dynamic_index_in_dim(qkv_all, c, 1, keepdims=False).reshape(2 * 576, D)
        proj_w = a_all[:, wq : wq + wp].reshape(D, D)
        small_all = jnp.sum(a_all[:, wq + wp :].astype(F32), 0)
        u_all = gather_plane(u_shard, direct)
        d_all = gather_plane(down_weight, direct)
        owner = (k % batch_count) * 4 + (x ^ (k // batch_count)) * 2 + c
    spread = (owner[None, :] == jnp.arange(devices)[:, None]).astype(F32)
    ub_all = tn(spread, small_all[8:12].reshape(devices, wf)).reshape(1, FF // 2)

    q, kk, v, ctx_own, ctx_other, probs, wr = attend(meta, inputs, other_in, qkv_w, small_all)
    ctx_in = core_swap(ctx_other)
    first, first_low, first_n, first_r = first_norm(meta, inputs, ctx_own, ctx_in, proj_w, small_all)
    first_in = core_swap(first_low)
    sums = ()
    kept = []
    at = 0
    for u, d in zip(u_all, d_all):
        width = u.shape[0] * wf
        up_w, dn_w = u.reshape(width, D), d.reshape(width, D)
        hid, slope, s0, s1 = ffn(
            meta, first_low, first_in, up_w, ub_all[:, at : at + width], dn_w, sums
        )
        sums = (s0, s1)
        at += width
        kept.append((up_w, dn_w, hid, slope))
    layer_out, sum_two, down_low, sums_two = second_norm(
        meta, first, sums[0], core_swap(sums[1]), small_all, cotangent
    )
    down_in = core_swap(down_low)

    sums = ()
    up_parts, down_parts, ub_parts = [], [], []
    for up_w, dn_w, hid, slope in reversed(kept):
        dg, ug, ub, s0, s1 = ffn_back(
            meta, down_low, down_in, first_low, first_in, up_w, dn_w, hid, slope, sums
        )
        sums = (s0, s1)
        n = up_w.shape[0] // wf
        down_parts.insert(0, dg.reshape(n, wf, D))
        up_parts.insert(0, ug.reshape(n, wf, D))
        ub_parts.insert(0, ub)
    sum_one, attn_low, sums_one = first_back(
        meta, sum_two, sums[0], core_swap(sums[1]), first_n, first_r, small_all
    )
    attn_in = core_swap(attn_low)
    a_grads, in_own, in_other, sums_zero = attend_back(
        meta,
        attn_low,
        attn_in,
        inputs,
        other_in,
        proj_w,
        wr,
        q,
        kk,
        v,
        ctx_own,
        ctx_other,
        probs,
    )
    inputs_grad = (sum_one + in_own + core_swap(in_other)).astype(BF16)

    wb = D // batch_count
    if direct:
        a_grads = a_grads.reshape(2, 4, 2, wb, D)

        def pick(xi, yi):
            return lax.dynamic_slice(a_grads, (xi, 0, yi, 0, 0), (1, 4, 1, wb, D)).reshape(4, wb, D)

        diag = pick(1 - x, 1 - y)
        a_total = scatter_plane(
            [pick(x, y), pick(1 - x, y), pick(x, 1 - y), diag[:2], diag[2:]], direct
        )
        a_mine = finish_z(
            lax.dynamic_index_in_dim(a_total, z, 0, keepdims=False),
            [lax.dynamic_index_in_dim(a_total, z ^ kz, 0, keepdims=False) for kz in (1, 2, 3)],
        )
        d_total = scatter_plane(down_parts, direct)
        d_mine = finish_z(d_total[0], d_total[1:])
        u_total = scatter_plane(up_parts, direct)
        u_mine = finish_z(u_total[0], u_total[1:])
    else:
        a_grads = a_grads.reshape(2, batch_count, wb, D)
        a_mine = scatter_plane(
            [
                lax.dynamic_index_in_dim(a_grads, x, 0, keepdims=False),
                lax.dynamic_index_in_dim(a_grads, 1 - x, 0, keepdims=False),
            ],
            direct,
        )
        d_mine = scatter_plane(down_parts, direct)
        u_mine = scatter_plane(up_parts, direct)
    qkv_grad = a_mine[:, :576].reshape(wb, 3, 3, HEAD_DIM).transpose(0, 2, 1, 3).reshape(wb, 576)
    proj_grad = a_mine[:, 576:].T
    up_grad = u_mine.T
    down_grad = d_mine

    vecs = jnp.concatenate([sums_zero, sums_one, sums_two])
    vecs = vecs.reshape(8, devices, wp).transpose(1, 0, 2).reshape(devices, 8 * wp)
    ubias = jnp.concatenate(ub_parts, 1).reshape(batch_count * 2, wf)
    ubias = lax.dot_general(
        spread, ubias, (((1,), (0,)), ((), ())), precision=lax.Precision.HIGHEST
    )
    packed = jnp.concatenate([vecs, ubias], 1)
    packed = lax.all_to_all(packed, ("batch", "head"), split_axis=0, concat_axis=0, tiled=True)
    packed = jnp.sum(packed, 0)
    qb_g, vb_g, pb_g, fg_g, fs_g, db_g, sg_g, ss_g = [
        packed[i * wp : (i + 1) * wp] for i in range(8)
    ]
    return (
        layer_out,
        inputs_grad,
        qkv_grad,
        qb_g,
        vb_g,
        proj_grad,
        pb_g,
        fg_g,
        fs_g,
        up_grad,
        packed[8 * wp :],
        down_grad,
        db_g,
        sg_g,
        ss_g,
    )


def solution(mesh):
    both = ("batch", "head")
    in_specs = (
        P(both, None),
        P("batch"),
        P("batch", None),
        P(None, both),
        P(both),
        P(both),
        P(None, both),
        P(both),
        P(both),
        P(both),
        P(None, both),
        P(both),
        P(both, None),
        P(both),
        P(both),
        P(both),
        P(both, None),
    )
    out_specs = (
        P(both, None),
        P(both, None),
        P("batch", "head"),
        P(both),
        P(both),
        P("head", "batch"),
        P(both),
        P(both),
        P(both),
        P(None, both),
        P(both),
        P(both, None),
        P(both),
        P(both),
        P(both),
    )
    return jax.shard_map(local, mesh=mesh, in_specs=in_specs, out_specs=out_specs, check_vma=False)
```

```python
import functools

import jax
import jax.numpy as jnp
from jax import lax
from jax.experimental import pallas as pl
from jax.experimental.pallas import tpu as pltpu
from jax.sharding import PartitionSpec as P

D = 768
HEADS = 12
HEAD_DIM = 64
FF = 3072
BIG = 512
SMALL = 128
UNITS = 4
NORM_EPS = 1e-12
F32 = jnp.float32
BF16 = jnp.bfloat16

CORE = [(i, i ^ 1) for i in range(4)]
XPAIR = [(i, i ^ 2) for i in range(4)]
YPAIR = [(i, i ^ 1) for i in range(8)]
ZPAIR = [[(i, i ^ (2 * k)) for i in range(8)] for k in range(4)]


def core_swap(v):
    return lax.ppermute(v, "head", CORE)


def x_swap(v):
    return lax.ppermute(v, "head", XPAIR)


def y_swap(v):
    return lax.ppermute(v, "batch", YPAIR)


def z_swap(v, k):
    return lax.ppermute(v, "batch", ZPAIR[k])


def after(value, other):
    return lax.optimization_barrier((value, other))[0]


def nt(a, b, out=F32):
    return lax.dot_general(a, b, (((1,), (1,)), ((), ())), preferred_element_type=F32).astype(out)


def nn(a, b, out=F32):
    return lax.dot_general(a, b, (((1,), (0,)), ((), ())), preferred_element_type=F32).astype(out)


def tn(a, b, out=F32):
    return lax.dot_general(a, b, (((0,), (0,)), ((), ())), preferred_element_type=F32).astype(out)


def gather_z(shard):
    got = [shard] + [z_swap(shard, k) for k in (1, 2, 3)]
    return jnp.stack(got[:2]), jnp.stack(got[2:])


def gather_xy(lo, hi):
    y_lo, x_hi = y_swap(lo), x_swap(hi)
    x_lo, y_hi = x_swap(lo), y_swap(hi)
    return [(lo, hi), (x_lo, x_hi), (y_lo, y_hi), (x_swap(y_lo), y_swap(x_hi))]


def gather_any(shard):
    whole = lax.all_gather(shard, "batch", axis=0)
    return [whole, x_swap(whole)]


def scatter_xy(parts):
    (g_lo, g_hi), (x_lo, x_hi), (y_lo, y_hi), (d_lo, d_hi) = parts
    from_x, from_y = x_swap(d_lo), y_swap(d_hi)
    y_hi, x_lo = y_swap(y_hi), x_swap(x_lo)
    y_lo, x_hi = y_swap(add_low(y_lo, from_x)), x_swap(add_low(x_hi, from_y))
    return combine(g_lo, g_hi, x_lo, x_hi, y_lo, y_hi)


def scatter_z(mine, others):
    return (mine,) + tuple(z_swap(others[k - 1], k) for k in (1, 2, 3))


def scatter_any(parts):
    total = parts[0].astype(F32) + x_swap(parts[1]).astype(F32)
    return lax.psum_scatter(total, "batch", scatter_dimension=0, tiled=False)


def est(flops, moved, trans=0):
    return pl.CostEstimate(flops=int(flops), bytes_accessed=int(moved), transcendentals=int(trans))


def call(kernel, out_shape, operands, scratch=(), cost=None, limit=16):
    vmem = pl.BlockSpec(memory_space=pltpu.VMEM)
    single = not isinstance(out_shape, (tuple, list))
    return pl.pallas_call(
        kernel,
        out_shape=out_shape,
        in_specs=[pl.BlockSpec(memory_space=pltpu.SMEM)] + [vmem] * (len(operands) - 1),
        out_specs=vmem if single else [vmem] * len(out_shape),
        scratch_shapes=list(scratch),
        compiler_params=pltpu.CompilerParams(vmem_limit_bytes=limit << 20),
        cost_estimate=cost,
    )(*operands)


def add_low(a, b):
    return (a.astype(F32) + b.astype(F32)).astype(BF16)


def shape(dims, dtype=BF16):
    return jax.ShapeDtypeStruct(dims, dtype)


def combine_kernel(_, g_lo, g_hi, x_lo, x_hi, y_lo, y_hi, mine, one, two, three):
    outs = (mine, one, two, three)
    for k in range(4):
        g, xx, yy = (g_lo, x_lo, y_lo) if k < 2 else (g_hi, x_hi, y_hi)
        total = g[k % 2].astype(F32) + xx[k % 2].astype(F32) + yy[k % 2].astype(F32)
        outs[k][...] = total.astype(outs[k].dtype)


def combine(*parts):
    rows = parts[0].shape[1]
    mine, *others = call(
        combine_kernel,
        (shape((rows, D), F32),) + (shape((rows, D)),) * 3,
        (jnp.zeros((1,), jnp.int32), *parts),
        cost=est(8 * rows * D, 24 * rows * D),
    )
    return mine, others


def total_of(refs):
    return refs[0][...] + refs[1][...].astype(F32) + refs[2][...].astype(F32) + refs[3][...].astype(F32)


def finish_attend_kernel(_, mine, one, two, three, qkv, proj):
    total = total_of((mine, one, two, three))
    for hh in range(3):
        for t in range(3):
            at, to = 192 * t + 64 * hh, 192 * hh + 64 * t
            qkv[:, to : to + 64] = total[:, at : at + 64]
    proj[...] = total[:, 576:].T


def finish_attend(parts):
    rows = parts[0].shape[0]
    return call(
        finish_attend_kernel,
        (shape((rows, 576), F32), shape((192, rows), F32)),
        (jnp.zeros((1,), jnp.int32), *parts),
        cost=est(8 * rows * D, 16 * rows * D),
    )


def finish_ffn_kernel(_, mine, one, two, three, up, down):
    half = mine.shape[0] // 2
    total = total_of((mine, one, two, three))
    up[...] = total[:half].T
    down[...] = total[half:]


def finish_ffn(parts):
    half = parts[0].shape[0] // 2
    return call(
        finish_ffn_kernel,
        (shape((D, half), F32), shape((half, D), F32)),
        (jnp.zeros((1,), jnp.int32), *parts),
        cost=est(8 * half * D, 32 * half * D),
    )


def flip(a, bit):
    return a + bit - 2 * a * bit


def order_kernel(rows_q, rows_p, place, *refs):
    sources, (wq, wp, small) = refs[:16], refs[16:]
    z, y, x, c = place[0], place[1], place[2], place[3]
    zl, zh = lax.rem(z, 2), lax.div(z, 2)
    p = flip(c, zl)
    total = jnp.zeros(small.shape, F32)
    for swapped in range(2):
        cc = c if swapped == 0 else 1 - c
        for spot in range(4):
            kx, ky = spot % 2, spot // 2
            pair = sources[8 * swapped + 2 * spot : 8 * swapped + 2 * spot + 2]
            j = flip(y, ky) * 4 + flip(x, kx) * 2 + cc
            for i in range(2):
                wq[flip(zh, i) * 8 + j] = pair[i][p, 0:rows_q]
            for kz in range(4):
                zi = flip(zl, kz % 2) + 2 * flip(zh, kz // 2)
                src = pair[kz // 2]
                wp[zi * 8 + j] = src[kz % 2, rows_q : rows_q + rows_p]
                total = total + src[kz % 2, rows_q + rows_p :].astype(F32)
    small[...] = total


def order_weights(own, swapped, place, rows_q, rows_p, rows_s):
    return call(
        functools.partial(order_kernel, rows_q, rows_p),
        (
            shape((16, rows_q, D)),
            shape((32, rows_p, D)),
            shape((rows_s, D), F32),
        ),
        (place, *own, *swapped),
        cost=est(1e6, 9e6),
    )


def live_units(meta):
    c, kind = meta[0], meta[1]
    first = meta[2]
    units = []
    for u in range(UNITS):
        far = jnp.clip(first - SMALL * u, 0, SMALL)
        units.append(jnp.where(kind == 1, far, meta[2 + u]))
    return c, kind, units


def place_of(index, c):
    return jnp.bitwise_xor(index, c * (BIG // 2))


def live_of(place, units):
    unit = lax.shift_right_logical(place, 7)
    inner = jnp.bitwise_and(place, SMALL - 1)
    count = jnp.where(
        unit < 2, jnp.where(unit == 0, units[0], units[1]), jnp.where(unit == 2, units[2], units[3])
    )
    return inner < count


def heads_of(row, c):
    parts = []
    for g in range(2):
        lo = row[:, 384 * g : 384 * g + 192]
        hi = row[:, 384 * g + 192 : 384 * g + 384]
        parts.append(jnp.where(c == 0, lo, hi))
    return jnp.concatenate(parts, 1)


def attend_kernel(meta, x0, x1, w, small, q, k, v, ctx0, ctx1, probs, wr, mask):
    c, kind, units = live_units(meta)
    half = x0.shape[0]
    for t in range(3):
        for hd in range(6):
            src = ((hd // 3) * 9 + (hd % 3) * 3 + t) * HEAD_DIM
            dst = (t * 6 + hd) * HEAD_DIM
            wr[dst : dst + HEAD_DIM] = w[src : src + HEAD_DIM]
    biases = (heads_of(small[0:1], c), None, heads_of(small[1:2], c))
    for t, ref in enumerate((q, k, v)):
        for i, xr in enumerate((x0, x1)):
            val = nt(xr[...], wr[384 * t : 384 * t + 384])
            if biases[t] is not None:
                val = val + biases[t]
            ref[half * i : half * i + half] = val.astype(BF16)
    rows = lax.broadcasted_iota(jnp.int32, (BIG, BIG), 0)
    cols = lax.broadcasted_iota(jnp.int32, (BIG, BIG), 1)
    prow, pcol = place_of(rows, c), place_of(cols, c)
    same = jnp.logical_or(
        kind == 1, lax.shift_right_logical(prow, 7) == lax.shift_right_logical(pcol, 7)
    )
    mask[...] = jnp.where(jnp.logical_and(same, live_of(pcol, units)), 0.0, -1e30)
    lane = lax.broadcasted_iota(jnp.int32, (half, 128), 1)
    for pair in range(3):
        lanes = slice(128 * pair, 128 * pair + 128)
        kp, vp = k[:, lanes], v[:, lanes]
        for i, ctx in enumerate((ctx0, ctx1)):
            rws = slice(half * i, half * i + half)
            qp = q[rws, lanes] * jnp.asarray(HEAD_DIM**-0.5, BF16)
            outs = []
            for e in range(2):
                mine = (lane < HEAD_DIM) if e == 0 else (lane >= HEAD_DIM)
                s = nt(jnp.where(mine, qp, jnp.zeros_like(qp)), kp) + mask[rws]
                ex = jnp.exp(s - jnp.max(s, -1, keepdims=True))
                pr = (ex * (1.0 / jnp.sum(ex, -1, keepdims=True))).astype(BF16)
                probs[2 * pair + e, rws] = pr
                outs.append(nn(pr, vp))
            ctx[:, lanes] = jnp.where(lane < HEAD_DIM, outs[0], outs[1]).astype(BF16)


def attend(meta, x0, x1, w, small):
    half = x0.shape[0]
    n = 2 * half
    return call(
        attend_kernel,
        (
            shape((n, 384)),
            shape((n, 384)),
            shape((n, 384)),
            shape((half, 384)),
            shape((half, 384)),
            shape((6, n, n)),
            shape((1152, D)),
        ),
        (meta, x0, x1, w, small),
        scratch=[pltpu.VMEM((n, n), F32)],
        cost=est(2 * n * D * 1152 + 8 * n * n * 384, 9e6, 6 * n * n),
    )


def norm(values):
    center = values - jnp.mean(values, -1, keepdims=True)
    spread = jnp.mean(center * center, -1, keepdims=True)
    scale = lax.rsqrt(spread + NORM_EPS)
    return center * scale, scale


def norm_back(cot, normal, scale, gain):
    w = cot * gain
    return scale * (
        w - jnp.mean(w, -1, keepdims=True) - normal * jnp.mean(w * normal, -1, keepdims=True)
    )


def first_kernel(meta, x, ctx_own, ctx_in, wp, small, first, low, normal, scale):
    c = meta[0]
    mine = pl.multiple_of(c * 384, 128)
    theirs = pl.multiple_of((1 - c) * 384, 128)
    attn = nt(ctx_own[...], wp[:, pl.ds(mine, 384)]) + nt(ctx_in[...], wp[:, pl.ds(theirs, 384)])
    n, r = norm(x[...].astype(F32) + attn + small[2:3])
    out = n * small[3:4] + small[4:5]
    first[...] = out
    low[...] = out.astype(BF16)
    normal[...] = n
    scale[...] = jnp.broadcast_to(r, scale.shape)


def first_norm(meta, x, ctx_own, ctx_in, wp, small):
    n = x.shape[0]
    return call(
        first_kernel,
        (shape((n, D), F32), shape((n, D)), shape((n, D), F32), shape((n, 128), F32)),
        (meta, x, ctx_own, ctx_in, wp, small),
        cost=est(2 * n * D * D, 5e6),
    )


def ffn_weights(refs):
    if len(refs[0].shape) == 2:
        return refs[0][...], refs[1][...]
    half = refs[0].shape[1] // 2
    blocks = [(r, i) for r in refs for i in range(r.shape[0])]
    up = jnp.concatenate([r[i, 0:half] for r, i in blocks])
    down = jnp.concatenate([r[i, half : 2 * half] for r, i in blocks])
    return up, down


def ffn_kernel(first, meta, x0, x1, ub, w0, w1, *refs):
    if first:
        in0 = in1 = None
    else:
        (in0, in1), refs = refs[:2], refs[2:]
    hid, slope, out0, out1 = refs
    half = x0.shape[0]
    uw, dw = ffn_weights((w0, w1))
    for i, (xr, before, out) in enumerate(((x0, in0, out0), (x1, in1, out1))):
        rws = slice(half * i, half * i + half)
        up = nt(xr[...], uw) + ub[...]
        phi = 0.5 + 0.5 * lax.erf(up * (2.0**-0.5))
        hd = (up * phi).astype(BF16)
        hid[rws] = hd
        slope[rws] = (phi + up * jnp.exp(-0.5 * up * up) * 0.3989422804014327).astype(BF16)
        part = nn(hd, dw)
        out[...] = part if before is None else before[...] + part


def ffn(meta, x0, x1, ub, weights, sums):
    half, width = x0.shape[0], ub.shape[1]
    n = 2 * half
    return call(
        functools.partial(ffn_kernel, not sums),
        (shape((n, width)), shape((n, width)), shape((half, D), F32), shape((half, D), F32)),
        (meta, x0, x1, ub, *weights, *sums),
        cost=est(4 * n * D * width, 4 * D * width + 5e6, 2 * n * width),
    )


def second_kernel(meta, first, part, got, small, cot, out, sum_two, low, sums):
    c, _, units = live_units(meta)
    n, r = norm(first[...] + (part[...] + got[...] + small[5:6]))
    out[...] = (n * small[6:7] + small[7:8]).astype(BF16)
    index = lax.broadcasted_iota(jnp.int32, (first.shape[0], 1), 0)
    live = live_of(place_of(index, c), units)
    oc = jnp.where(live, cot[...].astype(F32), 0.0)
    st = norm_back(oc, n, r, small[6:7])
    sum_two[...] = st
    lo = st.astype(BF16)
    low[...] = lo
    sums[0:1] = jnp.sum(lo.astype(F32), 0, keepdims=True)
    sums[1:2] = jnp.sum(oc * n, 0, keepdims=True)
    sums[2:3] = jnp.sum(oc, 0, keepdims=True)


def second_norm(meta, first, part, got, small, cot):
    n = first.shape[0]
    return call(
        second_kernel,
        (shape((n, D)), shape((n, D), F32), shape((n, D)), shape((3, D), F32)),
        (meta, first, part, got, small, cot),
        cost=est(40 * n * D, 5e6),
    )


def ffn_back_kernel(first, meta, d0, d1, x0, x1, w0, w1, hid, slope, *refs):
    if first:
        in0 = in1 = None
    else:
        (in0, in1), refs = refs[:2], refs[2:]
    g0, g1, ub, out0, out1 = refs
    half = x0.shape[0]
    uw, dw = ffn_weights((w0, w1))
    cots = []
    for i, (d, before, out) in enumerate(((d0, in0, out0), (d1, in1, out1))):
        rws = slice(half * i, half * i + half)
        uc = (nt(d[...], dw) * slope[rws].astype(F32)).astype(BF16)
        cots.append(uc)
        part = nn(uc, uw)
        out[...] = part if before is None else before[...] + part
    ub[...] = jnp.sum(cots[0].astype(F32), 0, keepdims=True) + jnp.sum(
        cots[1].astype(F32), 0, keepdims=True
    )
    dg = (tn(hid[0:half], d0[...]) + tn(hid[half : 2 * half], d1[...])).astype(BF16)
    ug = (tn(cots[0], x0[...]) + tn(cots[1], x1[...])).astype(BF16)
    if len(g0.shape) == 2:
        g0[...], g1[...] = ug, dg
    else:
        rows = g0.shape[1] // 2
        at = 0
        for g in (g0, g1):
            for i in range(g.shape[0]):
                g[i, 0:rows] = ug[at : at + rows]
                g[i, rows : 2 * rows] = dg[at : at + rows]
                at += rows


def ffn_back(meta, d0, d1, x0, x1, weights, hid, slope, sums):
    half, width = x0.shape[0], hid.shape[1]
    return call(
        functools.partial(ffn_back_kernel, not sums),
        (
            shape(weights[0].shape),
            shape(weights[1].shape),
            shape((1, width), F32),
            shape((half, D), F32),
            shape((half, D), F32),
        ),
        (meta, d0, d1, x0, x1, *weights, hid, slope, *sums),
        cost=est(16 * half * D * width, 8 * D * width + 5e6),
    )


def first_back_kernel(meta, sum_two, part, got, normal, scale, small, sum_one, low, sums):
    fc = sum_two[...] + part[...] + got[...]
    n = normal[...]
    so = norm_back(fc, n, scale[:, 0:1], small[3:4])
    sum_one[...] = so
    lo = so.astype(BF16)
    low[...] = lo
    sums[0:1] = jnp.sum(lo.astype(F32), 0, keepdims=True)
    sums[1:2] = jnp.sum(fc * n, 0, keepdims=True)
    sums[2:3] = jnp.sum(fc, 0, keepdims=True)


def first_back(meta, sum_two, part, got, normal, scale, small):
    n = sum_two.shape[0]
    return call(
        first_back_kernel,
        (shape((n, D), F32), shape((n, D)), shape((3, D), F32)),
        (meta, sum_two, part, got, normal, scale, small),
        cost=est(30 * n * D, 5e6),
    )


def attend_back_kernel(
    sets, meta, a0, a1, x0, x1, wp, wr, q, k, v, ctx0, ctx1, probs, *refs
):
    outs, (in0, in1, sums, dctx, cots, grads) = refs[:sets], refs[sets:]
    c = meta[0]
    half = a0.shape[0]
    n = 2 * half
    wpo = wp[:, pl.ds(pl.multiple_of(c * 384, 128), 384)]
    dctx[0:half] = nn(a0[...], wpo).astype(BF16)
    dctx[half:n] = nn(a1[...], wpo).astype(BF16)
    lane = lax.broadcasted_iota(jnp.int32, (n, 128), 1)
    zero = jnp.zeros((n, 128), BF16)
    scale = HEAD_DIM**-0.5
    heads = [[], [], []]
    for pair in range(3):
        lanes = slice(128 * pair, 128 * pair + 128)
        qp, kp, vp, dp = q[:, lanes], k[:, lanes], v[:, lanes], dctx[:, lanes]
        dq = dk = dv = 0.0
        for e in range(2):
            mine = (lane < HEAD_DIM) if e == 0 else (lane >= HEAD_DIM)
            dh, kh, qh = jnp.where(mine, dp, zero), jnp.where(mine, kp, zero), jnp.where(mine, qp, zero)
            pr = probs[2 * pair + e]
            dv = dv + tn(pr, dh)
            pf = pr.astype(F32)
            t = pf * nt(dh, vp)
            ds = (t - pf * jnp.sum(t, -1, keepdims=True)).astype(BF16)
            dq = dq + nn(ds, kh)
            dk = dk + tn(ds, qh)
        for t, val in enumerate((dq * scale, dk * scale, dv)):
            val = val.astype(BF16)
            for e in range(2):
                hd = 2 * pair + e
                g, hh = hd // 3, hd % 3
                at = 640 * g + 192 * t + 64 * hh
                cots[:, at : at + 64] = val[:, 64 * e : 64 * e + 64]
            heads[t].append(val)
    for g in range(2):
        cots[:, 640 * g + 576 : 640 * g + 640] = jnp.zeros((n, 64), BF16)
    parts = [jnp.concatenate(heads[t], 1) for t in range(3)]
    for i, out in enumerate((in0, in1)):
        rws = slice(half * i, half * i + half)
        total = 0.0
        for t in range(3):
            total = total + nn(parts[t][rws], wr[384 * t : 384 * t + 384])
        out[...] = total
    for row, t in ((0, 0), (1, 2)):
        s = jnp.sum(parts[t].astype(F32), 0, keepdims=True)
        for g in range(2):
            sg = s[:, 192 * g : 192 * g + 192]
            sums[row : row + 1, 384 * g : 384 * g + 192] = jnp.where(c == 0, sg, 0.0)
            sums[row : row + 1, 384 * g + 192 : 384 * g + 384] = jnp.where(c == 1, sg, 0.0)
    for d in range(3):
        at = slice(256 * d, 256 * d + 256)
        full = tn(x0[:, at], cots[0:half]) + tn(x1[:, at], cots[half:n])
        pg = tn(a0[:, at], ctx0[...]) + tn(a1[:, at], ctx1[...])
        for g in range(2):
            grads[g, at, 0:576] = full[:, 640 * g : 640 * g + 576].astype(BF16)
            grads[g, at, 576:768] = pg[:, 192 * g : 192 * g + 192].astype(BF16)
    if sets == 1:
        outs[0][...] = grads[...]
    else:
        z, y, x = meta[6], meta[7], meta[8]
        rows = outs[0].shape[1]
        for spot in range(4):
            g, yi = flip(x, spot % 2), flip(y, spot // 2)
            for kz in range(4):
                zi = flip(lax.rem(z, 2), kz % 2) + 2 * flip(lax.div(z, 2), kz // 2)
                at = pl.multiple_of((2 * zi + yi) * rows, rows)
                outs[2 * spot + kz // 2][kz % 2] = grads[g, pl.ds(at, rows), :]


def attend_back(direct, meta, a0, a1, x0, x1, wp, wr, q, k, v, ctx0, ctx1, probs):
    half = a0.shape[0]
    n = 2 * half
    sets = (shape((2, 96, D)),) * 8 if direct else (shape((2, D, D)),)
    return call(
        functools.partial(attend_back_kernel, len(sets)),
        (*sets, shape((half, D), F32), shape((half, D), F32), shape((2, D), F32)),
        (meta, a0, a1, x0, x1, wp, wr, q, k, v, ctx0, ctx1, probs),
        scratch=[
            pltpu.VMEM((n, 384), BF16),
            pltpu.VMEM((n, 1280), BF16),
            pltpu.VMEM((2, D, D), BF16),
        ],
        cost=est(2 * n * D * 3500 + 14 * n * n * 384, 14e6),
    )


def local(
    inputs,
    bucket,
    lengths,
    qkv_weight,
    query_bias,
    value_bias,
    proj_weight,
    proj_bias,
    first_gain,
    first_shift,
    up_weight,
    up_bias,
    down_weight,
    down_bias,
    second_gain,
    second_shift,
    cotangent,
):
    head_count = lax.axis_size("head")
    batch_count = lax.axis_size("batch")
    devices = head_count * batch_count
    direct = batch_count == 8
    b = lax.axis_index("batch")
    h = lax.axis_index("head")
    me = b * head_count + h
    x, c = h // 2, h % 2
    z, y = b // 2, b % 2
    wq, wp, wf = 3 * D // devices, D // devices, FF // devices

    vectors = jnp.stack(
        [
            query_bias,
            value_bias,
            proj_bias,
            first_gain,
            first_shift,
            down_bias,
            second_gain,
            second_shift,
        ]
    )
    small = lax.dynamic_update_slice(jnp.zeros((16, D), BF16), vectors, (0, me * wp))
    per_row = D // wf
    small = lax.dynamic_update_slice(
        small, up_bias[None, :], (8 + me // per_row, (me % per_row) * wf)
    )
    proj_t = proj_weight.T.reshape(wp, 2, 2, 192).transpose(0, 2, 1, 3).reshape(wp, D)
    a_shard = jnp.concatenate([qkv_weight.T, proj_t, small])
    f_shard = jnp.concatenate([up_weight.T, down_weight])
    other_in = core_swap(inputs)
    meta = jnp.concatenate(
        [
            jnp.stack([c, lax.dynamic_index_in_dim(bucket, x, 0, keepdims=False)]),
            lax.dynamic_index_in_dim(lengths, x, 0, keepdims=False),
            jnp.stack([z, y, x]),
        ]
    ).astype(jnp.int32)

    k = jnp.arange(batch_count * 2)
    if direct:
        a_lo, a_hi = gather_z(a_shard)
        f_lo, f_hi = gather_z(after(f_shard, a_lo))
        a_own = [v for pair in gather_xy(a_lo, a_hi) for v in pair]
        f_lo, f_hi, _ = lax.optimization_barrier((f_lo, f_hi, a_own))
        f_all = gather_xy(f_lo, f_hi)
        a_swapped = [core_swap(v) for v in a_own]
        place = jnp.stack([z, y, x, c]).astype(jnp.int32)
        qkv_w, proj_w, small_all = order_weights(a_own, a_swapped, place, wq, wp, 16)
        qkv_w = qkv_w.reshape(2 * 576, D)
        proj_w = proj_w.reshape(D, D)
        kz = jnp.array([0, 1, 2, 3] * 4)
        ky = jnp.array([0] * 8 + [1] * 8)
        kx = jnp.array([0] * 4 + [1] * 4 + [0] * 4 + [1] * 4)
        owner = (z ^ kz) * 8 + (y ^ ky) * 4 + (x ^ kx) * 2 + c
    else:
        a_all = lax.all_gather(a_shard, ("batch", "head"), axis=0)
        qkv_all = a_all[:, :wq].reshape(2, 2, 576, D)
        qkv_w = lax.dynamic_index_in_dim(qkv_all, c, 1, keepdims=False).reshape(2 * 576, D)
        proj_w = a_all[:, wq : wq + wp].reshape(D, D)
        small_all = jnp.sum(a_all[:, wq + wp :].astype(F32), 0)
        f_all = [
            (v[:, :wf].reshape(-1, D), v[:, wf:].reshape(-1, D)) for v in gather_any(f_shard)
        ]
        owner = (k % batch_count) * 4 + (x ^ (k // batch_count)) * 2 + c
    spread = (owner[None, :] == jnp.arange(devices)[:, None]).astype(F32)
    ub_all = tn(spread, small_all[8:12].reshape(devices, wf)).reshape(1, FF // 2)

    q, kk, v, ctx_own, ctx_other, probs, wr = attend(meta, inputs, other_in, qkv_w, small_all)
    ctx_in = core_swap(ctx_other)
    first, first_low, first_n, first_r = first_norm(meta, inputs, ctx_own, ctx_in, proj_w, small_all)
    first_in = core_swap(first_low)
    sums = ()
    kept = []
    width = FF // 2 // len(f_all)
    for i, weights in enumerate(f_all):
        ub = ub_all[:, i * width : i * width + width]
        hid, slope, *sums = ffn(meta, first_low, first_in, ub, weights, sums)
        kept.append((weights, hid, slope))
    layer_out, sum_two, down_low, sums_two = second_norm(
        meta, first, sums[0], core_swap(sums[1]), small_all, cotangent
    )
    down_in = core_swap(down_low)

    sums = ()
    f_parts, ub_parts = [], []
    for weights, hid, slope in reversed(kept):
        g0, g1, ub, *sums = ffn_back(
            meta, down_low, down_in, first_low, first_in, weights, hid, slope, sums
        )
        f_parts.insert(0, (g0, g1))
        ub_parts.insert(0, ub)
    sum_one, attn_low, sums_one = first_back(
        meta, sum_two, sums[0], core_swap(sums[1]), first_n, first_r, small_all
    )
    attn_in = core_swap(attn_low)
    *a_grads, in_own, in_other, sums_zero = attend_back(
        direct,
        meta,
        attn_low,
        attn_in,
        inputs,
        other_in,
        proj_w,
        wr,
        q,
        kk,
        v,
        ctx_own,
        ctx_other,
        probs,
    )
    inputs_grad = (sum_one + in_own + core_swap(in_other)).astype(BF16)

    if direct:
        f_sums = scatter_z(*scatter_xy(f_parts))
        up_grad, down_grad = finish_ffn(f_sums)
        a_parts = [tuple(a_grads[2 * i : 2 * i + 2]) for i in range(4)]
        qkv_grad, proj_grad = finish_attend(scatter_z(*scatter_xy(a_parts)))
    else:
        wb = D // batch_count
        a_grads = a_grads[0].reshape(2, batch_count, wb, D)
        a_mine = scatter_any(
            [
                lax.dynamic_index_in_dim(a_grads, x, 0, keepdims=False),
                lax.dynamic_index_in_dim(a_grads, 1 - x, 0, keepdims=False),
            ]
        )
        f_mine = scatter_any(
            [
                jnp.concatenate(
                    [ug.reshape(batch_count, wf, D), dg.reshape(batch_count, wf, D)], 1
                )
                for ug, dg in f_parts
            ]
        )
        qkv_grad = a_mine[:, :576].reshape(wb, 3, 3, HEAD_DIM).transpose(0, 2, 1, 3)
        qkv_grad = qkv_grad.reshape(wb, 576)
        proj_grad = a_mine[:, 576:].T
        up_grad, down_grad = f_mine[:wf].T, f_mine[wf:]

    vecs = jnp.concatenate([sums_zero, sums_one, sums_two])
    vecs = vecs.reshape(8, devices, wp).transpose(1, 0, 2).reshape(devices, 8 * wp)
    ubias = jnp.concatenate(ub_parts, 1).reshape(batch_count * 2, wf)
    ubias = lax.dot_general(
        spread, ubias, (((1,), (0,)), ((), ())), precision=lax.Precision.HIGHEST
    )
    packed = jnp.concatenate([vecs, ubias], 1)
    packed = lax.all_to_all(packed, ("batch", "head"), split_axis=0, concat_axis=0, tiled=True)
    packed = jnp.sum(packed, 0)
    qb_g, vb_g, pb_g, fg_g, fs_g, db_g, sg_g, ss_g = [
        packed[i * wp : (i + 1) * wp] for i in range(8)
    ]
    return (
        layer_out,
        inputs_grad,
        qkv_grad,
        qb_g,
        vb_g,
        proj_grad,
        pb_g,
        fg_g,
        fs_g,
        up_grad,
        packed[8 * wp :],
        down_grad,
        db_g,
        sg_g,
        ss_g,
    )


def solution(mesh):
    both = ("batch", "head")
    in_specs = (
        P(both, None),
        P("batch"),
        P("batch", None),
        P(None, both),
        P(both),
        P(both),
        P(None, both),
        P(both),
        P(both),
        P(both),
        P(None, both),
        P(both),
        P(both, None),
        P(both),
        P(both),
        P(both),
        P(both, None),
    )
    out_specs = (
        P(both, None),
        P(both, None),
        P("batch", "head"),
        P(both),
        P(both),
        P("head", "batch"),
        P(both),
        P(both),
        P(both),
        P(None, both),
        P(both),
        P(both, None),
        P(both),
        P(both),
        P(both),
    )
    return jax.shard_map(local, mesh=mesh, in_specs=in_specs, out_specs=out_specs, check_vma=False)
```

```python
import functools

import jax
import jax.numpy as jnp
from jax import lax
from jax.experimental import pallas as pl
from jax.experimental.pallas import tpu as pltpu
from jax.sharding import PartitionSpec as P

D = 768
HEADS = 12
HEAD_DIM = 64
FF = 3072
BIG = 512
SMALL = 128
UNITS = 4
NORM_EPS = 1e-12
F32 = jnp.float32
BF16 = jnp.bfloat16

CORE = [(i, i ^ 1) for i in range(4)]
XPAIR = [(i, i ^ 2) for i in range(4)]
YPAIR = [(i, i ^ 1) for i in range(8)]
ZPAIR = [[(i, i ^ (2 * k)) for i in range(8)] for k in range(4)]


def core_swap(v):
    return lax.ppermute(v, "head", CORE)


def x_swap(v):
    return lax.ppermute(v, "head", XPAIR)


def y_swap(v):
    return lax.ppermute(v, "batch", YPAIR)


def z_swap(v, k):
    return lax.ppermute(v, "batch", ZPAIR[k])


def after(value, other):
    return lax.optimization_barrier((value, other))[0]


def nt(a, b, out=F32):
    return lax.dot_general(a, b, (((1,), (1,)), ((), ())), preferred_element_type=F32).astype(out)


def nn(a, b, out=F32):
    return lax.dot_general(a, b, (((1,), (0,)), ((), ())), preferred_element_type=F32).astype(out)


def tn(a, b, out=F32):
    return lax.dot_general(a, b, (((0,), (0,)), ((), ())), preferred_element_type=F32).astype(out)


def z_line(shard):
    return [shard] + [z_swap(shard, k) for k in (1, 2, 3)]


def gather_four(z):
    x, y = x_swap(z), y_swap(z)
    return [z, x, y, x_swap(y[:2]), y_swap(x[2:])]


def gather_xy(lo, hi):
    y_lo, x_hi = y_swap(lo), x_swap(hi)
    x_lo, y_hi = x_swap(lo), y_swap(hi)
    return [(lo, hi), (x_lo, x_hi), (y_lo, y_hi), (x_swap(y_lo), y_swap(x_hi))]


def gather_any(shard):
    whole = lax.all_gather(shard, "batch", axis=0)
    return [whole, x_swap(whole)]


def scatter_first(parts):
    (g_lo, g_hi), (x_lo, x_hi), (y_lo, y_hi), (d_lo, d_hi) = parts
    from_x, from_y = x_swap(d_lo), y_swap(d_hi)
    y_lo, x_hi = add_low(y_lo, from_x), add_low(x_hi, from_y)
    return (g_lo, g_hi, x_lo, x_hi, y_lo, y_hi), (y_lo, x_hi)


def scatter_xy(g_lo, g_hi, x_lo, x_hi, y_lo, y_hi):
    y_hi, x_lo = y_swap(y_hi), x_swap(x_lo)
    y_lo, x_hi = y_swap(y_lo), x_swap(x_hi)
    return combine(g_lo, g_hi, x_lo, x_hi, y_lo, y_hi)


def scatter_z(mine, others):
    return (mine,) + tuple(z_swap(others[k - 1], k) for k in (1, 2, 3))


def scatter_any(parts):
    total = parts[0].astype(F32) + x_swap(parts[1]).astype(F32)
    return lax.psum_scatter(total, "batch", scatter_dimension=0, tiled=False)


def est(flops, moved, trans=0):
    return pl.CostEstimate(flops=int(flops), bytes_accessed=int(moved), transcendentals=int(trans))


def call(kernel, out_shape, operands, scratch=(), cost=None, limit=16, far_in=(), far_out=(), sems=0):
    vmem = pl.BlockSpec(memory_space=pltpu.VMEM)
    hbm = pl.BlockSpec(memory_space=pltpu.HBM)
    smem = pl.BlockSpec(memory_space=pltpu.SMEM)
    ins = [smem] + [hbm if i in far_in else vmem for i in range(1, len(operands))]
    outs = [hbm if i in far_out else vmem for i in range(len(out_shape))]
    scratch = list(scratch) + ([pltpu.SemaphoreType.DMA((sems,))] if sems else [])
    operands = [
        pltpu.with_memory_space_constraint(v, pltpu.HBM) if i in far_in else v
        for i, v in enumerate(operands)
    ]
    out_shape = [
        pltpu.HBM(v.shape, v.dtype) if i in far_out else v for i, v in enumerate(out_shape)
    ]
    return pl.pallas_call(
        kernel,
        out_shape=out_shape,
        in_specs=ins,
        out_specs=outs,
        scratch_shapes=scratch,
        compiler_params=pltpu.CompilerParams(vmem_limit_bytes=limit << 20),
        cost_estimate=cost,
    )(*operands)


class Copies:
    def __init__(self, sems):
        self.sems, self.used, self.open = sems, 0, []

    def start(self, src, dst):
        copy = pltpu.make_async_copy(src, dst, self.sems.at[self.used])
        self.used += 1
        copy.start()
        self.open.append(copy)
        return copy

    def wait(self, *copies):
        for copy in copies or list(self.open):
            copy.wait()
            self.open.remove(copy)


def add_low(a, b):
    return (a.astype(F32) + b.astype(F32)).astype(BF16)


def shape(dims, dtype=BF16):
    return jax.ShapeDtypeStruct(dims, dtype)


def combine_kernel(_, g_lo, g_hi, x_lo, x_hi, y_lo, y_hi, mine, one, two, three):
    outs = (mine, one, two, three)
    for k in range(4):
        g, xx, yy = (g_lo, x_lo, y_lo) if k < 2 else (g_hi, x_hi, y_hi)
        total = g[k % 2].astype(F32) + xx[k % 2].astype(F32) + yy[k % 2].astype(F32)
        outs[k][...] = total.astype(outs[k].dtype)


def combine(*parts):
    rows = parts[0].shape[1]
    mine, *others = call(
        combine_kernel,
        (shape((rows, D), F32),) + (shape((rows, D)),) * 3,
        (jnp.zeros((1,), jnp.int32), *parts),
        cost=est(8 * rows * D, 24 * rows * D),
    )
    return mine, others


def total_of(refs):
    return refs[0][...] + refs[1][...].astype(F32) + refs[2][...].astype(F32) + refs[3][...].astype(F32)


def finish_attend_kernel(_, mine, one, two, three, qkv, proj):
    total = total_of((mine, one, two, three))
    for hh in range(3):
        for t in range(3):
            at, to = 192 * t + 64 * hh, 192 * hh + 64 * t
            qkv[:, to : to + 64] = total[:, at : at + 64]
    proj[...] = total[:, 576:].T


def finish_attend(parts):
    rows = parts[0].shape[0]
    return call(
        finish_attend_kernel,
        (shape((rows, 576), F32), shape((192, rows), F32)),
        (jnp.zeros((1,), jnp.int32), *parts),
        cost=est(8 * rows * D, 16 * rows * D),
    )


def finish_ffn_kernel(_, mine, one, two, three, up, down):
    half = mine.shape[0] // 2
    total = total_of((mine, one, two, three))
    up[...] = total[:half].T
    down[...] = total[half:]


def finish_ffn(parts):
    half = parts[0].shape[0] // 2
    return call(
        finish_ffn_kernel,
        (shape((D, half), F32), shape((half, D), F32)),
        (jnp.zeros((1,), jnp.int32), *parts),
        cost=est(8 * half * D, 32 * half * D),
    )


def flip(a, bit):
    return a + bit - 2 * a * bit


def live_units(meta):
    c, kind = meta[0], meta[1]
    first = meta[2]
    units = []
    for u in range(UNITS):
        far = jnp.clip(first - SMALL * u, 0, SMALL)
        units.append(jnp.where(kind == 1, far, meta[2 + u]))
    return c, kind, units


def place_of(index, c):
    return jnp.bitwise_xor(index, c * (BIG // 2))


def live_of(place, units):
    unit = lax.shift_right_logical(place, 7)
    inner = jnp.bitwise_and(place, SMALL - 1)
    count = jnp.where(
        unit < 2, jnp.where(unit == 0, units[0], units[1]), jnp.where(unit == 2, units[2], units[3])
    )
    return inner < count


def heads_of(row, c):
    parts = []
    for g in range(2):
        lo = row[:, 384 * g : 384 * g + 192]
        hi = row[:, 384 * g + 192 : 384 * g + 384]
        parts.append(jnp.where(c == 0, lo, hi))
    return jnp.concatenate(parts, 1)


def fetch_shards(meta, copies, sources, slots):
    c, z, y, x = meta[0], meta[6], meta[7], meta[8]
    zl, zh = lax.rem(z, 2), lax.div(z, 2)
    for swapped in range(2):
        cc = c if swapped == 0 else 1 - c
        zs, xs, ys, xa, xb = sources[5 * swapped : 5 * swapped + 5]
        for kx, ky, pair in ((0, 0, (zs,)), (1, 0, (xs,)), (0, 1, (ys,)), (1, 1, (xa, xb))):
            j = flip(y, ky) * 4 + flip(x, kx) * 2 + cc
            for kz in range(4):
                src = pair[0].at[kz] if len(pair) == 1 else pair[kz // 2].at[kz % 2]
                zi = flip(zl, kz % 2) + 2 * flip(zh, kz // 2)
                copies.start(src, slots.at[zi * 8 + j])


def attend_kernel(rows_q, rows_p, meta, x0, x1, *refs):
    sources = 10 if rows_q else 2
    weights, refs = refs[:sources], refs[sources:]
    (ctx0, ctx1, q_out, k_out, v_out, ctx_out, probs_out, wr_out), refs = refs[:8], refs[8:]
    if rows_q:
        (wp_out, small_out), refs = refs[:2], refs[2:]
        (q, k, v, ctx, probs, wr, mask, xs, slots, wp, small, sems) = refs
    else:
        (q, k, v, ctx, probs, wr, mask, xs, w, small, sems) = refs
    copies = Copies(sems)
    c, kind, units = live_units(meta)
    half = x0.shape[0]
    copies.start(x0, xs.at[0:half])
    copies.start(x1, xs.at[half : 2 * half])
    if rows_q:
        fetch_shards(meta, copies, weights, slots)
    else:
        copies.start(weights[0], w)
        copies.start(weights[1], small)
    rows = lax.broadcasted_iota(jnp.int32, (BIG, BIG), 0)
    cols = lax.broadcasted_iota(jnp.int32, (BIG, BIG), 1)
    prow, pcol = place_of(rows, c), place_of(cols, c)
    same = jnp.logical_or(
        kind == 1, lax.shift_right_logical(prow, 7) == lax.shift_right_logical(pcol, 7)
    )
    mask[...] = jnp.where(jnp.logical_and(same, live_of(pcol, units)), 0.0, -1e30)
    copies.wait()
    if rows_q:
        for g in range(2):
            cuts = jnp.concatenate([slots[16 * g + 8 * c + j, 0:rows_q] for j in range(8)])
            for t in range(3):
                for hh in range(3):
                    src, dst = (hh * 3 + t) * HEAD_DIM, (t * 6 + g * 3 + hh) * HEAD_DIM
                    wr[dst : dst + HEAD_DIM] = cuts[src : src + HEAD_DIM]
        small[...] = sum(slots[i, rows_q + rows_p :].astype(F32) for i in range(32))
    else:
        for t in range(3):
            for hd in range(6):
                src = ((hd // 3) * 9 + (hd % 3) * 3 + t) * HEAD_DIM
                dst = (t * 6 + hd) * HEAD_DIM
                wr[dst : dst + HEAD_DIM] = w[src : src + HEAD_DIM]
    copies.start(wr, wr_out)
    biases = (heads_of(small[0:1], c), None, heads_of(small[1:2], c))
    for t, (ref, out) in enumerate(((q, q_out), (k, k_out), (v, v_out))):
        val = nt(xs[...], wr[384 * t : 384 * t + 384])
        if biases[t] is not None:
            val = val + biases[t]
        ref[...] = val.astype(BF16)
        copies.start(ref, out)
    if rows_q:
        for i in range(32):
            wp[rows_p * i : rows_p * i + rows_p] = slots[i, rows_q : rows_q + rows_p]
        copies.start(wp, wp_out)
        copies.start(small, small_out)
    lane = lax.broadcasted_iota(jnp.int32, (half, 128), 1)
    for pair in range(3):
        lanes = slice(128 * pair, 128 * pair + 128)
        kp, vp = k[:, lanes], v[:, lanes]
        for i, near in enumerate((ctx0, ctx1)):
            rws = slice(half * i, half * i + half)
            qp = q[rws, lanes] * jnp.asarray(HEAD_DIM**-0.5, BF16)
            outs = []
            for e in range(2):
                mine = (lane < HEAD_DIM) if e == 0 else (lane >= HEAD_DIM)
                s = nt(jnp.where(mine, qp, jnp.zeros_like(qp)), kp) + mask[rws]
                ex = jnp.exp(s - jnp.max(s, -1, keepdims=True))
                pr = (ex * (1.0 / jnp.sum(ex, -1, keepdims=True))).astype(BF16)
                probs[2 * pair + e, rws] = pr
                outs.append(nn(pr, vp))
            val = jnp.where(lane < HEAD_DIM, outs[0], outs[1]).astype(BF16)
            ctx[rws, lanes] = val
            near[:, lanes] = val
        for e in range(2):
            copies.start(probs.at[2 * pair + e], probs_out.at[2 * pair + e])
    copies.start(ctx, ctx_out)
    copies.wait()


def attend(meta, x0, x1, weights, rows_q=0, rows_p=0, rows_s=16):
    half = x0.shape[0]
    n = 2 * half
    direct = rows_q > 0
    outs = [
        shape((half, 384)),
        shape((half, 384)),
        shape((n, 384)),
        shape((n, 384)),
        shape((n, 384)),
        shape((n, 384)),
        shape((6, n, n)),
        shape((1152, D)),
    ]
    scratch = [pltpu.VMEM((n, 384), BF16)] * 4 + [
        pltpu.VMEM((6, n, n), BF16),
        pltpu.VMEM((1152, D), BF16),
        pltpu.VMEM((n, n), F32),
        pltpu.VMEM((n, D), BF16),
    ]
    if direct:
        outs += [shape((D, D)), shape((rows_s, D), F32)]
        scratch += [
            pltpu.VMEM((32, rows_q + rows_p + rows_s, D), BF16),
            pltpu.VMEM((D, D), BF16),
            pltpu.VMEM((rows_s, D), F32),
        ]
    else:
        scratch += [pltpu.VMEM((1152, D), BF16), pltpu.VMEM((rows_s, D), F32)]
    operands = (meta, x0, x1, *weights)
    return call(
        functools.partial(attend_kernel, rows_q, rows_p),
        outs,
        operands,
        scratch=scratch,
        cost=est(2 * n * D * 1152 + 8 * n * n * 384, 12e6, 6 * n * n),
        limit=32,
        far_in=range(1, len(operands)),
        far_out=range(2, len(outs)),
        sems=50,
    )


def norm(values):
    center = values - jnp.mean(values, -1, keepdims=True)
    spread = jnp.mean(center * center, -1, keepdims=True)
    scale = lax.rsqrt(spread + NORM_EPS)
    return center * scale, scale


def norm_back(cot, normal, scale, gain):
    w = cot * gain
    return scale * (
        w - jnp.mean(w, -1, keepdims=True) - normal * jnp.mean(w * normal, -1, keepdims=True)
    )


def first_kernel(
    meta, x_in, ctx_own, ctx_in, wp_in, small_in, low, first_out, normal_out, scale, x, wp, small, first, normal, sems
):
    copies = Copies(sems)
    for src, dst in ((wp_in, wp), (x_in, x), (small_in, small)):
        copies.start(src, dst)
    c = meta[0]
    copies.wait()
    mine = pl.multiple_of(c * 384, 128)
    theirs = pl.multiple_of((1 - c) * 384, 128)
    attn = nt(ctx_own[...], wp[:, pl.ds(mine, 384)]) + nt(ctx_in[...], wp[:, pl.ds(theirs, 384)])
    n, r = norm(x[...].astype(F32) + attn + small[2:3])
    normal[...] = n
    copies.start(normal, normal_out)
    out = n * small[3:4] + small[4:5]
    first[...] = out
    copies.start(first, first_out)
    low[...] = out.astype(BF16)
    scale[...] = jnp.broadcast_to(r, scale.shape)
    copies.wait()


def first_norm(meta, x, ctx_own, ctx_in, wp, small):
    n = x.shape[0]
    return call(
        first_kernel,
        (shape((n, D)), shape((n, D), F32), shape((n, D), F32), shape((n, 128), F32)),
        (meta, x, ctx_own, ctx_in, wp, small),
        scratch=[
            pltpu.VMEM((n, D), BF16),
            pltpu.VMEM((D, D), BF16),
            pltpu.VMEM((16, D), F32),
            pltpu.VMEM((n, D), F32),
            pltpu.VMEM((n, D), F32),
        ],
        cost=est(2 * n * D * D, 5e6),
        far_in=(1, 4, 5),
        far_out=(1, 2),
        sems=5,
    )


def ffn_weights(refs):
    if len(refs[0].shape) == 2:
        return refs[0][...], refs[1][...]
    half = refs[0].shape[1] // 2
    blocks = [(r, i) for r in refs for i in range(r.shape[0])]
    up = jnp.concatenate([r[i, 0:half] for r, i in blocks])
    down = jnp.concatenate([r[i, half : 2 * half] for r, i in blocks])
    return up, down


def ffn_kernel(first, meta, x0, x1, ub, w0_in, w1_in, *refs):
    if first:
        in0 = in1 = None
    else:
        (in0, in1), refs = refs[:2], refs[2:]
    hid_out, slope_out, out0, out1, w0, w1, hid, slope, sems = refs
    copies = Copies(sems)
    copies.start(w0_in, w0)
    copies.start(w1_in, w1)
    copies.wait()
    half = x0.shape[0]
    uw, dw = ffn_weights((w0, w1))
    for i, (xr, before, out) in enumerate(((x0, in0, out0), (x1, in1, out1))):
        rws = slice(half * i, half * i + half)
        up = nt(xr[...], uw) + ub[...]
        phi = 0.5 + 0.5 * lax.erf(up * (2.0**-0.5))
        hd = (up * phi).astype(BF16)
        hid[rws] = hd
        slope[rws] = (phi + up * jnp.exp(-0.5 * up * up) * 0.3989422804014327).astype(BF16)
        copies.start(hid.at[rws], hid_out.at[rws])
        copies.start(slope.at[rws], slope_out.at[rws])
        part = nn(hd, dw)
        out[...] = part if before is None else before[...] + part
    copies.wait()


def ffn(meta, x0, x1, ub, weights, sums):
    half, width = x0.shape[0], ub.shape[1]
    n = 2 * half
    return call(
        functools.partial(ffn_kernel, not sums),
        (shape((n, width)), shape((n, width)), shape((half, D), F32), shape((half, D), F32)),
        (meta, x0, x1, ub, *weights, *sums),
        scratch=[pltpu.VMEM(w.shape, BF16) for w in weights] + [pltpu.VMEM((n, width), BF16)] * 2,
        cost=est(4 * n * D * width, 4 * D * width + 5e6, 2 * n * width),
        far_in=(4, 5),
        far_out=(0, 1),
        sems=6,
    )


def second_kernel(
    meta, first_in, part, got, small_in, cot_in, out, sum_two, low, sums, first, small, cot, sems
):
    copies = Copies(sems)
    for src, dst in ((first_in, first), (small_in, small), (cot_in, cot)):
        copies.start(src, dst)
    c, _, units = live_units(meta)
    copies.wait()
    n, r = norm(first[...] + (part[...] + got[...] + small[5:6]))
    out[...] = (n * small[6:7] + small[7:8]).astype(BF16)
    index = lax.broadcasted_iota(jnp.int32, (first.shape[0], 1), 0)
    live = live_of(place_of(index, c), units)
    oc = jnp.where(live, cot[...].astype(F32), 0.0)
    st = norm_back(oc, n, r, small[6:7])
    sum_two[...] = st
    lo = st.astype(BF16)
    low[...] = lo
    sums[0:1] = jnp.sum(lo.astype(F32), 0, keepdims=True)
    sums[1:2] = jnp.sum(oc * n, 0, keepdims=True)
    sums[2:3] = jnp.sum(oc, 0, keepdims=True)


def second_norm(meta, first, part, got, small, cot):
    n = first.shape[0]
    return call(
        second_kernel,
        (shape((n, D)), shape((n, D), F32), shape((n, D)), shape((3, D), F32)),
        (meta, first, part, got, small, cot),
        scratch=[pltpu.VMEM((n, D), F32), pltpu.VMEM((16, D), F32), pltpu.VMEM((n, D), BF16)],
        cost=est(40 * n * D, 5e6),
        far_in=(1, 4, 5),
        sems=3,
    )


def ffn_back_kernel(first, meta, d0, d1, x0, x1, w0_in, w1_in, hid_in, slope_in, *refs):
    if first:
        in0 = in1 = None
    else:
        (in0, in1), refs = refs[:2], refs[2:]
    g0, g1, ub, out0, out1, w0, w1, hid, slope, sems = refs
    copies = Copies(sems)
    for src, dst in ((w0_in, w0), (w1_in, w1), (slope_in, slope), (hid_in, hid)):
        copies.start(src, dst)
    copies.wait()
    half = x0.shape[0]
    uw, dw = ffn_weights((w0, w1))
    cots = []
    for i, (d, before, out) in enumerate(((d0, in0, out0), (d1, in1, out1))):
        rws = slice(half * i, half * i + half)
        uc = (nt(d[...], dw) * slope[rws].astype(F32)).astype(BF16)
        cots.append(uc)
        part = nn(uc, uw)
        out[...] = part if before is None else before[...] + part
    ub[...] = jnp.sum(cots[0].astype(F32), 0, keepdims=True) + jnp.sum(
        cots[1].astype(F32), 0, keepdims=True
    )
    dg = (tn(hid[0:half], d0[...]) + tn(hid[half : 2 * half], d1[...])).astype(BF16)
    ug = (tn(cots[0], x0[...]) + tn(cots[1], x1[...])).astype(BF16)
    if len(g0.shape) == 2:
        g0[...], g1[...] = ug, dg
    else:
        rows = g0.shape[1] // 2
        at = 0
        for g in (g0, g1):
            for i in range(g.shape[0]):
                g[i, 0:rows] = ug[at : at + rows]
                g[i, rows : 2 * rows] = dg[at : at + rows]
                at += rows


def ffn_back(meta, d0, d1, x0, x1, weights, hid, slope, sums):
    half, width = x0.shape[0], hid.shape[1]
    return call(
        functools.partial(ffn_back_kernel, not sums),
        (
            shape(weights[0].shape),
            shape(weights[1].shape),
            shape((1, width), F32),
            shape((half, D), F32),
            shape((half, D), F32),
        ),
        (meta, d0, d1, x0, x1, *weights, hid, slope, *sums),
        scratch=[pltpu.VMEM(v.shape, BF16) for v in (*weights, hid, slope)],
        cost=est(1000, 1000),
        far_in=(5, 6, 7, 8),
        sems=4,
    )


def first_back_kernel(
    meta, sum_two, part, got, normal_in, scale, small_in, sum_one, low, sums, normal, small, sems
):
    copies = Copies(sems)
    copies.start(normal_in, normal)
    copies.start(small_in, small)
    copies.wait()
    fc = sum_two[...] + part[...] + got[...]
    n = normal[...]
    so = norm_back(fc, n, scale[:, 0:1], small[3:4])
    sum_one[...] = so
    lo = so.astype(BF16)
    low[...] = lo
    sums[0:1] = jnp.sum(lo.astype(F32), 0, keepdims=True)
    sums[1:2] = jnp.sum(fc * n, 0, keepdims=True)
    sums[2:3] = jnp.sum(fc, 0, keepdims=True)


def first_back(meta, sum_two, part, got, normal, scale, small):
    n = sum_two.shape[0]
    return call(
        first_back_kernel,
        (shape((n, D), F32), shape((n, D)), shape((3, D), F32)),
        (meta, sum_two, part, got, normal, scale, small),
        scratch=[pltpu.VMEM((n, D), F32), pltpu.VMEM((16, D), F32)],
        cost=est(30 * n * D, 5e6),
        far_in=(4, 6),
        sems=2,
    )


def attend_back_kernel(sets, meta, a0, a1, *refs):
    far, outs, (in0, in1, sums), refs = refs[:9], refs[9 : 9 + sets], refs[9 + sets : 12 + sets], refs[12 + sets :]
    wp, v, probs, k, q, wr, x0, x1, ctx, dctx, cots, grads, sems = refs
    copies = Copies(sems)
    near = (wp, v, probs, k, q, wr, x0, x1, ctx)
    got = [copies.start(src, dst) for src, dst in zip(far, near)]
    c = meta[0]
    half = a0.shape[0]
    n = 2 * half
    copies.wait(got[0])
    wpo = wp[:, pl.ds(pl.multiple_of(c * 384, 128), 384)]
    dctx[0:half] = nn(a0[...], wpo).astype(BF16)
    dctx[half:n] = nn(a1[...], wpo).astype(BF16)
    copies.wait()
    lane = lax.broadcasted_iota(jnp.int32, (n, 128), 1)
    zero = jnp.zeros((n, 128), BF16)
    scale = HEAD_DIM**-0.5
    heads = [[], [], []]
    for pair in range(3):
        lanes = slice(128 * pair, 128 * pair + 128)
        qp, kp, vp, dp = q[:, lanes], k[:, lanes], v[:, lanes], dctx[:, lanes]
        dq = dk = dv = 0.0
        for e in range(2):
            mine = (lane < HEAD_DIM) if e == 0 else (lane >= HEAD_DIM)
            dh, kh, qh = jnp.where(mine, dp, zero), jnp.where(mine, kp, zero), jnp.where(mine, qp, zero)
            pr = probs[2 * pair + e]
            dv = dv + tn(pr, dh)
            pf = pr.astype(F32)
            t = pf * nt(dh, vp)
            ds = (t - pf * jnp.sum(t, -1, keepdims=True)).astype(BF16)
            dq = dq + nn(ds, kh)
            dk = dk + tn(ds, qh)
        for t, val in enumerate((dq * scale, dk * scale, dv)):
            val = val.astype(BF16)
            for e in range(2):
                hd = 2 * pair + e
                g, hh = hd // 3, hd % 3
                at = 640 * g + 192 * t + 64 * hh
                cots[:, at : at + 64] = val[:, 64 * e : 64 * e + 64]
            heads[t].append(val)
    for g in range(2):
        cots[:, 640 * g + 576 : 640 * g + 640] = jnp.zeros((n, 64), BF16)
    parts = [jnp.concatenate(heads[t], 1) for t in range(3)]
    for i, out in enumerate((in0, in1)):
        rws = slice(half * i, half * i + half)
        total = 0.0
        for t in range(3):
            total = total + nn(parts[t][rws], wr[384 * t : 384 * t + 384])
        out[...] = total
    for row, t in ((0, 0), (1, 2)):
        s = jnp.sum(parts[t].astype(F32), 0, keepdims=True)
        for g in range(2):
            sg = s[:, 192 * g : 192 * g + 192]
            sums[row : row + 1, 384 * g : 384 * g + 192] = jnp.where(c == 0, sg, 0.0)
            sums[row : row + 1, 384 * g + 192 : 384 * g + 384] = jnp.where(c == 1, sg, 0.0)
    for d in range(3):
        at = slice(256 * d, 256 * d + 256)
        full = tn(x0[:, at], cots[0:half]) + tn(x1[:, at], cots[half:n])
        pg = tn(a0[:, at], ctx[0:half]) + tn(a1[:, at], ctx[half:n])
        for g in range(2):
            grads[g, at, 0:576] = full[:, 640 * g : 640 * g + 576].astype(BF16)
            grads[g, at, 576:768] = pg[:, 192 * g : 192 * g + 192].astype(BF16)
    if sets == 1:
        copies.start(grads, outs[0])
    else:
        z, y, x = meta[6], meta[7], meta[8]
        rows = outs[0].shape[1]
        for spot in (3, 2, 1, 0):
            g, yi = flip(x, spot % 2), flip(y, spot // 2)
            for kz in range(4):
                zi = flip(lax.rem(z, 2), kz % 2) + 2 * flip(lax.div(z, 2), kz // 2)
                at = pl.multiple_of((2 * zi + yi) * rows, rows)
                copies.start(grads.at[g, pl.ds(at, rows)], outs[2 * spot + kz // 2].at[kz % 2])
    copies.wait()


def attend_back(direct, meta, a0, a1, x0, x1, wp, wr, q, k, v, ctx, probs):
    half = a0.shape[0]
    n = 2 * half
    sets = (shape((2, 96, D)),) * 8 if direct else (shape((2, D, D)),)
    far = (wp, v, probs, k, q, wr, x0, x1, ctx)
    return call(
        functools.partial(attend_back_kernel, len(sets)),
        (*sets, shape((half, D), F32), shape((half, D), F32), shape((2, D), F32)),
        (meta, a0, a1, *far),
        scratch=[pltpu.VMEM(f.shape, BF16) for f in far]
        + [pltpu.VMEM((n, 384), BF16), pltpu.VMEM((n, 1280), BF16), pltpu.VMEM((2, D, D), BF16)],
        cost=est(2 * n * D * 3500 + 14 * n * n * 384, 14e6),
        limit=32,
        far_in=range(3, 12),
        far_out=range(len(sets)),
        sems=26,
    )


def local(
    inputs,
    bucket,
    lengths,
    qkv_weight,
    query_bias,
    value_bias,
    proj_weight,
    proj_bias,
    first_gain,
    first_shift,
    up_weight,
    up_bias,
    down_weight,
    down_bias,
    second_gain,
    second_shift,
    cotangent,
):
    head_count = lax.axis_size("head")
    batch_count = lax.axis_size("batch")
    devices = head_count * batch_count
    direct = batch_count == 8
    b = lax.axis_index("batch")
    h = lax.axis_index("head")
    me = b * head_count + h
    x, c = h // 2, h % 2
    z, y = b // 2, b % 2
    wq, wp, wf = 3 * D // devices, D // devices, FF // devices

    vectors = jnp.stack(
        [
            query_bias,
            value_bias,
            proj_bias,
            first_gain,
            first_shift,
            down_bias,
            second_gain,
            second_shift,
        ]
    )
    small = lax.dynamic_update_slice(jnp.zeros((16, D), BF16), vectors, (0, me * wp))
    per_row = D // wf
    small = lax.dynamic_update_slice(
        small, up_bias[None, :], (8 + me // per_row, (me % per_row) * wf)
    )
    proj_t = proj_weight.T.reshape(wp, 2, 2, 192).transpose(0, 2, 1, 3).reshape(wp, D)
    a_shard = jnp.concatenate([qkv_weight.T, proj_t, small])
    f_shard = jnp.concatenate([up_weight.T, down_weight])
    other_in = core_swap(inputs)
    meta = jnp.concatenate(
        [
            jnp.stack([c, lax.dynamic_index_in_dim(bucket, x, 0, keepdims=False)]),
            lax.dynamic_index_in_dim(lengths, x, 0, keepdims=False),
            jnp.stack([z, y, x]),
        ]
    ).astype(jnp.int32)

    k = jnp.arange(batch_count * 2)
    if direct:
        a_z = jnp.stack(z_line(a_shard))
        f_z = z_line(after(f_shard, a_z))
        f_lo, f_hi = jnp.stack(f_z[:2]), jnp.stack(f_z[2:])
        a_own = gather_four(a_z)
        f_lo, f_hi, _ = lax.optimization_barrier((f_lo, f_hi, a_own))
        f_all = gather_xy(f_lo, f_hi)
        a_swapped = [core_swap(v) for v in a_own]
        ctx_own, ctx_other, q, kk, v, ctx, probs, wr, proj_w, small_all = attend(
            meta, inputs, other_in, (*a_own, *a_swapped), wq, wp
        )
        kz = jnp.array([0, 1, 2, 3] * 4)
        ky = jnp.array([0] * 8 + [1] * 8)
        kx = jnp.array([0] * 4 + [1] * 4 + [0] * 4 + [1] * 4)
        owner = (z ^ kz) * 8 + (y ^ ky) * 4 + (x ^ kx) * 2 + c
    else:
        a_all = lax.all_gather(a_shard, ("batch", "head"), axis=0)
        qkv_all = a_all[:, :wq].reshape(2, 2, 576, D)
        qkv_w = lax.dynamic_index_in_dim(qkv_all, c, 1, keepdims=False).reshape(2 * 576, D)
        proj_w = a_all[:, wq : wq + wp].reshape(D, D)
        small_all = jnp.sum(a_all[:, wq + wp :].astype(F32), 0)
        ctx_own, ctx_other, q, kk, v, ctx, probs, wr = attend(
            meta, inputs, other_in, (qkv_w, small_all)
        )
        f_all = [
            (v[:, :wf].reshape(-1, D), v[:, wf:].reshape(-1, D)) for v in gather_any(f_shard)
        ]
        owner = (k % batch_count) * 4 + (x ^ (k // batch_count)) * 2 + c
    spread = (owner[None, :] == jnp.arange(devices)[:, None]).astype(F32)
    ub_all = tn(spread, small_all[8:12].reshape(devices, wf)).reshape(1, FF // 2)

    ctx_in = core_swap(ctx_other)
    first_low, first, first_n, first_r = first_norm(meta, inputs, ctx_own, ctx_in, proj_w, small_all)
    first_in = core_swap(first_low)
    sums = ()
    kept = []
    width = FF // 2 // len(f_all)
    for i, weights in enumerate(f_all):
        ub = ub_all[:, i * width : i * width + width]
        hid, slope, *sums = ffn(meta, first_low, first_in, ub, weights, sums)
        kept.append((weights, hid, slope))
    layer_out, sum_two, down_low, sums_two = second_norm(
        meta, first, sums[0], core_swap(sums[1]), small_all, cotangent
    )
    down_in = core_swap(down_low)

    sums = ()
    f_parts, ub_parts = [], []
    for weights, hid, slope in reversed(kept):
        g0, g1, ub, *sums = ffn_back(
            meta, down_low, down_in, first_low, first_in, weights, hid, slope, sums
        )
        f_parts.insert(0, (g0, g1))
        ub_parts.insert(0, ub)
    part_own, part_other = sums
    if direct:
        f_parts, f_moved = scatter_first(f_parts)
        part_other = lax.optimization_barrier((part_other, f_moved))[0]
    sum_one, attn_low, sums_one = first_back(
        meta, sum_two, part_own, core_swap(part_other), first_n, first_r, small_all
    )
    attn_in = core_swap(attn_low)
    *a_grads, in_own, in_other, sums_zero = attend_back(
        direct,
        meta,
        attn_low,
        attn_in,
        inputs,
        other_in,
        proj_w,
        wr,
        q,
        kk,
        v,
        ctx,
        probs,
    )
    inputs_grad = (sum_one + in_own + core_swap(in_other)).astype(BF16)

    if direct:
        f_sums = scatter_z(*scatter_xy(*f_parts))
        up_grad, down_grad = finish_ffn(f_sums)
        a_parts = [tuple(a_grads[2 * i : 2 * i + 2]) for i in range(4)]
        a_parts, _ = scatter_first(a_parts)
        qkv_grad, proj_grad = finish_attend(scatter_z(*scatter_xy(*a_parts)))
    else:
        wb = D // batch_count
        a_grads = a_grads[0].reshape(2, batch_count, wb, D)
        a_mine = scatter_any(
            [
                lax.dynamic_index_in_dim(a_grads, x, 0, keepdims=False),
                lax.dynamic_index_in_dim(a_grads, 1 - x, 0, keepdims=False),
            ]
        )
        f_mine = scatter_any(
            [
                jnp.concatenate(
                    [ug.reshape(batch_count, wf, D), dg.reshape(batch_count, wf, D)], 1
                )
                for ug, dg in f_parts
            ]
        )
        qkv_grad = a_mine[:, :576].reshape(wb, 3, 3, HEAD_DIM).transpose(0, 2, 1, 3)
        qkv_grad = qkv_grad.reshape(wb, 576)
        proj_grad = a_mine[:, 576:].T
        up_grad, down_grad = f_mine[:wf].T, f_mine[wf:]

    vecs = jnp.concatenate([sums_zero, sums_one, sums_two])
    vecs = vecs.reshape(8, devices, wp).transpose(1, 0, 2).reshape(devices, 8 * wp)
    ubias = jnp.concatenate(ub_parts, 1).reshape(batch_count * 2, wf)
    ubias = lax.dot_general(
        spread, ubias, (((1,), (0,)), ((), ())), precision=lax.Precision.HIGHEST
    )
    packed = jnp.concatenate([vecs, ubias], 1)
    packed = lax.all_to_all(packed, ("batch", "head"), split_axis=0, concat_axis=0, tiled=True)
    packed = jnp.sum(packed, 0)
    qb_g, vb_g, pb_g, fg_g, fs_g, db_g, sg_g, ss_g = [
        packed[i * wp : (i + 1) * wp] for i in range(8)
    ]
    return (
        layer_out,
        inputs_grad,
        qkv_grad,
        qb_g,
        vb_g,
        proj_grad,
        pb_g,
        fg_g,
        fs_g,
        up_grad,
        packed[8 * wp :],
        down_grad,
        db_g,
        sg_g,
        ss_g,
    )


def solution(mesh):
    both = ("batch", "head")
    in_specs = (
        P(both, None),
        P("batch"),
        P("batch", None),
        P(None, both),
        P(both),
        P(both),
        P(None, both),
        P(both),
        P(both),
        P(both),
        P(None, both),
        P(both),
        P(both, None),
        P(both),
        P(both),
        P(both),
        P(both, None),
    )
    out_specs = (
        P(both, None),
        P(both, None),
        P("batch", "head"),
        P(both),
        P(both),
        P("head", "batch"),
        P(both),
        P(both),
        P(both),
        P(None, both),
        P(both),
        P(both, None),
        P(both),
        P(both),
        P(both),
    )
    return jax.shard_map(local, mesh=mesh, in_specs=in_specs, out_specs=out_specs, check_vma=False)
```

```python
import functools

import jax
import jax.numpy as jnp
from jax import lax
from jax.experimental import pallas as pl
from jax.experimental.pallas import tpu as pltpu
from jax.sharding import PartitionSpec as P

D = 768
HEADS = 12
HEAD_DIM = 64
FF = 3072
BIG = 512
SMALL = 128
UNITS = 4
NORM_EPS = 1e-12
F32 = jnp.float32
BF16 = jnp.bfloat16

CORE = [(i, i ^ 1) for i in range(4)]
XPAIR = [(i, i ^ 2) for i in range(4)]
YPAIR = [(i, i ^ 1) for i in range(8)]
ZPAIR = [[(i, i ^ (2 * k)) for i in range(8)] for k in range(4)]


def core_swap(v):
    return lax.ppermute(v, "head", CORE)


def x_swap(v):
    return lax.ppermute(v, "head", XPAIR)


def y_swap(v):
    return lax.ppermute(v, "batch", YPAIR)


def z_swap(v, k):
    return lax.ppermute(v, "batch", ZPAIR[k])


def after(value, other):
    return lax.optimization_barrier((value, other))[0]


def nt(a, b, out=F32):
    return lax.dot_general(a, b, (((1,), (1,)), ((), ())), preferred_element_type=F32).astype(out)


def nn(a, b, out=F32):
    return lax.dot_general(a, b, (((1,), (0,)), ((), ())), preferred_element_type=F32).astype(out)


def tn(a, b, out=F32):
    return lax.dot_general(a, b, (((0,), (0,)), ((), ())), preferred_element_type=F32).astype(out)


def z_line(shard):
    return [shard] + [z_swap(shard, k) for k in (1, 2, 3)]


def gather_four(z):
    x, y = x_swap(z), y_swap(z)
    return [z, x, y, x_swap(y[:2]), y_swap(x[2:])]


def gather_any(shard):
    whole = lax.all_gather(shard, "batch", axis=0)
    return [whole, x_swap(whole)]


def scatter_xy(z, x, y):
    return z, x_swap(x), y_swap(y)


def scatter_z(others):
    return [z_swap(others[k - 1], k) for k in (1, 2, 3)]


def scatter_any(parts):
    total = parts[0].astype(F32) + x_swap(parts[1]).astype(F32)
    return lax.psum_scatter(total, "batch", scatter_dimension=0, tiled=False)


def est(flops, moved, trans=0):
    return pl.CostEstimate(flops=int(flops), bytes_accessed=int(moved), transcendentals=int(trans))


def call(kernel, out_shape, operands, scratch=(), cost=None, limit=16, far_in=(), far_out=(), sems=0):
    vmem = pl.BlockSpec(memory_space=pltpu.VMEM)
    hbm = pl.BlockSpec(memory_space=pltpu.HBM)
    smem = pl.BlockSpec(memory_space=pltpu.SMEM)
    ins = [hbm if i in far_in else vmem for i in range(len(operands))]
    ins = [smem if v.dtype == jnp.int32 else spec for spec, v in zip(ins, operands)]
    outs = [hbm if i in far_out else vmem for i in range(len(out_shape))]
    scratch = list(scratch) + ([pltpu.SemaphoreType.DMA((sems,))] if sems else [])
    operands = [
        pltpu.with_memory_space_constraint(v, pltpu.HBM) if i in far_in else v
        for i, v in enumerate(operands)
    ]
    out_shape = [
        pltpu.HBM(v.shape, v.dtype) if i in far_out else v for i, v in enumerate(out_shape)
    ]
    return pl.pallas_call(
        kernel,
        out_shape=out_shape,
        in_specs=ins,
        out_specs=outs,
        scratch_shapes=scratch,
        compiler_params=pltpu.CompilerParams(vmem_limit_bytes=limit << 20),
        cost_estimate=cost,
    )(*operands)


class Copies:
    def __init__(self, sems):
        self.sems, self.used, self.open = sems, 0, []

    def start(self, src, dst):
        copy = pltpu.make_async_copy(src, dst, self.sems.at[self.used])
        self.used += 1
        copy.start()
        self.open.append(copy)
        return copy

    def wait(self, *copies):
        for copy in copies or list(self.open):
            copy.wait()
            self.open.remove(copy)


def add_low(a, b):
    return (a.astype(F32) + b.astype(F32)).astype(BF16)


def shape(dims, dtype=BF16):
    return jax.ShapeDtypeStruct(dims, dtype)


def add_moved_kernel(x, for_x, y, for_y, x_out, y_out):
    y_out[0:2] = add_low(y[0:2], for_y[...])
    y_out[2:4] = y[2:4]
    x_out[0:2] = x[0:2]
    x_out[2:4] = add_low(x[2:4], for_x[...])


def add_moved(x, for_x, y, for_y):
    return call(
        add_moved_kernel,
        (shape(x.shape), shape(y.shape)),
        (x, for_x, y, for_y),
        cost=est(1000, 1000),
        limit=8,
    )


def combine_kernel(parts, z, x, y, *refs):
    outs, (mine, low, sems) = refs[: 1 + 3 * parts], refs[1 + 3 * parts :]
    copies = Copies(sems)
    rows = z.shape[1] // parts
    for k in (1, 2, 3, 0):
        total = z[k].astype(F32) + x[k].astype(F32) + y[k].astype(F32)
        if k == 0:
            mine[...] = total
            copies.start(mine, outs[0])
        else:
            low[k - 1] = total.astype(BF16)
            for i in range(parts):
                copies.start(low.at[k - 1, pl.ds(rows * i, rows)], outs[1 + 3 * i + k - 1])
    copies.wait()


def combine(z, x, y, parts):
    rows = z.shape[1]
    mine, *others = call(
        functools.partial(combine_kernel, parts),
        (shape((rows, D), F32),) + (shape((rows // parts, D)),) * (3 * parts),
        (z, x, y),
        scratch=[pltpu.VMEM((rows, D), F32), pltpu.VMEM((3, rows, D), BF16)],
        cost=est(1000, 1000),
        limit=8,
        far_out=range(1 + 3 * parts),
        sems=1 + 3 * parts,
    )
    return mine, [others[3 * i : 3 * i + 3] for i in range(parts)]


def total_of(refs):
    return refs[0][...] + refs[1][...].astype(F32) + refs[2][...].astype(F32) + refs[3][...].astype(F32)


def finish_attend_kernel(mine, one, two, three, qkv, proj):
    total = total_of((mine, one, two, three))
    for hh in range(3):
        for t in range(3):
            at, to = 192 * t + 64 * hh, 192 * hh + 64 * t
            qkv[:, to : to + 64] = total[:, at : at + 64]
    proj[...] = total[:, 576:]


def finish_attend(parts):
    rows = parts[0].shape[0]
    return call(
        finish_attend_kernel,
        (shape((rows, 576), F32), shape((rows, 192), F32)),
        tuple(parts),
        cost=est(8 * rows * D, 16 * rows * D),
    )


def finish_ffn_kernel(mine, *refs):
    ups, downs, (up, down) = refs[:3], refs[3:6], refs[6:]
    half = mine.shape[0] // 2
    up[...] = mine[0:half] + sum(r[...].astype(F32) for r in ups)
    down[...] = mine[half:] + sum(r[...].astype(F32) for r in downs)


def finish_ffn(mine, ups, downs):
    half = mine.shape[0] // 2
    return call(
        finish_ffn_kernel,
        (shape((half, D), F32), shape((half, D), F32)),
        (mine, *ups, *downs),
        cost=est(1000, 1000),
        limit=8,
    )


def exchange_kernel(zero, one, two, *refs):
    ubs, out = refs[:4], refs[4]
    vecs = jnp.concatenate([zero[...], one[...], two[...]])
    width = D // out.shape[0]
    out[...] = jnp.zeros(out.shape, F32)
    for i in range(out.shape[0]):
        out[i, 0:8, 0:width] = vecs[:, width * i : width * i + width]
    for spot in range(4):
        for kz in range(4):
            out[slot_of(spot, kz), 0:1, 24:120] = ubs[spot][:, 96 * kz : 96 * kz + 96]


def exchange_terms(zero, one, two, ubs, devices):
    return call(
        exchange_kernel,
        (shape((devices, 8, 128), F32),),
        (zero, one, two, *ubs),
        cost=est(1000, 1000),
        limit=8,
    )[0]


def flip(a, bit):
    return a + bit - 2 * a * bit


def pack_kernel(qkv_in, proj_in, up_in, down_in, bias, vectors, a_out, fa_out, fb_out, a, p, f, sems):
    rows_q, rows_p, half = qkv_in.shape[0], proj_in.shape[0], down_in.shape[0]
    copies = Copies(sems)
    copies.start(qkv_in, a.at[pl.ds(0, rows_q)])
    copies.start(proj_in, p)
    copies.start(up_in, f.at[pl.ds(0, half)])
    copies.start(down_in, f.at[pl.ds(half, half)])
    width = vectors.shape[1]
    b, h = lax.axis_index("batch"), lax.axis_index("head")
    me = b * lax.axis_size("head") + h
    v = vectors[...].astype(F32)
    v = jnp.concatenate([v] * (D // width), 1)
    lane = lax.broadcasted_iota(jnp.int32, (8, D), 1)
    mine = jnp.logical_and(lane >= me * width, lane < me * width + width)
    v = jnp.where(mine, v, 0.0)
    extra = jnp.concatenate([bias[...].astype(F32), jnp.zeros((1, D - half), F32)], 1)
    v = jnp.concatenate([v, extra, jnp.zeros((7, D), F32)])
    copies.wait()
    a_out[0:rows_q] = a[0:rows_q]
    q = p[...]
    a_out[rows_q : rows_q + rows_p] = jnp.concatenate(
        [q[:, 192 * i : 192 * i + 192] for i in (0, 2, 1, 3)], 1
    )
    a_out[rows_q + rows_p :] = v.astype(BF16)
    fa_out[...] = f[0 : fa_out.shape[0]]
    fb_out[...] = f[fa_out.shape[0] :]


def pack(qkv, proj, up, down, bias, vectors):
    rows, half = qkv.shape[0] + proj.shape[0] + 16, down.shape[0]
    return call(
        pack_kernel,
        (shape((rows, D)), shape((rows, D)), shape((2 * half - rows, D))),
        (qkv, proj, up, down, bias[None], jnp.stack(vectors)),
        scratch=[
            pltpu.VMEM((rows, D), BF16),
            pltpu.VMEM(proj.shape, BF16),
            pltpu.VMEM((2 * half, D), BF16),
        ],
        cost=est(1000, 1000),
        limit=8,
        far_in=(0, 1, 2, 3),
        sems=4,
    )


def place_here():
    b, h = lax.axis_index("batch"), lax.axis_index("head")
    return lax.rem(h, 2), lax.div(b, 2), lax.rem(b, 2), lax.div(h, 2)


def live_units(bucket, lengths):
    x = place_here()[3]
    kind, first = bucket[x], lengths[x, 0]
    units = []
    for u in range(UNITS):
        far = jnp.clip(first - SMALL * u, 0, SMALL)
        units.append(jnp.where(kind == 1, far, lengths[x, u]))
    return kind, units


def place_of(index, c):
    return jnp.bitwise_xor(index, c * (BIG // 2))


def live_of(place, units):
    unit = lax.shift_right_logical(place, 7)
    inner = jnp.bitwise_and(place, SMALL - 1)
    count = jnp.where(
        unit < 2, jnp.where(unit == 0, units[0], units[1]), jnp.where(unit == 2, units[2], units[3])
    )
    return inner < count


def heads_of(row, c):
    parts = []
    for g in range(2):
        lo = row[:, 384 * g : 384 * g + 192]
        hi = row[:, 384 * g + 192 : 384 * g + 384]
        parts.append(jnp.where(c == 0, lo, hi))
    return jnp.concatenate(parts, 1)


def fetch_shards(copies, sources, slots):
    c, z, y, x = place_here()
    zl, zh = lax.rem(z, 2), lax.div(z, 2)
    for swapped in range(2):
        cc = c if swapped == 0 else 1 - c
        zs, xs, ys, xa, xb = sources[5 * swapped : 5 * swapped + 5]
        for kx, ky, pair in ((0, 0, (zs,)), (1, 0, (xs,)), (0, 1, (ys,)), (1, 1, (xa, xb))):
            j = flip(y, ky) * 4 + flip(x, kx) * 2 + cc
            for kz in range(4):
                src = pair[0].at[kz] if len(pair) == 1 else pair[kz // 2].at[kz % 2]
                zi = flip(zl, kz % 2) + 2 * flip(zh, kz // 2)
                copies.start(src, slots.at[zi * 8 + j])


def slot_of(spot, kz):
    c, z, y, x = place_here()
    zi = flip(lax.rem(z, 2), kz % 2) + 2 * flip(lax.div(z, 2), kz // 2)
    return zi * 8 + flip(y, spot // 2) * 4 + flip(x, spot % 2) * 2 + c


def bias_order(slots, row, out):
    for spot in range(4):
        for kz in range(4):
            b = slots[slot_of(spot, kz), row : row + 1, 0:128].astype(F32)
            at = 384 * spot + 96 * kz
            out[:, at : at + 96] = b[:, 0:96]


def attend_kernel(rows_q, rows_p, bucket, lengths, x0, x1, *refs):
    sources = 10 if rows_q else 2
    weights, refs = refs[:sources], refs[sources:]
    (ctx0, ctx1, q_out, k_out, v_out, ctx_out, probs_out, wr_out), refs = refs[:8], refs[8:]
    if rows_q:
        (ub_out, wp_out, small_out), refs = refs[:3], refs[3:]
        (q, k, v, ctx, probs, wr, mask, xs, slots, wp, small, sems) = refs
    else:
        (q, k, v, ctx, probs, wr, mask, xs, w, small, sems) = refs
    copies = Copies(sems)
    c = place_here()[0]
    kind, units = live_units(bucket, lengths)
    half = x0.shape[0]
    copies.start(x0, xs.at[0:half])
    copies.start(x1, xs.at[half : 2 * half])
    if rows_q:
        fetch_shards(copies, weights, slots)
    else:
        copies.start(weights[0], w)
        copies.start(weights[1], small)
    rows = lax.broadcasted_iota(jnp.int32, (BIG, BIG), 0)
    cols = lax.broadcasted_iota(jnp.int32, (BIG, BIG), 1)
    prow, pcol = place_of(rows, c), place_of(cols, c)
    same = jnp.logical_or(
        kind == 1, lax.shift_right_logical(prow, 7) == lax.shift_right_logical(pcol, 7)
    )
    mask[...] = jnp.where(jnp.logical_and(same, live_of(pcol, units)), 0.0, -1e30)
    copies.wait()
    if rows_q:
        for g in range(2):
            cuts = jnp.concatenate([slots[16 * g + 8 * c + j, 0:rows_q] for j in range(8)])
            for t in range(3):
                for hh in range(3):
                    src, dst = (hh * 3 + t) * HEAD_DIM, (t * 6 + g * 3 + hh) * HEAD_DIM
                    wr[dst : dst + HEAD_DIM] = cuts[src : src + HEAD_DIM]
        small[...] = sum(slots[i, rows_q + rows_p :].astype(F32) for i in range(32))
    else:
        for t in range(3):
            for hd in range(6):
                src = ((hd // 3) * 9 + (hd % 3) * 3 + t) * HEAD_DIM
                dst = (t * 6 + hd) * HEAD_DIM
                wr[dst : dst + HEAD_DIM] = w[src : src + HEAD_DIM]
    copies.start(wr, wr_out)
    biases = (heads_of(small[0:1], c), None, heads_of(small[1:2], c))
    for t, (ref, out) in enumerate(((q, q_out), (k, k_out), (v, v_out))):
        val = nt(xs[...], wr[384 * t : 384 * t + 384])
        if biases[t] is not None:
            val = val + biases[t]
        ref[...] = val.astype(BF16)
        copies.start(ref, out)
    if rows_q:
        for i in range(32):
            wp[rows_p * i : rows_p * i + rows_p] = slots[i, rows_q : rows_q + rows_p]
        copies.start(wp, wp_out)
        copies.start(small, small_out)
        bias_order(slots, rows_q + rows_p + 8, ub_out)
    lane = lax.broadcasted_iota(jnp.int32, (half, 128), 1)
    for pair in range(3):
        lanes = slice(128 * pair, 128 * pair + 128)
        kp, vp = k[:, lanes], v[:, lanes]
        for i, near in enumerate((ctx0, ctx1)):
            rws = slice(half * i, half * i + half)
            qp = q[rws, lanes] * jnp.asarray(HEAD_DIM**-0.5, BF16)
            outs = []
            for e in range(2):
                mine = (lane < HEAD_DIM) if e == 0 else (lane >= HEAD_DIM)
                s = nt(jnp.where(mine, qp, jnp.zeros_like(qp)), kp) + mask[rws]
                ex = jnp.exp(s - jnp.max(s, -1, keepdims=True))
                pr = (ex * (1.0 / jnp.sum(ex, -1, keepdims=True))).astype(BF16)
                probs[2 * pair + e, rws] = pr
                outs.append(nn(pr, vp))
            val = jnp.where(lane < HEAD_DIM, outs[0], outs[1]).astype(BF16)
            ctx[rws, lanes] = val
            near[:, lanes] = val
        for e in range(2):
            copies.start(probs.at[2 * pair + e], probs_out.at[2 * pair + e])
    copies.start(ctx, ctx_out)
    copies.wait()


def attend(bucket, lengths, x0, x1, weights, rows_q=0, rows_p=0, rows_s=16):
    half = x0.shape[0]
    n = 2 * half
    direct = rows_q > 0
    outs = [
        shape((half, 384)),
        shape((half, 384)),
        shape((n, 384)),
        shape((n, 384)),
        shape((n, 384)),
        shape((n, 384)),
        shape((6, n, n)),
        shape((1152, D)),
    ]
    scratch = [pltpu.VMEM((n, 384), BF16)] * 4 + [
        pltpu.VMEM((6, n, n), BF16),
        pltpu.VMEM((1152, D), BF16),
        pltpu.VMEM((n, n), F32),
        pltpu.VMEM((n, D), BF16),
    ]
    if direct:
        outs += [shape((1, FF // 2), F32), shape((D, D)), shape((rows_s, D), F32)]
        scratch += [
            pltpu.VMEM((32, rows_q + rows_p + rows_s, D), BF16),
            pltpu.VMEM((D, D), BF16),
            pltpu.VMEM((rows_s, D), F32),
        ]
    else:
        scratch += [pltpu.VMEM((1152, D), BF16), pltpu.VMEM((rows_s, D), F32)]
    operands = (bucket, lengths, x0, x1, *weights)
    return call(
        functools.partial(attend_kernel, rows_q, rows_p),
        outs,
        operands,
        scratch=scratch,
        cost=est(2 * n * D * 1152 + 8 * n * n * 384, 12e6, 6 * n * n),
        limit=32,
        far_in=range(2, len(operands)),
        far_out=[i for i in range(2, len(outs)) if i != 8],
        sems=50,
    )


def norm(values):
    center = values - jnp.mean(values, -1, keepdims=True)
    spread = jnp.mean(center * center, -1, keepdims=True)
    scale = lax.rsqrt(spread + NORM_EPS)
    return center * scale, scale


def norm_back(cot, normal, scale, gain):
    w = cot * gain
    return scale * (
        w - jnp.mean(w, -1, keepdims=True) - normal * jnp.mean(w * normal, -1, keepdims=True)
    )


def first_kernel(
    x_in, ctx_own, ctx_in, wp_in, small_in, low, first_out, normal_out, scale, x, wp, small, first, normal, sems
):
    copies = Copies(sems)
    for src, dst in ((wp_in, wp), (x_in, x), (small_in, small)):
        copies.start(src, dst)
    c = place_here()[0]
    copies.wait()
    mine = pl.multiple_of(c * 384, 128)
    theirs = pl.multiple_of((1 - c) * 384, 128)
    attn = nt(ctx_own[...], wp[:, pl.ds(mine, 384)]) + nt(ctx_in[...], wp[:, pl.ds(theirs, 384)])
    n, r = norm(x[...].astype(F32) + attn + small[2:3])
    normal[...] = n
    copies.start(normal, normal_out)
    out = n * small[3:4] + small[4:5]
    first[...] = out
    copies.start(first, first_out)
    low[...] = out.astype(BF16)
    scale[...] = jnp.broadcast_to(r, scale.shape)
    copies.wait()


def first_norm(x, ctx_own, ctx_in, wp, small):
    n = x.shape[0]
    return call(
        first_kernel,
        (shape((n, D)), shape((n, D), F32), shape((n, D), F32), shape((n, 128), F32)),
        (x, ctx_own, ctx_in, wp, small),
        scratch=[
            pltpu.VMEM((n, D), BF16),
            pltpu.VMEM((D, D), BF16),
            pltpu.VMEM((16, D), F32),
            pltpu.VMEM((n, D), F32),
            pltpu.VMEM((n, D), F32),
        ],
        cost=est(2 * n * D * D, 5e6),
        far_in=(0, 3, 4),
        far_out=(1, 2),
        sems=5,
    )


def ffn_weights(refs):
    if len(refs[0].shape) == 2:
        return refs[0][...], refs[1][...]
    half = refs[0].shape[1] // 2
    blocks = [(r, i) for r in refs for i in range(r.shape[0])]
    up = jnp.concatenate([r[i, 0:half] for r, i in blocks])
    down = jnp.concatenate([r[i, half : 2 * half] for r, i in blocks])
    return up, down


def ffn_kernel(first, count, x0, x1, ub, *refs):
    far, refs = refs[:count], refs[count:]
    if first:
        in0 = in1 = None
    else:
        (in0, in1), refs = refs[:2], refs[2:]
    (hid_out, slope_out, out0, out1), refs = refs[:4], refs[4:]
    near, (hid, slope, sems) = refs[:count], refs[count:]
    copies = Copies(sems)
    for src, dst in zip(far, near):
        copies.start(src, dst)
    copies.wait()
    half = x0.shape[0]
    uw, dw = ffn_weights(near)
    for i, (xr, before, out) in enumerate(((x0, in0, out0), (x1, in1, out1))):
        rws = slice(half * i, half * i + half)
        up = nt(xr[...], uw) + ub[...]
        phi = 0.5 + 0.5 * lax.erf(up * (2.0**-0.5))
        hd = (up * phi).astype(BF16)
        hid[rws] = hd
        slope[rws] = (phi + up * jnp.exp(-0.5 * up * up) * 0.3989422804014327).astype(BF16)
        copies.start(hid.at[rws], hid_out.at[rws])
        copies.start(slope.at[rws], slope_out.at[rws])
        part = nn(hd, dw)
        part = part if before is None else before[...] + part
        out[...] = part.astype(out.dtype)
    copies.wait()


def ffn(x0, x1, ub, weights, sums, last):
    half, width, count = x0.shape[0], ub.shape[1], len(weights)
    n = 2 * half
    return call(
        functools.partial(ffn_kernel, not sums, count),
        (
            shape((n, width)),
            shape((n, width)),
            shape((half, D), F32),
            shape((half, D), BF16 if last else F32),
        ),
        (x0, x1, ub, *weights, *sums),
        scratch=[pltpu.VMEM(w.shape, BF16) for w in weights] + [pltpu.VMEM((n, width), BF16)] * 2,
        cost=est(4 * n * D * width, 4 * D * width + 5e6, 2 * n * width),
        far_in=range(3, 3 + count),
        far_out=(0, 1),
        sems=4 + count,
    )


def second_kernel(
    bucket, lengths, first_in, part, got, small_in, cot_in, out, sum_two, low, sums, first, small, cot, sems
):
    copies = Copies(sems)
    for src, dst in ((first_in, first), (small_in, small), (cot_in, cot)):
        copies.start(src, dst)
    c = place_here()[0]
    _, units = live_units(bucket, lengths)
    copies.wait()
    n, r = norm(first[...] + (part[...] + got[...].astype(F32) + small[5:6]))
    out[...] = (n * small[6:7] + small[7:8]).astype(BF16)
    index = lax.broadcasted_iota(jnp.int32, (first.shape[0], 1), 0)
    live = live_of(place_of(index, c), units)
    oc = jnp.where(live, cot[...].astype(F32), 0.0)
    st = norm_back(oc, n, r, small[6:7])
    sum_two[...] = st
    lo = st.astype(BF16)
    low[...] = lo
    sums[0:1] = jnp.sum(lo.astype(F32), 0, keepdims=True)
    sums[1:2] = jnp.sum(oc * n, 0, keepdims=True)
    sums[2:3] = jnp.sum(oc, 0, keepdims=True)


def second_norm(bucket, lengths, first, part, got, small, cot):
    n = first.shape[0]
    return call(
        second_kernel,
        (shape((n, D)), shape((n, D), F32), shape((n, D)), shape((3, D), F32)),
        (bucket, lengths, first, part, got, small, cot),
        scratch=[pltpu.VMEM((n, D), F32), pltpu.VMEM((16, D), F32), pltpu.VMEM((n, D), BF16)],
        cost=est(40 * n * D, 5e6),
        far_in=(2, 5, 6),
        sems=3,
    )


def ffn_back_kernel(first, lead, count, d0, d1, x0, x1, *refs):
    far, hid_in, slope_in, refs = refs[:count], refs[count], refs[count + 1], refs[count + 2 :]
    if first:
        in0 = in1 = None
    else:
        (in0, in1), refs = refs[:2], refs[2:]
    outs, (ub, out0, out1), near, (hid, slope, sems) = (
        refs[:count],
        refs[count : count + 3],
        refs[count + 3 : 2 * count + 3],
        refs[2 * count + 3 :],
    )
    copies = Copies(sems)
    half, width = x0.shape[0], hid.shape[1]
    for src, dst in zip(far, near):
        copies.start(src, dst)
    copies.start(slope_in.at[:, pl.ds(lead, width)], slope)
    copies.start(hid_in.at[:, pl.ds(lead, width)], hid)
    copies.wait()
    uw, dw = ffn_weights(near)
    cots = []
    for i, (d, before, out) in enumerate(((d0, in0, out0), (d1, in1, out1))):
        rws = slice(half * i, half * i + half)
        uc = (nt(d[...], dw) * slope[rws].astype(F32)).astype(BF16)
        cots.append(uc)
        part = nn(uc, uw)
        part = part if before is None else before[...] + part
        out[...] = part.astype(out.dtype)
    ub[...] = jnp.sum(cots[0].astype(F32), 0, keepdims=True) + jnp.sum(
        cots[1].astype(F32), 0, keepdims=True
    )
    dg = (tn(hid[0:half], d0[...]) + tn(hid[half : 2 * half], d1[...])).astype(BF16)
    ug = (tn(cots[0], x0[...]) + tn(cots[1], x1[...])).astype(BF16)
    if len(outs[0].shape) == 2:
        outs[0][...], outs[1][...] = ug, dg
    else:
        rows = outs[0].shape[1] // 2
        at = 0
        for g in outs:
            for i in range(g.shape[0]):
                g[i, 0:rows] = ug[at : at + rows]
                g[i, rows : 2 * rows] = dg[at : at + rows]
                at += rows


def ffn_back(d0, d1, x0, x1, weights, kept, lead, sums, last):
    half, count = x0.shape[0], len(weights)
    flat = len(weights[0].shape) == 2
    width = weights[0].shape[0] if flat else sum(w.shape[0] * w.shape[1] // 2 for w in weights)
    near = [pltpu.VMEM(w.shape, BF16) for w in weights]
    *grads, ub, s0, s1 = call(
        functools.partial(ffn_back_kernel, not sums, lead, count),
        (
            *[shape(w.shape) for w in weights],
            shape((1, width), F32),
            shape((half, D), F32),
            shape((half, D), BF16 if last else F32),
        ),
        (d0, d1, x0, x1, *weights, *kept, *sums),
        scratch=near + [pltpu.VMEM((2 * half, width), BF16)] * 2,
        cost=est(1000, 1000),
        far_in=range(4, 6 + count),
        sems=2 + count,
    )
    return grads, ub, (s0, s1)


def first_back_kernel(
    sum_two, part, got, normal_in, scale, small_in, *refs
):
    *refs, sum_one, low, sums, normal, small, sems = refs
    copies = Copies(sems)
    copies.start(normal_in, normal)
    copies.start(small_in, small)
    copies.wait()
    fc = sum_two[...] + part[...] + got[...].astype(F32)
    n = normal[...]
    so = norm_back(fc, n, scale[:, 0:1], small[3:4])
    sum_one[...] = so
    lo = so.astype(BF16)
    low[...] = lo
    sums[0:1] = jnp.sum(lo.astype(F32), 0, keepdims=True)
    sums[1:2] = jnp.sum(fc * n, 0, keepdims=True)
    sums[2:3] = jnp.sum(fc, 0, keepdims=True)
    if refs:
        add_moved_kernel(*refs)


def first_back(sum_two, part, got, normal, scale, small, moved=()):
    n = sum_two.shape[0]
    outs = [shape(moved[0].shape), shape(moved[2].shape)] if moved else []
    *added, sum_one, low, sums = call(
        first_back_kernel,
        (*outs, shape((n, D), F32), shape((n, D)), shape((3, D), F32)),
        (sum_two, part, got, normal, scale, small, *moved),
        scratch=[pltpu.VMEM((n, D), F32), pltpu.VMEM((16, D), F32)],
        cost=est(1000, 1000),
        far_in=(3, 5),
        sems=2,
    )
    return added, sum_one, low, sums


def attend_back_kernel(sets, a0, a1, *refs):
    far, outs, (in0, in1, sums), refs = refs[:9], refs[9 : 9 + sets], refs[9 + sets : 12 + sets], refs[12 + sets :]
    wp, v, probs, k, q, wr, x0, x1, ctx, dctx, cots, grads, sems = refs
    copies = Copies(sems)
    near = (wp, v, probs, k, q, wr, x0, x1, ctx)
    got = [copies.start(src, dst) for src, dst in zip(far, near)]
    c, z, y, x = place_here()
    half = a0.shape[0]
    n = 2 * half
    copies.wait(got[0])
    wpo = wp[:, pl.ds(pl.multiple_of(c * 384, 128), 384)]
    dctx[0:half] = nn(a0[...], wpo).astype(BF16)
    dctx[half:n] = nn(a1[...], wpo).astype(BF16)
    copies.wait()
    lane = lax.broadcasted_iota(jnp.int32, (n, 128), 1)
    zero = jnp.zeros((n, 128), BF16)
    scale = HEAD_DIM**-0.5
    heads = [[], [], []]
    for pair in range(3):
        lanes = slice(128 * pair, 128 * pair + 128)
        qp, kp, vp, dp = q[:, lanes], k[:, lanes], v[:, lanes], dctx[:, lanes]
        dq = dk = dv = 0.0
        for e in range(2):
            mine = (lane < HEAD_DIM) if e == 0 else (lane >= HEAD_DIM)
            dh, kh, qh = jnp.where(mine, dp, zero), jnp.where(mine, kp, zero), jnp.where(mine, qp, zero)
            pr = probs[2 * pair + e]
            dv = dv + tn(pr, dh)
            pf = pr.astype(F32)
            t = pf * nt(dh, vp)
            ds = (t - pf * jnp.sum(t, -1, keepdims=True)).astype(BF16)
            dq = dq + nn(ds, kh)
            dk = dk + tn(ds, qh)
        for t, val in enumerate((dq * scale, dk * scale, dv)):
            val = val.astype(BF16)
            for e in range(2):
                hd = 2 * pair + e
                g, hh = hd // 3, hd % 3
                at = 640 * g + 192 * t + 64 * hh
                cots[:, at : at + 64] = val[:, 64 * e : 64 * e + 64]
            heads[t].append(val)
    for g in range(2):
        cots[:, 640 * g + 576 : 640 * g + 640] = jnp.zeros((n, 64), BF16)
    parts = [jnp.concatenate(heads[t], 1) for t in range(3)]
    for i, out in enumerate((in0, in1)):
        rws = slice(half * i, half * i + half)
        total = 0.0
        for t in range(3):
            total = total + nn(parts[t][rws], wr[384 * t : 384 * t + 384])
        out[...] = total
    for row, t in ((0, 0), (1, 2)):
        s = jnp.sum(parts[t].astype(F32), 0, keepdims=True)
        for g in range(2):
            sg = s[:, 192 * g : 192 * g + 192]
            sums[row : row + 1, 384 * g : 384 * g + 192] = jnp.where(c == 0, sg, 0.0)
            sums[row : row + 1, 384 * g + 192 : 384 * g + 384] = jnp.where(c == 1, sg, 0.0)
    for d in range(3):
        at = slice(256 * d, 256 * d + 256)
        full = tn(x0[:, at], cots[0:half]) + tn(x1[:, at], cots[half:n])
        pg = tn(a0[:, at], ctx[0:half]) + tn(a1[:, at], ctx[half:n])
        for g in range(2):
            grads[g, at, 0:576] = full[:, 640 * g : 640 * g + 576].astype(BF16)
            grads[g, at, 576:768] = pg[:, 192 * g : 192 * g + 192].astype(BF16)
    if sets == 1:
        copies.start(grads, outs[0])
    else:
        rows = outs[0].shape[1]
        for spot in (3, 2, 1, 0):
            g, yi = flip(x, spot % 2), flip(y, spot // 2)
            for kz in range(4):
                zi = flip(lax.rem(z, 2), kz % 2) + 2 * flip(lax.div(z, 2), kz // 2)
                at = pl.multiple_of((2 * zi + yi) * rows, rows)
                dst = outs[spot].at[kz] if spot < 3 else outs[3 + kz // 2].at[kz % 2]
                copies.start(grads.at[g, pl.ds(at, rows)], dst)
    copies.wait()


def attend_back(direct, a0, a1, x0, x1, wp, wr, q, k, v, ctx, probs):
    half = a0.shape[0]
    n = 2 * half
    sets = (shape((2, D, D)),)
    if direct:
        sets = (shape((4, 96, D)),) * 3 + (shape((2, 96, D)),) * 2
    far = (wp, v, probs, k, q, wr, x0, x1, ctx)
    return call(
        functools.partial(attend_back_kernel, len(sets)),
        (*sets, shape((half, D), F32), shape((half, D), F32), shape((2, D), F32)),
        (a0, a1, *far),
        scratch=[pltpu.VMEM(f.shape, BF16) for f in far]
        + [pltpu.VMEM((n, 384), BF16), pltpu.VMEM((n, 1280), BF16), pltpu.VMEM((2, D, D), BF16)],
        cost=est(1000, 1000),
        limit=32,
        far_in=range(2, 11),
        far_out=range(len(sets)),
        sems=26,
    )


def local(
    inputs,
    bucket,
    lengths,
    qkv_weight,
    query_bias,
    value_bias,
    proj_weight,
    proj_bias,
    first_gain,
    first_shift,
    up_weight,
    up_bias,
    down_weight,
    down_bias,
    second_gain,
    second_shift,
    cotangent,
):
    head_count = lax.axis_size("head")
    batch_count = lax.axis_size("batch")
    devices = head_count * batch_count
    direct = batch_count == 8
    b = lax.axis_index("batch")
    h = lax.axis_index("head")
    me = b * head_count + h
    x, c = h // 2, h % 2
    z, y = b // 2, b % 2
    wq, wp, wf = 3 * D // devices, D // devices, FF // devices

    vectors = [
        query_bias,
        value_bias,
        proj_bias,
        first_gain,
        first_shift,
        down_bias,
        second_gain,
        second_shift,
    ]
    if direct:
        a_shard, fa_shard, fb_shard = pack(
            qkv_weight.T, proj_weight.T, up_weight.T, down_weight, up_bias, vectors
        )
    else:
        small = lax.dynamic_update_slice(
            jnp.zeros((16, D), BF16), jnp.stack(vectors), (0, me * wp)
        )
        per_row = D // wf
        small = lax.dynamic_update_slice(
            small, up_bias[None, :], (8 + me // per_row, (me % per_row) * wf)
        )
        proj_t = proj_weight.T.reshape(wp, 2, 2, 192).transpose(0, 2, 1, 3).reshape(wp, D)
        a_shard = jnp.concatenate([qkv_weight.T, proj_t, small])
    other_in = core_swap(inputs)
    k = jnp.arange(batch_count * 2)
    if direct:
        a_z = jnp.stack(z_line(a_shard))
        a_z, other_in = lax.optimization_barrier((a_z, other_in))
        fa_z = z_line(after(fa_shard, a_z))
        a_x, a_y = x_swap(a_z), y_swap(a_z)
        a_x, a_y, fa_z = lax.optimization_barrier((a_x, a_y, fa_z))
        fb_z = z_line(after(fb_shard, fa_z))
        a_d = [x_swap(a_y[:2]), y_swap(a_x[2:])]
        a_d, fb_z = lax.optimization_barrier((a_d, fb_z))
        a_own = [a_z, a_x, a_y, *a_d]
        a_swapped = [core_swap(v) for v in after(a_own, fb_z)]
        f_z = jnp.stack([jnp.concatenate(pair) for pair in zip(fa_z, fb_z)])
        f_x, f_y, *f_d = gather_four(f_z)[1:]
        ctx_own, ctx_other, q, kk, v, ctx, probs, wr, ub_all, proj_w, small_all = attend(
            bucket, lengths, inputs, other_in, (*a_own, *a_swapped), wq, wp
        )
        f_all = [[f_z], [f_x, f_y], f_d]
    else:
        a_all = lax.all_gather(a_shard, ("batch", "head"), axis=0)
        qkv_all = a_all[:, :wq].reshape(2, 2, 576, D)
        qkv_w = lax.dynamic_index_in_dim(qkv_all, c, 1, keepdims=False).reshape(2 * 576, D)
        proj_w = a_all[:, wq : wq + wp].reshape(D, D)
        small_all = jnp.sum(a_all[:, wq + wp :].astype(F32), 0)
        ctx_own, ctx_other, q, kk, v, ctx, probs, wr = attend(
            bucket, lengths, inputs, other_in, (qkv_w, small_all)
        )
        f_shard = jnp.concatenate([up_weight.T, down_weight])
        f_all = [
            (v[:, :wf].reshape(-1, D), v[:, wf:].reshape(-1, D)) for v in gather_any(f_shard)
        ]
        owner = (k % batch_count) * 4 + (x ^ (k // batch_count)) * 2 + c
    if not direct:
        spread = (owner[None, :] == jnp.arange(devices)[:, None]).astype(F32)
        ub_all = tn(spread, small_all[8:12].reshape(devices, wf)).reshape(1, FF // 2)

    ctx_in = core_swap(ctx_other)
    first_low, first, first_n, first_r = first_norm(inputs, ctx_own, ctx_in, proj_w, small_all)
    first_in = core_swap(first_low)
    sums = ()
    kept = []
    at = 0
    for weights in f_all:
        width = (384, 768, 384)[len(kept)] if direct else FF // 4
        hid, slope, *sums = ffn(
            first_low,
            first_in,
            ub_all[:, at : at + width],
            weights,
            sums,
            len(kept) == len(f_all) - 1,
        )
        kept.append((hid, slope))
        at += width
    layer_out, sum_two, down_low, sums_two = second_norm(
        bucket, lengths, first, sums[0], core_swap(sums[1]), small_all, cotangent
    )
    down_in = core_swap(down_low)

    sums = ()
    f_parts, ub_parts = [], []
    if direct:
        sets = (([f_z], 0, 0), ([f_x], 1, 0), ([f_y], 1, 384), (f_d, 2, 0))
        for weights, which, lead in reversed(sets):
            grads, ub, sums = ffn_back(
                down_low, down_in, first_low, first_in, weights, kept[which], lead, sums, which + lead == 0
            )
            f_parts = grads + f_parts
            ub_parts.insert(0, ub)
    else:
        for weights, pair in zip(f_all, kept):
            grads, ub, sums = ffn_back(
                down_low, down_in, first_low, first_in, weights, pair, 0, sums, len(f_parts) == len(f_all) - 1
            )
            f_parts.append(grads)
            ub_parts.append(ub)
    part_own, part_other = sums
    moved = ()
    if direct:
        moved = (f_parts[1], y_swap(f_parts[4]), f_parts[2], x_swap(f_parts[3]))
        part_other = after(part_other, moved)
    added, sum_one, attn_low, sums_one = first_back(
        sum_two, part_own, core_swap(part_other), first_n, first_r, small_all, moved
    )
    attn_in = core_swap(attn_low)
    *a_grads, in_own, in_other, sums_zero = attend_back(
        direct,
        attn_low,
        attn_in,
        inputs,
        other_in,
        proj_w,
        wr,
        q,
        kk,
        v,
        ctx,
        probs,
    )
    inputs_grad = (sum_one + in_own + core_swap(in_other)).astype(BF16)

    if direct:
        f_mine, (f_ups, f_downs) = combine(*scatter_xy(f_parts[0], *added), 2)
        terms = exchange_terms(sums_zero, sums_one, sums_two, ub_parts, devices)
        terms = lax.all_to_all(terms, ("batch", "head"), split_axis=0, concat_axis=0, tiled=True)
        a_zz, a_xx, a_yy, d_lo, d_hi = a_grads
        d_lo, d_hi = after((d_lo, d_hi), (f_ups, inputs_grad, terms))
        d_lo, d_hi = x_swap(d_lo), y_swap(d_hi)
        f_ups = scatter_z(f_ups)
        d_lo, d_hi, f_ups = lax.optimization_barrier((d_lo, d_hi, f_ups))
        a_xx, a_yy = add_moved(a_xx, d_hi, a_yy, d_lo)
        a_sets = scatter_xy(a_zz, a_xx, a_yy)
        f_downs = scatter_z(after(f_downs, f_ups))
        a_sets, f_downs = lax.optimization_barrier((a_sets, f_downs))
        a_mine, (a_others,) = combine(*a_sets, 1)
        up_grad, down_grad = finish_ffn(f_mine, f_ups, f_downs)
        up_grad = up_grad.T
        terms = jnp.sum(terms, 0)
        packed = jnp.concatenate([terms[:, :wp].reshape(-1), terms[0, wp : wp + wf]])
        qkv_grad, proj_grad = finish_attend((a_mine, *scatter_z(a_others)))
        proj_grad = proj_grad.T
    else:
        vecs = jnp.concatenate([sums_zero, sums_one, sums_two])
        vecs = vecs.reshape(8, devices, wp).transpose(1, 0, 2).reshape(devices, 8 * wp)
        ubias = jnp.concatenate(ub_parts).reshape(batch_count * 2, wf)
        ubias = lax.dot_general(
            spread, ubias, (((1,), (0,)), ((), ())), precision=lax.Precision.HIGHEST
        )
        packed = jnp.concatenate([vecs, ubias], 1)
        packed = lax.all_to_all(
            packed, ("batch", "head"), split_axis=0, concat_axis=0, tiled=True
        )
        packed = jnp.sum(packed, 0)
        wb = D // batch_count
        a_grads = a_grads[0].reshape(2, batch_count, wb, D)
        a_mine = scatter_any(
            [
                lax.dynamic_index_in_dim(a_grads, x, 0, keepdims=False),
                lax.dynamic_index_in_dim(a_grads, 1 - x, 0, keepdims=False),
            ]
        )
        f_mine = scatter_any(
            [
                jnp.concatenate(
                    [ug.reshape(batch_count, wf, D), dg.reshape(batch_count, wf, D)], 1
                )
                for ug, dg in f_parts
            ]
        )
        qkv_grad = a_mine[:, :576].reshape(wb, 3, 3, HEAD_DIM).transpose(0, 2, 1, 3)
        qkv_grad = qkv_grad.reshape(wb, 576)
        proj_grad = a_mine[:, 576:].T
        up_grad, down_grad = f_mine[:wf].T, f_mine[wf:]
    qb_g, vb_g, pb_g, fg_g, fs_g, db_g, sg_g, ss_g = [
        packed[i * wp : (i + 1) * wp] for i in range(8)
    ]
    return (
        layer_out,
        inputs_grad,
        qkv_grad,
        qb_g,
        vb_g,
        proj_grad,
        pb_g,
        fg_g,
        fs_g,
        up_grad,
        packed[8 * wp :],
        down_grad,
        db_g,
        sg_g,
        ss_g,
    )


def solution(mesh):
    both = ("batch", "head")
    in_specs = (
        P(both, None),
        P("batch"),
        P("batch", None),
        P(None, both),
        P(both),
        P(both),
        P(None, both),
        P(both),
        P(both),
        P(both),
        P(None, both),
        P(both),
        P(both, None),
        P(both),
        P(both),
        P(both),
        P(both, None),
    )
    out_specs = (
        P(both, None),
        P(both, None),
        P("batch", "head"),
        P(both),
        P(both),
        P("head", "batch"),
        P(both),
        P(both),
        P(both),
        P(None, both),
        P(both),
        P(both, None),
        P(both),
        P(both),
        P(both),
    )
    return jax.shard_map(local, mesh=mesh, in_specs=in_specs, out_specs=out_specs, check_vma=False)
```

```python
import functools

import jax
import jax.numpy as jnp
from jax import lax
from jax.experimental import pallas as pl
from jax.experimental.pallas import tpu as pltpu
from jax.sharding import PartitionSpec as P

D = 768
HEADS = 12
HEAD_DIM = 64
FF = 3072
BIG = 512
SMALL = 128
UNITS = 4
NORM_EPS = 1e-12
F32 = jnp.float32
BF16 = jnp.bfloat16

FIRST = 112

CORE = [(i, i ^ 1) for i in range(4)]
XPAIR = [(i, i ^ 2) for i in range(4)]
YPAIR = [(i, i ^ 1) for i in range(8)]
ZPAIR = [[(i, i ^ (2 * k)) for i in range(8)] for k in range(4)]


def core_swap(v):
    return lax.ppermute(v, "head", CORE)


def x_swap(v):
    return lax.ppermute(v, "head", XPAIR)


def y_swap(v):
    return lax.ppermute(v, "batch", YPAIR)


def z_swap(v, k):
    return lax.ppermute(v, "batch", ZPAIR[k])


def after(value, other):
    return lax.optimization_barrier((value, other))[0]


def nt(a, b, out=F32):
    return lax.dot_general(a, b, (((1,), (1,)), ((), ())), preferred_element_type=F32).astype(out)


def nn(a, b, out=F32):
    return lax.dot_general(a, b, (((1,), (0,)), ((), ())), preferred_element_type=F32).astype(out)


def tn(a, b, out=F32):
    return lax.dot_general(a, b, (((0,), (0,)), ((), ())), preferred_element_type=F32).astype(out)


def z_line(shard):
    return [shard] + [z_swap(shard, k) for k in (1, 2, 3)]


def gather_four(z):
    x, y = x_swap(z), y_swap(z)
    return [z, x, y, x_swap(y[:2]), y_swap(x[2:])]


def gather_any(shard):
    whole = lax.all_gather(shard, "batch", axis=0)
    return [whole, x_swap(whole)]


def scatter_xy(z, x, y):
    return z, x_swap(x), y_swap(y)


def scatter_z(others):
    return [z_swap(others[k - 1], k) for k in (1, 2, 3)]


def scatter_any(parts):
    total = parts[0].astype(F32) + x_swap(parts[1]).astype(F32)
    return lax.psum_scatter(total, "batch", scatter_dimension=0, tiled=False)


def est(flops, moved, trans=0):
    return pl.CostEstimate(flops=int(flops), bytes_accessed=int(moved), transcendentals=int(trans))


def call(kernel, out_shape, operands, scratch=(), cost=None, limit=16, far_in=(), far_out=(), sems=0):
    vmem = pl.BlockSpec(memory_space=pltpu.VMEM)
    hbm = pl.BlockSpec(memory_space=pltpu.HBM)
    smem = pl.BlockSpec(memory_space=pltpu.SMEM)
    ins = [hbm if i in far_in else vmem for i in range(len(operands))]
    ins = [smem if v.dtype == jnp.int32 else spec for spec, v in zip(ins, operands)]
    outs = [hbm if i in far_out else vmem for i in range(len(out_shape))]
    scratch = list(scratch) + ([pltpu.SemaphoreType.DMA((sems,))] if sems else [])
    operands = [
        pltpu.with_memory_space_constraint(v, pltpu.HBM) if i in far_in else v
        for i, v in enumerate(operands)
    ]
    out_shape = [
        pltpu.HBM(v.shape, v.dtype) if i in far_out else v for i, v in enumerate(out_shape)
    ]
    return pl.pallas_call(
        kernel,
        out_shape=out_shape,
        in_specs=ins,
        out_specs=outs,
        scratch_shapes=scratch,
        compiler_params=pltpu.CompilerParams(vmem_limit_bytes=limit << 20),
        cost_estimate=cost,
    )(*operands)


class Copies:
    def __init__(self, sems):
        self.sems, self.used, self.open = sems, 0, []

    def start(self, src, dst):
        copy = pltpu.make_async_copy(src, dst, self.sems.at[self.used])
        self.used += 1
        copy.start()
        self.open.append(copy)
        return copy

    def wait(self, *copies):
        for copy in copies or list(self.open):
            copy.wait()
            self.open.remove(copy)


def add_low(a, b):
    return (a.astype(F32) + b.astype(F32)).astype(BF16)


def shape(dims, dtype=BF16):
    return jax.ShapeDtypeStruct(dims, dtype)


def add_moved_kernel(x, for_x, y, for_y, x_out, y_out):
    y_out[0:2] = add_low(y[0:2], for_y[...])
    y_out[2:4] = y[2:4]
    x_out[0:2] = x[0:2]
    x_out[2:4] = add_low(x[2:4], for_x[...])


def add_moved(x, for_x, y, for_y):
    return call(
        add_moved_kernel,
        (shape(x.shape), shape(y.shape)),
        (x, for_x, y, for_y),
        cost=est(1000, 1000),
        limit=8,
    )


def combine_kernel(parts, z, x, y, *refs):
    outs, (mine, low, sems) = refs[: 1 + 3 * parts], refs[1 + 3 * parts :]
    copies = Copies(sems)
    rows = z.shape[1] // parts
    for k in (1, 2, 3, 0):
        total = z[k].astype(F32) + x[k].astype(F32) + y[k].astype(F32)
        if k == 0:
            mine[...] = total
            copies.start(mine, outs[0])
        else:
            low[k - 1] = total.astype(BF16)
            for i in range(parts):
                copies.start(low.at[k - 1, pl.ds(rows * i, rows)], outs[1 + 3 * i + k - 1])
    copies.wait()


def combine(z, x, y, parts):
    rows = z.shape[1]
    mine, *others = call(
        functools.partial(combine_kernel, parts),
        (shape((rows, D), F32),) + (shape((rows // parts, D)),) * (3 * parts),
        (z, x, y),
        scratch=[pltpu.VMEM((rows, D), F32), pltpu.VMEM((3, rows, D), BF16)],
        cost=est(1000, 1000),
        limit=8,
        far_out=range(1 + 3 * parts),
        sems=1 + 3 * parts,
    )
    return mine, [others[3 * i : 3 * i + 3] for i in range(parts)]


def total_of(refs):
    return refs[0][...] + refs[1][...].astype(F32) + refs[2][...].astype(F32) + refs[3][...].astype(F32)


def finish_attend_kernel(mine, one, two, three, qkv, proj):
    total = total_of((mine, one, two, three))
    for hh in range(3):
        for t in range(3):
            at, to = 192 * t + 64 * hh, 192 * hh + 64 * t
            qkv[:, to : to + 64] = total[:, at : at + 64]
    proj[...] = total[:, 576:].T


def finish_attend(parts):
    rows = parts[0].shape[0]
    return call(
        finish_attend_kernel,
        (shape((rows, 576), F32), shape((192, rows), F32)),
        tuple(parts),
        cost=est(8 * rows * D, 16 * rows * D),
    )


def finish_ffn_kernel(mine, *refs):
    ups, downs, (up, down) = refs[:3], refs[3:6], refs[6:]
    half = mine.shape[0] // 2
    up[...] = mine[0:half] + sum(r[...].astype(F32) for r in ups)
    down[...] = mine[half:] + sum(r[...].astype(F32) for r in downs)


def finish_ffn(mine, ups, downs):
    half = mine.shape[0] // 2
    return call(
        finish_ffn_kernel,
        (shape((half, D), F32), shape((half, D), F32)),
        (mine, *ups, *downs),
        cost=est(1000, 1000),
        limit=8,
    )


def exchange_kernel(zero, one, two, *refs):
    ubs, out = refs[:4], refs[4]
    vecs = jnp.concatenate([zero[...], one[...], two[...]])
    width = D // out.shape[0]
    out[...] = jnp.zeros(out.shape, F32)
    for i in range(out.shape[0]):
        out[i, 0:8, 0:width] = vecs[:, width * i : width * i + width]
    for spot in range(4):
        for kz in range(4):
            out[slot_of(spot, kz), 0:1, 24:120] = ubs[spot][:, 96 * kz : 96 * kz + 96]


def exchange_terms(zero, one, two, ubs, devices):
    return call(
        exchange_kernel,
        (shape((devices, 8, 128), F32),),
        (zero, one, two, *ubs),
        cost=est(1000, 1000),
        limit=8,
    )[0]


def flip(a, bit):
    return a + bit - 2 * a * bit


def pack_kernel(qkv_in, proj_in, up_in, down_in, bias, vectors, a_out, fa_out, fb_out, a, p, f, sems):
    rows_q, rows_p, half = qkv_in.shape[0], proj_in.shape[0], down_in.shape[0]
    copies = Copies(sems)
    copies.start(qkv_in, a.at[pl.ds(0, rows_q)])
    copies.start(proj_in, p)
    copies.start(up_in, f.at[pl.ds(0, half)])
    copies.start(down_in, f.at[pl.ds(half, half)])
    width = vectors.shape[1]
    b, h = lax.axis_index("batch"), lax.axis_index("head")
    me = b * lax.axis_size("head") + h
    v = vectors[...].astype(F32)
    v = jnp.concatenate([v] * (D // width), 1)
    lane = lax.broadcasted_iota(jnp.int32, (8, D), 1)
    mine = jnp.logical_and(lane >= me * width, lane < me * width + width)
    v = jnp.where(mine, v, 0.0)
    gap = jnp.zeros((1, D // 2 - half), F32)
    none = jnp.zeros((1, D // 2), F32)
    row = bias[...].astype(F32)
    early = jnp.concatenate([none, row, gap], 1)
    late = jnp.concatenate([row, gap, none], 1)
    extra = jnp.where(me < lax.axis_size("batch") * lax.axis_size("head") // 2, early, late)
    v = v + jnp.concatenate([extra, jnp.zeros((7, D), F32)])
    copies.wait()
    a_out[0:rows_q] = a[0:rows_q]
    q = p[...]
    a_out[rows_q : rows_q + rows_p] = jnp.concatenate(
        [q[:, 192 * i : 192 * i + 192] for i in (0, 2, 1, 3)], 1
    )
    a_out[rows_q + rows_p :] = v.astype(BF16)
    fa_out[...] = f[0 : fa_out.shape[0]]
    fb_out[...] = f[fa_out.shape[0] :]


def pack(qkv, proj, up, down, bias, vectors):
    rows, half = qkv.shape[0] + proj.shape[0] + 8, down.shape[0]
    return call(
        pack_kernel,
        (shape((rows, D)), shape((FIRST, D)), shape((2 * half - FIRST, D))),
        (qkv, proj, up, down, bias[None], jnp.stack(vectors)),
        scratch=[
            pltpu.VMEM((rows, D), BF16),
            pltpu.VMEM(proj.shape, BF16),
            pltpu.VMEM((2 * half, D), BF16),
        ],
        cost=est(1000, 1000),
        limit=8,
        far_in=(0, 1, 2, 3),
        sems=4,
    )


def place_here():
    b, h = lax.axis_index("batch"), lax.axis_index("head")
    return lax.rem(h, 2), lax.div(b, 2), lax.rem(b, 2), lax.div(h, 2)


def live_units(bucket, lengths):
    x = place_here()[3]
    kind, first = bucket[x], lengths[x, 0]
    units = []
    for u in range(UNITS):
        far = jnp.clip(first - SMALL * u, 0, SMALL)
        units.append(jnp.where(kind == 1, far, lengths[x, u]))
    return kind, units


def place_of(index, c):
    return jnp.bitwise_xor(index, c * (BIG // 2))


def live_of(place, units):
    unit = lax.shift_right_logical(place, 7)
    inner = jnp.bitwise_and(place, SMALL - 1)
    count = jnp.where(
        unit < 2, jnp.where(unit == 0, units[0], units[1]), jnp.where(unit == 2, units[2], units[3])
    )
    return inner < count


def heads_of(row, c):
    parts = []
    for g in range(2):
        lo = row[:, 384 * g : 384 * g + 192]
        hi = row[:, 384 * g + 192 : 384 * g + 384]
        parts.append(jnp.where(c == 0, lo, hi))
    return jnp.concatenate(parts, 1)


def fetch_shards(copies, sources, slots):
    c, z, y, x = place_here()
    zl, zh = lax.rem(z, 2), lax.div(z, 2)
    for swapped in range(2):
        cc = c if swapped == 0 else 1 - c
        zs, xs, ys, xa, xb = sources[5 * swapped : 5 * swapped + 5]
        for kx, ky, pair in ((0, 0, (zs,)), (1, 0, (xs,)), (0, 1, (ys,)), (1, 1, (xa, xb))):
            j = flip(y, ky) * 4 + flip(x, kx) * 2 + cc
            for kz in range(4):
                src = pair[0].at[kz] if len(pair) == 1 else pair[kz // 2].at[kz % 2]
                zi = flip(zl, kz % 2) + 2 * flip(zh, kz // 2)
                copies.start(src, slots.at[zi * 8 + j])


def slot_of(spot, kz):
    c, z, y, x = place_here()
    zi = flip(lax.rem(z, 2), kz % 2) + 2 * flip(lax.div(z, 2), kz // 2)
    return zi * 8 + flip(y, spot // 2) * 4 + flip(x, spot % 2) * 2 + c


def bias_order(slots, row, out):
    for spot in range(4):
        for kz in range(4):
            i = slot_of(spot, kz)
            b = slots[i, row : row + 1].astype(F32)
            b = jnp.where(i < 16, b[:, D // 2 : D // 2 + 96], b[:, 0:96])
            at = 384 * spot + 96 * kz
            out[:, at : at + 96] = b


def attend_kernel(rows_q, rows_p, bucket, lengths, x0, x1, *refs):
    sources = 10 if rows_q else 2
    weights, refs = refs[:sources], refs[sources:]
    (ctx0, ctx1, q, k, v, ctx, probs, wr), refs = refs[:8], refs[8:]
    if rows_q:
        (ub_out, wp, small, mask, xs, slots, sems) = refs
    else:
        (mask, xs, w, small, sems) = refs
    copies = Copies(sems)
    c = place_here()[0]
    kind, units = live_units(bucket, lengths)
    half = x0.shape[0]
    copies.start(x0, xs.at[0:half])
    copies.start(x1, xs.at[half : 2 * half])
    if rows_q:
        fetch_shards(copies, weights, slots)
    else:
        copies.start(weights[0], w)
        copies.start(weights[1], small)
    rows = lax.broadcasted_iota(jnp.int32, (BIG, BIG), 0)
    cols = lax.broadcasted_iota(jnp.int32, (BIG, BIG), 1)
    prow, pcol = place_of(rows, c), place_of(cols, c)
    same = jnp.logical_or(
        kind == 1, lax.shift_right_logical(prow, 7) == lax.shift_right_logical(pcol, 7)
    )
    mask[...] = jnp.where(jnp.logical_and(same, live_of(pcol, units)), 0.0, -1e30)
    copies.wait()
    if rows_q:
        for g in range(2):
            cuts = jnp.concatenate([slots[16 * g + 8 * c + j, 0:rows_q] for j in range(8)])
            for t in range(3):
                for hh in range(3):
                    src, dst = (hh * 3 + t) * HEAD_DIM, (t * 6 + g * 3 + hh) * HEAD_DIM
                    wr[dst : dst + HEAD_DIM] = cuts[src : src + HEAD_DIM]
        lane = lax.broadcasted_iota(jnp.int32, (8, D), 1)
        small[...] = sum(
            jnp.where(
                jnp.logical_and(lane >= rows_p * i, lane < rows_p * i + rows_p),
                slots[i, rows_q + rows_p :].astype(F32),
                0.0,
            )
            for i in range(32)
        )
    else:
        for t in range(3):
            for hd in range(6):
                src = ((hd // 3) * 9 + (hd % 3) * 3 + t) * HEAD_DIM
                dst = (t * 6 + hd) * HEAD_DIM
                wr[dst : dst + HEAD_DIM] = w[src : src + HEAD_DIM]
    biases = (heads_of(small[0:1], c), None, heads_of(small[1:2], c))
    for t, ref in enumerate((q, k, v)):
        val = nt(xs[...], wr[384 * t : 384 * t + 384])
        if biases[t] is not None:
            val = val + biases[t]
        ref[...] = val.astype(BF16)
    if rows_q:
        for i in range(32):
            wp[rows_p * i : rows_p * i + rows_p] = slots[i, rows_q : rows_q + rows_p]
        bias_order(slots, rows_q + rows_p, ub_out)
    lane = lax.broadcasted_iota(jnp.int32, (half, 128), 1)
    for pair in range(3):
        lanes = slice(128 * pair, 128 * pair + 128)
        kp, vp = k[:, lanes], v[:, lanes]
        for i, near in enumerate((ctx0, ctx1)):
            rws = slice(half * i, half * i + half)
            qp = q[rws, lanes] * jnp.asarray(HEAD_DIM**-0.5, BF16)
            outs = []
            for e in range(2):
                mine = (lane < HEAD_DIM) if e == 0 else (lane >= HEAD_DIM)
                s = nt(jnp.where(mine, qp, jnp.zeros_like(qp)), kp) + mask[rws]
                ex = jnp.exp(s - jnp.max(s, -1, keepdims=True))
                pr = (ex * (1.0 / jnp.sum(ex, -1, keepdims=True))).astype(BF16)
                probs[2 * pair + e, rws] = pr
                outs.append(nn(pr, vp))
            val = jnp.where(lane < HEAD_DIM, outs[0], outs[1]).astype(BF16)
            ctx[rws, lanes] = val
            near[:, lanes] = val


def attend(bucket, lengths, x0, x1, weights, rows_q=0, rows_p=0, rows_s=16):
    rows_s = 8 if rows_q else rows_s
    half = x0.shape[0]
    n = 2 * half
    direct = rows_q > 0
    outs = [
        shape((half, 384)),
        shape((half, 384)),
        shape((n, 384)),
        shape((n, 384)),
        shape((n, 384)),
        shape((n, 384)),
        shape((6, n, n)),
        shape((1152, D)),
    ]
    scratch = [pltpu.VMEM((n, n), F32), pltpu.VMEM((n, D), BF16)]
    if direct:
        outs += [shape((1, FF // 2), F32), shape((D, D)), shape((rows_s, D), F32)]
        scratch += [pltpu.VMEM((32, rows_q + rows_p + rows_s, D), BF16)]
    else:
        scratch += [pltpu.VMEM((1152, D), BF16), pltpu.VMEM((rows_s, D), F32)]
    operands = (bucket, lengths, x0, x1, *weights)
    return call(
        functools.partial(attend_kernel, rows_q, rows_p),
        outs,
        operands,
        scratch=scratch,
        cost=est(2 * n * D * 1152 + 8 * n * n * 384, 12e6, 6 * n * n),
        limit=32,
        far_in=range(2, len(operands)),
        sems=50,
    )


def norm(values):
    center = values - jnp.mean(values, -1, keepdims=True)
    spread = jnp.mean(center * center, -1, keepdims=True)
    scale = lax.rsqrt(spread + NORM_EPS)
    return center * scale, scale


def norm_back(cot, normal, scale, gain):
    w = cot * gain
    return scale * (
        w - jnp.mean(w, -1, keepdims=True) - normal * jnp.mean(w * normal, -1, keepdims=True)
    )


def first_kernel(x, ctx_own, ctx_in, wp, small, low, first, normal, scale):
    c = place_here()[0]
    mine = pl.multiple_of(c * 384, 128)
    theirs = pl.multiple_of((1 - c) * 384, 128)
    attn = nt(ctx_own[...], wp[:, pl.ds(mine, 384)]) + nt(ctx_in[...], wp[:, pl.ds(theirs, 384)])
    n, r = norm(x[...].astype(F32) + attn + small[2:3])
    normal[...] = n
    out = n * small[3:4] + small[4:5]
    first[...] = out
    low[...] = out.astype(BF16)
    scale[...] = jnp.broadcast_to(r, scale.shape)


def first_norm(x, ctx_own, ctx_in, wp, small):
    n = x.shape[0]
    return call(
        first_kernel,
        (shape((n, D)), shape((n, D), F32), shape((n, D), F32), shape((n, 128), F32)),
        (x, ctx_own, ctx_in, wp, small),
        cost=est(2 * n * D * D, 5e6),
        limit=8,
    )


def ffn_weights(refs):
    if len(refs[0].shape) == 2:
        return refs[0][...], refs[1][...]
    half = refs[0].shape[1] // 2
    blocks = [(r, i) for r in refs for i in range(r.shape[0])]
    up = jnp.concatenate([r[i, 0:half] for r, i in blocks])
    down = jnp.concatenate([r[i, half : 2 * half] for r, i in blocks])
    return up, down


def ffn_kernel(first, count, x0, x1, ub, *refs):
    far, refs = refs[:count], refs[count:]
    if first:
        in0 = in1 = None
    else:
        (in0, in1), refs = refs[:2], refs[2:]
    hid, slope, out0, out1 = refs
    half = x0.shape[0]
    uw, dw = ffn_weights(far)
    for i, (xr, before, out) in enumerate(((x0, in0, out0), (x1, in1, out1))):
        rws = slice(half * i, half * i + half)
        up = nt(xr[...], uw) + ub[...]
        phi = 0.5 + 0.5 * lax.erf(up * (2.0**-0.5))
        hd = (up * phi).astype(BF16)
        hid[rws] = hd
        slope[rws] = (phi + up * jnp.exp(-0.5 * up * up) * 0.3989422804014327).astype(BF16)
        part = nn(hd, dw)
        part = part if before is None else before[...] + part
        out[...] = part.astype(out.dtype)


def ffn(x0, x1, ub, weights, sums, last):
    half, width, count = x0.shape[0], ub.shape[1], len(weights)
    n = 2 * half
    return call(
        functools.partial(ffn_kernel, not sums, count),
        (
            shape((n, width)),
            shape((n, width)),
            shape((half, D), F32),
            shape((half, D), BF16 if last else F32),
        ),
        (x0, x1, ub, *weights, *sums),
        cost=est(4 * n * D * width, 4 * D * width + 5e6, 2 * n * width),
    )


def second_kernel(
    bucket, lengths, first, part, got, small, cot, out, sum_two, low, sums
):
    c = place_here()[0]
    _, units = live_units(bucket, lengths)
    n, r = norm(first[...] + (part[...] + got[...].astype(F32) + small[5:6]))
    out[...] = (n * small[6:7] + small[7:8]).astype(BF16)
    index = lax.broadcasted_iota(jnp.int32, (first.shape[0], 1), 0)
    live = live_of(place_of(index, c), units)
    oc = jnp.where(live, cot[...].astype(F32), 0.0)
    st = norm_back(oc, n, r, small[6:7])
    sum_two[...] = st
    lo = st.astype(BF16)
    low[...] = lo
    sums[0:1] = jnp.sum(lo.astype(F32), 0, keepdims=True)
    sums[1:2] = jnp.sum(oc * n, 0, keepdims=True)
    sums[2:3] = jnp.sum(oc, 0, keepdims=True)


def second_norm(bucket, lengths, first, part, got, small, cot):
    n = first.shape[0]
    return call(
        second_kernel,
        (shape((n, D)), shape((n, D), F32), shape((n, D)), shape((3, D), F32)),
        (bucket, lengths, first, part, got, small, cot),
        cost=est(40 * n * D, 5e6),
        limit=8,
    )


def ffn_back_kernel(first, lead, count, d0, d1, x0, x1, *refs):
    far, hid_in, slope_in, refs = refs[:count], refs[count], refs[count + 1], refs[count + 2 :]
    if first:
        in0 = in1 = None
    else:
        (in0, in1), refs = refs[:2], refs[2:]
    outs, (ub, out0, out1) = refs[:count], refs[count:]
    half, width = x0.shape[0], ub.shape[1]
    slope, hid = slope_in.at[:, pl.ds(lead, width)], hid_in.at[:, pl.ds(lead, width)]
    uw, dw = ffn_weights(far)
    cots = []
    for i, (d, before, out) in enumerate(((d0, in0, out0), (d1, in1, out1))):
        rws = slice(half * i, half * i + half)
        uc = (nt(d[...], dw) * slope[rws].astype(F32)).astype(BF16)
        cots.append(uc)
        part = nn(uc, uw)
        part = part if before is None else before[...] + part
        out[...] = part.astype(out.dtype)
    ub[...] = jnp.sum(cots[0].astype(F32), 0, keepdims=True) + jnp.sum(
        cots[1].astype(F32), 0, keepdims=True
    )
    dg = (tn(hid[0:half], d0[...]) + tn(hid[half : 2 * half], d1[...])).astype(BF16)
    ug = (tn(cots[0], x0[...]) + tn(cots[1], x1[...])).astype(BF16)
    if len(outs[0].shape) == 2:
        outs[0][...], outs[1][...] = ug, dg
    else:
        rows = outs[0].shape[1] // 2
        at = 0
        for g in outs:
            for i in range(g.shape[0]):
                g[i, 0:rows] = ug[at : at + rows]
                g[i, rows : 2 * rows] = dg[at : at + rows]
                at += rows


def ffn_back(d0, d1, x0, x1, weights, kept, lead, sums, last):
    half, count = x0.shape[0], len(weights)
    flat = len(weights[0].shape) == 2
    width = weights[0].shape[0] if flat else sum(w.shape[0] * w.shape[1] // 2 for w in weights)
    *grads, ub, s0, s1 = call(
        functools.partial(ffn_back_kernel, not sums, lead, count),
        (
            *[shape(w.shape) for w in weights],
            shape((1, width), F32),
            shape((half, D), F32),
            shape((half, D), BF16 if last else F32),
        ),
        (d0, d1, x0, x1, *weights, *kept, *sums),
        cost=est(1000, 1000),
    )
    return grads, ub, (s0, s1)


def first_back_kernel(
    sum_two, part, got, normal, scale, small, *refs
):
    *refs, sum_one, low, sums = refs
    fc = sum_two[...] + part[...] + got[...].astype(F32)
    n = normal[...]
    so = norm_back(fc, n, scale[:, 0:1], small[3:4])
    sum_one[...] = so
    lo = so.astype(BF16)
    low[...] = lo
    sums[0:1] = jnp.sum(lo.astype(F32), 0, keepdims=True)
    sums[1:2] = jnp.sum(fc * n, 0, keepdims=True)
    sums[2:3] = jnp.sum(fc, 0, keepdims=True)
    if refs:
        add_moved_kernel(*refs)


def first_back(sum_two, part, got, normal, scale, small, moved=()):
    n = sum_two.shape[0]
    outs = [shape(moved[0].shape), shape(moved[2].shape)] if moved else []
    *added, sum_one, low, sums = call(
        first_back_kernel,
        (*outs, shape((n, D), F32), shape((n, D)), shape((3, D), F32)),
        (sum_two, part, got, normal, scale, small, *moved),
        cost=est(1000, 1000),
        limit=8,
    )
    return added, sum_one, low, sums


def attend_back_kernel(sets, a0, a1, *refs):
    far, outs, (in0, in1, sums), refs = refs[:9], refs[9 : 9 + sets], refs[9 + sets : 12 + sets], refs[12 + sets :]
    wp, v, probs, k, q, wr, x0, x1, ctx = far
    dctx, cots, grads, sems = refs
    copies = Copies(sems)
    c, z, y, x = place_here()
    half = a0.shape[0]
    n = 2 * half
    wpo = wp[:, pl.ds(pl.multiple_of(c * 384, 128), 384)]
    dctx[0:half] = nn(a0[...], wpo).astype(BF16)
    dctx[half:n] = nn(a1[...], wpo).astype(BF16)
    lane = lax.broadcasted_iota(jnp.int32, (n, 128), 1)
    zero = jnp.zeros((n, 128), BF16)
    scale = HEAD_DIM**-0.5
    heads = [[], [], []]
    for pair in range(3):
        lanes = slice(128 * pair, 128 * pair + 128)
        qp, kp, vp, dp = q[:, lanes], k[:, lanes], v[:, lanes], dctx[:, lanes]
        dq = dk = dv = 0.0
        for e in range(2):
            mine = (lane < HEAD_DIM) if e == 0 else (lane >= HEAD_DIM)
            dh, kh, qh = jnp.where(mine, dp, zero), jnp.where(mine, kp, zero), jnp.where(mine, qp, zero)
            pr = probs[2 * pair + e]
            dv = dv + tn(pr, dh)
            pf = pr.astype(F32)
            t = pf * nt(dh, vp)
            ds = (t - pf * jnp.sum(t, -1, keepdims=True)).astype(BF16)
            dq = dq + nn(ds, kh)
            dk = dk + tn(ds, qh)
        for t, val in enumerate((dq * scale, dk * scale, dv)):
            val = val.astype(BF16)
            for e in range(2):
                hd = 2 * pair + e
                g, hh = hd // 3, hd % 3
                at = 640 * g + 192 * t + 64 * hh
                cots[:, at : at + 64] = val[:, 64 * e : 64 * e + 64]
            heads[t].append(val)
    for g in range(2):
        cots[:, 640 * g + 576 : 640 * g + 640] = jnp.zeros((n, 64), BF16)
    parts = [jnp.concatenate(heads[t], 1) for t in range(3)]
    for i, out in enumerate((in0, in1)):
        rws = slice(half * i, half * i + half)
        total = 0.0
        for t in range(3):
            total = total + nn(parts[t][rws], wr[384 * t : 384 * t + 384])
        out[...] = total
    for row, t in ((0, 0), (1, 2)):
        s = jnp.sum(parts[t].astype(F32), 0, keepdims=True)
        for g in range(2):
            sg = s[:, 192 * g : 192 * g + 192]
            sums[row : row + 1, 384 * g : 384 * g + 192] = jnp.where(c == 0, sg, 0.0)
            sums[row : row + 1, 384 * g + 192 : 384 * g + 384] = jnp.where(c == 1, sg, 0.0)
    for d in range(3):
        at = slice(256 * d, 256 * d + 256)
        full = tn(x0[:, at], cots[0:half]) + tn(x1[:, at], cots[half:n])
        pg = tn(a0[:, at], ctx[0:half]) + tn(a1[:, at], ctx[half:n])
        for g in range(2):
            grads[g, at, 0:576] = full[:, 640 * g : 640 * g + 576].astype(BF16)
            grads[g, at, 576:768] = pg[:, 192 * g : 192 * g + 192].astype(BF16)
    if sets == 1:
        copies.start(grads, outs[0])
    else:
        rows = outs[0].shape[1]
        for spot in (3, 2, 1, 0):
            g, yi = flip(x, spot % 2), flip(y, spot // 2)
            for kz in range(4):
                zi = flip(lax.rem(z, 2), kz % 2) + 2 * flip(lax.div(z, 2), kz // 2)
                at = pl.multiple_of((2 * zi + yi) * rows, rows)
                dst = outs[spot].at[kz] if spot < 3 else outs[3 + kz // 2].at[kz % 2]
                copies.start(grads.at[g, pl.ds(at, rows)], dst)
    copies.wait()


def attend_back(direct, a0, a1, x0, x1, wp, wr, q, k, v, ctx, probs):
    half = a0.shape[0]
    n = 2 * half
    sets = (shape((2, D, D)),)
    if direct:
        sets = (shape((4, 96, D)),) * 3 + (shape((2, 96, D)),) * 2
    far = (wp, v, probs, k, q, wr, x0, x1, ctx)
    return call(
        functools.partial(attend_back_kernel, len(sets)),
        (*sets, shape((half, D), F32), shape((half, D), F32), shape((2, D), F32)),
        (a0, a1, *far),
        scratch=[
            pltpu.VMEM((n, 384), BF16),
            pltpu.VMEM((n, 1280), BF16),
            pltpu.VMEM((2, D, D), BF16),
        ],
        cost=est(1000, 1000),
        limit=16,
        far_out=range(len(sets)),
        sems=17,
    )


def local(
    inputs,
    bucket,
    lengths,
    qkv_weight,
    query_bias,
    value_bias,
    proj_weight,
    proj_bias,
    first_gain,
    first_shift,
    up_weight,
    up_bias,
    down_weight,
    down_bias,
    second_gain,
    second_shift,
    cotangent,
):
    head_count = lax.axis_size("head")
    batch_count = lax.axis_size("batch")
    devices = head_count * batch_count
    direct = batch_count == 8
    b = lax.axis_index("batch")
    h = lax.axis_index("head")
    me = b * head_count + h
    x, c = h // 2, h % 2
    z, y = b // 2, b % 2
    wq, wp, wf = 3 * D // devices, D // devices, FF // devices

    vectors = [
        query_bias,
        value_bias,
        proj_bias,
        first_gain,
        first_shift,
        down_bias,
        second_gain,
        second_shift,
    ]
    if direct:
        a_shard, fa_shard, fb_shard = pack(
            qkv_weight.T, proj_weight.T, up_weight.T, down_weight, up_bias, vectors
        )
    else:
        small = lax.dynamic_update_slice(
            jnp.zeros((16, D), BF16), jnp.stack(vectors), (0, me * wp)
        )
        per_row = D // wf
        small = lax.dynamic_update_slice(
            small, up_bias[None, :], (8 + me // per_row, (me % per_row) * wf)
        )
        proj_t = proj_weight.T.reshape(wp, 2, 2, 192).transpose(0, 2, 1, 3).reshape(wp, D)
        a_shard = jnp.concatenate([qkv_weight.T, proj_t, small])
    other_in = core_swap(inputs)
    k = jnp.arange(batch_count * 2)
    if direct:
        a_z = jnp.stack(z_line(a_shard))
        a_z, other_in = lax.optimization_barrier((a_z, other_in))
        fa_z = z_line(after(fa_shard, a_z))
        a_x, a_y = x_swap(a_z), y_swap(a_z)
        a_x, a_y, fa_z = lax.optimization_barrier((a_x, a_y, fa_z))
        fb_z = z_line(after(fb_shard, fa_z))
        a_d = [x_swap(a_y[:2]), y_swap(a_x[2:])]
        a_d, fb_z = lax.optimization_barrier((a_d, fb_z))
        a_own = [a_z, a_x, a_y, *a_d]
        a_swapped = [core_swap(v) for v in after(a_own, fb_z)]
        f_z = jnp.stack([jnp.concatenate(pair) for pair in zip(fa_z, fb_z)])
        f_x, f_y, *f_d = gather_four(f_z)[1:]
        ctx_own, ctx_other, q, kk, v, ctx, probs, wr, ub_all, proj_w, small_all = attend(
            bucket, lengths, inputs, other_in, (*a_own, *a_swapped), wq, wp
        )
        f_all = [[f_z], [f_x, f_y], f_d]
    else:
        a_all = lax.all_gather(a_shard, ("batch", "head"), axis=0)
        qkv_all = a_all[:, :wq].reshape(2, 2, 576, D)
        qkv_w = lax.dynamic_index_in_dim(qkv_all, c, 1, keepdims=False).reshape(2 * 576, D)
        proj_w = a_all[:, wq : wq + wp].reshape(D, D)
        small_all = jnp.sum(a_all[:, wq + wp :].astype(F32), 0)
        ctx_own, ctx_other, q, kk, v, ctx, probs, wr = attend(
            bucket, lengths, inputs, other_in, (qkv_w, small_all)
        )
        f_shard = jnp.concatenate([up_weight.T, down_weight])
        f_all = [
            (v[:, :wf].reshape(-1, D), v[:, wf:].reshape(-1, D)) for v in gather_any(f_shard)
        ]
        owner = (k % batch_count) * 4 + (x ^ (k // batch_count)) * 2 + c
    if not direct:
        spread = (owner[None, :] == jnp.arange(devices)[:, None]).astype(F32)
        ub_all = tn(spread, small_all[8:12].reshape(devices, wf)).reshape(1, FF // 2)

    ctx_in = core_swap(ctx_other)
    first_low, first, first_n, first_r = first_norm(inputs, ctx_own, ctx_in, proj_w, small_all)
    first_in = core_swap(first_low)
    sums = ()
    kept = []
    at = 0
    for weights in f_all:
        width = (384, 768, 384)[len(kept)] if direct else FF // 4
        hid, slope, *sums = ffn(
            first_low,
            first_in,
            ub_all[:, at : at + width],
            weights,
            sums,
            len(kept) == len(f_all) - 1,
        )
        kept.append((hid, slope))
        at += width
    layer_out, sum_two, down_low, sums_two = second_norm(
        bucket, lengths, first, sums[0], core_swap(sums[1]), small_all, cotangent
    )
    down_in = core_swap(down_low)

    sums = ()
    f_parts, ub_parts = [], []
    if direct:
        sets = (([f_z], 0, 0), ([f_x], 1, 0), ([f_y], 1, 384), (f_d, 2, 0))
        for weights, which, lead in reversed(sets):
            grads, ub, sums = ffn_back(
                down_low, down_in, first_low, first_in, weights, kept[which], lead, sums, which + lead == 0
            )
            f_parts = grads + f_parts
            ub_parts.insert(0, ub)
    else:
        for weights, pair in zip(f_all, kept):
            grads, ub, sums = ffn_back(
                down_low, down_in, first_low, first_in, weights, pair, 0, sums, len(f_parts) == len(f_all) - 1
            )
            f_parts.append(grads)
            ub_parts.append(ub)
    part_own, part_other = sums
    moved = ()
    if direct:
        moved = (f_parts[1], y_swap(f_parts[4]), f_parts[2], x_swap(f_parts[3]))
        part_other = after(part_other, moved)
    added, sum_one, attn_low, sums_one = first_back(
        sum_two, part_own, core_swap(part_other), first_n, first_r, small_all, moved
    )
    attn_in = core_swap(attn_low)
    *a_grads, in_own, in_other, sums_zero = attend_back(
        direct,
        attn_low,
        attn_in,
        inputs,
        other_in,
        proj_w,
        wr,
        q,
        kk,
        v,
        ctx,
        probs,
    )
    in_got = core_swap(in_other)
    inputs_grad = (sum_one + in_own + in_got).astype(BF16)

    if direct:
        f_sets = scatter_xy(f_parts[0], *added)
        f_mine, (f_ups, f_downs) = combine(*f_sets, 2)
        terms = exchange_terms(sums_zero, sums_one, sums_two, ub_parts, devices)
        terms = lax.all_to_all(terms, ("batch", "head"), split_axis=0, concat_axis=0, tiled=True)
        a_zz, a_xx, a_yy, d_lo, d_hi = a_grads
        d_lo, d_hi = after((d_lo, d_hi), (f_sets, in_got, terms))
        d_lo, d_hi = x_swap(d_lo), y_swap(d_hi)
        f_ups = scatter_z(f_ups)
        d_lo, d_hi, f_ups = lax.optimization_barrier((d_lo, d_hi, f_ups))
        a_xx, a_yy = add_moved(a_xx, d_hi, a_yy, d_lo)
        a_sets = scatter_xy(a_zz, a_xx, a_yy)
        f_downs = scatter_z(after(f_downs, f_ups))
        a_sets, f_downs, _ = lax.optimization_barrier((a_sets, f_downs, inputs_grad))
        a_mine, (a_others,) = combine(*a_sets, 1)
        up_grad, down_grad = finish_ffn(f_mine, f_ups, f_downs)
        up_grad = up_grad.T
        terms = jnp.sum(terms, 0)
        packed = jnp.concatenate([terms[:, :wp].reshape(-1), terms[0, wp : wp + wf]])
        qkv_grad, proj_grad = finish_attend((a_mine, *scatter_z(a_others)))
    else:
        vecs = jnp.concatenate([sums_zero, sums_one, sums_two])
        vecs = vecs.reshape(8, devices, wp).transpose(1, 0, 2).reshape(devices, 8 * wp)
        ubias = jnp.concatenate(ub_parts).reshape(batch_count * 2, wf)
        ubias = lax.dot_general(
            spread, ubias, (((1,), (0,)), ((), ())), precision=lax.Precision.HIGHEST
        )
        packed = jnp.concatenate([vecs, ubias], 1)
        packed = lax.all_to_all(
            packed, ("batch", "head"), split_axis=0, concat_axis=0, tiled=True
        )
        packed = jnp.sum(packed, 0)
        wb = D // batch_count
        a_grads = a_grads[0].reshape(2, batch_count, wb, D)
        a_mine = scatter_any(
            [
                lax.dynamic_index_in_dim(a_grads, x, 0, keepdims=False),
                lax.dynamic_index_in_dim(a_grads, 1 - x, 0, keepdims=False),
            ]
        )
        f_mine = scatter_any(
            [
                jnp.concatenate(
                    [ug.reshape(batch_count, wf, D), dg.reshape(batch_count, wf, D)], 1
                )
                for ug, dg in f_parts
            ]
        )
        qkv_grad = a_mine[:, :576].reshape(wb, 3, 3, HEAD_DIM).transpose(0, 2, 1, 3)
        qkv_grad = qkv_grad.reshape(wb, 576)
        proj_grad = a_mine[:, 576:].T
        up_grad, down_grad = f_mine[:wf].T, f_mine[wf:]
    qb_g, vb_g, pb_g, fg_g, fs_g, db_g, sg_g, ss_g = [
        packed[i * wp : (i + 1) * wp] for i in range(8)
    ]
    return (
        layer_out,
        inputs_grad,
        qkv_grad,
        qb_g,
        vb_g,
        proj_grad,
        pb_g,
        fg_g,
        fs_g,
        up_grad,
        packed[8 * wp :],
        down_grad,
        db_g,
        sg_g,
        ss_g,
    )


def solution(mesh):
    both = ("batch", "head")
    in_specs = (
        P(both, None),
        P("batch"),
        P("batch", None),
        P(None, both),
        P(both),
        P(both),
        P(None, both),
        P(both),
        P(both),
        P(both),
        P(None, both),
        P(both),
        P(both, None),
        P(both),
        P(both),
        P(both),
        P(both, None),
    )
    out_specs = (
        P(both, None),
        P(both, None),
        P("batch", "head"),
        P(both),
        P(both),
        P("head", "batch"),
        P(both),
        P(both),
        P(both),
        P(None, both),
        P(both),
        P(both, None),
        P(both),
        P(both),
        P(both),
    )
    return jax.shard_map(local, mesh=mesh, in_specs=in_specs, out_specs=out_specs, check_vma=False)
```

```python
import functools

import jax
import jax.numpy as jnp
from jax import lax
from jax.experimental import pallas as pl
from jax.experimental.pallas import tpu as pltpu
from jax.sharding import PartitionSpec as P

D = 768
HEADS = 12
HEAD_DIM = 64
FF = 3072
BIG = 512
SMALL = 128
UNITS = 4
NORM_EPS = 1e-12
F32 = jnp.float32
BF16 = jnp.bfloat16

ONE, TWO = 80, 16
FIRST = 104

CORE = [(i, i ^ 1) for i in range(4)]
XPAIR = [(i, i ^ 2) for i in range(4)]
YPAIR = [(i, i ^ 1) for i in range(8)]
ZPAIR = [[(i, i ^ (2 * k)) for i in range(8)] for k in range(4)]


def core_swap(v):
    return lax.ppermute(v, "head", CORE)


def x_swap(v):
    return lax.ppermute(v, "head", XPAIR)


def y_swap(v):
    return lax.ppermute(v, "batch", YPAIR)


def z_swap(v, k):
    return lax.ppermute(v, "batch", ZPAIR[k])


def after(value, other):
    return lax.optimization_barrier((value, other))[0]


def nt(a, b, out=F32):
    return lax.dot_general(a, b, (((1,), (1,)), ((), ())), preferred_element_type=F32).astype(out)


def nn(a, b, out=F32):
    return lax.dot_general(a, b, (((1,), (0,)), ((), ())), preferred_element_type=F32).astype(out)


def tn(a, b, out=F32):
    return lax.dot_general(a, b, (((0,), (0,)), ((), ())), preferred_element_type=F32).astype(out)


def z_line(shard):
    return [shard] + [z_swap(shard, k) for k in (1, 2, 3)]


def gather_four(z):
    x, y = x_swap(z), y_swap(z)
    return [z, x, y, x_swap(y[:2]), y_swap(x[2:])]


def gather_any(shard):
    whole = lax.all_gather(shard, "batch", axis=0)
    return [whole, x_swap(whole)]


def scatter_xy(z, x, y):
    return z, x_swap(x), y_swap(y)


def scatter_z(others):
    return [z_swap(others[k - 1], k) for k in (1, 2, 3)]


def scatter_any(parts):
    total = parts[0].astype(F32) + x_swap(parts[1]).astype(F32)
    return lax.psum_scatter(total, "batch", scatter_dimension=0, tiled=False)


def est(flops, moved, trans=0):
    return pl.CostEstimate(flops=int(flops), bytes_accessed=int(moved), transcendentals=int(trans))


def call(kernel, out_shape, operands, scratch=(), cost=None, limit=16, far_in=(), far_out=(), sems=0):
    vmem = pl.BlockSpec(memory_space=pltpu.VMEM)
    hbm = pl.BlockSpec(memory_space=pltpu.HBM)
    smem = pl.BlockSpec(memory_space=pltpu.SMEM)
    ins = [hbm if i in far_in else vmem for i in range(len(operands))]
    ins = [smem if v.dtype == jnp.int32 else spec for spec, v in zip(ins, operands)]
    outs = [hbm if i in far_out else vmem for i in range(len(out_shape))]
    scratch = list(scratch) + ([pltpu.SemaphoreType.DMA((sems,))] if sems else [])
    operands = [
        pltpu.with_memory_space_constraint(v, pltpu.HBM) if i in far_in else v
        for i, v in enumerate(operands)
    ]
    out_shape = [
        pltpu.HBM(v.shape, v.dtype) if i in far_out else v for i, v in enumerate(out_shape)
    ]
    return pl.pallas_call(
        kernel,
        out_shape=out_shape,
        in_specs=ins,
        out_specs=outs,
        scratch_shapes=scratch,
        compiler_params=pltpu.CompilerParams(vmem_limit_bytes=limit << 20),
        cost_estimate=cost,
    )(*operands)


class Copies:
    def __init__(self, sems):
        self.sems, self.used, self.open = sems, 0, []

    def start(self, src, dst):
        copy = pltpu.make_async_copy(src, dst, self.sems.at[self.used])
        self.used += 1
        copy.start()
        self.open.append(copy)
        return copy

    def wait(self, *copies):
        for copy in copies or list(self.open):
            copy.wait()
            self.open.remove(copy)


def add_low(a, b):
    return (a.astype(F32) + b.astype(F32)).astype(BF16)


def shape(dims, dtype=BF16):
    return jax.ShapeDtypeStruct(dims, dtype)


def add_moved_kernel(x, for_x, y, for_y, x_out, y_out):
    y_out[0:2] = add_low(y[0:2], for_y[...])
    y_out[2:4] = y[2:4]
    x_out[0:2] = x[0:2]
    x_out[2:4] = add_low(x[2:4], for_x[...])


def add_moved(x, for_x, y, for_y):
    return call(
        add_moved_kernel,
        (shape(x.shape), shape(y.shape)),
        (x, for_x, y, for_y),
        cost=est(1000, 1000),
        limit=8,
    )


def combine_kernel(parts, z, x, y, *refs):
    outs, (mine, low, sems) = refs[: 1 + 3 * parts], refs[1 + 3 * parts :]
    copies = Copies(sems)
    rows = z.shape[1] // parts
    for k in (1, 2, 3, 0):
        total = z[k].astype(F32) + x[k].astype(F32) + y[k].astype(F32)
        if k == 0:
            mine[...] = total
            copies.start(mine, outs[0])
        else:
            low[k - 1] = total.astype(BF16)
            for i in range(parts):
                copies.start(low.at[k - 1, pl.ds(rows * i, rows)], outs[1 + 3 * i + k - 1])
    copies.wait()


def combine(z, x, y, parts):
    rows = z.shape[1]
    mine, *others = call(
        functools.partial(combine_kernel, parts),
        (shape((rows, D), F32),) + (shape((rows // parts, D)),) * (3 * parts),
        (z, x, y),
        scratch=[pltpu.VMEM((rows, D), F32), pltpu.VMEM((3, rows, D), BF16)],
        cost=est(1000, 1000),
        limit=8,
        far_out=range(1 + 3 * parts),
        sems=1 + 3 * parts,
    )
    return mine, [others[3 * i : 3 * i + 3] for i in range(parts)]


def total_of(refs):
    return refs[0][...] + refs[1][...].astype(F32) + refs[2][...].astype(F32) + refs[3][...].astype(F32)


def finish_attend_kernel(mine, one, two, three, qkv, proj):
    total = total_of((mine, one, two, three))
    for hh in range(3):
        for t in range(3):
            at, to = 192 * t + 64 * hh, 192 * hh + 64 * t
            qkv[:, to : to + 64] = total[:, at : at + 64]
    proj[...] = total[:, 576:].T


def finish_attend(parts):
    rows = parts[0].shape[0]
    return call(
        finish_attend_kernel,
        (shape((rows, 576), F32), shape((192, rows), F32)),
        tuple(parts),
        cost=est(8 * rows * D, 16 * rows * D),
    )


def finish_ffn_kernel(mine, *refs):
    ups, downs, (up, down) = refs[:3], refs[3:6], refs[6:]
    half = mine.shape[0] // 2
    up[...] = mine[0:half] + sum(r[...].astype(F32) for r in ups)
    down[...] = mine[half:] + sum(r[...].astype(F32) for r in downs)


def finish_ffn(mine, ups, downs):
    half = mine.shape[0] // 2
    return call(
        finish_ffn_kernel,
        (shape((half, D), F32), shape((half, D), F32)),
        (mine, *ups, *downs),
        cost=est(1000, 1000),
        limit=8,
    )


def exchange_kernel(zero, one, two, *refs):
    ubs, out = refs[:4], refs[4]
    vecs = jnp.concatenate([zero[...], one[...], two[...]])
    width = D // out.shape[0]
    out[...] = jnp.zeros(out.shape, F32)
    for i in range(out.shape[0]):
        out[i, 0:8, 0:width] = vecs[:, width * i : width * i + width]
    for spot in range(4):
        for kz in range(4):
            to, ub = slot_of(spot, kz), ubs[spot]
            out[to, 0:1, 24 : 24 + ONE] = ub[:, ONE * kz : ONE * kz + ONE]
            at = 4 * ONE + TWO * kz
            out[to, 0:1, 24 + ONE : 24 + ONE + TWO] = ub[:, at : at + TWO]


def exchange_terms(zero, one, two, ubs, devices):
    return call(
        exchange_kernel,
        (shape((devices, 8, 128), F32),),
        (zero, one, two, *ubs),
        cost=est(1000, 1000),
        limit=8,
    )[0]


def flip(a, bit):
    return a + bit - 2 * a * bit


def pack_kernel(qkv_in, proj_in, up_in, down_in, bias, vectors, a_out, one_a, one_b, two, a, p, f, sems):
    rows_q, rows_p, half = qkv_in.shape[0], proj_in.shape[0], down_in.shape[0]
    copies = Copies(sems)
    copies.start(qkv_in, a.at[pl.ds(0, rows_q)])
    copies.start(proj_in, p)
    copies.start(up_in, f.at[pl.ds(0, half)])
    copies.start(down_in, f.at[pl.ds(half, half)])
    width = vectors.shape[1]
    b, h = lax.axis_index("batch"), lax.axis_index("head")
    me = b * lax.axis_size("head") + h
    v = vectors[...].astype(F32)
    v = jnp.concatenate([v] * (D // width), 1)
    lane = lax.broadcasted_iota(jnp.int32, (8, D), 1)
    mine = jnp.logical_and(lane >= me * width, lane < me * width + width)
    v = jnp.where(mine, v, 0.0)
    gap = jnp.zeros((1, D // 2 - half), F32)
    none = jnp.zeros((1, D // 2), F32)
    row = bias[...].astype(F32)
    early = jnp.concatenate([none, row, gap], 1)
    late = jnp.concatenate([row, gap, none], 1)
    extra = jnp.where(me < lax.axis_size("batch") * lax.axis_size("head") // 2, early, late)
    v = v + jnp.concatenate([extra, jnp.zeros((7, D), F32)])
    copies.wait()
    a_out[0:rows_q] = a[0:rows_q]
    q = p[...]
    a_out[rows_q : rows_q + rows_p] = jnp.concatenate(
        [q[:, 192 * i : 192 * i + 192] for i in (0, 2, 1, 3)], 1
    )
    a_out[rows_q + rows_p :] = v.astype(BF16)
    one = jnp.concatenate([f[0:ONE], f[half : half + ONE]])
    one_a[...], one_b[...] = one[0:FIRST], one[FIRST:]
    two[0:TWO], two[TWO:] = f[ONE:half], f[half + ONE :]


def pack(qkv, proj, up, down, bias, vectors):
    rows, half = qkv.shape[0] + proj.shape[0] + 8, down.shape[0]
    return call(
        pack_kernel,
        (
            shape((rows, D)),
            shape((FIRST, D)),
            shape((2 * ONE - FIRST, D)),
            shape((2 * TWO, D)),
        ),
        (qkv, proj, up, down, bias[None], jnp.stack(vectors)),
        scratch=[
            pltpu.VMEM((rows, D), BF16),
            pltpu.VMEM(proj.shape, BF16),
            pltpu.VMEM((2 * half, D), BF16),
        ],
        cost=est(1000, 1000),
        limit=8,
        far_in=(0, 1, 2, 3),
        sems=4,
    )


def place_here():
    b, h = lax.axis_index("batch"), lax.axis_index("head")
    return lax.rem(h, 2), lax.div(b, 2), lax.rem(b, 2), lax.div(h, 2)


def live_units(bucket, lengths):
    x = place_here()[3]
    kind, first = bucket[x], lengths[x, 0]
    units = []
    for u in range(UNITS):
        far = jnp.clip(first - SMALL * u, 0, SMALL)
        units.append(jnp.where(kind == 1, far, lengths[x, u]))
    return kind, units


def place_of(index, c):
    return jnp.bitwise_xor(index, c * (BIG // 2))


def live_of(place, units):
    unit = lax.shift_right_logical(place, 7)
    inner = jnp.bitwise_and(place, SMALL - 1)
    count = jnp.where(
        unit < 2, jnp.where(unit == 0, units[0], units[1]), jnp.where(unit == 2, units[2], units[3])
    )
    return inner < count


def heads_of(row, c):
    parts = []
    for g in range(2):
        lo = row[:, 384 * g : 384 * g + 192]
        hi = row[:, 384 * g + 192 : 384 * g + 384]
        parts.append(jnp.where(c == 0, lo, hi))
    return jnp.concatenate(parts, 1)


def fetch_shards(copies, sources, slots):
    c, z, y, x = place_here()
    zl, zh = lax.rem(z, 2), lax.div(z, 2)
    for swapped in range(2):
        cc = c if swapped == 0 else 1 - c
        zs, xs, ys, xa, xb = sources[5 * swapped : 5 * swapped + 5]
        for kx, ky, pair in ((0, 0, (zs,)), (1, 0, (xs,)), (0, 1, (ys,)), (1, 1, (xa, xb))):
            j = flip(y, ky) * 4 + flip(x, kx) * 2 + cc
            for kz in range(4):
                src = pair[0].at[kz] if len(pair) == 1 else pair[kz // 2].at[kz % 2]
                zi = flip(zl, kz % 2) + 2 * flip(zh, kz // 2)
                copies.start(src, slots.at[zi * 8 + j])


def slot_of(spot, kz):
    c, z, y, x = place_here()
    zi = flip(lax.rem(z, 2), kz % 2) + 2 * flip(lax.div(z, 2), kz // 2)
    return zi * 8 + flip(y, spot // 2) * 4 + flip(x, spot % 2) * 2 + c


def bias_order(slots, row, out):
    for spot in range(4):
        for kz in range(4):
            i = slot_of(spot, kz)
            b = slots[i, row : row + 1].astype(F32)
            b = jnp.where(i < 16, b[:, D // 2 : D // 2 + 96], b[:, 0:96])
            at = 4 * ONE * spot + ONE * kz
            out[:, at : at + ONE] = b[:, 0:ONE]
            at = 16 * ONE + 4 * TWO * spot + TWO * kz
            out[:, at : at + TWO] = b[:, ONE:]


def attend_kernel(rows_q, rows_p, bucket, lengths, x0, x1, *refs):
    sources = 10 if rows_q else 2
    weights, refs = refs[:sources], refs[sources:]
    (ctx0, ctx1, q, k, v, ctx, probs, wr), refs = refs[:8], refs[8:]
    if rows_q:
        (ub_out, wp, small, mask, xs, slots, sems) = refs
    else:
        (mask, xs, w, small, sems) = refs
    copies = Copies(sems)
    c = place_here()[0]
    kind, units = live_units(bucket, lengths)
    half = x0.shape[0]
    copies.start(x0, xs.at[0:half])
    copies.start(x1, xs.at[half : 2 * half])
    if rows_q:
        fetch_shards(copies, weights, slots)
    else:
        copies.start(weights[0], w)
        copies.start(weights[1], small)
    rows = lax.broadcasted_iota(jnp.int32, (BIG, BIG), 0)
    cols = lax.broadcasted_iota(jnp.int32, (BIG, BIG), 1)
    prow, pcol = place_of(rows, c), place_of(cols, c)
    same = jnp.logical_or(
        kind == 1, lax.shift_right_logical(prow, 7) == lax.shift_right_logical(pcol, 7)
    )
    mask[...] = jnp.where(jnp.logical_and(same, live_of(pcol, units)), 0.0, -1e30)
    copies.wait()
    if rows_q:
        for g in range(2):
            cuts = jnp.concatenate([slots[16 * g + 8 * c + j, 0:rows_q] for j in range(8)])
            for t in range(3):
                for hh in range(3):
                    src, dst = (hh * 3 + t) * HEAD_DIM, (t * 6 + g * 3 + hh) * HEAD_DIM
                    wr[dst : dst + HEAD_DIM] = cuts[src : src + HEAD_DIM]
        lane = lax.broadcasted_iota(jnp.int32, (8, D), 1)
        small[...] = sum(
            jnp.where(
                jnp.logical_and(lane >= rows_p * i, lane < rows_p * i + rows_p),
                slots[i, rows_q + rows_p :].astype(F32),
                0.0,
            )
            for i in range(32)
        )
    else:
        for t in range(3):
            for hd in range(6):
                src = ((hd // 3) * 9 + (hd % 3) * 3 + t) * HEAD_DIM
                dst = (t * 6 + hd) * HEAD_DIM
                wr[dst : dst + HEAD_DIM] = w[src : src + HEAD_DIM]
    biases = (heads_of(small[0:1], c), None, heads_of(small[1:2], c))
    for t, ref in enumerate((q, k, v)):
        val = nt(xs[...], wr[384 * t : 384 * t + 384])
        if biases[t] is not None:
            val = val + biases[t]
        ref[...] = val.astype(BF16)
    if rows_q:
        for i in range(32):
            wp[rows_p * i : rows_p * i + rows_p] = slots[i, rows_q : rows_q + rows_p]
        bias_order(slots, rows_q + rows_p, ub_out)
    lane = lax.broadcasted_iota(jnp.int32, (half, 128), 1)
    for pair in range(3):
        lanes = slice(128 * pair, 128 * pair + 128)
        kp, vp = k[:, lanes], v[:, lanes]
        for i, near in enumerate((ctx0, ctx1)):
            rws = slice(half * i, half * i + half)
            qp = q[rws, lanes] * jnp.asarray(HEAD_DIM**-0.5, BF16)
            outs = []
            for e in range(2):
                mine = (lane < HEAD_DIM) if e == 0 else (lane >= HEAD_DIM)
                s = nt(jnp.where(mine, qp, jnp.zeros_like(qp)), kp) + mask[rws]
                ex = jnp.exp(s - jnp.max(s, -1, keepdims=True))
                pr = (ex * (1.0 / jnp.sum(ex, -1, keepdims=True))).astype(BF16)
                probs[2 * pair + e, rws] = pr
                outs.append(nn(pr, vp))
            val = jnp.where(lane < HEAD_DIM, outs[0], outs[1]).astype(BF16)
            ctx[rws, lanes] = val
            near[:, lanes] = val


def attend(bucket, lengths, x0, x1, weights, rows_q=0, rows_p=0, rows_s=16):
    rows_s = 8 if rows_q else rows_s
    half = x0.shape[0]
    n = 2 * half
    direct = rows_q > 0
    outs = [
        shape((half, 384)),
        shape((half, 384)),
        shape((n, 384)),
        shape((n, 384)),
        shape((n, 384)),
        shape((n, 384)),
        shape((6, n, n)),
        shape((1152, D)),
    ]
    scratch = [pltpu.VMEM((n, n), F32), pltpu.VMEM((n, D), BF16)]
    if direct:
        outs += [shape((1, FF // 2), F32), shape((D, D)), shape((rows_s, D), F32)]
        scratch += [pltpu.VMEM((32, rows_q + rows_p + rows_s, D), BF16)]
    else:
        scratch += [pltpu.VMEM((1152, D), BF16), pltpu.VMEM((rows_s, D), F32)]
    operands = (bucket, lengths, x0, x1, *weights)
    return call(
        functools.partial(attend_kernel, rows_q, rows_p),
        outs,
        operands,
        scratch=scratch,
        cost=est(2 * n * D * 1152 + 8 * n * n * 384, 12e6, 6 * n * n),
        limit=32,
        far_in=range(2, len(operands)),
        sems=50,
    )


def norm(values):
    center = values - jnp.mean(values, -1, keepdims=True)
    spread = jnp.mean(center * center, -1, keepdims=True)
    scale = lax.rsqrt(spread + NORM_EPS)
    return center * scale, scale


def norm_back(cot, normal, scale, gain):
    w = cot * gain
    return scale * (
        w - jnp.mean(w, -1, keepdims=True) - normal * jnp.mean(w * normal, -1, keepdims=True)
    )


def first_kernel(x, ctx_own, ctx_in, wp, small, low, first, normal, scale):
    c = place_here()[0]
    mine = pl.multiple_of(c * 384, 128)
    theirs = pl.multiple_of((1 - c) * 384, 128)
    attn = nt(ctx_own[...], wp[:, pl.ds(mine, 384)]) + nt(ctx_in[...], wp[:, pl.ds(theirs, 384)])
    n, r = norm(x[...].astype(F32) + attn + small[2:3])
    normal[...] = n
    out = n * small[3:4] + small[4:5]
    first[...] = out
    low[...] = out.astype(BF16)
    scale[...] = jnp.broadcast_to(r, scale.shape)


def first_norm(x, ctx_own, ctx_in, wp, small):
    n = x.shape[0]
    return call(
        first_kernel,
        (shape((n, D)), shape((n, D), F32), shape((n, D), F32), shape((n, 128), F32)),
        (x, ctx_own, ctx_in, wp, small),
        cost=est(2 * n * D * D, 5e6),
        limit=8,
    )


def ffn_weights(refs):
    if len(refs[0].shape) == 2:
        return refs[0][...], refs[1][...]
    return stacked(ones_of(refs) if refs[0].shape[1] == 2 * ONE else twos_of(refs, range(4)))


def ones_of(refs):
    return [(r, i) for r in refs for i in range(r.shape[0])]


def twos_of(refs, spots):
    along_z = [(r, i) for r in refs for i in range(0, r.shape[0], 4)]
    return [(r, i + spot) for spot in spots for r, i in along_z]


def stacked(blocks):
    up = jnp.concatenate([r[i, 0 : r.shape[1] // 2] for r, i in blocks])
    down = jnp.concatenate([r[i, r.shape[1] // 2 :] for r, i in blocks])
    return up, down


def ffn_kernel(first, count, x0, x1, ub, *refs):
    far, refs = refs[:count], refs[count:]
    if first:
        in0 = in1 = None
    else:
        (in0, in1), refs = refs[:2], refs[2:]
    hid, slope, out0, out1 = refs
    half = x0.shape[0]
    uw, dw = ffn_weights(far)
    for i, (xr, before, out) in enumerate(((x0, in0, out0), (x1, in1, out1))):
        rws = slice(half * i, half * i + half)
        up = nt(xr[...], uw) + ub[...]
        phi = 0.5 + 0.5 * lax.erf(up * (2.0**-0.5))
        hd = (up * phi).astype(BF16)
        hid[rws] = hd
        slope[rws] = (phi + up * jnp.exp(-0.5 * up * up) * 0.3989422804014327).astype(BF16)
        part = nn(hd, dw)
        part = part if before is None else before[...] + part
        out[...] = part.astype(out.dtype)


def ffn(x0, x1, ub, weights, sums, last):
    half, width, count = x0.shape[0], ub.shape[1], len(weights)
    n = 2 * half
    return call(
        functools.partial(ffn_kernel, not sums, count),
        (
            shape((n, width)),
            shape((n, width)),
            shape((half, D), F32),
            shape((half, D), BF16 if last else F32),
        ),
        (x0, x1, ub, *weights, *sums),
        cost=est(4 * n * D * width, 4 * D * width + 5e6, 2 * n * width),
    )


def second_kernel(
    bucket, lengths, first, part, got, small, cot, out, sum_two, low, sums
):
    c = place_here()[0]
    _, units = live_units(bucket, lengths)
    n, r = norm(first[...] + (part[...] + got[...].astype(F32) + small[5:6]))
    out[...] = (n * small[6:7] + small[7:8]).astype(BF16)
    index = lax.broadcasted_iota(jnp.int32, (first.shape[0], 1), 0)
    live = live_of(place_of(index, c), units)
    oc = jnp.where(live, cot[...].astype(F32), 0.0)
    st = norm_back(oc, n, r, small[6:7])
    sum_two[...] = st
    lo = st.astype(BF16)
    low[...] = lo
    sums[0:1] = jnp.sum(lo.astype(F32), 0, keepdims=True)
    sums[1:2] = jnp.sum(oc * n, 0, keepdims=True)
    sums[2:3] = jnp.sum(oc, 0, keepdims=True)


def second_norm(bucket, lengths, first, part, got, small, cot):
    n = first.shape[0]
    return call(
        second_kernel,
        (shape((n, D)), shape((n, D), F32), shape((n, D)), shape((3, D), F32)),
        (bucket, lengths, first, part, got, small, cot),
        cost=est(40 * n * D, 5e6),
        limit=8,
    )


def ffn_back_kernel(first, spot, count, d0, d1, x0, x1, *refs):
    weights, refs = refs[:count], refs[count:]
    if spot is None:
        hid, slope = refs[0], refs[1]
        refs = refs[2:]
        uw, dw = ffn_weights(weights)
    else:
        (hid1, slope1, hid2, slope2), refs = refs[:4], refs[4:]
        tail = slice(4 * TWO * spot, 4 * TWO * spot + 4 * TWO)
        hid = jnp.concatenate([hid1[...], hid2[:, tail]], 1)
        slope = jnp.concatenate([slope1[...], slope2[:, tail]], 1)
        uw, dw = stacked(ones_of(weights[:-3]) + twos_of(weights[-3:], [spot]))
    if first:
        in0 = in1 = None
    else:
        (in0, in1), refs = refs[:2], refs[2:]
    *outs, ub, out0, out1 = refs
    half = x0.shape[0]
    cots = []
    for i, (d, before, out) in enumerate(((d0, in0, out0), (d1, in1, out1))):
        rws = slice(half * i, half * i + half)
        uc = (nt(d[...], dw) * slope[rws].astype(F32)).astype(BF16)
        cots.append(uc)
        part = nn(uc, uw)
        part = part if before is None else before[...] + part
        out[...] = part.astype(out.dtype)
    ub[...] = jnp.sum(cots[0].astype(F32), 0, keepdims=True) + jnp.sum(
        cots[1].astype(F32), 0, keepdims=True
    )
    dg = (tn(hid[0:half], d0[...]) + tn(hid[half : 2 * half], d1[...])).astype(BF16)
    ug = (tn(cots[0], x0[...]) + tn(cots[1], x1[...])).astype(BF16)
    if spot is None:
        outs[0][...], outs[1][...] = ug, dg
        return
    rows = ONE + TWO
    for k in range(4):
        out, i = (outs[0], k) if len(outs) == 1 else (outs[k // 2], k % 2)
        for at, g in ((0, ug), (rows, dg)):
            out[i, at : at + ONE] = g[ONE * k : ONE * k + ONE]
            low = 4 * ONE + TWO * k
            out[i, at + ONE : at + rows] = g[low : low + TWO]


def ffn_back(d0, d1, x0, x1, spot, weights, kept, sums, last):
    half, count = x0.shape[0], len(weights)
    if spot is None:
        outs, width = [shape(w.shape) for w in weights], weights[0].shape[0]
    else:
        width = 4 * (ONE + TWO)
        outs = [shape((2, width // 2, D))] * 2 if spot == 3 else [shape((4, width // 2, D))]
    *grads, ub, s0, s1 = call(
        functools.partial(ffn_back_kernel, not sums, spot, count),
        (
            *outs,
            shape((1, width), F32),
            shape((half, D), F32),
            shape((half, D), BF16 if last else F32),
        ),
        (d0, d1, x0, x1, *weights, *kept, *sums),
        cost=est(1000, 1000),
    )
    return grads, ub, (s0, s1)


def first_back_kernel(
    sum_two, part, got, normal, scale, small, *refs
):
    *refs, sum_one, low, sums = refs
    fc = sum_two[...] + part[...] + got[...].astype(F32)
    n = normal[...]
    so = norm_back(fc, n, scale[:, 0:1], small[3:4])
    sum_one[...] = so
    lo = so.astype(BF16)
    low[...] = lo
    sums[0:1] = jnp.sum(lo.astype(F32), 0, keepdims=True)
    sums[1:2] = jnp.sum(fc * n, 0, keepdims=True)
    sums[2:3] = jnp.sum(fc, 0, keepdims=True)
    if refs:
        add_moved_kernel(*refs)


def first_back(sum_two, part, got, normal, scale, small, moved=()):
    n = sum_two.shape[0]
    outs = [shape(moved[0].shape), shape(moved[2].shape)] if moved else []
    *added, sum_one, low, sums = call(
        first_back_kernel,
        (*outs, shape((n, D), F32), shape((n, D)), shape((3, D), F32)),
        (sum_two, part, got, normal, scale, small, *moved),
        cost=est(1000, 1000),
        limit=8,
    )
    return added, sum_one, low, sums


def attend_back_kernel(sets, a0, a1, *refs):
    far, outs, (in0, in1, sums), refs = refs[:9], refs[9 : 9 + sets], refs[9 + sets : 12 + sets], refs[12 + sets :]
    wp, v, probs, k, q, wr, x0, x1, ctx = far
    dctx, cots, grads, sems = refs
    copies = Copies(sems)
    c, z, y, x = place_here()
    half = a0.shape[0]
    n = 2 * half
    wpo = wp[:, pl.ds(pl.multiple_of(c * 384, 128), 384)]
    dctx[0:half] = nn(a0[...], wpo).astype(BF16)
    dctx[half:n] = nn(a1[...], wpo).astype(BF16)
    lane = lax.broadcasted_iota(jnp.int32, (n, 128), 1)
    zero = jnp.zeros((n, 128), BF16)
    scale = HEAD_DIM**-0.5
    heads = [[], [], []]
    for pair in range(3):
        lanes = slice(128 * pair, 128 * pair + 128)
        qp, kp, vp, dp = q[:, lanes], k[:, lanes], v[:, lanes], dctx[:, lanes]
        dq = dk = dv = 0.0
        for e in range(2):
            mine = (lane < HEAD_DIM) if e == 0 else (lane >= HEAD_DIM)
            dh, kh, qh = jnp.where(mine, dp, zero), jnp.where(mine, kp, zero), jnp.where(mine, qp, zero)
            pr = probs[2 * pair + e]
            dv = dv + tn(pr, dh)
            pf = pr.astype(F32)
            t = pf * nt(dh, vp)
            ds = (t - pf * jnp.sum(t, -1, keepdims=True)).astype(BF16)
            dq = dq + nn(ds, kh)
            dk = dk + tn(ds, qh)
        for t, val in enumerate((dq * scale, dk * scale, dv)):
            val = val.astype(BF16)
            for e in range(2):
                hd = 2 * pair + e
                g, hh = hd // 3, hd % 3
                at = 640 * g + 192 * t + 64 * hh
                cots[:, at : at + 64] = val[:, 64 * e : 64 * e + 64]
            heads[t].append(val)
    for g in range(2):
        cots[:, 640 * g + 576 : 640 * g + 640] = jnp.zeros((n, 64), BF16)
    parts = [jnp.concatenate(heads[t], 1) for t in range(3)]
    for i, out in enumerate((in0, in1)):
        rws = slice(half * i, half * i + half)
        total = 0.0
        for t in range(3):
            total = total + nn(parts[t][rws], wr[384 * t : 384 * t + 384])
        out[...] = total
    for row, t in ((0, 0), (1, 2)):
        s = jnp.sum(parts[t].astype(F32), 0, keepdims=True)
        for g in range(2):
            sg = s[:, 192 * g : 192 * g + 192]
            sums[row : row + 1, 384 * g : 384 * g + 192] = jnp.where(c == 0, sg, 0.0)
            sums[row : row + 1, 384 * g + 192 : 384 * g + 384] = jnp.where(c == 1, sg, 0.0)
    for d in range(3):
        at = slice(256 * d, 256 * d + 256)
        full = tn(x0[:, at], cots[0:half]) + tn(x1[:, at], cots[half:n])
        pg = tn(a0[:, at], ctx[0:half]) + tn(a1[:, at], ctx[half:n])
        for g in range(2):
            grads[g, at, 0:576] = full[:, 640 * g : 640 * g + 576].astype(BF16)
            grads[g, at, 576:768] = pg[:, 192 * g : 192 * g + 192].astype(BF16)
    if sets == 1:
        copies.start(grads, outs[0])
    else:
        rows = outs[0].shape[1]
        for spot in (3, 2, 1, 0):
            g, yi = flip(x, spot % 2), flip(y, spot // 2)
            for kz in range(4):
                zi = flip(lax.rem(z, 2), kz % 2) + 2 * flip(lax.div(z, 2), kz // 2)
                at = pl.multiple_of((2 * zi + yi) * rows, rows)
                dst = outs[spot].at[kz] if spot < 3 else outs[3 + kz // 2].at[kz % 2]
                copies.start(grads.at[g, pl.ds(at, rows)], dst)
    copies.wait()


def attend_back(direct, a0, a1, x0, x1, wp, wr, q, k, v, ctx, probs):
    half = a0.shape[0]
    n = 2 * half
    sets = (shape((2, D, D)),)
    if direct:
        sets = (shape((4, 96, D)),) * 3 + (shape((2, 96, D)),) * 2
    far = (wp, v, probs, k, q, wr, x0, x1, ctx)
    return call(
        functools.partial(attend_back_kernel, len(sets)),
        (*sets, shape((half, D), F32), shape((half, D), F32), shape((2, D), F32)),
        (a0, a1, *far),
        scratch=[
            pltpu.VMEM((n, 384), BF16),
            pltpu.VMEM((n, 1280), BF16),
            pltpu.VMEM((2, D, D), BF16),
        ],
        cost=est(1000, 1000),
        limit=16,
        far_out=range(len(sets)),
        sems=17,
    )


def local(
    inputs,
    bucket,
    lengths,
    qkv_weight,
    query_bias,
    value_bias,
    proj_weight,
    proj_bias,
    first_gain,
    first_shift,
    up_weight,
    up_bias,
    down_weight,
    down_bias,
    second_gain,
    second_shift,
    cotangent,
):
    head_count = lax.axis_size("head")
    batch_count = lax.axis_size("batch")
    devices = head_count * batch_count
    direct = batch_count == 8
    b = lax.axis_index("batch")
    h = lax.axis_index("head")
    me = b * head_count + h
    x, c = h // 2, h % 2
    z, y = b // 2, b % 2
    wq, wp, wf = 3 * D // devices, D // devices, FF // devices

    vectors = [
        query_bias,
        value_bias,
        proj_bias,
        first_gain,
        first_shift,
        down_bias,
        second_gain,
        second_shift,
    ]
    if direct:
        a_shard, one_a, one_b, two = pack(
            qkv_weight.T, proj_weight.T, up_weight.T, down_weight, up_bias, vectors
        )
    else:
        small = lax.dynamic_update_slice(
            jnp.zeros((16, D), BF16), jnp.stack(vectors), (0, me * wp)
        )
        per_row = D // wf
        small = lax.dynamic_update_slice(
            small, up_bias[None, :], (8 + me // per_row, (me % per_row) * wf)
        )
        proj_t = proj_weight.T.reshape(wp, 2, 2, 192).transpose(0, 2, 1, 3).reshape(wp, D)
        a_shard = jnp.concatenate([qkv_weight.T, proj_t, small])
    other_in = core_swap(inputs)
    k = jnp.arange(batch_count * 2)
    if direct:
        a_z = z_line(a_shard)
        two = after(two, a_z[1])
        two_x, two_y = x_swap(two), y_swap(two)
        two_d = jnp.concatenate([x_swap(two_y[:TWO]), y_swap(two_x[TWO:])])
        two_lo = jnp.stack([two, two_x, two_y, two_d])
        a_z, two_lo, other_in = lax.optimization_barrier((jnp.stack(a_z), two_lo, other_in))
        one_a = z_line(after(one_a, a_z))
        a_x, a_y = x_swap(a_z), y_swap(a_z)
        a_x, a_y, one_a, two_lo = lax.optimization_barrier((a_x, a_y, one_a, two_lo))
        one_b = after(one_b, one_a)
        near = z_swap(jnp.concatenate([one_b, two_lo.reshape(8 * TWO, D)]), 1)
        one_b = [one_b, None, z_swap(one_b, 2), z_swap(one_b, 3)]
        a_d = [x_swap(a_y[:2]), y_swap(a_x[2:])]
        near, one_b[2], one_b[3], a_d = lax.optimization_barrier((near, one_b[2], one_b[3], a_d))
        one_b[1], two_hi = near[: 2 * ONE - FIRST], near[2 * ONE - FIRST :].reshape(two_lo.shape)
        a_own = [a_z, a_x, a_y, *a_d]
        a_swapped = [core_swap(v) for v in after(a_own, near)]
        one_z = jnp.stack([jnp.concatenate(pair) for pair in zip(one_a, one_b)])
        one_x, one_y = x_swap(one_z), y_swap(one_z)
        two_far = z_swap(jnp.concatenate([two_lo, two_hi]), 2)
        one_x, one_y, two_far = lax.optimization_barrier((one_x, one_y, two_far))
        one_d = [x_swap(one_y[:2]), y_swap(one_x[2:])]
        twos = [two_lo, two_hi, two_far]
        ctx_own, ctx_other, q, kk, v, ctx, probs, wr, ub_all, proj_w, small_all = attend(
            bucket, lengths, inputs, other_in, (*a_own, *a_swapped), wq, wp
        )
        f_all = [[one_z], [one_x], [one_y], twos, one_d]
    else:
        a_all = lax.all_gather(a_shard, ("batch", "head"), axis=0)
        qkv_all = a_all[:, :wq].reshape(2, 2, 576, D)
        qkv_w = lax.dynamic_index_in_dim(qkv_all, c, 1, keepdims=False).reshape(2 * 576, D)
        proj_w = a_all[:, wq : wq + wp].reshape(D, D)
        small_all = jnp.sum(a_all[:, wq + wp :].astype(F32), 0)
        ctx_own, ctx_other, q, kk, v, ctx, probs, wr = attend(
            bucket, lengths, inputs, other_in, (qkv_w, small_all)
        )
        f_shard = jnp.concatenate([up_weight.T, down_weight])
        f_all = [
            (v[:, :wf].reshape(-1, D), v[:, wf:].reshape(-1, D)) for v in gather_any(f_shard)
        ]
        owner = (k % batch_count) * 4 + (x ^ (k // batch_count)) * 2 + c
    if not direct:
        spread = (owner[None, :] == jnp.arange(devices)[:, None]).astype(F32)
        ub_all = tn(spread, small_all[8:12].reshape(devices, wf)).reshape(1, FF // 2)

    ctx_in = core_swap(ctx_other)
    first_low, first, first_n, first_r = first_norm(inputs, ctx_own, ctx_in, proj_w, small_all)
    first_in = core_swap(first_low)
    sums = ()
    kept = []
    starts = (0, FF // 4)
    if direct:
        starts = (0, 4 * ONE, 8 * ONE, 16 * ONE, 12 * ONE)
    for weights, at in zip(f_all, starts):
        width = FF // 4
        if direct:
            width = 16 * TWO if len(kept) == 3 else 4 * ONE
        hid, slope, *sums = ffn(
            first_low,
            first_in,
            ub_all[:, at : at + width],
            weights,
            sums,
            len(kept) == len(f_all) - 1,
        )
        kept.append((hid, slope))
    layer_out, sum_two, down_low, sums_two = second_norm(
        bucket, lengths, first, sums[0], core_swap(sums[1]), small_all, cotangent
    )
    down_in = core_swap(down_low)

    sums = ()
    f_parts, ub_parts = [], []
    if direct:
        for spot, i in ((3, 4), (2, 2), (1, 1), (0, 0)):
            weights, both = (*f_all[i], *twos), (*kept[i], *kept[3])
            grads, ub, sums = ffn_back(
                down_low, down_in, first_low, first_in, spot, weights, both, sums, spot == 0
            )
            f_parts = grads + f_parts
            ub_parts.insert(0, ub)
    else:
        for weights, pair in zip(f_all, kept):
            grads, ub, sums = ffn_back(
                down_low,
                down_in,
                first_low,
                first_in,
                None,
                weights,
                pair,
                sums,
                len(f_parts) == len(f_all) - 1,
            )
            f_parts.append(grads)
            ub_parts.append(ub)
    part_own, part_other = sums
    moved = ()
    if direct:
        moved = (f_parts[1], y_swap(f_parts[4]), f_parts[2], x_swap(f_parts[3]))
        part_other = after(part_other, moved)
    added, sum_one, attn_low, sums_one = first_back(
        sum_two, part_own, core_swap(part_other), first_n, first_r, small_all, moved
    )
    attn_in = core_swap(attn_low)
    *a_grads, in_own, in_other, sums_zero = attend_back(
        direct,
        attn_low,
        attn_in,
        inputs,
        other_in,
        proj_w,
        wr,
        q,
        kk,
        v,
        ctx,
        probs,
    )
    in_got = core_swap(in_other)
    inputs_grad = (sum_one + in_own + in_got).astype(BF16)

    if direct:
        f_sets = scatter_xy(f_parts[0], *added)
        f_mine, (f_ups, f_downs) = combine(*f_sets, 2)
        terms = exchange_terms(sums_zero, sums_one, sums_two, ub_parts, devices)
        terms = lax.all_to_all(terms, ("batch", "head"), split_axis=0, concat_axis=0, tiled=True)
        a_zz, a_xx, a_yy, d_lo, d_hi = a_grads
        d_lo, d_hi = after((d_lo, d_hi), (f_sets, in_got, terms))
        d_lo, d_hi = x_swap(d_lo), y_swap(d_hi)
        f_ups = scatter_z(f_ups)
        d_lo, d_hi, f_ups = lax.optimization_barrier((d_lo, d_hi, f_ups))
        a_xx, a_yy = add_moved(a_xx, d_hi, a_yy, d_lo)
        a_sets = scatter_xy(a_zz, a_xx, a_yy)
        f_downs = scatter_z(after(f_downs, f_ups))
        a_sets, f_downs, _ = lax.optimization_barrier((a_sets, f_downs, inputs_grad))
        a_mine, (a_others,) = combine(*a_sets, 1)
        up_grad, down_grad = finish_ffn(f_mine, f_ups, f_downs)
        up_grad = up_grad.T
        terms = jnp.sum(terms, 0)
        packed = jnp.concatenate([terms[:, :wp].reshape(-1), terms[0, wp : wp + wf]])
        qkv_grad, proj_grad = finish_attend((a_mine, *scatter_z(a_others)))
    else:
        vecs = jnp.concatenate([sums_zero, sums_one, sums_two])
        vecs = vecs.reshape(8, devices, wp).transpose(1, 0, 2).reshape(devices, 8 * wp)
        ubias = jnp.concatenate(ub_parts).reshape(batch_count * 2, wf)
        ubias = lax.dot_general(
            spread, ubias, (((1,), (0,)), ((), ())), precision=lax.Precision.HIGHEST
        )
        packed = jnp.concatenate([vecs, ubias], 1)
        packed = lax.all_to_all(
            packed, ("batch", "head"), split_axis=0, concat_axis=0, tiled=True
        )
        packed = jnp.sum(packed, 0)
        wb = D // batch_count
        a_grads = a_grads[0].reshape(2, batch_count, wb, D)
        a_mine = scatter_any(
            [
                lax.dynamic_index_in_dim(a_grads, x, 0, keepdims=False),
                lax.dynamic_index_in_dim(a_grads, 1 - x, 0, keepdims=False),
            ]
        )
        f_mine = scatter_any(
            [
                jnp.concatenate(
                    [ug.reshape(batch_count, wf, D), dg.reshape(batch_count, wf, D)], 1
                )
                for ug, dg in f_parts
            ]
        )
        qkv_grad = a_mine[:, :576].reshape(wb, 3, 3, HEAD_DIM).transpose(0, 2, 1, 3)
        qkv_grad = qkv_grad.reshape(wb, 576)
        proj_grad = a_mine[:, 576:].T
        up_grad, down_grad = f_mine[:wf].T, f_mine[wf:]
    qb_g, vb_g, pb_g, fg_g, fs_g, db_g, sg_g, ss_g = [
        packed[i * wp : (i + 1) * wp] for i in range(8)
    ]
    return (
        layer_out,
        inputs_grad,
        qkv_grad,
        qb_g,
        vb_g,
        proj_grad,
        pb_g,
        fg_g,
        fs_g,
        up_grad,
        packed[8 * wp :],
        down_grad,
        db_g,
        sg_g,
        ss_g,
    )


def solution(mesh):
    both = ("batch", "head")
    in_specs = (
        P(both, None),
        P("batch"),
        P("batch", None),
        P(None, both),
        P(both),
        P(both),
        P(None, both),
        P(both),
        P(both),
        P(both),
        P(None, both),
        P(both),
        P(both, None),
        P(both),
        P(both),
        P(both),
        P(both, None),
    )
    out_specs = (
        P(both, None),
        P(both, None),
        P("batch", "head"),
        P(both),
        P(both),
        P("head", "batch"),
        P(both),
        P(both),
        P(both),
        P(None, both),
        P(both),
        P(both, None),
        P(both),
        P(both),
        P(both),
    )
    return jax.shard_map(local, mesh=mesh, in_specs=in_specs, out_specs=out_specs, check_vma=False)
```

```python
import functools

import jax
import jax.numpy as jnp
from jax import lax
from jax.experimental import pallas as pl
from jax.experimental.pallas import tpu as pltpu
from jax.sharding import PartitionSpec as P

D = 768
HEADS = 12
HEAD_DIM = 64
FF = 3072
BIG = 512
SMALL = 128
UNITS = 4
NORM_EPS = 1e-12
F32 = jnp.float32
BF16 = jnp.bfloat16

ONE, TWO = 80, 16
FIRST = 104

CORE = [(i, i ^ 1) for i in range(4)]
XPAIR = [(i, i ^ 2) for i in range(4)]
YPAIR = [(i, i ^ 1) for i in range(8)]
ZPAIR = [[(i, i ^ (2 * k)) for i in range(8)] for k in range(4)]


def core_swap(v):
    return lax.ppermute(v, "head", CORE)


def x_swap(v):
    return lax.ppermute(v, "head", XPAIR)


def y_swap(v):
    return lax.ppermute(v, "batch", YPAIR)


def z_swap(v, k):
    return lax.ppermute(v, "batch", ZPAIR[k])


def after(value, other):
    return lax.optimization_barrier((value, other))[0]


def nt(a, b, out=F32):
    return lax.dot_general(a, b, (((1,), (1,)), ((), ())), preferred_element_type=F32).astype(out)


def nn(a, b, out=F32):
    return lax.dot_general(a, b, (((1,), (0,)), ((), ())), preferred_element_type=F32).astype(out)


def tn(a, b, out=F32):
    return lax.dot_general(a, b, (((0,), (0,)), ((), ())), preferred_element_type=F32).astype(out)


def z_line(shard):
    return [shard] + [z_swap(shard, k) for k in (1, 2, 3)]


def gather_four(z):
    x, y = x_swap(z), y_swap(z)
    return [z, x, y, x_swap(y[:2]), y_swap(x[2:])]


def gather_any(shard):
    whole = lax.all_gather(shard, "batch", axis=0)
    return [whole, x_swap(whole)]


def scatter_xy(z, x, y):
    return z, x_swap(x), y_swap(y)


def scatter_z(others):
    return [z_swap(others[k - 1], k) for k in (1, 2, 3)]


def scatter_any(parts):
    total = parts[0].astype(F32) + x_swap(parts[1]).astype(F32)
    return lax.psum_scatter(total, "batch", scatter_dimension=0, tiled=False)


def est(flops, moved, trans=0):
    return pl.CostEstimate(flops=int(flops), bytes_accessed=int(moved), transcendentals=int(trans))


def call(kernel, out_shape, operands, scratch=(), cost=None, limit=16, far_in=(), far_out=(), sems=0):
    vmem = pl.BlockSpec(memory_space=pltpu.VMEM)
    hbm = pl.BlockSpec(memory_space=pltpu.HBM)
    smem = pl.BlockSpec(memory_space=pltpu.SMEM)
    ins = [hbm if i in far_in else vmem for i in range(len(operands))]
    ins = [smem if v.dtype == jnp.int32 else spec for spec, v in zip(ins, operands)]
    outs = [hbm if i in far_out else vmem for i in range(len(out_shape))]
    scratch = list(scratch) + ([pltpu.SemaphoreType.DMA((sems,))] if sems else [])
    operands = [
        pltpu.with_memory_space_constraint(v, pltpu.HBM) if i in far_in else v
        for i, v in enumerate(operands)
    ]
    out_shape = [
        pltpu.HBM(v.shape, v.dtype) if i in far_out else v for i, v in enumerate(out_shape)
    ]
    return pl.pallas_call(
        kernel,
        out_shape=out_shape,
        in_specs=ins,
        out_specs=outs,
        scratch_shapes=scratch,
        compiler_params=pltpu.CompilerParams(vmem_limit_bytes=limit << 20),
        cost_estimate=cost,
    )(*operands)


class Copies:
    def __init__(self, sems):
        self.sems, self.used, self.open = sems, 0, []

    def start(self, src, dst):
        copy = pltpu.make_async_copy(src, dst, self.sems.at[self.used])
        self.used += 1
        copy.start()
        self.open.append(copy)
        return copy

    def wait(self, *copies):
        for copy in copies or list(self.open):
            copy.wait()
            self.open.remove(copy)


def add_low(a, b):
    return (a.astype(F32) + b.astype(F32)).astype(BF16)


def shape(dims, dtype=BF16):
    return jax.ShapeDtypeStruct(dims, dtype)


def add_first_kernel(x_up, x_down, for_x, y_up, y_down, for_y, *outs):
    half = x_up.shape[1]
    for i, (x, y) in enumerate(((x_up, y_up), (x_down, y_down))):
        rows = slice(half * i, half * i + half)
        x_out, y_out = outs[2 * i : 2 * i + 2]
        x_out[0:2] = x[0:2]
        y_out[2:4] = y[2:4]
        for k in range(2):
            x_out[2 + k] = add_low(x[2 + k], for_x[k, rows])
            y_out[k] = add_low(y[k], for_y[k, rows])


def combine_kernel(z, x, y, *refs):
    outs, (mine, low, sems) = refs[:4], refs[4:]
    sum_places(z, x, y, outs, mine, low, Copies(sems)).wait()


def sum_places(z, x, y, outs, mine, low, copies, arrived=None):
    for i, k in enumerate((1, 2, 3, 0)):
        if arrived:
            copies.wait(*arrived[i])
        total = z[k].astype(F32) + x[k].astype(F32) + y[k].astype(F32)
        if k == 0:
            mine[...] = total
            copies.start(mine, outs[0])
        else:
            low[k - 1] = total.astype(BF16)
            copies.start(low.at[k - 1], outs[k])
    return copies


def combine(z, x, y):
    rows = z.shape[1]
    mine, *others = call(
        combine_kernel,
        (shape((rows, D), F32),) + (shape((rows, D)),) * 3,
        (z, x, y),
        scratch=[pltpu.VMEM((rows, D), F32), pltpu.VMEM((3, rows, D), BF16)],
        cost=est(1000, 1000),
        limit=8,
        far_out=range(4),
        sems=4,
    )
    return mine, others


def combine_last_kernel(z, x, y, mine, *refs):
    outs, (low, sems) = refs[:3], refs[3:]
    copies = Copies(sems)
    for k in (1, 2, 3, 0):
        total = z[k].astype(F32) + x[k].astype(F32) + y[k].astype(F32)
        if k == 0:
            mine[...] = total
        else:
            low[k - 1] = total.astype(BF16)
            copies.start(low.at[k - 1], outs[k - 1])
    copies.wait()


def combine_last(z, x, y):
    rows = z.shape[1]
    mine, *others = call(
        combine_last_kernel,
        (shape((rows, D), F32),) + (shape((rows, D)),) * 3,
        (z, x, y),
        scratch=[pltpu.VMEM((3, rows, D), BF16)],
        cost=est(1000, 1000),
        limit=8,
        far_out=range(1, 4),
        sems=3,
    )
    return mine, others


def turn_kernel(x, y, z, by_x_far, by_y_far, x_out, y_out, *refs):
    outs, (by_x, by_y, mine, low, sems) = refs[:4], refs[4:]
    copies = Copies(sems)
    arrived = []
    for k in (1, 2, 3, 0, 4):
        rows = pl.ds(k, 1 if k < 4 else 2)
        arrived.append(
            (
                copies.start(by_x_far.at[rows], by_x.at[rows]),
                copies.start(by_y_far.at[rows], by_y.at[rows]),
            )
        )
    sum_places(z, by_x, by_y, outs, mine, low, copies, arrived)
    copies.wait(*arrived[4])
    y_out[0:2] = add_low(y[0:2], by_x[4:6])
    y_out[2:4] = y[2:4]
    x_out[0:2] = x[0:2]
    x_out[2:4] = add_low(x[2:4], by_y[4:6])
    copies.wait()


def turn(x, y, z, by_x, by_y):
    rows = z.shape[1]
    x, y, mine, *others = call(
        turn_kernel,
        (shape(x.shape), shape(y.shape), shape((rows, D), F32)) + (shape((rows, D)),) * 3,
        (x, y, z, by_x, by_y),
        scratch=[pltpu.VMEM(by_x.shape, BF16)] * 2
        + [pltpu.VMEM((rows, D), F32), pltpu.VMEM((3, rows, D), BF16)],
        cost=est(1000, 1000),
        limit=8,
        far_in=(3, 4),
        far_out=range(2, 6),
        sems=14,
    )
    return (x, y), mine, others


def total_of(refs):
    return refs[0][...] + refs[1][...].astype(F32) + refs[2][...].astype(F32) + refs[3][...].astype(F32)


def finish_attend_kernel(mine, one, two, three, qkv, proj):
    total = total_of((mine, one, two, three))
    for hh in range(3):
        for t in range(3):
            at, to = 192 * t + 64 * hh, 192 * hh + 64 * t
            qkv[:, to : to + 64] = total[:, at : at + 64]
    proj[...] = total[:, 576:].T


def finish_attend(parts):
    rows = parts[0].shape[0]
    return call(
        finish_attend_kernel,
        (shape((rows, 576), F32), shape((192, rows), F32)),
        tuple(parts),
        cost=est(8 * rows * D, 16 * rows * D),
        limit=8,
    )


def finish_ffn_kernel(*refs):
    up, down = refs[8:]
    up[...], down[...] = total_of(refs[0:4]), total_of(refs[4:8])


def finish_ffn(ups, downs):
    dims = ups[0].shape
    return call(
        finish_ffn_kernel,
        (shape(dims, F32), shape(dims, F32)),
        (*ups, *downs),
        cost=est(1000, 1000),
        limit=8,
    )


def exchange_kernel(zero, one, two, *refs):
    ubs, out = refs[:4], refs[4]
    vecs = jnp.concatenate([zero[...], one[...], two[...]])
    width = D // out.shape[0]
    out[...] = jnp.zeros(out.shape, F32)
    for i in range(out.shape[0]):
        out[i, 0:8, 0:width] = vecs[:, width * i : width * i + width]
    for spot in range(4):
        for kz in range(4):
            to, ub = slot_of(spot, kz), ubs[spot]
            out[to, 0:1, 24 : 24 + ONE] = ub[:, ONE * kz : ONE * kz + ONE]
            at = 4 * ONE + TWO * kz
            out[to, 0:1, 24 + ONE : 24 + ONE + TWO] = ub[:, at : at + TWO]


def exchange_terms(zero, one, two, ubs, devices):
    return call(
        exchange_kernel,
        (shape((devices, 8, 128), F32),),
        (zero, one, two, *ubs),
        cost=est(1000, 1000),
        limit=8,
    )[0]


def flip(a, bit):
    return a + bit - 2 * a * bit


def pack_kernel(qkv_in, proj_in, up_in, down_in, bias_in, *refs):
    vectors_in, (a_out, one_a, one_b, two, a, p, f, bias, vectors, sems) = refs[:8], refs[8:]
    rows_q, rows_p, half = qkv_in.shape[0], proj_in.shape[0], down_in.shape[0]
    copies = Copies(sems)
    copies.start(qkv_in, a.at[pl.ds(0, rows_q)])
    copies.start(proj_in, p)
    copies.start(up_in, f.at[pl.ds(0, half)])
    copies.start(down_in, f.at[pl.ds(half, half)])
    copies.start(bias_in, bias)
    for i, r in enumerate(vectors_in):
        copies.start(r, vectors.at[i])
    width = vectors.shape[2]
    b, h = lax.axis_index("batch"), lax.axis_index("head")
    me = b * lax.axis_size("head") + h
    copies.wait()
    v = jnp.concatenate([vectors[i] for i in range(8)]).astype(F32)
    v = jnp.concatenate([v] * (D // width), 1)
    lane = lax.broadcasted_iota(jnp.int32, (8, D), 1)
    mine = jnp.logical_and(lane >= me * width, lane < me * width + width)
    v = jnp.where(mine, v, 0.0)
    gap = jnp.zeros((1, D // 2 - half), F32)
    none = jnp.zeros((1, D // 2), F32)
    row = bias[...].astype(F32)
    early = jnp.concatenate([none, row, gap], 1)
    late = jnp.concatenate([row, gap, none], 1)
    extra = jnp.where(me < lax.axis_size("batch") * lax.axis_size("head") // 2, early, late)
    v = v + jnp.concatenate([extra, jnp.zeros((7, D), F32)])
    a_out[0:rows_q] = a[0:rows_q]
    q = p[...]
    a_out[rows_q : rows_q + rows_p] = jnp.concatenate(
        [q[:, 192 * i : 192 * i + 192] for i in (0, 2, 1, 3)], 1
    )
    a_out[rows_q + rows_p :] = v.astype(BF16)
    one = jnp.concatenate([f[0:ONE], f[half : half + ONE]])
    one_a[...], one_b[...] = one[0:FIRST], one[FIRST:]
    two[0:TWO], two[TWO:] = f[ONE:half], f[half + ONE :]


def pack(qkv, proj, up, down, bias, vectors):
    rows, half = qkv.shape[0] + proj.shape[0] + 8, down.shape[0]
    return call(
        pack_kernel,
        (
            shape((rows, D)),
            shape((FIRST, D)),
            shape((2 * ONE - FIRST, D)),
            shape((2 * TWO, D)),
        ),
        (qkv, proj, up, down, bias[None], *[v[None] for v in vectors]),
        scratch=[
            pltpu.VMEM((rows, D), BF16),
            pltpu.VMEM(proj.shape, BF16),
            pltpu.VMEM((2 * half, D), BF16),
            pltpu.VMEM((1,) + bias.shape, BF16),
            pltpu.VMEM((8, 1) + vectors[0].shape, BF16),
        ],
        cost=est(1000, 1000),
        limit=8,
        far_in=range(13),
        sems=13,
    )


def place_here():
    b, h = lax.axis_index("batch"), lax.axis_index("head")
    return lax.rem(h, 2), lax.div(b, 2), lax.rem(b, 2), lax.div(h, 2)


def live_units(bucket, lengths):
    x = place_here()[3]
    kind, first = bucket[x], lengths[x, 0]
    units = []
    for u in range(UNITS):
        far = jnp.clip(first - SMALL * u, 0, SMALL)
        units.append(jnp.where(kind == 1, far, lengths[x, u]))
    return kind, units


def place_of(index, c):
    return jnp.bitwise_xor(index, c * (BIG // 2))


def live_of(place, units):
    unit = lax.shift_right_logical(place, 7)
    inner = jnp.bitwise_and(place, SMALL - 1)
    count = jnp.where(
        unit < 2, jnp.where(unit == 0, units[0], units[1]), jnp.where(unit == 2, units[2], units[3])
    )
    return inner < count


def heads_of(row, c):
    parts = []
    for g in range(2):
        lo = row[:, 384 * g : 384 * g + 192]
        hi = row[:, 384 * g + 192 : 384 * g + 384]
        parts.append(jnp.where(c == 0, lo, hi))
    return jnp.concatenate(parts, 1)


def fetch_shards(copies, sources, slots):
    c, z, y, x = place_here()
    zl, zh = lax.rem(z, 2), lax.div(z, 2)
    for swapped in range(2):
        cc = c if swapped == 0 else 1 - c
        zs, xs, ys, xa, xb = sources[5 * swapped : 5 * swapped + 5]
        for kx, ky, pair in ((0, 0, (zs,)), (1, 0, (xs,)), (0, 1, (ys,)), (1, 1, (xa, xb))):
            j = flip(y, ky) * 4 + flip(x, kx) * 2 + cc
            for kz in range(4):
                src = pair[0].at[kz] if len(pair) == 1 else pair[kz // 2].at[kz % 2]
                zi = flip(zl, kz % 2) + 2 * flip(zh, kz // 2)
                copies.start(src, slots.at[zi * 8 + j])


def slot_of(spot, kz):
    c, z, y, x = place_here()
    zi = flip(lax.rem(z, 2), kz % 2) + 2 * flip(lax.div(z, 2), kz // 2)
    return zi * 8 + flip(y, spot // 2) * 4 + flip(x, spot % 2) * 2 + c


def bias_order(slots, row, out):
    for spot in range(4):
        for kz in range(4):
            i = slot_of(spot, kz)
            b = slots[i, row : row + 1].astype(F32)
            b = jnp.where(i < 16, b[:, D // 2 : D // 2 + 96], b[:, 0:96])
            at = 4 * ONE * spot + ONE * kz
            out[:, at : at + ONE] = b[:, 0:ONE]
            at = 16 * ONE + 4 * TWO * spot + TWO * kz
            out[:, at : at + TWO] = b[:, ONE:]


def attend_kernel(rows_q, rows_p, bucket, lengths, x0, x1, *refs):
    sources = 10 if rows_q else 2
    weights, refs = refs[:sources], refs[sources:]
    (ctx0, ctx1, q, k, v, ctx, probs, wr), refs = refs[:8], refs[8:]
    if rows_q:
        (ub_out, wp, small, mask, xs, slots, sems) = refs
    else:
        (mask, xs, w, small, sems) = refs
    copies = Copies(sems)
    c = place_here()[0]
    kind, units = live_units(bucket, lengths)
    half = x0.shape[0]
    copies.start(x0, xs.at[0:half])
    copies.start(x1, xs.at[half : 2 * half])
    if rows_q:
        fetch_shards(copies, weights, slots)
    else:
        copies.start(weights[0], w)
        copies.start(weights[1], small)
    rows = lax.broadcasted_iota(jnp.int32, (BIG, BIG), 0)
    cols = lax.broadcasted_iota(jnp.int32, (BIG, BIG), 1)
    prow, pcol = place_of(rows, c), place_of(cols, c)
    same = jnp.logical_or(
        kind == 1, lax.shift_right_logical(prow, 7) == lax.shift_right_logical(pcol, 7)
    )
    mask[...] = jnp.where(jnp.logical_and(same, live_of(pcol, units)), 0.0, -1e30)
    copies.wait()
    if rows_q:
        for g in range(2):
            cuts = jnp.concatenate([slots[16 * g + 8 * c + j, 0:rows_q] for j in range(8)])
            for t in range(3):
                for hh in range(3):
                    src, dst = (hh * 3 + t) * HEAD_DIM, (t * 6 + g * 3 + hh) * HEAD_DIM
                    wr[dst : dst + HEAD_DIM] = cuts[src : src + HEAD_DIM]
        lane = lax.broadcasted_iota(jnp.int32, (8, D), 1)
        small[...] = sum(
            jnp.where(
                jnp.logical_and(lane >= rows_p * i, lane < rows_p * i + rows_p),
                slots[i, rows_q + rows_p :].astype(F32),
                0.0,
            )
            for i in range(32)
        )
    else:
        for t in range(3):
            for hd in range(6):
                src = ((hd // 3) * 9 + (hd % 3) * 3 + t) * HEAD_DIM
                dst = (t * 6 + hd) * HEAD_DIM
                wr[dst : dst + HEAD_DIM] = w[src : src + HEAD_DIM]
    biases = (heads_of(small[0:1], c), None, heads_of(small[1:2], c))
    for t, ref in enumerate((q, k, v)):
        val = nt(xs[...], wr[384 * t : 384 * t + 384])
        if biases[t] is not None:
            val = val + biases[t]
        ref[...] = val.astype(BF16)
    if rows_q:
        for i in range(32):
            wp[rows_p * i : rows_p * i + rows_p] = slots[i, rows_q : rows_q + rows_p]
        bias_order(slots, rows_q + rows_p, ub_out)
    lane = lax.broadcasted_iota(jnp.int32, (half, 128), 1)
    for pair in range(3):
        lanes = slice(128 * pair, 128 * pair + 128)
        kp, vp = k[:, lanes], v[:, lanes]
        for i, near in enumerate((ctx0, ctx1)):
            rws = slice(half * i, half * i + half)
            qp = q[rws, lanes] * jnp.asarray(HEAD_DIM**-0.5, BF16)
            outs = []
            for e in range(2):
                mine = (lane < HEAD_DIM) if e == 0 else (lane >= HEAD_DIM)
                s = nt(jnp.where(mine, qp, jnp.zeros_like(qp)), kp) + mask[rws]
                ex = jnp.exp(s - jnp.max(s, -1, keepdims=True))
                pr = (ex * (1.0 / jnp.sum(ex, -1, keepdims=True))).astype(BF16)
                probs[2 * pair + e, rws] = pr
                outs.append(nn(pr, vp))
            val = jnp.where(lane < HEAD_DIM, outs[0], outs[1]).astype(BF16)
            ctx[rws, lanes] = val
            near[:, lanes] = val


def attend(bucket, lengths, x0, x1, weights, rows_q=0, rows_p=0, rows_s=16):
    rows_s = 8 if rows_q else rows_s
    half = x0.shape[0]
    n = 2 * half
    direct = rows_q > 0
    outs = [
        shape((half, 384)),
        shape((half, 384)),
        shape((n, 384)),
        shape((n, 384)),
        shape((n, 384)),
        shape((n, 384)),
        shape((6, n, n)),
        shape((1152, D)),
    ]
    scratch = [pltpu.VMEM((n, n), F32), pltpu.VMEM((n, D), BF16)]
    if direct:
        outs += [shape((1, FF // 2), F32), shape((D, D)), shape((rows_s, D), F32)]
        scratch += [pltpu.VMEM((32, rows_q + rows_p + rows_s, D), BF16)]
    else:
        scratch += [pltpu.VMEM((1152, D), BF16), pltpu.VMEM((rows_s, D), F32)]
    operands = (bucket, lengths, x0, x1, *weights)
    return call(
        functools.partial(attend_kernel, rows_q, rows_p),
        outs,
        operands,
        scratch=scratch,
        cost=est(2 * n * D * 1152 + 8 * n * n * 384, 12e6, 6 * n * n),
        limit=32,
        far_in=range(2, len(operands)),
        sems=50,
    )


def norm(values):
    center = values - jnp.mean(values, -1, keepdims=True)
    spread = jnp.mean(center * center, -1, keepdims=True)
    scale = lax.rsqrt(spread + NORM_EPS)
    return center * scale, scale


def norm_back(cot, normal, scale, gain):
    w = cot * gain
    return scale * (
        w - jnp.mean(w, -1, keepdims=True) - normal * jnp.mean(w * normal, -1, keepdims=True)
    )


def first_kernel(x, ctx_own, ctx_in, wp, small, low, first, normal, scale):
    c = place_here()[0]
    mine = pl.multiple_of(c * 384, 128)
    theirs = pl.multiple_of((1 - c) * 384, 128)
    attn = nt(ctx_own[...], wp[:, pl.ds(mine, 384)]) + nt(ctx_in[...], wp[:, pl.ds(theirs, 384)])
    n, r = norm(x[...].astype(F32) + attn + small[2:3])
    normal[...] = n
    out = n * small[3:4] + small[4:5]
    first[...] = out
    low[...] = out.astype(BF16)
    scale[...] = jnp.broadcast_to(r, scale.shape)


def first_norm(x, ctx_own, ctx_in, wp, small):
    n = x.shape[0]
    return call(
        first_kernel,
        (shape((n, D)), shape((n, D), F32), shape((n, D), F32), shape((n, 128), F32)),
        (x, ctx_own, ctx_in, wp, small),
        cost=est(2 * n * D * D, 5e6),
        limit=8,
    )


def ffn_weights(refs):
    if len(refs[0].shape) == 2:
        return refs[0][...], refs[1][...]
    return stacked(ones_of(refs) if refs[0].shape[1] == 2 * ONE else twos_of(refs, range(4)))


def ones_of(refs):
    return [(r, i) for r in refs for i in range(r.shape[0])]


def twos_of(refs, spots):
    along_z = [(r, i) for r in refs for i in range(0, r.shape[0], 4)]
    return [(r, i + spot) for spot in spots for r, i in along_z]


def stacked(blocks):
    up = jnp.concatenate([r[i, 0 : r.shape[1] // 2] for r, i in blocks])
    down = jnp.concatenate([r[i, r.shape[1] // 2 :] for r, i in blocks])
    return up, down


def ffn_kernel(first, count, x0, x1, ub, *refs):
    far, refs = refs[:count], refs[count:]
    if first:
        in0 = in1 = None
    else:
        (in0, in1), refs = refs[:2], refs[2:]
    hid, slope, out0, out1 = refs
    half = x0.shape[0]
    uw, dw = ffn_weights(far)
    for i, (xr, before, out) in enumerate(((x0, in0, out0), (x1, in1, out1))):
        rws = slice(half * i, half * i + half)
        up = nt(xr[...], uw) + ub[...]
        phi = 0.5 + 0.5 * lax.erf(up * (2.0**-0.5))
        hd = (up * phi).astype(BF16)
        hid[rws] = hd
        slope[rws] = (phi + up * jnp.exp(-0.5 * up * up) * 0.3989422804014327).astype(BF16)
        part = nn(hd, dw)
        part = part if before is None else before[...] + part
        out[...] = part.astype(out.dtype)


def ffn(x0, x1, ub, weights, sums, last):
    half, width, count = x0.shape[0], ub.shape[1], len(weights)
    n = 2 * half
    return call(
        functools.partial(ffn_kernel, not sums, count),
        (
            shape((n, width)),
            shape((n, width)),
            shape((half, D), F32),
            shape((half, D), BF16 if last else F32),
        ),
        (x0, x1, ub, *weights, *sums),
        cost=est(4 * n * D * width, 4 * D * width + 5e6, 2 * n * width),
    )


def second_kernel(
    bucket, lengths, first, part, got, small, cot, out, sum_two, low, sums
):
    c = place_here()[0]
    _, units = live_units(bucket, lengths)
    n, r = norm(first[...] + (part[...] + got[...].astype(F32) + small[5:6]))
    out[...] = (n * small[6:7] + small[7:8]).astype(BF16)
    index = lax.broadcasted_iota(jnp.int32, (first.shape[0], 1), 0)
    live = live_of(place_of(index, c), units)
    oc = jnp.where(live, cot[...].astype(F32), 0.0)
    st = norm_back(oc, n, r, small[6:7])
    sum_two[...] = st
    lo = st.astype(BF16)
    low[...] = lo
    sums[0:1] = jnp.sum(lo.astype(F32), 0, keepdims=True)
    sums[1:2] = jnp.sum(oc * n, 0, keepdims=True)
    sums[2:3] = jnp.sum(oc, 0, keepdims=True)


def second_norm(bucket, lengths, first, part, got, small, cot):
    n = first.shape[0]
    return call(
        second_kernel,
        (shape((n, D)), shape((n, D), F32), shape((n, D)), shape((3, D), F32)),
        (bucket, lengths, first, part, got, small, cot),
        cost=est(40 * n * D, 5e6),
        limit=8,
    )


def ffn_back_kernel(first, spot, count, d0, d1, x0, x1, *refs):
    weights, refs = refs[:count], refs[count:]
    if spot is None:
        hid, slope = refs[0], refs[1]
        refs = refs[2:]
        uw, dw = ffn_weights(weights)
    else:
        (hid1, slope1, hid2, slope2), refs = refs[:4], refs[4:]
        tail = slice(4 * TWO * spot, 4 * TWO * spot + 4 * TWO)
        hid = jnp.concatenate([hid1[...], hid2[:, tail]], 1)
        slope = jnp.concatenate([slope1[...], slope2[:, tail]], 1)
        uw, dw = stacked(ones_of(weights[:-3]) + twos_of(weights[-3:], [spot]))
    if first:
        in0 = in1 = None
    else:
        (in0, in1), refs = refs[:2], refs[2:]
    *outs, ub, out0, out1 = refs
    half = x0.shape[0]
    cots = []
    for i, (d, before, out) in enumerate(((d0, in0, out0), (d1, in1, out1))):
        rws = slice(half * i, half * i + half)
        uc = (nt(d[...], dw) * slope[rws].astype(F32)).astype(BF16)
        cots.append(uc)
        part = nn(uc, uw)
        part = part if before is None else before[...] + part
        out[...] = part.astype(out.dtype)
    ub[...] = jnp.sum(cots[0].astype(F32), 0, keepdims=True) + jnp.sum(
        cots[1].astype(F32), 0, keepdims=True
    )
    dg = (tn(hid[0:half], d0[...]) + tn(hid[half : 2 * half], d1[...])).astype(BF16)
    ug = (tn(cots[0], x0[...]) + tn(cots[1], x1[...])).astype(BF16)
    if spot is None:
        outs[0][...], outs[1][...] = ug, dg
        return
    rows = ONE + TWO
    for k in range(4):
        for e, g in enumerate((ug, dg)):
            out, i, at = (outs[k // 2], k % 2, rows * e) if spot == 3 else (outs[e], k, 0)
            out[i, at : at + ONE] = g[ONE * k : ONE * k + ONE]
            low = 4 * ONE + TWO * k
            out[i, at + ONE : at + rows] = g[low : low + TWO]


def ffn_back(d0, d1, x0, x1, spot, weights, kept, sums, last):
    half, count = x0.shape[0], len(weights)
    if spot is None:
        outs, width = [shape(w.shape) for w in weights], weights[0].shape[0]
    else:
        width = 4 * (ONE + TWO)
        rows = ONE + TWO
        outs = [shape((2, 2 * rows, D)) if spot == 3 else shape((4, rows, D))] * 2
    *grads, ub, s0, s1 = call(
        functools.partial(ffn_back_kernel, not sums, spot, count),
        (
            *outs,
            shape((1, width), F32),
            shape((half, D), F32),
            shape((half, D), BF16 if last else F32),
        ),
        (d0, d1, x0, x1, *weights, *kept, *sums),
        cost=est(1000, 1000),
    )
    return grads, ub, (s0, s1)


def first_back_kernel(
    sum_two, part, got, normal, scale, small, *refs
):
    *refs, sum_one, low, sums = refs
    fc = sum_two[...] + part[...] + got[...].astype(F32)
    n = normal[...]
    so = norm_back(fc, n, scale[:, 0:1], small[3:4])
    sum_one[...] = so
    lo = so.astype(BF16)
    low[...] = lo
    sums[0:1] = jnp.sum(lo.astype(F32), 0, keepdims=True)
    sums[1:2] = jnp.sum(fc * n, 0, keepdims=True)
    sums[2:3] = jnp.sum(fc, 0, keepdims=True)
    if refs:
        add_first_kernel(*refs)


def first_back(sum_two, part, got, normal, scale, small, moved=()):
    n = sum_two.shape[0]
    outs = [shape(moved[i].shape) for i in (0, 3, 1, 4)] if moved else []
    *added, sum_one, low, sums = call(
        first_back_kernel,
        (*outs, shape((n, D), F32), shape((n, D)), shape((3, D), F32)),
        (sum_two, part, got, normal, scale, small, *moved),
        cost=est(1000, 1000),
        limit=8,
    )
    return added, sum_one, low, sums


def attend_back_kernel(sets, a0, a1, *refs):
    downs, refs = ((), refs) if sets == 1 else (refs[:2], refs[2:])
    far, outs, (in0, in1, sums), refs = refs[:9], refs[9 : 9 + sets], refs[9 + sets : 12 + sets], refs[12 + sets :]
    wp, v, probs, k, q, wr, x0, x1, ctx = far
    dctx, cots, grads, sems = refs
    copies = Copies(sems)
    for down, out in zip(downs, outs[3:]):
        copies.start(down, out.at[pl.ds(0, 4)])
    c, z, y, x = place_here()
    half = a0.shape[0]
    n = 2 * half
    wpo = wp[:, pl.ds(pl.multiple_of(c * 384, 128), 384)]
    dctx[0:half] = nn(a0[...], wpo).astype(BF16)
    dctx[half:n] = nn(a1[...], wpo).astype(BF16)
    lane = lax.broadcasted_iota(jnp.int32, (n, 128), 1)
    zero = jnp.zeros((n, 128), BF16)
    scale = HEAD_DIM**-0.5
    heads = [[], [], []]
    for pair in range(3):
        lanes = slice(128 * pair, 128 * pair + 128)
        qp, kp, vp, dp = q[:, lanes], k[:, lanes], v[:, lanes], dctx[:, lanes]
        dq = dk = dv = 0.0
        for e in range(2):
            mine = (lane < HEAD_DIM) if e == 0 else (lane >= HEAD_DIM)
            dh, kh, qh = jnp.where(mine, dp, zero), jnp.where(mine, kp, zero), jnp.where(mine, qp, zero)
            pr = probs[2 * pair + e]
            dv = dv + tn(pr, dh)
            pf = pr.astype(F32)
            t = pf * nt(dh, vp)
            ds = (t - pf * jnp.sum(t, -1, keepdims=True)).astype(BF16)
            dq = dq + nn(ds, kh)
            dk = dk + tn(ds, qh)
        for t, val in enumerate((dq * scale, dk * scale, dv)):
            val = val.astype(BF16)
            for e in range(2):
                hd = 2 * pair + e
                g, hh = hd // 3, hd % 3
                at = 640 * g + 192 * t + 64 * hh
                cots[:, at : at + 64] = val[:, 64 * e : 64 * e + 64]
            heads[t].append(val)
    for g in range(2):
        cots[:, 640 * g + 576 : 640 * g + 640] = jnp.zeros((n, 64), BF16)
    parts = [jnp.concatenate(heads[t], 1) for t in range(3)]
    for i, out in enumerate((in0, in1)):
        rws = slice(half * i, half * i + half)
        total = 0.0
        for t in range(3):
            total = total + nn(parts[t][rws], wr[384 * t : 384 * t + 384])
        out[...] = total
    for row, t in ((0, 0), (1, 2)):
        s = jnp.sum(parts[t].astype(F32), 0, keepdims=True)
        for g in range(2):
            sg = s[:, 192 * g : 192 * g + 192]
            sums[row : row + 1, 384 * g : 384 * g + 192] = jnp.where(c == 0, sg, 0.0)
            sums[row : row + 1, 384 * g + 192 : 384 * g + 384] = jnp.where(c == 1, sg, 0.0)
    for d in range(3):
        at = slice(256 * d, 256 * d + 256)
        full = tn(x0[:, at], cots[0:half]) + tn(x1[:, at], cots[half:n])
        pg = tn(a0[:, at], ctx[0:half]) + tn(a1[:, at], ctx[half:n])
        for g in range(2):
            grads[g, at, 0:576] = full[:, 640 * g : 640 * g + 576].astype(BF16)
            grads[g, at, 576:768] = pg[:, 192 * g : 192 * g + 192].astype(BF16)
    if sets == 1:
        copies.start(grads, outs[0])
    else:
        rows = outs[0].shape[1]
        for spot in (3, 2, 1, 0):
            g, yi = flip(x, spot % 2), flip(y, spot // 2)
            for kz in range(4):
                zi = flip(lax.rem(z, 2), kz % 2) + 2 * flip(lax.div(z, 2), kz // 2)
                at = pl.multiple_of((2 * zi + yi) * rows, rows)
                dst = outs[spot].at[kz] if spot < 3 else outs[3 + kz // 2].at[4 + kz % 2]
                copies.start(grads.at[g, pl.ds(at, rows)], dst)
    copies.wait()


def attend_back(downs, a0, a1, x0, x1, wp, wr, q, k, v, ctx, probs):
    half = a0.shape[0]
    n = 2 * half
    sets = (shape((2, D, D)),)
    if downs:
        sets = (shape((4, 96, D)),) * 3 + (shape((6, 96, D)),) * 2
    far = (wp, v, probs, k, q, wr, x0, x1, ctx)
    return call(
        functools.partial(attend_back_kernel, len(sets)),
        (*sets, shape((half, D), F32), shape((half, D), F32), shape((2, D), F32)),
        (a0, a1, *downs, *far),
        scratch=[
            pltpu.VMEM((n, 384), BF16),
            pltpu.VMEM((n, 1280), BF16),
            pltpu.VMEM((2, D, D), BF16),
        ],
        cost=est(8e9, 14e6),
        limit=16,
        far_out=range(len(sets)),
        sems=20,
    )


def local(
    inputs,
    bucket,
    lengths,
    qkv_weight,
    query_bias,
    value_bias,
    proj_weight,
    proj_bias,
    first_gain,
    first_shift,
    up_weight,
    up_bias,
    down_weight,
    down_bias,
    second_gain,
    second_shift,
    cotangent,
):
    head_count = lax.axis_size("head")
    batch_count = lax.axis_size("batch")
    devices = head_count * batch_count
    direct = batch_count == 8
    b = lax.axis_index("batch")
    h = lax.axis_index("head")
    me = b * head_count + h
    x, c = h // 2, h % 2
    z, y = b // 2, b % 2
    wq, wp, wf = 3 * D // devices, D // devices, FF // devices

    vectors = [
        query_bias,
        value_bias,
        proj_bias,
        first_gain,
        first_shift,
        down_bias,
        second_gain,
        second_shift,
    ]
    if direct:
        a_shard, one_a, one_b, two = pack(
            qkv_weight.T, proj_weight.T, up_weight.T, down_weight, up_bias, vectors
        )
    else:
        small = lax.dynamic_update_slice(
            jnp.zeros((16, D), BF16), jnp.stack(vectors), (0, me * wp)
        )
        per_row = D // wf
        small = lax.dynamic_update_slice(
            small, up_bias[None, :], (8 + me // per_row, (me % per_row) * wf)
        )
        proj_t = proj_weight.T.reshape(wp, 2, 2, 192).transpose(0, 2, 1, 3).reshape(wp, D)
        a_shard = jnp.concatenate([qkv_weight.T, proj_t, small])
    other_in = core_swap(inputs)
    k = jnp.arange(batch_count * 2)
    if direct:
        a_z = z_line(a_shard)
        two = after(two, a_z[1])
        two_x, two_y = x_swap(two), y_swap(two)
        two_d = jnp.concatenate([x_swap(two_y[:TWO]), y_swap(two_x[TWO:])])
        two_lo = jnp.stack([two, two_x, two_y, two_d])
        a_z, two_lo, other_in = lax.optimization_barrier((jnp.stack(a_z), two_lo, other_in))
        one_a = z_line(after(one_a, a_z))
        a_x, a_y = x_swap(a_z), y_swap(a_z)
        a_x, a_y, one_a, two_lo = lax.optimization_barrier((a_x, a_y, one_a, two_lo))
        one_b = after(one_b, one_a)
        near = z_swap(jnp.concatenate([one_b, two_lo.reshape(8 * TWO, D)]), 1)
        one_b = [one_b, None, z_swap(one_b, 2), z_swap(one_b, 3)]
        a_d = [x_swap(a_y[:2]), y_swap(a_x[2:])]
        near, one_b[2], one_b[3], a_d = lax.optimization_barrier((near, one_b[2], one_b[3], a_d))
        one_b[1], two_hi = near[: 2 * ONE - FIRST], near[2 * ONE - FIRST :].reshape(two_lo.shape)
        a_own = [a_z, a_x, a_y, *a_d]
        one_z = jnp.stack([jnp.concatenate(pair) for pair in zip(one_a, one_b)])
        one_z, a_own = lax.optimization_barrier((one_z, a_own))
        one_x, one_y = x_swap(one_z), y_swap(one_z)
        a_swapped = [core_swap(v) for v in a_own]
        two_far = z_swap(jnp.concatenate([two_lo, two_hi]), 2)
        one_x, one_y, two_far = lax.optimization_barrier((one_x, one_y, two_far))
        one_d = [x_swap(one_y[:2]), y_swap(one_x[2:])]
        twos = [two_lo, two_hi, two_far]
        ctx_own, ctx_other, q, kk, v, ctx, probs, wr, ub_all, proj_w, small_all = attend(
            bucket, lengths, inputs, other_in, (*a_own, *a_swapped), wq, wp
        )
        f_all = [[one_z], [one_x], [one_y], twos, one_d]
    else:
        a_all = lax.all_gather(a_shard, ("batch", "head"), axis=0)
        qkv_all = a_all[:, :wq].reshape(2, 2, 576, D)
        qkv_w = lax.dynamic_index_in_dim(qkv_all, c, 1, keepdims=False).reshape(2 * 576, D)
        proj_w = a_all[:, wq : wq + wp].reshape(D, D)
        small_all = jnp.sum(a_all[:, wq + wp :].astype(F32), 0)
        ctx_own, ctx_other, q, kk, v, ctx, probs, wr = attend(
            bucket, lengths, inputs, other_in, (qkv_w, small_all)
        )
        f_shard = jnp.concatenate([up_weight.T, down_weight])
        f_all = [
            (v[:, :wf].reshape(-1, D), v[:, wf:].reshape(-1, D)) for v in gather_any(f_shard)
        ]
        owner = (k % batch_count) * 4 + (x ^ (k // batch_count)) * 2 + c
    if not direct:
        spread = (owner[None, :] == jnp.arange(devices)[:, None]).astype(F32)
        ub_all = tn(spread, small_all[8:12].reshape(devices, wf)).reshape(1, FF // 2)

    ctx_in = core_swap(ctx_other)
    first_low, first, first_n, first_r = first_norm(inputs, ctx_own, ctx_in, proj_w, small_all)
    first_in = core_swap(first_low)
    sums = ()
    kept = []
    starts = (0, FF // 4)
    if direct:
        starts = (0, 4 * ONE, 8 * ONE, 16 * ONE, 12 * ONE)
    for weights, at in zip(f_all, starts):
        width = FF // 4
        if direct:
            width = 16 * TWO if len(kept) == 3 else 4 * ONE
        hid, slope, *sums = ffn(
            first_low,
            first_in,
            ub_all[:, at : at + width],
            weights,
            sums,
            len(kept) == len(f_all) - 1,
        )
        kept.append((hid, slope))
    layer_out, sum_two, down_low, sums_two = second_norm(
        bucket, lengths, first, sums[0], core_swap(sums[1]), small_all, cotangent
    )
    down_in = core_swap(down_low)

    sums = ()
    f_parts, ub_parts = [], []
    if direct:
        for spot, i in ((3, 4), (2, 2), (1, 1), (0, 0)):
            weights, both = (*f_all[i], *twos), (*kept[i], *kept[3])
            grads, ub, sums = ffn_back(
                down_low, down_in, first_low, first_in, spot, weights, both, sums, spot == 0
            )
            f_parts.append(grads)
            ub_parts.insert(0, ub)
    else:
        for weights, pair in zip(f_all, kept):
            grads, ub, sums = ffn_back(
                down_low,
                down_in,
                first_low,
                first_in,
                None,
                weights,
                pair,
                sums,
                len(f_parts) == len(f_all) - 1,
            )
            f_parts.append(grads)
            ub_parts.append(ub)
    part_own, part_other = sums
    moved = ()
    if direct:
        (d_lo, d_hi), y_sets, x_sets, z_sets = f_parts
        moved = (*x_sets, y_swap(d_hi), *y_sets, x_swap(d_lo))
        part_other = after(part_other, moved)
    added, sum_one, attn_low, sums_one = first_back(
        sum_two, part_own, core_swap(part_other), first_n, first_r, small_all, moved
    )
    attn_in = core_swap(attn_low)
    *a_grads, in_own, in_other, sums_zero = attend_back(
        added[2:],
        attn_low,
        attn_in,
        inputs,
        other_in,
        proj_w,
        wr,
        q,
        kk,
        v,
        ctx,
        probs,
    )
    in_got = core_swap(in_other)
    inputs_grad = (sum_one + in_own + in_got).astype(BF16)

    if direct:
        up_sets = scatter_xy(z_sets[0], *added[:2])
        terms = exchange_terms(sums_zero, sums_one, sums_two, ub_parts, devices)
        a_zz, a_xx, a_yy, by_x, by_y = a_grads
        by_x, by_y, up_sets = lax.optimization_barrier((by_x, by_y, up_sets))
        by_x, by_y = x_swap(by_x), y_swap(by_y)
        up_mine, up_others = combine(*up_sets)
        terms = after(terms, up_others)
        terms = lax.all_to_all(terms, ("batch", "head"), split_axis=0, concat_axis=0, tiled=True)
        up_others = scatter_z(up_others)
        by_x, by_y, up_others, terms, _ = lax.optimization_barrier(
            (by_x, by_y, up_others, terms, inputs_grad)
        )
        a_xy, down_mine, down_others = turn(a_xx, a_yy, z_sets[1], by_x, by_y)
        a_sets = scatter_xy(a_zz, *a_xy)
        down_others = scatter_z(down_others)
        a_sets, down_others = lax.optimization_barrier((a_sets, down_others))
        a_mine, a_others = combine_last(*a_sets)
        a_others = scatter_z(a_others)
        up_grad, down_grad = finish_ffn((up_mine, *up_others), (down_mine, *down_others))
        up_grad = up_grad.T
        terms = jnp.sum(terms, 0)
        packed = jnp.concatenate([terms[:, :wp].reshape(-1), terms[0, wp : wp + wf]])
        qkv_grad, proj_grad = finish_attend((a_mine, *a_others))
    else:
        vecs = jnp.concatenate([sums_zero, sums_one, sums_two])
        vecs = vecs.reshape(8, devices, wp).transpose(1, 0, 2).reshape(devices, 8 * wp)
        ubias = jnp.concatenate(ub_parts).reshape(batch_count * 2, wf)
        ubias = lax.dot_general(
            spread, ubias, (((1,), (0,)), ((), ())), precision=lax.Precision.HIGHEST
        )
        packed = jnp.concatenate([vecs, ubias], 1)
        packed = lax.all_to_all(
            packed, ("batch", "head"), split_axis=0, concat_axis=0, tiled=True
        )
        packed = jnp.sum(packed, 0)
        wb = D // batch_count
        a_grads = a_grads[0].reshape(2, batch_count, wb, D)
        a_mine = scatter_any(
            [
                lax.dynamic_index_in_dim(a_grads, x, 0, keepdims=False),
                lax.dynamic_index_in_dim(a_grads, 1 - x, 0, keepdims=False),
            ]
        )
        f_mine = scatter_any(
            [
                jnp.concatenate(
                    [ug.reshape(batch_count, wf, D), dg.reshape(batch_count, wf, D)], 1
                )
                for ug, dg in f_parts
            ]
        )
        qkv_grad = a_mine[:, :576].reshape(wb, 3, 3, HEAD_DIM).transpose(0, 2, 1, 3)
        qkv_grad = qkv_grad.reshape(wb, 576)
        proj_grad = a_mine[:, 576:].T
        up_grad, down_grad = f_mine[:wf].T, f_mine[wf:]
    qb_g, vb_g, pb_g, fg_g, fs_g, db_g, sg_g, ss_g = [
        packed[i * wp : (i + 1) * wp] for i in range(8)
    ]
    return (
        layer_out,
        inputs_grad,
        qkv_grad,
        qb_g,
        vb_g,
        proj_grad,
        pb_g,
        fg_g,
        fs_g,
        up_grad,
        packed[8 * wp :],
        down_grad,
        db_g,
        sg_g,
        ss_g,
    )


def solution(mesh):
    both = ("batch", "head")
    in_specs = (
        P(both, None),
        P("batch"),
        P("batch", None),
        P(None, both),
        P(both),
        P(both),
        P(None, both),
        P(both),
        P(both),
        P(both),
        P(None, both),
        P(both),
        P(both, None),
        P(both),
        P(both),
        P(both),
        P(both, None),
    )
    out_specs = (
        P(both, None),
        P(both, None),
        P("batch", "head"),
        P(both),
        P(both),
        P("head", "batch"),
        P(both),
        P(both),
        P(both),
        P(None, both),
        P(both),
        P(both, None),
        P(both),
        P(both),
        P(both),
    )
    return jax.shard_map(local, mesh=mesh, in_specs=in_specs, out_specs=out_specs, check_vma=False)
```

```python
import functools

import jax
import jax.numpy as jnp
from jax import lax
from jax.experimental import pallas as pl
from jax.experimental.pallas import tpu as pltpu
from jax.sharding import PartitionSpec as P

D = 768
HEADS = 12
HEAD_DIM = 64
FF = 3072
BIG = 512
SMALL = 128
UNITS = 4
NORM_EPS = 1e-12
F32 = jnp.float32
BF16 = jnp.bfloat16

ONE, TWO = 80, 16
FIRST = 104

CORE = [(i, i ^ 1) for i in range(4)]
XPAIR = [(i, i ^ 2) for i in range(4)]
YPAIR = [(i, i ^ 1) for i in range(8)]
ZPAIR = [[(i, i ^ (2 * k)) for i in range(8)] for k in range(4)]


def core_swap(v):
    return lax.ppermute(v, "head", CORE)


def x_swap(v):
    return lax.ppermute(v, "head", XPAIR)


def y_swap(v):
    return lax.ppermute(v, "batch", YPAIR)


def z_swap(v, k):
    return lax.ppermute(v, "batch", ZPAIR[k])


def after(value, other):
    return lax.optimization_barrier((value, other))[0]


def nt(a, b, out=F32):
    return lax.dot_general(a, b, (((1,), (1,)), ((), ())), preferred_element_type=F32).astype(out)


def nn(a, b, out=F32):
    return lax.dot_general(a, b, (((1,), (0,)), ((), ())), preferred_element_type=F32).astype(out)


def tn(a, b, out=F32):
    return lax.dot_general(a, b, (((0,), (0,)), ((), ())), preferred_element_type=F32).astype(out)


def z_line(shard):
    return [shard] + [z_swap(shard, k) for k in (1, 2, 3)]


def gather_four(z):
    x, y = x_swap(z), y_swap(z)
    return [z, x, y, x_swap(y[:2]), y_swap(x[2:])]


def gather_any(shard):
    whole = lax.all_gather(shard, "batch", axis=0)
    return [whole, x_swap(whole)]


def scatter_xy(z, x, y):
    return z, x_swap(x), y_swap(y)


def scatter_z(others):
    return [z_swap(others[k - 1], k) for k in (1, 2, 3)]


def scatter_any(parts):
    total = parts[0].astype(F32) + x_swap(parts[1]).astype(F32)
    return lax.psum_scatter(total, "batch", scatter_dimension=0, tiled=False)


def est(flops, moved, trans=0):
    return pl.CostEstimate(flops=int(flops), bytes_accessed=int(moved), transcendentals=int(trans))


def call(kernel, out_shape, operands, scratch=(), cost=None, limit=16, far_in=(), far_out=(), sems=0):
    vmem = pl.BlockSpec(memory_space=pltpu.VMEM)
    hbm = pl.BlockSpec(memory_space=pltpu.HBM)
    smem = pl.BlockSpec(memory_space=pltpu.SMEM)
    ins = [hbm if i in far_in else vmem for i in range(len(operands))]
    ins = [smem if v.dtype == jnp.int32 else spec for spec, v in zip(ins, operands)]
    outs = [hbm if i in far_out else vmem for i in range(len(out_shape))]
    scratch = list(scratch) + ([pltpu.SemaphoreType.DMA((sems,))] if sems else [])
    operands = [
        pltpu.with_memory_space_constraint(v, pltpu.HBM) if i in far_in else v
        for i, v in enumerate(operands)
    ]
    out_shape = [
        pltpu.HBM(v.shape, v.dtype) if i in far_out else v for i, v in enumerate(out_shape)
    ]
    return pl.pallas_call(
        kernel,
        out_shape=out_shape,
        in_specs=ins,
        out_specs=outs,
        scratch_shapes=scratch,
        compiler_params=pltpu.CompilerParams(vmem_limit_bytes=limit << 20),
        cost_estimate=cost,
    )(*operands)


class Copies:
    def __init__(self, sems):
        self.sems, self.used, self.open = sems, 0, []

    def start(self, src, dst):
        copy = pltpu.make_async_copy(src, dst, self.sems.at[self.used])
        self.used += 1
        copy.start()
        self.open.append(copy)
        return copy

    def wait(self, *copies):
        for copy in copies or list(self.open):
            copy.wait()
            self.open.remove(copy)


def add_low(a, b):
    return (a.astype(F32) + b.astype(F32)).astype(BF16)


def shape(dims, dtype=BF16):
    return jax.ShapeDtypeStruct(dims, dtype)


def add_first_kernel(x_up, x_down, for_x, y_up, y_down, for_y, *outs):
    half = x_up.shape[1]
    for i, (x, y) in enumerate(((x_up, y_up), (x_down, y_down))):
        rows = slice(half * i, half * i + half)
        x_out, y_out = outs[2 * i : 2 * i + 2]
        x_out[0:2] = x[0:2]
        y_out[2:4] = y[2:4]
        for k in range(2):
            x_out[2 + k] = add_low(x[2 + k], for_x[k, rows])
            y_out[k] = add_low(y[k], for_y[k, rows])


def combine_kernel(z, x, y, *refs):
    outs, (mine, low, sems) = refs[:4], refs[4:]
    sum_places(z, x, y, outs, mine, low, Copies(sems)).wait()


def sum_places(z, x, y, outs, mine, low, copies, arrived=None):
    for i, k in enumerate((1, 2, 3, 0)):
        if arrived:
            copies.wait(*arrived[i])
        total = z[k].astype(F32) + x[k].astype(F32) + y[k].astype(F32)
        if k == 0:
            mine[...] = total
            copies.start(mine, outs[0])
        else:
            low[k - 1] = total.astype(BF16)
            copies.start(low.at[k - 1], outs[k])
    return copies


def combine(z, x, y):
    rows = z.shape[1]
    mine, *others = call(
        combine_kernel,
        (shape((rows, D), F32),) + (shape((rows, D)),) * 3,
        (z, x, y),
        scratch=[pltpu.VMEM((rows, D), F32), pltpu.VMEM((3, rows, D), BF16)],
        cost=est(1000, 1000),
        limit=8,
        far_out=range(4),
        sems=4,
    )
    return mine, others


def combine_last_kernel(z, x, y, mine, *refs):
    outs, (low, sems) = refs[:3], refs[3:]
    copies = Copies(sems)
    for k in (1, 2, 3, 0):
        total = z[k].astype(F32) + x[k].astype(F32) + y[k].astype(F32)
        if k == 0:
            mine[...] = total
        else:
            low[k - 1] = total.astype(BF16)
            copies.start(low.at[k - 1], outs[k - 1])
    copies.wait()


def combine_last(z, x, y):
    rows = z.shape[1]
    mine, *others = call(
        combine_last_kernel,
        (shape((rows, D), F32),) + (shape((rows, D)),) * 3,
        (z, x, y),
        scratch=[pltpu.VMEM((3, rows, D), BF16)],
        cost=est(1000, 1000),
        limit=8,
        far_out=range(1, 4),
        sems=3,
    )
    return mine, others


def turn_kernel(x, y, z, by_x_far, by_y_far, x_out, y_out, *refs):
    outs, (by_x, by_y, mine, low, sems) = refs[:4], refs[4:]
    copies = Copies(sems)
    arrived = []
    for k in (1, 2, 3, 0, 4):
        rows = pl.ds(k, 1 if k < 4 else 2)
        arrived.append(
            (
                copies.start(by_x_far.at[rows], by_x.at[rows]),
                copies.start(by_y_far.at[rows], by_y.at[rows]),
            )
        )
    sum_places(z, by_x, by_y, outs, mine, low, copies, arrived)
    copies.wait(*arrived[4])
    y_out[0:2] = add_low(y[0:2], by_x[4:6])
    y_out[2:4] = y[2:4]
    x_out[0:2] = x[0:2]
    x_out[2:4] = add_low(x[2:4], by_y[4:6])
    copies.wait()


def turn(x, y, z, by_x, by_y):
    rows = z.shape[1]
    x, y, mine, *others = call(
        turn_kernel,
        (shape(x.shape), shape(y.shape), shape((rows, D), F32)) + (shape((rows, D)),) * 3,
        (x, y, z, by_x, by_y),
        scratch=[pltpu.VMEM(by_x.shape, BF16)] * 2
        + [pltpu.VMEM((rows, D), F32), pltpu.VMEM((3, rows, D), BF16)],
        cost=est(1000, 1000),
        limit=8,
        far_in=(3, 4),
        far_out=range(2, 6),
        sems=14,
    )
    return (x, y), mine, others


def total_of(refs):
    return refs[0][...] + refs[1][...].astype(F32) + refs[2][...].astype(F32) + refs[3][...].astype(F32)


def finish_attend_kernel(mine, one, two, three, qkv, proj):
    total = total_of((mine, one, two, three))
    for hh in range(3):
        for t in range(3):
            at, to = 192 * t + 64 * hh, 192 * hh + 64 * t
            qkv[:, to : to + 64] = total[:, at : at + 64]
    proj[...] = total[:, 576:].T


def finish_attend(parts):
    rows = parts[0].shape[0]
    return call(
        finish_attend_kernel,
        (shape((rows, 576), F32), shape((192, rows), F32)),
        tuple(parts),
        cost=est(8 * rows * D, 16 * rows * D),
        limit=8,
    )


def finish_ffn_kernel(*refs):
    up, down = refs[8:]
    up[...], down[...] = total_of(refs[0:4]), total_of(refs[4:8])


def finish_ffn(ups, downs):
    dims = ups[0].shape
    return call(
        finish_ffn_kernel,
        (shape(dims, F32), shape(dims, F32)),
        (*ups, *downs),
        cost=est(1000, 1000),
        limit=8,
    )


def exchange_kernel(zero, one, two, *refs):
    ubs, out = refs[:4], refs[4]
    vecs = jnp.concatenate([zero[...], one[...], two[...]])
    width = D // out.shape[0]
    vecs = vecs.astype(BF16)
    out[...] = jnp.zeros(out.shape, BF16)
    for i in range(out.shape[0]):
        out[i, 0:8, 0:width] = vecs[:, width * i : width * i + width]
    for spot in range(4):
        for kz in range(4):
            to, ub = slot_of(spot, kz), ubs[spot][...].astype(BF16)
            out[to, 0:1, 24 : 24 + ONE] = ub[:, ONE * kz : ONE * kz + ONE]
            at = 4 * ONE + TWO * kz
            out[to, 0:1, 24 + ONE : 24 + ONE + TWO] = ub[:, at : at + TWO]


def exchange_terms(zero, one, two, ubs, devices):
    return call(
        exchange_kernel,
        (shape((devices, 8, 128)),),
        (zero, one, two, *ubs),
        cost=est(1000, 1000),
        limit=8,
    )[0]


def flip(a, bit):
    return a + bit - 2 * a * bit


def pack_kernel(qkv_in, proj_in, up_in, down_in, bias_in, *refs):
    vectors_in, (a_out, one_a, one_b, two, a, p, f, bias, vectors, sems) = refs[:8], refs[8:]
    rows_q, rows_p, half = qkv_in.shape[0], proj_in.shape[0], down_in.shape[0]
    copies = Copies(sems)
    copies.start(qkv_in, a.at[pl.ds(0, rows_q)])
    copies.start(proj_in, p)
    copies.start(up_in, f.at[pl.ds(0, half)])
    copies.start(down_in, f.at[pl.ds(half, half)])
    copies.start(bias_in, bias)
    for i, r in enumerate(vectors_in):
        copies.start(r, vectors.at[i])
    width = vectors.shape[2]
    b, h = lax.axis_index("batch"), lax.axis_index("head")
    me = b * lax.axis_size("head") + h
    copies.wait()
    v = jnp.concatenate([vectors[i] for i in range(8)]).astype(F32)
    v = jnp.concatenate([v] * (D // width), 1)
    lane = lax.broadcasted_iota(jnp.int32, (8, D), 1)
    mine = jnp.logical_and(lane >= me * width, lane < me * width + width)
    v = jnp.where(mine, v, 0.0)
    gap = jnp.zeros((1, D // 2 - half), F32)
    none = jnp.zeros((1, D // 2), F32)
    row = bias[...].astype(F32)
    early = jnp.concatenate([none, row, gap], 1)
    late = jnp.concatenate([row, gap, none], 1)
    extra = jnp.where(me < lax.axis_size("batch") * lax.axis_size("head") // 2, early, late)
    v = v + jnp.concatenate([extra, jnp.zeros((7, D), F32)])
    a_out[0:rows_q] = a[0:rows_q]
    q = p[...]
    a_out[rows_q : rows_q + rows_p] = jnp.concatenate(
        [q[:, 192 * i : 192 * i + 192] for i in (0, 2, 1, 3)], 1
    )
    a_out[rows_q + rows_p :] = v.astype(BF16)
    one = jnp.concatenate([f[0:ONE], f[half : half + ONE]])
    one_a[...], one_b[...] = one[0:FIRST], one[FIRST:]
    two[0:TWO], two[TWO:] = f[ONE:half], f[half + ONE :]


def pack(qkv, proj, up, down, bias, vectors):
    rows, half = qkv.shape[0] + proj.shape[0] + 8, down.shape[0]
    return call(
        pack_kernel,
        (
            shape((rows, D)),
            shape((FIRST, D)),
            shape((2 * ONE - FIRST, D)),
            shape((2 * TWO, D)),
        ),
        (qkv, proj, up, down, bias[None], *[v[None] for v in vectors]),
        scratch=[
            pltpu.VMEM((rows, D), BF16),
            pltpu.VMEM(proj.shape, BF16),
            pltpu.VMEM((2 * half, D), BF16),
            pltpu.VMEM((1,) + bias.shape, BF16),
            pltpu.VMEM((8, 1) + vectors[0].shape, BF16),
        ],
        cost=est(1000, 1000),
        limit=8,
        far_in=range(13),
        sems=13,
    )


def place_here():
    b, h = lax.axis_index("batch"), lax.axis_index("head")
    return lax.rem(h, 2), lax.div(b, 2), lax.rem(b, 2), lax.div(h, 2)


def live_units(bucket, lengths):
    x = place_here()[3]
    kind, first = bucket[x], lengths[x, 0]
    units = []
    for u in range(UNITS):
        far = jnp.clip(first - SMALL * u, 0, SMALL)
        units.append(jnp.where(kind == 1, far, lengths[x, u]))
    return kind, units


def place_of(index, c):
    return jnp.bitwise_xor(index, c * (BIG // 2))


def live_of(place, units):
    unit = lax.shift_right_logical(place, 7)
    inner = jnp.bitwise_and(place, SMALL - 1)
    count = jnp.where(
        unit < 2, jnp.where(unit == 0, units[0], units[1]), jnp.where(unit == 2, units[2], units[3])
    )
    return inner < count


def heads_of(row, c):
    parts = []
    for g in range(2):
        lo = row[:, 384 * g : 384 * g + 192]
        hi = row[:, 384 * g + 192 : 384 * g + 384]
        parts.append(jnp.where(c == 0, lo, hi))
    return jnp.concatenate(parts, 1)


def fetch_shards(copies, sources, slots):
    c, z, y, x = place_here()
    zl, zh = lax.rem(z, 2), lax.div(z, 2)
    for swapped in range(2):
        cc = c if swapped == 0 else 1 - c
        zs, xs, ys, xa, xb = sources[5 * swapped : 5 * swapped + 5]
        for kx, ky, pair in ((0, 0, (zs,)), (1, 0, (xs,)), (0, 1, (ys,)), (1, 1, (xa, xb))):
            j = flip(y, ky) * 4 + flip(x, kx) * 2 + cc
            for kz in range(4):
                src = pair[0].at[kz] if len(pair) == 1 else pair[kz // 2].at[kz % 2]
                zi = flip(zl, kz % 2) + 2 * flip(zh, kz // 2)
                copies.start(src, slots.at[zi * 8 + j])


def slot_of(spot, kz):
    c, z, y, x = place_here()
    zi = flip(lax.rem(z, 2), kz % 2) + 2 * flip(lax.div(z, 2), kz // 2)
    return zi * 8 + flip(y, spot // 2) * 4 + flip(x, spot % 2) * 2 + c


def bias_order(slots, row, out):
    for spot in range(4):
        for kz in range(4):
            i = slot_of(spot, kz)
            b = slots[i, row : row + 1].astype(F32)
            b = jnp.where(i < 16, b[:, D // 2 : D // 2 + 96], b[:, 0:96])
            at = 4 * ONE * spot + ONE * kz
            out[:, at : at + ONE] = b[:, 0:ONE]
            at = 16 * ONE + 4 * TWO * spot + TWO * kz
            out[:, at : at + TWO] = b[:, ONE:]


def attend_kernel(rows_q, rows_p, bucket, lengths, x0, x1, *refs):
    sources = 10 if rows_q else 2
    weights, refs = refs[:sources], refs[sources:]
    (ctx0, ctx1, q, k, v, ctx, probs, wr), refs = refs[:8], refs[8:]
    if rows_q:
        (ub_out, wp, small, mask, xs, slots, sems) = refs
    else:
        (mask, xs, w, small, sems) = refs
    copies = Copies(sems)
    c = place_here()[0]
    kind, units = live_units(bucket, lengths)
    half = x0.shape[0]
    copies.start(x0, xs.at[0:half])
    copies.start(x1, xs.at[half : 2 * half])
    if rows_q:
        fetch_shards(copies, weights, slots)
    else:
        copies.start(weights[0], w)
        copies.start(weights[1], small)
    rows = lax.broadcasted_iota(jnp.int32, (BIG, BIG), 0)
    cols = lax.broadcasted_iota(jnp.int32, (BIG, BIG), 1)
    prow, pcol = place_of(rows, c), place_of(cols, c)
    same = jnp.logical_or(
        kind == 1, lax.shift_right_logical(prow, 7) == lax.shift_right_logical(pcol, 7)
    )
    mask[...] = jnp.where(jnp.logical_and(same, live_of(pcol, units)), 0.0, -1e30)
    copies.wait()
    if rows_q:
        for g in range(2):
            cuts = jnp.concatenate([slots[16 * g + 8 * c + j, 0:rows_q] for j in range(8)])
            for t in range(3):
                for hh in range(3):
                    src, dst = (hh * 3 + t) * HEAD_DIM, (t * 6 + g * 3 + hh) * HEAD_DIM
                    wr[dst : dst + HEAD_DIM] = cuts[src : src + HEAD_DIM]
        lane = lax.broadcasted_iota(jnp.int32, (8, D), 1)
        small[...] = sum(
            jnp.where(
                jnp.logical_and(lane >= rows_p * i, lane < rows_p * i + rows_p),
                slots[i, rows_q + rows_p :].astype(F32),
                0.0,
            )
            for i in range(32)
        )
    else:
        for t in range(3):
            for hd in range(6):
                src = ((hd // 3) * 9 + (hd % 3) * 3 + t) * HEAD_DIM
                dst = (t * 6 + hd) * HEAD_DIM
                wr[dst : dst + HEAD_DIM] = w[src : src + HEAD_DIM]
    biases = (heads_of(small[0:1], c), None, heads_of(small[1:2], c))
    for t, ref in enumerate((q, k, v)):
        val = nt(xs[...], wr[384 * t : 384 * t + 384])
        if biases[t] is not None:
            val = val + biases[t]
        ref[...] = val.astype(BF16)
    if rows_q:
        for i in range(32):
            wp[rows_p * i : rows_p * i + rows_p] = slots[i, rows_q : rows_q + rows_p]
        bias_order(slots, rows_q + rows_p, ub_out)
    lane = lax.broadcasted_iota(jnp.int32, (half, 128), 1)
    for pair in range(3):
        lanes = slice(128 * pair, 128 * pair + 128)
        kp, vp = k[:, lanes], v[:, lanes]
        for i, near in enumerate((ctx0, ctx1)):
            rws = slice(half * i, half * i + half)
            qp = q[rws, lanes] * jnp.asarray(HEAD_DIM**-0.5, BF16)
            outs = []
            for e in range(2):
                mine = (lane < HEAD_DIM) if e == 0 else (lane >= HEAD_DIM)
                s = nt(jnp.where(mine, qp, jnp.zeros_like(qp)), kp) + mask[rws]
                ex = jnp.exp(s - jnp.max(s, -1, keepdims=True))
                pr = (ex * (1.0 / jnp.sum(ex, -1, keepdims=True))).astype(BF16)
                probs[2 * pair + e, rws] = pr
                outs.append(nn(pr, vp))
            val = jnp.where(lane < HEAD_DIM, outs[0], outs[1]).astype(BF16)
            ctx[rws, lanes] = val
            near[:, lanes] = val


def attend(bucket, lengths, x0, x1, weights, rows_q=0, rows_p=0, rows_s=16):
    rows_s = 8 if rows_q else rows_s
    half = x0.shape[0]
    n = 2 * half
    direct = rows_q > 0
    outs = [
        shape((half, 384)),
        shape((half, 384)),
        shape((n, 384)),
        shape((n, 384)),
        shape((n, 384)),
        shape((n, 384)),
        shape((6, n, n)),
        shape((1152, D)),
    ]
    scratch = [pltpu.VMEM((n, n), F32), pltpu.VMEM((n, D), BF16)]
    if direct:
        outs += [shape((1, FF // 2), F32), shape((D, D)), shape((rows_s, D), F32)]
        scratch += [pltpu.VMEM((32, rows_q + rows_p + rows_s, D), BF16)]
    else:
        scratch += [pltpu.VMEM((1152, D), BF16), pltpu.VMEM((rows_s, D), F32)]
    operands = (bucket, lengths, x0, x1, *weights)
    return call(
        functools.partial(attend_kernel, rows_q, rows_p),
        outs,
        operands,
        scratch=scratch,
        cost=est(1000, 1000),
        limit=32,
        far_in=range(2, len(operands)),
        sems=50,
    )


def norm(values):
    center = values - jnp.mean(values, -1, keepdims=True)
    spread = jnp.mean(center * center, -1, keepdims=True)
    scale = lax.rsqrt(spread + NORM_EPS)
    return center * scale, scale


def norm_back(cot, normal, scale, gain):
    w = cot * gain
    return scale * (
        w - jnp.mean(w, -1, keepdims=True) - normal * jnp.mean(w * normal, -1, keepdims=True)
    )


def first_kernel(x, ctx_own, ctx_in, wp, small, low, first, normal, scale):
    c = place_here()[0]
    mine = pl.multiple_of(c * 384, 128)
    theirs = pl.multiple_of((1 - c) * 384, 128)
    attn = nt(ctx_own[...], wp[:, pl.ds(mine, 384)]) + nt(ctx_in[...], wp[:, pl.ds(theirs, 384)])
    n, r = norm(x[...].astype(F32) + attn + small[2:3])
    normal[...] = n
    out = n * small[3:4] + small[4:5]
    first[...] = out
    low[...] = out.astype(BF16)
    scale[...] = jnp.broadcast_to(r, scale.shape)


def first_norm(x, ctx_own, ctx_in, wp, small):
    n = x.shape[0]
    return call(
        first_kernel,
        (shape((n, D)), shape((n, D), F32), shape((n, D), F32), shape((n, 128), F32)),
        (x, ctx_own, ctx_in, wp, small),
        cost=est(1000, 1000),
        limit=8,
    )


def ffn_weights(refs):
    if len(refs[0].shape) == 2:
        return refs[0][...], refs[1][...]
    return stacked(ones_of(refs) if refs[0].shape[1] == 2 * ONE else twos_of(refs, range(4)))


def ones_of(refs):
    return [(r, i) for r in refs for i in range(r.shape[0])]


def twos_of(refs, spots):
    along_z = [(r, i) for r in refs for i in range(0, r.shape[0], 4)]
    return [(r, i + spot) for spot in spots for r, i in along_z]


def stacked(blocks):
    up = jnp.concatenate([r[i, 0 : r.shape[1] // 2] for r, i in blocks])
    down = jnp.concatenate([r[i, r.shape[1] // 2 :] for r, i in blocks])
    return up, down


def ffn_kernel(first, count, x0, x1, ub, *refs):
    far, refs = refs[:count], refs[count:]
    if first:
        in0 = in1 = None
    else:
        (in0, in1), refs = refs[:2], refs[2:]
    hid, slope, out0, out1 = refs
    half = x0.shape[0]
    uw, dw = ffn_weights(far)
    for i, (xr, before, out) in enumerate(((x0, in0, out0), (x1, in1, out1))):
        rws = slice(half * i, half * i + half)
        up = nt(xr[...], uw) + ub[...]
        phi = 0.5 + 0.5 * lax.erf(up * (2.0**-0.5))
        hd = (up * phi).astype(BF16)
        hid[rws] = hd
        slope[rws] = (phi + up * jnp.exp(-0.5 * up * up) * 0.3989422804014327).astype(BF16)
        part = nn(hd, dw)
        part = part if before is None else before[...] + part
        out[...] = part.astype(out.dtype)


def ffn(x0, x1, ub, weights, sums, last):
    half, width, count = x0.shape[0], ub.shape[1], len(weights)
    n = 2 * half
    return call(
        functools.partial(ffn_kernel, not sums, count),
        (
            shape((n, width)),
            shape((n, width)),
            shape((half, D), F32),
            shape((half, D), BF16 if last else F32),
        ),
        (x0, x1, ub, *weights, *sums),
        cost=est(4 * n * D * width, 4 * D * width + 5e6, 2 * n * width),
    )


def second_kernel(bucket, lengths, first, part, got, small, cot, low, sum_two, normal):
    c = place_here()[0]
    _, units = live_units(bucket, lengths)
    n, r = norm(first[...] + (part[...] + got[...].astype(F32) + small[5:6]))
    index = lax.broadcasted_iota(jnp.int32, (first.shape[0], 1), 0)
    live = live_of(place_of(index, c), units)
    oc = jnp.where(live, cot[...].astype(F32), 0.0)
    st = norm_back(oc, n, r, small[6:7])
    low[...] = st.astype(BF16)
    sum_two[...] = st
    normal[...] = n


def second_norm(bucket, lengths, first, part, got, small, cot):
    n = first.shape[0]
    return call(
        second_kernel,
        (shape((n, D)), shape((n, D), F32), shape((n, D), F32)),
        (bucket, lengths, first, part, got, small, cot),
        cost=est(1000, 1000),
        limit=8,
    )


def second_rest_kernel(bucket, lengths, normal, small, cot, low, out, sums):
    c = place_here()[0]
    _, units = live_units(bucket, lengths)
    n = normal[...]
    out[...] = (n * small[6:7] + small[7:8]).astype(BF16)
    index = lax.broadcasted_iota(jnp.int32, (normal.shape[0], 1), 0)
    live = live_of(place_of(index, c), units)
    oc = jnp.where(live, cot[...].astype(F32), 0.0)
    sums[0:1] = jnp.sum(low[...].astype(F32), 0, keepdims=True)
    sums[1:2] = jnp.sum(oc * n, 0, keepdims=True)
    sums[2:3] = jnp.sum(oc, 0, keepdims=True)


def second_rest(bucket, lengths, normal, small, cot, low):
    n = normal.shape[0]
    return call(
        second_rest_kernel,
        (shape((n, D)), shape((3, D), F32)),
        (bucket, lengths, normal, small, cot, low),
        cost=est(1000, 1000),
        limit=8,
    )


def ffn_back_kernel(first, spot, count, d0, d1, x0, x1, *refs):
    weights, refs = refs[:count], refs[count:]
    if spot is None:
        hid, slope = refs[0], refs[1]
        refs = refs[2:]
        uw, dw = ffn_weights(weights)
    else:
        (hid1, slope1, hid2, slope2), refs = refs[:4], refs[4:]
        tail = slice(4 * TWO * spot, 4 * TWO * spot + 4 * TWO)
        hid = jnp.concatenate([hid1[...], hid2[:, tail]], 1)
        slope = jnp.concatenate([slope1[...], slope2[:, tail]], 1)
        uw, dw = stacked(ones_of(weights[:-3]) + twos_of(weights[-3:], [spot]))
    if first:
        in0 = in1 = None
    else:
        (in0, in1), refs = refs[:2], refs[2:]
    *outs, ub, out0, out1 = refs
    half = x0.shape[0]
    cots = []
    for i, (d, before, out) in enumerate(((d0, in0, out0), (d1, in1, out1))):
        rws = slice(half * i, half * i + half)
        uc = (nt(d[...], dw) * slope[rws].astype(F32)).astype(BF16)
        cots.append(uc)
        part = nn(uc, uw)
        part = part if before is None else before[...] + part
        out[...] = part.astype(out.dtype)
    ub[...] = jnp.sum(cots[0].astype(F32), 0, keepdims=True) + jnp.sum(
        cots[1].astype(F32), 0, keepdims=True
    )
    dg = (tn(hid[0:half], d0[...]) + tn(hid[half : 2 * half], d1[...])).astype(BF16)
    ug = (tn(cots[0], x0[...]) + tn(cots[1], x1[...])).astype(BF16)
    if spot is None:
        outs[0][...], outs[1][...] = ug, dg
        return
    rows = ONE + TWO
    for k in range(4):
        for e, g in enumerate((ug, dg)):
            out, i, at = (outs[k // 2], k % 2, rows * e) if spot == 3 else (outs[e], k, 0)
            out[i, at : at + ONE] = g[ONE * k : ONE * k + ONE]
            low = 4 * ONE + TWO * k
            out[i, at + ONE : at + rows] = g[low : low + TWO]


def ffn_back(d0, d1, x0, x1, spot, weights, kept, sums, last):
    half, count = x0.shape[0], len(weights)
    if spot is None:
        outs, width = [shape(w.shape) for w in weights], weights[0].shape[0]
    else:
        width = 4 * (ONE + TWO)
        rows = ONE + TWO
        outs = [shape((2, 2 * rows, D)) if spot == 3 else shape((4, rows, D))] * 2
    *grads, ub, s0, s1 = call(
        functools.partial(ffn_back_kernel, not sums, spot, count),
        (
            *outs,
            shape((1, width), F32),
            shape((half, D), F32),
            shape((half, D), BF16 if last else F32),
        ),
        (d0, d1, x0, x1, *weights, *kept, *sums),
        cost=est(1000, 1000),
    )
    return grads, ub, (s0, s1)


def first_back_kernel(
    sum_two, part, got, normal, scale, small, *refs
):
    *refs, sum_one, low, sums = refs
    fc = sum_two[...] + part[...] + got[...].astype(F32)
    n = normal[...]
    so = norm_back(fc, n, scale[:, 0:1], small[3:4])
    sum_one[...] = so
    lo = so.astype(BF16)
    low[...] = lo
    sums[0:1] = jnp.sum(lo.astype(F32), 0, keepdims=True)
    sums[1:2] = jnp.sum(fc * n, 0, keepdims=True)
    sums[2:3] = jnp.sum(fc, 0, keepdims=True)
    if refs:
        add_first_kernel(*refs)


def first_back(sum_two, part, got, normal, scale, small, moved=()):
    n = sum_two.shape[0]
    outs = [shape(moved[i].shape) for i in (0, 3, 1, 4)] if moved else []
    *added, sum_one, low, sums = call(
        first_back_kernel,
        (*outs, shape((n, D), F32), shape((n, D)), shape((3, D), F32)),
        (sum_two, part, got, normal, scale, small, *moved),
        cost=est(1000, 1000),
        limit=8,
    )
    return added, sum_one, low, sums


def attend_back_kernel(sets, a0, a1, *refs):
    downs, refs = ((), refs) if sets == 1 else (refs[:2], refs[2:])
    far, outs, (in0, in1, sums), refs = refs[:9], refs[9 : 9 + sets], refs[9 + sets : 12 + sets], refs[12 + sets :]
    wp, v, probs, k, q, wr, x0, x1, ctx = far
    dctx, cots, grads, sems = refs
    copies = Copies(sems)
    for down, out in zip(downs, outs[3:]):
        copies.start(down, out.at[pl.ds(0, 4)])
    c, z, y, x = place_here()
    half = a0.shape[0]
    n = 2 * half
    wpo = wp[:, pl.ds(pl.multiple_of(c * 384, 128), 384)]
    dctx[0:half] = nn(a0[...], wpo).astype(BF16)
    dctx[half:n] = nn(a1[...], wpo).astype(BF16)
    lane = lax.broadcasted_iota(jnp.int32, (n, 128), 1)
    zero = jnp.zeros((n, 128), BF16)
    scale = HEAD_DIM**-0.5
    heads = [[], [], []]
    for pair in range(3):
        lanes = slice(128 * pair, 128 * pair + 128)
        qp, kp, vp, dp = q[:, lanes], k[:, lanes], v[:, lanes], dctx[:, lanes]
        dq = dk = dv = 0.0
        for e in range(2):
            mine = (lane < HEAD_DIM) if e == 0 else (lane >= HEAD_DIM)
            dh, kh, qh = jnp.where(mine, dp, zero), jnp.where(mine, kp, zero), jnp.where(mine, qp, zero)
            pr = probs[2 * pair + e]
            dv = dv + tn(pr, dh)
            pf = pr.astype(F32)
            t = pf * nt(dh, vp)
            ds = (t - pf * jnp.sum(t, -1, keepdims=True)).astype(BF16)
            dq = dq + nn(ds, kh)
            dk = dk + tn(ds, qh)
        for t, val in enumerate((dq * scale, dk * scale, dv)):
            val = val.astype(BF16)
            for e in range(2):
                hd = 2 * pair + e
                g, hh = hd // 3, hd % 3
                at = 640 * g + 192 * t + 64 * hh
                cots[:, at : at + 64] = val[:, 64 * e : 64 * e + 64]
            heads[t].append(val)
    for g in range(2):
        cots[:, 640 * g + 576 : 640 * g + 640] = jnp.zeros((n, 64), BF16)
    parts = [jnp.concatenate(heads[t], 1) for t in range(3)]
    for i, out in enumerate((in0, in1)):
        rws = slice(half * i, half * i + half)
        total = 0.0
        for t in range(3):
            total = total + nn(parts[t][rws], wr[384 * t : 384 * t + 384])
        out[...] = total
    for row, t in ((0, 0), (1, 2)):
        s = jnp.sum(parts[t].astype(F32), 0, keepdims=True)
        for g in range(2):
            sg = s[:, 192 * g : 192 * g + 192]
            sums[row : row + 1, 384 * g : 384 * g + 192] = jnp.where(c == 0, sg, 0.0)
            sums[row : row + 1, 384 * g + 192 : 384 * g + 384] = jnp.where(c == 1, sg, 0.0)
    for d in range(3):
        at = slice(256 * d, 256 * d + 256)
        full = tn(x0[:, at], cots[0:half]) + tn(x1[:, at], cots[half:n])
        pg = tn(a0[:, at], ctx[0:half]) + tn(a1[:, at], ctx[half:n])
        for g in range(2):
            grads[g, at, 0:576] = full[:, 640 * g : 640 * g + 576].astype(BF16)
            grads[g, at, 576:768] = pg[:, 192 * g : 192 * g + 192].astype(BF16)
    if sets == 1:
        copies.start(grads, outs[0])
    else:
        rows = outs[0].shape[1]
        for spot in (3, 2, 1, 0):
            g, yi = flip(x, spot % 2), flip(y, spot // 2)
            for kz in range(4):
                zi = flip(lax.rem(z, 2), kz % 2) + 2 * flip(lax.div(z, 2), kz // 2)
                at = pl.multiple_of((2 * zi + yi) * rows, rows)
                dst = outs[spot].at[kz] if spot < 3 else outs[3 + kz // 2].at[4 + kz % 2]
                copies.start(grads.at[g, pl.ds(at, rows)], dst)
    copies.wait()


def attend_back(downs, a0, a1, x0, x1, wp, wr, q, k, v, ctx, probs):
    half = a0.shape[0]
    n = 2 * half
    sets = (shape((2, D, D)),)
    if downs:
        sets = (shape((4, 96, D)),) * 3 + (shape((6, 96, D)),) * 2
    far = (wp, v, probs, k, q, wr, x0, x1, ctx)
    return call(
        functools.partial(attend_back_kernel, len(sets)),
        (*sets, shape((half, D), F32), shape((half, D), F32), shape((2, D), F32)),
        (a0, a1, *downs, *far),
        scratch=[
            pltpu.VMEM((n, 384), BF16),
            pltpu.VMEM((n, 1280), BF16),
            pltpu.VMEM((2, D, D), BF16),
        ],
        cost=est(8e9, 14e6),
        limit=16,
        far_out=range(len(sets)),
        sems=20,
    )


def local(
    inputs,
    bucket,
    lengths,
    qkv_weight,
    query_bias,
    value_bias,
    proj_weight,
    proj_bias,
    first_gain,
    first_shift,
    up_weight,
    up_bias,
    down_weight,
    down_bias,
    second_gain,
    second_shift,
    cotangent,
):
    head_count = lax.axis_size("head")
    batch_count = lax.axis_size("batch")
    devices = head_count * batch_count
    direct = batch_count == 8
    b = lax.axis_index("batch")
    h = lax.axis_index("head")
    me = b * head_count + h
    x, c = h // 2, h % 2
    z, y = b // 2, b % 2
    wq, wp, wf = 3 * D // devices, D // devices, FF // devices

    vectors = [
        query_bias,
        value_bias,
        proj_bias,
        first_gain,
        first_shift,
        down_bias,
        second_gain,
        second_shift,
    ]
    if direct:
        a_shard, one_a, one_b, two = pack(
            qkv_weight.T, proj_weight.T, up_weight.T, down_weight, up_bias, vectors
        )
    else:
        small = lax.dynamic_update_slice(
            jnp.zeros((16, D), BF16), jnp.stack(vectors), (0, me * wp)
        )
        per_row = D // wf
        small = lax.dynamic_update_slice(
            small, up_bias[None, :], (8 + me // per_row, (me % per_row) * wf)
        )
        proj_t = proj_weight.T.reshape(wp, 2, 2, 192).transpose(0, 2, 1, 3).reshape(wp, D)
        a_shard = jnp.concatenate([qkv_weight.T, proj_t, small])
    other_in = core_swap(inputs)
    k = jnp.arange(batch_count * 2)
    if direct:
        a_z = z_line(a_shard)
        two = after(two, a_z[1])
        two_x, two_y = x_swap(two), y_swap(two)
        two_d = jnp.concatenate([x_swap(two_y[:TWO]), y_swap(two_x[TWO:])])
        two_lo = jnp.stack([two, two_x, two_y, two_d])
        a_z, two_lo, other_in = lax.optimization_barrier((jnp.stack(a_z), two_lo, other_in))
        one_a = z_line(after(one_a, a_z))
        a_x, a_y = x_swap(a_z), y_swap(a_z)
        a_x, a_y, one_a, two_lo = lax.optimization_barrier((a_x, a_y, one_a, two_lo))
        one_b = after(one_b, one_a)
        near = z_swap(jnp.concatenate([one_b, two_lo.reshape(8 * TWO, D)]), 1)
        one_b = [one_b, None, z_swap(one_b, 2), z_swap(one_b, 3)]
        a_d = [x_swap(a_y[:2]), y_swap(a_x[2:])]
        near, one_b[2], one_b[3], a_d = lax.optimization_barrier((near, one_b[2], one_b[3], a_d))
        one_b[1], two_hi = near[: 2 * ONE - FIRST], near[2 * ONE - FIRST :].reshape(two_lo.shape)
        a_own = [a_z, a_x, a_y, *a_d]
        one_z = jnp.stack([jnp.concatenate(pair) for pair in zip(one_a, one_b)])
        one_z, a_own = lax.optimization_barrier((one_z, a_own))
        one_x, one_y = x_swap(one_z), y_swap(one_z)
        a_swapped = [core_swap(v) for v in a_own]
        two_far = z_swap(jnp.concatenate([two_lo, two_hi]), 2)
        one_x, one_y, two_far = lax.optimization_barrier((one_x, one_y, two_far))
        one_d = [x_swap(one_y[:2]), y_swap(one_x[2:])]
        twos = [two_lo, two_hi, two_far]
        ctx_own, ctx_other, q, kk, v, ctx, probs, wr, ub_all, proj_w, small_all = attend(
            bucket, lengths, inputs, other_in, (*a_own, *a_swapped), wq, wp
        )
        f_all = [[one_z], [one_x], [one_y], twos, one_d]
    else:
        a_all = lax.all_gather(a_shard, ("batch", "head"), axis=0)
        qkv_all = a_all[:, :wq].reshape(2, 2, 576, D)
        qkv_w = lax.dynamic_index_in_dim(qkv_all, c, 1, keepdims=False).reshape(2 * 576, D)
        proj_w = a_all[:, wq : wq + wp].reshape(D, D)
        small_all = jnp.sum(a_all[:, wq + wp :].astype(F32), 0)
        ctx_own, ctx_other, q, kk, v, ctx, probs, wr = attend(
            bucket, lengths, inputs, other_in, (qkv_w, small_all)
        )
        f_shard = jnp.concatenate([up_weight.T, down_weight])
        f_all = [
            (v[:, :wf].reshape(-1, D), v[:, wf:].reshape(-1, D)) for v in gather_any(f_shard)
        ]
        owner = (k % batch_count) * 4 + (x ^ (k // batch_count)) * 2 + c
    if not direct:
        spread = (owner[None, :] == jnp.arange(devices)[:, None]).astype(F32)
        ub_all = tn(spread, small_all[8:12].reshape(devices, wf)).reshape(1, FF // 2)

    ctx_in = core_swap(ctx_other)
    first_low, first, first_n, first_r = first_norm(inputs, ctx_own, ctx_in, proj_w, small_all)
    first_in = core_swap(first_low)
    sums = ()
    kept = []
    starts = (0, FF // 4)
    if direct:
        starts = (0, 4 * ONE, 8 * ONE, 16 * ONE, 12 * ONE)
    for weights, at in zip(f_all, starts):
        width = FF // 4
        if direct:
            width = 16 * TWO if len(kept) == 3 else 4 * ONE
        hid, slope, *sums = ffn(
            first_low,
            first_in,
            ub_all[:, at : at + width],
            weights,
            sums,
            len(kept) == len(f_all) - 1,
        )
        kept.append((hid, slope))
    down_low, sum_two, second_n = second_norm(
        bucket, lengths, first, sums[0], core_swap(sums[1]), small_all, cotangent
    )
    down_in = core_swap(down_low)

    sums = ()
    f_parts, ub_parts = [], []
    if direct:
        for spot, i in ((3, 4), (2, 2), (1, 1), (0, 0)):
            weights, both = (*f_all[i], *twos), (*kept[i], *kept[3])
            grads, ub, sums = ffn_back(
                down_low, down_in, first_low, first_in, spot, weights, both, sums, spot == 0
            )
            f_parts.append(grads)
            ub_parts.insert(0, ub)
    else:
        for weights, pair in zip(f_all, kept):
            grads, ub, sums = ffn_back(
                down_low,
                down_in,
                first_low,
                first_in,
                None,
                weights,
                pair,
                sums,
                len(f_parts) == len(f_all) - 1,
            )
            f_parts.append(grads)
            ub_parts.append(ub)
    part_own, part_other = sums
    layer_out, sums_two = second_rest(
        bucket, lengths, after(second_n, part_other), small_all, cotangent, down_low
    )
    sum_two = after(sum_two, sums_two)
    moved = ()
    if direct:
        (d_lo, d_hi), y_sets, x_sets, z_sets = f_parts
        moved = (*x_sets, y_swap(d_hi), *y_sets, x_swap(d_lo))
    added, sum_one, attn_low, sums_one = first_back(
        sum_two, part_own, core_swap(part_other), first_n, first_r, small_all, moved
    )
    attn_in = core_swap(attn_low)
    *a_grads, in_own, in_other, sums_zero = attend_back(
        added[2:],
        attn_low,
        attn_in,
        inputs,
        other_in,
        proj_w,
        wr,
        q,
        kk,
        v,
        ctx,
        probs,
    )
    in_got = core_swap(in_other)
    inputs_grad = (sum_one + in_own + in_got).astype(BF16)

    if direct:
        up_sets = scatter_xy(z_sets[0], *added[:2])
        a_zz, a_xx, a_yy, by_x, by_y = a_grads
        by_x, by_y, up_sets = lax.optimization_barrier((by_x, by_y, up_sets))
        by_x, by_y = x_swap(by_x), y_swap(by_y)
        up_mine, up_others = combine(*up_sets)
        sums_zero = after(sums_zero, up_others)
        terms = exchange_terms(sums_zero, sums_one, sums_two, ub_parts, devices)
        terms = lax.all_to_all(terms, ("batch", "head"), split_axis=0, concat_axis=0, tiled=True)
        up_others = scatter_z(up_others)
        by_x, by_y, up_others, terms, _ = lax.optimization_barrier(
            (by_x, by_y, up_others, terms, inputs_grad)
        )
        a_xy, down_mine, down_others = turn(a_xx, a_yy, z_sets[1], by_x, by_y)
        a_sets = scatter_xy(a_zz, *a_xy)
        down_others = scatter_z(down_others)
        a_sets, down_others = lax.optimization_barrier((a_sets, down_others))
        a_mine, a_others = combine_last(*a_sets)
        a_others = scatter_z(a_others)
        up_grad, down_grad = finish_ffn((up_mine, *up_others), (down_mine, *down_others))
        up_grad = up_grad.T
        terms = jnp.sum(terms.astype(F32), 0)
        packed = jnp.concatenate([terms[:, :wp].reshape(-1), terms[0, wp : wp + wf]])
        qkv_grad, proj_grad = finish_attend((a_mine, *a_others))
    else:
        vecs = jnp.concatenate([sums_zero, sums_one, sums_two])
        vecs = vecs.reshape(8, devices, wp).transpose(1, 0, 2).reshape(devices, 8 * wp)
        ubias = jnp.concatenate(ub_parts).reshape(batch_count * 2, wf)
        ubias = lax.dot_general(
            spread, ubias, (((1,), (0,)), ((), ())), precision=lax.Precision.HIGHEST
        )
        packed = jnp.concatenate([vecs, ubias], 1)
        packed = lax.all_to_all(
            packed, ("batch", "head"), split_axis=0, concat_axis=0, tiled=True
        )
        packed = jnp.sum(packed, 0)
        wb = D // batch_count
        a_grads = a_grads[0].reshape(2, batch_count, wb, D)
        a_mine = scatter_any(
            [
                lax.dynamic_index_in_dim(a_grads, x, 0, keepdims=False),
                lax.dynamic_index_in_dim(a_grads, 1 - x, 0, keepdims=False),
            ]
        )
        f_mine = scatter_any(
            [
                jnp.concatenate(
                    [ug.reshape(batch_count, wf, D), dg.reshape(batch_count, wf, D)], 1
                )
                for ug, dg in f_parts
            ]
        )
        qkv_grad = a_mine[:, :576].reshape(wb, 3, 3, HEAD_DIM).transpose(0, 2, 1, 3)
        qkv_grad = qkv_grad.reshape(wb, 576)
        proj_grad = a_mine[:, 576:].T
        up_grad, down_grad = f_mine[:wf].T, f_mine[wf:]
    qb_g, vb_g, pb_g, fg_g, fs_g, db_g, sg_g, ss_g = [
        packed[i * wp : (i + 1) * wp] for i in range(8)
    ]
    return (
        layer_out,
        inputs_grad,
        qkv_grad,
        qb_g,
        vb_g,
        proj_grad,
        pb_g,
        fg_g,
        fs_g,
        up_grad,
        packed[8 * wp :],
        down_grad,
        db_g,
        sg_g,
        ss_g,
    )


def solution(mesh):
    both = ("batch", "head")
    in_specs = (
        P(both, None),
        P("batch"),
        P("batch", None),
        P(None, both),
        P(both),
        P(both),
        P(None, both),
        P(both),
        P(both),
        P(both),
        P(None, both),
        P(both),
        P(both, None),
        P(both),
        P(both),
        P(both),
        P(both, None),
    )
    out_specs = (
        P(both, None),
        P(both, None),
        P("batch", "head"),
        P(both),
        P(both),
        P("head", "batch"),
        P(both),
        P(both),
        P(both),
        P(None, both),
        P(both),
        P(both, None),
        P(both),
        P(both),
        P(both),
    )
    return jax.shard_map(local, mesh=mesh, in_specs=in_specs, out_specs=out_specs, check_vma=False)
```

```python
import functools

import jax
import jax.numpy as jnp
from jax import lax
from jax.experimental import pallas as pl
from jax.experimental.pallas import tpu as pltpu
from jax.sharding import PartitionSpec as P

D = 768
HEADS = 12
HEAD_DIM = 64
FF = 3072
BIG = 512
SMALL = 128
UNITS = 4
NORM_EPS = 1e-12
F32 = jnp.float32
BF16 = jnp.bfloat16

ONE, TWO = 80, 16
FIRST = 104

CORE = [(i, i ^ 1) for i in range(4)]
XPAIR = [(i, i ^ 2) for i in range(4)]
YPAIR = [(i, i ^ 1) for i in range(8)]
ZPAIR = [[(i, i ^ (2 * k)) for i in range(8)] for k in range(4)]


def core_swap(v):
    return lax.ppermute(v, "head", CORE)


def x_swap(v):
    return lax.ppermute(v, "head", XPAIR)


def y_swap(v):
    return lax.ppermute(v, "batch", YPAIR)


def z_swap(v, k):
    return lax.ppermute(v, "batch", ZPAIR[k])


def after(value, other):
    return lax.optimization_barrier((value, other))[0]


def nt(a, b, out=F32):
    return lax.dot_general(a, b, (((1,), (1,)), ((), ())), preferred_element_type=F32).astype(out)


def nn(a, b, out=F32):
    return lax.dot_general(a, b, (((1,), (0,)), ((), ())), preferred_element_type=F32).astype(out)


def tn(a, b, out=F32):
    return lax.dot_general(a, b, (((0,), (0,)), ((), ())), preferred_element_type=F32).astype(out)


def z_line(shard):
    return [shard] + [z_swap(shard, k) for k in (1, 2, 3)]


def gather_four(z):
    x, y = x_swap(z), y_swap(z)
    return [z, x, y, x_swap(y[:2]), y_swap(x[2:])]


def gather_any(shard):
    whole = lax.all_gather(shard, "batch", axis=0)
    return [whole, x_swap(whole)]


def scatter_xy(z, x, y):
    return z, x_swap(x), y_swap(y)


def scatter_z(others):
    return [z_swap(others[k - 1], k) for k in (1, 2, 3)]


def scatter_any(parts):
    total = parts[0].astype(F32) + x_swap(parts[1]).astype(F32)
    return lax.psum_scatter(total, "batch", scatter_dimension=0, tiled=False)


def est(flops, moved, trans=0):
    return pl.CostEstimate(flops=int(flops), bytes_accessed=int(moved), transcendentals=int(trans))


def call(kernel, out_shape, operands, scratch=(), cost=None, limit=16, far_in=(), far_out=(), sems=0):
    vmem = pl.BlockSpec(memory_space=pltpu.VMEM)
    hbm = pl.BlockSpec(memory_space=pltpu.HBM)
    smem = pl.BlockSpec(memory_space=pltpu.SMEM)
    ins = [hbm if i in far_in else vmem for i in range(len(operands))]
    ins = [smem if v.dtype == jnp.int32 else spec for spec, v in zip(ins, operands)]
    outs = [hbm if i in far_out else vmem for i in range(len(out_shape))]
    scratch = list(scratch) + ([pltpu.SemaphoreType.DMA((sems,))] if sems else [])
    operands = [
        pltpu.with_memory_space_constraint(v, pltpu.HBM) if i in far_in else v
        for i, v in enumerate(operands)
    ]
    out_shape = [
        pltpu.HBM(v.shape, v.dtype) if i in far_out else v for i, v in enumerate(out_shape)
    ]
    return pl.pallas_call(
        kernel,
        out_shape=out_shape,
        in_specs=ins,
        out_specs=outs,
        scratch_shapes=scratch,
        compiler_params=pltpu.CompilerParams(vmem_limit_bytes=limit << 20),
        cost_estimate=cost,
    )(*operands)


class Copies:
    def __init__(self, sems):
        self.sems, self.used, self.open = sems, 0, []

    def start(self, src, dst):
        copy = pltpu.make_async_copy(src, dst, self.sems.at[self.used])
        self.used += 1
        copy.start()
        self.open.append(copy)
        return copy

    def wait(self, *copies):
        for copy in copies or list(self.open):
            copy.wait()
            self.open.remove(copy)


def add_low(a, b):
    return (a.astype(F32) + b.astype(F32)).astype(BF16)


def shape(dims, dtype=BF16):
    return jax.ShapeDtypeStruct(dims, dtype)


def add_first_kernel(x_up, x_down, for_x, y_up, y_down, for_y, *outs):
    half = x_up.shape[1]
    for i, (x, y) in enumerate(((x_up, y_up), (x_down, y_down))):
        rows = slice(half * i, half * i + half)
        x_out, y_out = outs[2 * i : 2 * i + 2]
        x_out[0:2] = x[0:2]
        y_out[2:4] = y[2:4]
        for k in range(2):
            x_out[2 + k] = add_low(x[2 + k], for_x[k, rows])
            y_out[k] = add_low(y[k], for_y[k, rows])


def combine_kernel(z, x, y, *refs):
    outs, (mine, low, sems) = refs[:4], refs[4:]
    sum_places(z, x, y, outs, mine, low, Copies(sems)).wait()


def sum_places(z, x, y, outs, mine, low, copies, arrived=None):
    for i, k in enumerate((1, 2, 3, 0)):
        if arrived:
            copies.wait(*arrived[i])
        total = z[k].astype(F32) + x[k].astype(F32) + y[k].astype(F32)
        if k == 0:
            mine[...] = total
            copies.start(mine, outs[0])
        else:
            low[k - 1] = total.astype(BF16)
            copies.start(low.at[k - 1], outs[k])
    return copies


def combine(z, x, y):
    rows = z.shape[1]
    mine, *others = call(
        combine_kernel,
        (shape((rows, D), F32),) + (shape((rows, D)),) * 3,
        (z, x, y),
        scratch=[pltpu.VMEM((rows, D), F32), pltpu.VMEM((3, rows, D), BF16)],
        cost=est(1000, 1000),
        limit=8,
        far_out=range(4),
        sems=4,
    )
    return mine, others


def combine_last_kernel(z, x, y, mine, *refs):
    outs, (low, sems) = refs[:3], refs[3:]
    copies = Copies(sems)
    for k in (1, 2, 3, 0):
        total = z[k].astype(F32) + x[k].astype(F32) + y[k].astype(F32)
        if k == 0:
            mine[...] = total
        else:
            low[k - 1] = total.astype(BF16)
            copies.start(low.at[k - 1], outs[k - 1])
    copies.wait()


def combine_last(z, x, y):
    rows = z.shape[1]
    mine, *others = call(
        combine_last_kernel,
        (shape((rows, D), F32),) + (shape((rows, D)),) * 3,
        (z, x, y),
        scratch=[pltpu.VMEM((3, rows, D), BF16)],
        cost=est(1000, 1000),
        limit=8,
        far_out=range(1, 4),
        sems=3,
    )
    return mine, others


def turn_kernel(x, y, z, by_x_far, by_y_far, x_out, y_out, *refs):
    outs, (by_x, by_y, mine, low, sems) = refs[:4], refs[4:]
    copies = Copies(sems)
    arrived = []
    for k in (1, 2, 3, 0, 4):
        rows = pl.ds(k, 1 if k < 4 else 2)
        arrived.append(
            (
                copies.start(by_x_far.at[rows], by_x.at[rows]),
                copies.start(by_y_far.at[rows], by_y.at[rows]),
            )
        )
    sum_places(z, by_x, by_y, outs, mine, low, copies, arrived)
    copies.wait(*arrived[4])
    y_out[0:2] = add_low(y[0:2], by_x[4:6])
    y_out[2:4] = y[2:4]
    x_out[0:2] = x[0:2]
    x_out[2:4] = add_low(x[2:4], by_y[4:6])
    copies.wait()


def turn(x, y, z, by_x, by_y):
    rows = z.shape[1]
    x, y, mine, *others = call(
        turn_kernel,
        (shape(x.shape), shape(y.shape), shape((rows, D), F32)) + (shape((rows, D)),) * 3,
        (x, y, z, by_x, by_y),
        scratch=[pltpu.VMEM(by_x.shape, BF16)] * 2
        + [pltpu.VMEM((rows, D), F32), pltpu.VMEM((3, rows, D), BF16)],
        cost=est(1000, 1000),
        limit=8,
        far_in=(3, 4),
        far_out=range(2, 6),
        sems=14,
    )
    return (x, y), mine, others


def total_of(refs):
    return refs[0][...] + refs[1][...].astype(F32) + refs[2][...].astype(F32) + refs[3][...].astype(F32)


def finish_attend_kernel(mine, one, two, three, qkv, proj):
    total = total_of((mine, one, two, three))
    for hh in range(3):
        for t in range(3):
            at, to = 192 * t + 64 * hh, 192 * hh + 64 * t
            qkv[:, to : to + 64] = total[:, at : at + 64]
    proj[...] = total[:, 576:].T


def finish_attend(parts):
    rows = parts[0].shape[0]
    return call(
        finish_attend_kernel,
        (shape((rows, 576), F32), shape((192, rows), F32)),
        tuple(parts),
        cost=est(8 * rows * D, 16 * rows * D),
        limit=8,
    )


def finish_ffn_kernel(*refs):
    up, down = refs[8:]
    up[...], down[...] = total_of(refs[0:4]), total_of(refs[4:8])


def finish_ffn(ups, downs):
    dims = ups[0].shape
    return call(
        finish_ffn_kernel,
        (shape(dims, F32), shape(dims, F32)),
        (*ups, *downs),
        cost=est(1000, 1000),
        limit=8,
    )


def exchange_kernel(zero, one, two, *refs):
    ubs, out = refs[:4], refs[4]
    vecs = jnp.concatenate([zero[...], one[...], two[...]])
    width = D // out.shape[0]
    vecs = vecs.astype(BF16)
    out[...] = jnp.zeros(out.shape, BF16)
    for i in range(out.shape[0]):
        out[i, 0:8, 0:width] = vecs[:, width * i : width * i + width]
    for spot in range(4):
        for kz in range(4):
            to, ub = slot_of(spot, kz), ubs[spot][...].astype(BF16)
            out[to, 0:1, 24 : 24 + ONE] = ub[:, ONE * kz : ONE * kz + ONE]
            at = 4 * ONE + TWO * kz
            out[to, 0:1, 24 + ONE : 24 + ONE + TWO] = ub[:, at : at + TWO]


def exchange_terms(zero, one, two, ubs, devices):
    return call(
        exchange_kernel,
        (shape((devices, 8, 128)),),
        (zero, one, two, *ubs),
        cost=est(1000, 1000),
        limit=8,
    )[0]


def flip(a, bit):
    return a + bit - 2 * a * bit


def pack_kernel(qkv_in, proj_in, up_in, down_in, bias_in, *refs):
    vectors_in, (a_out, one_a, one_b, two, a, p, f, bias, vectors, sems) = refs[:8], refs[8:]
    rows_q, rows_p, half = qkv_in.shape[0], proj_in.shape[0], down_in.shape[0]
    copies = Copies(sems)
    copies.start(qkv_in, a.at[pl.ds(0, rows_q)])
    copies.start(proj_in, p)
    copies.start(up_in, f.at[pl.ds(0, half)])
    copies.start(down_in, f.at[pl.ds(half, half)])
    copies.start(bias_in, bias)
    for i, r in enumerate(vectors_in):
        copies.start(r, vectors.at[i])
    width = vectors.shape[2]
    b, h = lax.axis_index("batch"), lax.axis_index("head")
    me = b * lax.axis_size("head") + h
    copies.wait()
    v = jnp.concatenate([vectors[i] for i in range(8)]).astype(F32)
    v = jnp.concatenate([v] * (D // width), 1)
    lane = lax.broadcasted_iota(jnp.int32, (8, D), 1)
    mine = jnp.logical_and(lane >= me * width, lane < me * width + width)
    v = jnp.where(mine, v, 0.0)
    gap = jnp.zeros((1, D // 2 - half), F32)
    none = jnp.zeros((1, D // 2), F32)
    row = bias[...].astype(F32)
    early = jnp.concatenate([none, row, gap], 1)
    late = jnp.concatenate([row, gap, none], 1)
    extra = jnp.where(me < lax.axis_size("batch") * lax.axis_size("head") // 2, early, late)
    v = v + jnp.concatenate([extra, jnp.zeros((7, D), F32)])
    a_out[0:rows_q] = a[0:rows_q]
    q = p[...]
    a_out[rows_q : rows_q + rows_p] = jnp.concatenate(
        [q[:, 192 * i : 192 * i + 192] for i in (0, 2, 1, 3)], 1
    )
    a_out[rows_q + rows_p :] = v.astype(BF16)
    one = jnp.concatenate([f[0:ONE], f[half : half + ONE]])
    one_a[...], one_b[...] = one[0:FIRST], one[FIRST:]
    two[0:TWO], two[TWO:] = f[ONE:half], f[half + ONE :]


def pack(qkv, proj, up, down, bias, vectors):
    rows, half = qkv.shape[0] + proj.shape[0] + 8, down.shape[0]
    return call(
        pack_kernel,
        (
            shape((rows, D)),
            shape((FIRST, D)),
            shape((2 * ONE - FIRST, D)),
            shape((2 * TWO, D)),
        ),
        (qkv, proj, up, down, bias[None], *[v[None] for v in vectors]),
        scratch=[
            pltpu.VMEM((rows, D), BF16),
            pltpu.VMEM(proj.shape, BF16),
            pltpu.VMEM((2 * half, D), BF16),
            pltpu.VMEM((1,) + bias.shape, BF16),
            pltpu.VMEM((8, 1) + vectors[0].shape, BF16),
        ],
        cost=est(1000, 1000),
        limit=8,
        far_in=range(13),
        sems=13,
    )


def place_here():
    b, h = lax.axis_index("batch"), lax.axis_index("head")
    return lax.rem(h, 2), lax.div(b, 2), lax.rem(b, 2), lax.div(h, 2)


def live_units(bucket, lengths):
    x = place_here()[3]
    kind, first = bucket[x], lengths[x, 0]
    units = []
    for u in range(UNITS):
        far = jnp.clip(first - SMALL * u, 0, SMALL)
        units.append(jnp.where(kind == 1, far, lengths[x, u]))
    return kind, units


def place_of(index, c):
    return jnp.bitwise_xor(index, c * (BIG // 2))


def live_of(place, units):
    unit = lax.shift_right_logical(place, 7)
    inner = jnp.bitwise_and(place, SMALL - 1)
    count = jnp.where(
        unit < 2, jnp.where(unit == 0, units[0], units[1]), jnp.where(unit == 2, units[2], units[3])
    )
    return inner < count


def heads_of(row, c):
    parts = []
    for g in range(2):
        lo = row[:, 384 * g : 384 * g + 192]
        hi = row[:, 384 * g + 192 : 384 * g + 384]
        parts.append(jnp.where(c == 0, lo, hi))
    return jnp.concatenate(parts, 1)


def fetch_shards(copies, sources, slots):
    c, z, y, x = place_here()
    zl, zh = lax.rem(z, 2), lax.div(z, 2)
    for swapped in range(2):
        cc = c if swapped == 0 else 1 - c
        zs, xs, ys, xa, xb = sources[5 * swapped : 5 * swapped + 5]
        for kx, ky, pair in ((0, 0, (zs,)), (1, 0, (xs,)), (0, 1, (ys,)), (1, 1, (xa, xb))):
            j = flip(y, ky) * 4 + flip(x, kx) * 2 + cc
            for kz in range(4):
                src = pair[0].at[kz] if len(pair) == 1 else pair[kz // 2].at[kz % 2]
                zi = flip(zl, kz % 2) + 2 * flip(zh, kz // 2)
                copies.start(src, slots.at[zi * 8 + j])


def slot_of(spot, kz):
    c, z, y, x = place_here()
    zi = flip(lax.rem(z, 2), kz % 2) + 2 * flip(lax.div(z, 2), kz // 2)
    return zi * 8 + flip(y, spot // 2) * 4 + flip(x, spot % 2) * 2 + c


def bias_order(slots, row, out):
    for spot in range(4):
        for kz in range(4):
            i = slot_of(spot, kz)
            b = slots[i, row : row + 1].astype(F32)
            b = jnp.where(i < 16, b[:, D // 2 : D // 2 + 96], b[:, 0:96])
            at = 4 * ONE * spot + ONE * kz
            out[:, at : at + ONE] = b[:, 0:ONE]
            at = 16 * ONE + 4 * TWO * spot + TWO * kz
            out[:, at : at + TWO] = b[:, ONE:]


def attend_kernel(rows_q, rows_p, bucket, lengths, x0, x1, *refs):
    sources = 10 if rows_q else 2
    weights, refs = refs[:sources], refs[sources:]
    (ctx0, ctx1, q, k, v, ctx, probs, wr), refs = refs[:8], refs[8:]
    if rows_q:
        (ub_out, wp, small, mask, xs, slots, sems) = refs
    else:
        (mask, xs, w, small, sems) = refs
    copies = Copies(sems)
    c = place_here()[0]
    kind, units = live_units(bucket, lengths)
    half = x0.shape[0]
    copies.start(x0, xs.at[0:half])
    copies.start(x1, xs.at[half : 2 * half])
    if rows_q:
        fetch_shards(copies, weights, slots)
    else:
        copies.start(weights[0], w)
        copies.start(weights[1], small)
    rows = lax.broadcasted_iota(jnp.int32, (BIG, BIG), 0)
    cols = lax.broadcasted_iota(jnp.int32, (BIG, BIG), 1)
    prow, pcol = place_of(rows, c), place_of(cols, c)
    same = jnp.logical_or(
        kind == 1, lax.shift_right_logical(prow, 7) == lax.shift_right_logical(pcol, 7)
    )
    mask[...] = jnp.where(jnp.logical_and(same, live_of(pcol, units)), 0.0, -1e30)
    copies.wait()
    if rows_q:
        for g in range(2):
            cuts = jnp.concatenate([slots[16 * g + 8 * c + j, 0:rows_q] for j in range(8)])
            for t in range(3):
                for hh in range(3):
                    src, dst = (hh * 3 + t) * HEAD_DIM, (t * 6 + g * 3 + hh) * HEAD_DIM
                    wr[dst : dst + HEAD_DIM] = cuts[src : src + HEAD_DIM]
        lane = lax.broadcasted_iota(jnp.int32, (8, D), 1)
        small[...] = sum(
            jnp.where(
                jnp.logical_and(lane >= rows_p * i, lane < rows_p * i + rows_p),
                slots[i, rows_q + rows_p :].astype(F32),
                0.0,
            )
            for i in range(32)
        )
    else:
        for t in range(3):
            for hd in range(6):
                src = ((hd // 3) * 9 + (hd % 3) * 3 + t) * HEAD_DIM
                dst = (t * 6 + hd) * HEAD_DIM
                wr[dst : dst + HEAD_DIM] = w[src : src + HEAD_DIM]
    biases = (heads_of(small[0:1], c), None, heads_of(small[1:2], c))
    for t, ref in enumerate((q, k, v)):
        val = nt(xs[...], wr[384 * t : 384 * t + 384])
        if biases[t] is not None:
            val = val + biases[t]
        ref[...] = val.astype(BF16)
    if rows_q:
        for i in range(32):
            wp[rows_p * i : rows_p * i + rows_p] = slots[i, rows_q : rows_q + rows_p]
        bias_order(slots, rows_q + rows_p, ub_out)
    lane = lax.broadcasted_iota(jnp.int32, (half, 128), 1)
    for pair in range(3):
        lanes = slice(128 * pair, 128 * pair + 128)
        kp, vp = k[:, lanes], v[:, lanes]
        for i, near in enumerate((ctx0, ctx1)):
            rws = slice(half * i, half * i + half)
            qp = q[rws, lanes] * jnp.asarray(HEAD_DIM**-0.5, BF16)
            outs = []
            for e in range(2):
                mine = (lane < HEAD_DIM) if e == 0 else (lane >= HEAD_DIM)
                s = nt(jnp.where(mine, qp, jnp.zeros_like(qp)), kp) + mask[rws]
                ex = jnp.exp(s - jnp.max(s, -1, keepdims=True))
                pr = (ex * (1.0 / jnp.sum(ex, -1, keepdims=True))).astype(BF16)
                probs[2 * pair + e, rws] = pr
                outs.append(nn(pr, vp))
            val = jnp.where(lane < HEAD_DIM, outs[0], outs[1]).astype(BF16)
            ctx[rws, lanes] = val
            near[:, lanes] = val


def attend(bucket, lengths, x0, x1, weights, rows_q=0, rows_p=0, rows_s=16):
    rows_s = 8 if rows_q else rows_s
    half = x0.shape[0]
    n = 2 * half
    direct = rows_q > 0
    outs = [
        shape((half, 384)),
        shape((half, 384)),
        shape((n, 384)),
        shape((n, 384)),
        shape((n, 384)),
        shape((n, 384)),
        shape((6, n, n)),
        shape((1152, D)),
    ]
    scratch = [pltpu.VMEM((n, n), F32), pltpu.VMEM((n, D), BF16)]
    if direct:
        outs += [shape((1, FF // 2), F32), shape((D, D)), shape((rows_s, D), F32)]
        scratch += [pltpu.VMEM((32, rows_q + rows_p + rows_s, D), BF16)]
    else:
        scratch += [pltpu.VMEM((1152, D), BF16), pltpu.VMEM((rows_s, D), F32)]
    operands = (bucket, lengths, x0, x1, *weights)
    return call(
        functools.partial(attend_kernel, rows_q, rows_p),
        outs,
        operands,
        scratch=scratch,
        cost=est(1000, 1000),
        limit=32,
        far_in=range(2, len(operands)),
        sems=50,
    )


def norm(values):
    center = values - jnp.mean(values, -1, keepdims=True)
    spread = jnp.mean(center * center, -1, keepdims=True)
    scale = lax.rsqrt(spread + NORM_EPS)
    return center * scale, scale


def norm_back(cot, normal, scale, gain):
    w = cot * gain
    return scale * (
        w - jnp.mean(w, -1, keepdims=True) - normal * jnp.mean(w * normal, -1, keepdims=True)
    )


def first_kernel(x, ctx_own, ctx_in, wp, small, low, first, normal, scale):
    c = place_here()[0]
    mine = pl.multiple_of(c * 384, 128)
    theirs = pl.multiple_of((1 - c) * 384, 128)
    attn = nt(ctx_own[...], wp[:, pl.ds(mine, 384)]) + nt(ctx_in[...], wp[:, pl.ds(theirs, 384)])
    n, r = norm(x[...].astype(F32) + attn + small[2:3])
    normal[...] = n
    out = n * small[3:4] + small[4:5]
    first[...] = out
    low[...] = out.astype(BF16)
    scale[...] = jnp.broadcast_to(r, scale.shape)


def first_norm(x, ctx_own, ctx_in, wp, small):
    n = x.shape[0]
    return call(
        first_kernel,
        (shape((n, D)), shape((n, D), F32), shape((n, D), F32), shape((n, 128), F32)),
        (x, ctx_own, ctx_in, wp, small),
        cost=est(1000, 1000),
        limit=8,
    )


def ffn_weights(refs):
    if len(refs[0].shape) == 2:
        return refs[0][...], refs[1][...]
    return stacked(ones_of(refs) if refs[0].shape[1] == 2 * ONE else twos_of(refs, range(4)))


def ones_of(refs):
    return [(r, i) for r in refs for i in range(r.shape[0])]


def twos_of(refs, spots):
    along_z = [(r, i) for r in refs for i in range(0, r.shape[0], 4)]
    return [(r, i + spot) for spot in spots for r, i in along_z]


def stacked(blocks):
    up = jnp.concatenate([r[i, 0 : r.shape[1] // 2] for r, i in blocks])
    down = jnp.concatenate([r[i, r.shape[1] // 2 :] for r, i in blocks])
    return up, down


def ffn_kernel(first, count, x0, x1, ub, *refs):
    far, refs = refs[:count], refs[count:]
    if first:
        in0 = in1 = None
    else:
        (in0, in1), refs = refs[:2], refs[2:]
    hid, slope, out0, out1 = refs
    half = x0.shape[0]
    uw, dw = ffn_weights(far)
    for i, (xr, before, out) in enumerate(((x0, in0, out0), (x1, in1, out1))):
        rws = slice(half * i, half * i + half)
        up = nt(xr[...], uw) + ub[...]
        phi = 0.5 + 0.5 * lax.erf(up * (2.0**-0.5))
        hd = (up * phi).astype(BF16)
        hid[rws] = hd
        slope[rws] = (phi + up * jnp.exp(-0.5 * up * up) * 0.3989422804014327).astype(BF16)
        part = nn(hd, dw)
        part = part if before is None else before[...] + part
        out[...] = part.astype(out.dtype)


def ffn(x0, x1, ub, weights, sums, last):
    half, width, count = x0.shape[0], ub.shape[1], len(weights)
    n = 2 * half
    return call(
        functools.partial(ffn_kernel, not sums, count),
        (
            shape((n, width)),
            shape((n, width)),
            shape((half, D), F32),
            shape((half, D), BF16 if last else F32),
        ),
        (x0, x1, ub, *weights, *sums),
        cost=est(4 * n * D * width, 4 * D * width + 5e6, 2 * n * width),
    )


def second_kernel(bucket, lengths, first, part, got, small, cot, low, sum_two, normal):
    c = place_here()[0]
    _, units = live_units(bucket, lengths)
    n, r = norm(first[...] + (part[...] + got[...].astype(F32) + small[5:6]))
    index = lax.broadcasted_iota(jnp.int32, (first.shape[0], 1), 0)
    live = live_of(place_of(index, c), units)
    oc = jnp.where(live, cot[...].astype(F32), 0.0)
    st = norm_back(oc, n, r, small[6:7])
    low[...] = st.astype(BF16)
    sum_two[...] = st
    normal[...] = n


def second_norm(bucket, lengths, first, part, got, small, cot):
    n = first.shape[0]
    return call(
        second_kernel,
        (shape((n, D)), shape((n, D), F32), shape((n, D), F32)),
        (bucket, lengths, first, part, got, small, cot),
        cost=est(1000, 1000),
        limit=8,
    )


def second_rest_kernel(bucket, lengths, normal, small, cot, low, out, sums):
    c = place_here()[0]
    _, units = live_units(bucket, lengths)
    n = normal[...]
    out[...] = (n * small[6:7] + small[7:8]).astype(BF16)
    index = lax.broadcasted_iota(jnp.int32, (normal.shape[0], 1), 0)
    live = live_of(place_of(index, c), units)
    oc = jnp.where(live, cot[...].astype(F32), 0.0)
    sums[0:1] = jnp.sum(low[...].astype(F32), 0, keepdims=True)
    sums[1:2] = jnp.sum(oc * n, 0, keepdims=True)
    sums[2:3] = jnp.sum(oc, 0, keepdims=True)


def second_rest(bucket, lengths, normal, small, cot, low):
    n = normal.shape[0]
    return call(
        second_rest_kernel,
        (shape((n, D)), shape((3, D), F32)),
        (bucket, lengths, normal, small, cot, low),
        cost=est(1000, 1000),
        limit=8,
    )


def ffn_back_kernel(first, spot, count, d0, d1, x0, x1, *refs):
    weights, refs = refs[:count], refs[count:]
    if spot is None:
        hid, slope = refs[0], refs[1]
        refs = refs[2:]
        uw, dw = ffn_weights(weights)
    else:
        (hid1, slope1, hid2, slope2), refs = refs[:4], refs[4:]
        tail = slice(4 * TWO * spot, 4 * TWO * spot + 4 * TWO)
        hid = jnp.concatenate([hid1[...], hid2[:, tail]], 1)
        slope = jnp.concatenate([slope1[...], slope2[:, tail]], 1)
        uw, dw = stacked(ones_of(weights[:-3]) + twos_of(weights[-3:], [spot]))
    if first:
        in0 = in1 = None
    else:
        (in0, in1), refs = refs[:2], refs[2:]
    *outs, ub, out0, out1 = refs
    half = x0.shape[0]
    cots = []
    for i, (d, before, out) in enumerate(((d0, in0, out0), (d1, in1, out1))):
        rws = slice(half * i, half * i + half)
        uc = (nt(d[...], dw) * slope[rws].astype(F32)).astype(BF16)
        cots.append(uc)
        part = nn(uc, uw)
        part = part if before is None else before[...] + part
        out[...] = part.astype(out.dtype)
    ub[...] = jnp.sum(cots[0].astype(F32), 0, keepdims=True) + jnp.sum(
        cots[1].astype(F32), 0, keepdims=True
    )
    dg = (tn(hid[0:half], d0[...]) + tn(hid[half : 2 * half], d1[...])).astype(BF16)
    ug = (tn(cots[0], x0[...]) + tn(cots[1], x1[...])).astype(BF16)
    if spot is None:
        outs[0][...], outs[1][...] = ug, dg
        return
    rows = ONE + TWO
    for k in range(4):
        for e, g in enumerate((ug, dg)):
            out, i, at = (outs[k // 2], k % 2, rows * e) if spot == 3 else (outs[e], k, 0)
            out[i, at : at + ONE] = g[ONE * k : ONE * k + ONE]
            low = 4 * ONE + TWO * k
            out[i, at + ONE : at + rows] = g[low : low + TWO]


def ffn_back(d0, d1, x0, x1, spot, weights, kept, sums, last):
    half, count = x0.shape[0], len(weights)
    if spot is None:
        outs, width = [shape(w.shape) for w in weights], weights[0].shape[0]
    else:
        width = 4 * (ONE + TWO)
        rows = ONE + TWO
        outs = [shape((2, 2 * rows, D)) if spot == 3 else shape((4, rows, D))] * 2
    *grads, ub, s0, s1 = call(
        functools.partial(ffn_back_kernel, not sums, spot, count),
        (
            *outs,
            shape((1, width), F32),
            shape((half, D), F32),
            shape((half, D), BF16 if last else F32),
        ),
        (d0, d1, x0, x1, *weights, *kept, *sums),
        cost=est(1000, 1000),
    )
    return grads, ub, (s0, s1)


def first_back_kernel(
    sum_two, part, got, normal, scale, small, *refs
):
    *refs, sum_one, low, sums = refs
    fc = sum_two[...] + part[...] + got[...].astype(F32)
    n = normal[...]
    so = norm_back(fc, n, scale[:, 0:1], small[3:4])
    sum_one[...] = so
    lo = so.astype(BF16)
    low[...] = lo
    sums[0:1] = jnp.sum(lo.astype(F32), 0, keepdims=True)
    sums[1:2] = jnp.sum(fc * n, 0, keepdims=True)
    sums[2:3] = jnp.sum(fc, 0, keepdims=True)
    if refs:
        add_first_kernel(*refs)


def first_back(sum_two, part, got, normal, scale, small, moved=()):
    n = sum_two.shape[0]
    outs = [shape(moved[i].shape) for i in (0, 3, 1, 4)] if moved else []
    *added, sum_one, low, sums = call(
        first_back_kernel,
        (*outs, shape((n, D), F32), shape((n, D)), shape((3, D), F32)),
        (sum_two, part, got, normal, scale, small, *moved),
        cost=est(1000, 1000),
        limit=8,
    )
    return added, sum_one, low, sums


def attend_back_kernel(sets, a0, a1, *refs):
    downs, refs = ((), refs) if sets == 1 else (refs[:2], refs[2:])
    far, outs, (in0, in1, sums), refs = refs[:9], refs[9 : 9 + sets], refs[9 + sets : 12 + sets], refs[12 + sets :]
    wp, v, probs, k, q, wr, x0, x1, ctx = far
    dctx, cots, grads, sems = refs
    copies = Copies(sems)
    for down, out in zip(downs, outs[3:]):
        copies.start(down, out.at[pl.ds(0, 4)])
    c, z, y, x = place_here()
    half = a0.shape[0]
    n = 2 * half
    wpo = wp[:, pl.ds(pl.multiple_of(c * 384, 128), 384)]
    dctx[0:half] = nn(a0[...], wpo).astype(BF16)
    dctx[half:n] = nn(a1[...], wpo).astype(BF16)
    lane = lax.broadcasted_iota(jnp.int32, (n, 128), 1)
    zero = jnp.zeros((n, 128), BF16)
    scale = HEAD_DIM**-0.5
    heads = [[], [], []]
    for pair in range(3):
        lanes = slice(128 * pair, 128 * pair + 128)
        qp, kp, vp, dp = q[:, lanes], k[:, lanes], v[:, lanes], dctx[:, lanes]
        dq = dk = dv = 0.0
        for e in range(2):
            mine = (lane < HEAD_DIM) if e == 0 else (lane >= HEAD_DIM)
            dh, kh, qh = jnp.where(mine, dp, zero), jnp.where(mine, kp, zero), jnp.where(mine, qp, zero)
            pr = probs[2 * pair + e]
            dv = dv + tn(pr, dh)
            pf = pr.astype(F32)
            t = pf * nt(dh, vp)
            ds = (t - pf * jnp.sum(t, -1, keepdims=True)).astype(BF16)
            dq = dq + nn(ds, kh)
            dk = dk + tn(ds, qh)
        for t, val in enumerate((dq * scale, dk * scale, dv)):
            val = val.astype(BF16)
            for e in range(2):
                hd = 2 * pair + e
                g, hh = hd // 3, hd % 3
                at = 640 * g + 192 * t + 64 * hh
                cots[:, at : at + 64] = val[:, 64 * e : 64 * e + 64]
            heads[t].append(val)
    for g in range(2):
        cots[:, 640 * g + 576 : 640 * g + 640] = jnp.zeros((n, 64), BF16)
    parts = [jnp.concatenate(heads[t], 1) for t in range(3)]
    for i, out in enumerate((in0, in1)):
        rws = slice(half * i, half * i + half)
        total = 0.0
        for t in range(3):
            total = total + nn(parts[t][rws], wr[384 * t : 384 * t + 384])
        out[...] = total.astype(out.dtype)
    for row, t in ((0, 0), (1, 2)):
        s = jnp.sum(parts[t].astype(F32), 0, keepdims=True)
        for g in range(2):
            sg = s[:, 192 * g : 192 * g + 192]
            sums[row : row + 1, 384 * g : 384 * g + 192] = jnp.where(c == 0, sg, 0.0)
            sums[row : row + 1, 384 * g + 192 : 384 * g + 384] = jnp.where(c == 1, sg, 0.0)
    for d in range(3):
        at = slice(256 * d, 256 * d + 256)
        full = tn(x0[:, at], cots[0:half]) + tn(x1[:, at], cots[half:n])
        pg = tn(a0[:, at], ctx[0:half]) + tn(a1[:, at], ctx[half:n])
        for g in range(2):
            grads[g, at, 0:576] = full[:, 640 * g : 640 * g + 576].astype(BF16)
            grads[g, at, 576:768] = pg[:, 192 * g : 192 * g + 192].astype(BF16)
    if sets == 1:
        copies.start(grads, outs[0])
    else:
        rows = outs[0].shape[1]
        for spot in (3, 2, 1, 0):
            g, yi = flip(x, spot % 2), flip(y, spot // 2)
            for kz in range(4):
                zi = flip(lax.rem(z, 2), kz % 2) + 2 * flip(lax.div(z, 2), kz // 2)
                at = pl.multiple_of((2 * zi + yi) * rows, rows)
                dst = outs[spot].at[kz] if spot < 3 else outs[3 + kz // 2].at[4 + kz % 2]
                copies.start(grads.at[g, pl.ds(at, rows)], dst)
    copies.wait()


def attend_back(downs, a0, a1, x0, x1, wp, wr, q, k, v, ctx, probs):
    half = a0.shape[0]
    n = 2 * half
    sets = (shape((2, D, D)),)
    if downs:
        sets = (shape((4, 96, D)),) * 3 + (shape((6, 96, D)),) * 2
    far = (wp, v, probs, k, q, wr, x0, x1, ctx)
    return call(
        functools.partial(attend_back_kernel, len(sets)),
        (*sets, shape((half, D), F32), shape((half, D)), shape((2, D), F32)),
        (a0, a1, *downs, *far),
        scratch=[
            pltpu.VMEM((n, 384), BF16),
            pltpu.VMEM((n, 1280), BF16),
            pltpu.VMEM((2, D, D), BF16),
        ],
        cost=est(8e9, 14e6),
        limit=16,
        far_out=range(len(sets)),
        sems=20,
    )


def local(
    inputs,
    bucket,
    lengths,
    qkv_weight,
    query_bias,
    value_bias,
    proj_weight,
    proj_bias,
    first_gain,
    first_shift,
    up_weight,
    up_bias,
    down_weight,
    down_bias,
    second_gain,
    second_shift,
    cotangent,
):
    head_count = lax.axis_size("head")
    batch_count = lax.axis_size("batch")
    devices = head_count * batch_count
    direct = batch_count == 8
    b = lax.axis_index("batch")
    h = lax.axis_index("head")
    me = b * head_count + h
    x, c = h // 2, h % 2
    z, y = b // 2, b % 2
    wq, wp, wf = 3 * D // devices, D // devices, FF // devices

    vectors = [
        query_bias,
        value_bias,
        proj_bias,
        first_gain,
        first_shift,
        down_bias,
        second_gain,
        second_shift,
    ]
    if direct:
        a_shard, one_a, one_b, two = pack(
            qkv_weight.T, proj_weight.T, up_weight.T, down_weight, up_bias, vectors
        )
    else:
        small = lax.dynamic_update_slice(
            jnp.zeros((16, D), BF16), jnp.stack(vectors), (0, me * wp)
        )
        per_row = D // wf
        small = lax.dynamic_update_slice(
            small, up_bias[None, :], (8 + me // per_row, (me % per_row) * wf)
        )
        proj_t = proj_weight.T.reshape(wp, 2, 2, 192).transpose(0, 2, 1, 3).reshape(wp, D)
        a_shard = jnp.concatenate([qkv_weight.T, proj_t, small])
    other_in = core_swap(inputs)
    k = jnp.arange(batch_count * 2)
    if direct:
        a_z = z_line(a_shard)
        two = after(two, a_z[1])
        two_x, two_y = x_swap(two), y_swap(two)
        two_d = jnp.concatenate([x_swap(two_y[:TWO]), y_swap(two_x[TWO:])])
        two_lo = jnp.stack([two, two_x, two_y, two_d])
        a_z, two_lo, other_in = lax.optimization_barrier((jnp.stack(a_z), two_lo, other_in))
        one_a = after(one_a, a_z)
        near = z_swap(jnp.concatenate([one_a, two_lo.reshape(8 * TWO, D)]), 1)
        one_a = [one_a, None, z_swap(one_a, 2), z_swap(one_a, 3)]
        a_x, a_y = x_swap(a_z), y_swap(a_z)
        a_x, a_y, near, one_a[2], one_a[3] = lax.optimization_barrier(
            (a_x, a_y, near, one_a[2], one_a[3])
        )
        one_a[1], two_hi = near[:FIRST], near[FIRST:].reshape(two_lo.shape)
        one_b = z_line(after(one_b, near))
        a_d = [x_swap(a_y[:2]), y_swap(a_x[2:])]
        one_b, a_d = lax.optimization_barrier((one_b, a_d))
        a_own = [a_z, a_x, a_y, *a_d]
        one_z = jnp.stack([jnp.concatenate(pair) for pair in zip(one_a, one_b)])
        one_z, a_own = lax.optimization_barrier((one_z, a_own))
        one_x, one_y = x_swap(one_z), y_swap(one_z)
        a_swapped = [core_swap(v) for v in a_own]
        two_far = z_swap(jnp.concatenate([two_lo, two_hi]), 2)
        one_x, one_y, two_far = lax.optimization_barrier((one_x, one_y, two_far))
        one_d = [x_swap(one_y[:2]), y_swap(one_x[2:])]
        twos = [two_lo, two_hi, two_far]
        ctx_own, ctx_other, q, kk, v, ctx, probs, wr, ub_all, proj_w, small_all = attend(
            bucket, lengths, inputs, other_in, (*a_own, *a_swapped), wq, wp
        )
        f_all = [[one_z], [one_x], [one_y], twos, one_d]
    else:
        a_all = lax.all_gather(a_shard, ("batch", "head"), axis=0)
        qkv_all = a_all[:, :wq].reshape(2, 2, 576, D)
        qkv_w = lax.dynamic_index_in_dim(qkv_all, c, 1, keepdims=False).reshape(2 * 576, D)
        proj_w = a_all[:, wq : wq + wp].reshape(D, D)
        small_all = jnp.sum(a_all[:, wq + wp :].astype(F32), 0)
        ctx_own, ctx_other, q, kk, v, ctx, probs, wr = attend(
            bucket, lengths, inputs, other_in, (qkv_w, small_all)
        )
        f_shard = jnp.concatenate([up_weight.T, down_weight])
        f_all = [
            (v[:, :wf].reshape(-1, D), v[:, wf:].reshape(-1, D)) for v in gather_any(f_shard)
        ]
        owner = (k % batch_count) * 4 + (x ^ (k // batch_count)) * 2 + c
    if not direct:
        spread = (owner[None, :] == jnp.arange(devices)[:, None]).astype(F32)
        ub_all = tn(spread, small_all[8:12].reshape(devices, wf)).reshape(1, FF // 2)

    ctx_in = core_swap(ctx_other)
    first_low, first, first_n, first_r = first_norm(inputs, ctx_own, ctx_in, proj_w, small_all)
    first_in = core_swap(first_low)
    sums = ()
    kept = []
    starts = (0, FF // 4)
    if direct:
        starts = (0, 4 * ONE, 8 * ONE, 16 * ONE, 12 * ONE)
    for weights, at in zip(f_all, starts):
        width = FF // 4
        if direct:
            width = 16 * TWO if len(kept) == 3 else 4 * ONE
        hid, slope, *sums = ffn(
            first_low,
            first_in,
            ub_all[:, at : at + width],
            weights,
            sums,
            len(kept) == len(f_all) - 1,
        )
        kept.append((hid, slope))
    down_low, sum_two, second_n = second_norm(
        bucket, lengths, first, sums[0], core_swap(sums[1]), small_all, cotangent
    )
    down_in = core_swap(down_low)

    sums = ()
    f_parts, ub_parts = [], []
    if direct:
        for spot, i in ((3, 4), (2, 2), (1, 1), (0, 0)):
            weights, both = (*f_all[i], *twos), (*kept[i], *kept[3])
            grads, ub, sums = ffn_back(
                down_low, down_in, first_low, first_in, spot, weights, both, sums, spot == 0
            )
            f_parts.append(grads)
            ub_parts.insert(0, ub)
    else:
        for weights, pair in zip(f_all, kept):
            grads, ub, sums = ffn_back(
                down_low,
                down_in,
                first_low,
                first_in,
                None,
                weights,
                pair,
                sums,
                len(f_parts) == len(f_all) - 1,
            )
            f_parts.append(grads)
            ub_parts.append(ub)
    part_own, part_other = sums
    layer_out, sums_two = second_rest(
        bucket, lengths, after(second_n, part_other), small_all, cotangent, down_low
    )
    sum_two = after(sum_two, sums_two)
    moved = ()
    if direct:
        (d_lo, d_hi), y_sets, x_sets, z_sets = f_parts
        moved = (*x_sets, y_swap(d_hi), *y_sets, x_swap(d_lo))
    added, sum_one, attn_low, sums_one = first_back(
        sum_two, part_own, core_swap(part_other), first_n, first_r, small_all, moved
    )
    attn_in = core_swap(attn_low)
    *a_grads, in_own, in_other, sums_zero = attend_back(
        added[2:],
        attn_low,
        attn_in,
        inputs,
        other_in,
        proj_w,
        wr,
        q,
        kk,
        v,
        ctx,
        probs,
    )
    in_got = core_swap(in_other)
    inputs_grad = (sum_one + in_own + in_got).astype(BF16)

    if direct:
        up_sets = scatter_xy(z_sets[0], *added[:2])
        a_zz, a_xx, a_yy, by_x, by_y = a_grads
        by_x, by_y, up_sets, in_got = lax.optimization_barrier((by_x, by_y, up_sets, in_got))
        by_x, by_y = x_swap(by_x), y_swap(by_y)
        up_mine, up_others = combine(*up_sets)
        sums_zero = after(sums_zero, up_others)
        terms = exchange_terms(sums_zero, sums_one, sums_two, ub_parts, devices)
        terms = lax.all_to_all(terms, ("batch", "head"), split_axis=0, concat_axis=0, tiled=True)
        up_others = scatter_z(up_others)
        by_x, by_y, up_others, terms, _ = lax.optimization_barrier(
            (by_x, by_y, up_others, terms, inputs_grad)
        )
        a_xy, down_mine, down_others = turn(a_xx, a_yy, z_sets[1], by_x, by_y)
        a_sets = scatter_xy(a_zz, *a_xy)
        down_others = scatter_z(down_others)
        a_sets, down_others = lax.optimization_barrier((a_sets, down_others))
        a_mine, a_others = combine_last(*a_sets)
        a_others = scatter_z(a_others)
        up_grad, down_grad = finish_ffn((up_mine, *up_others), (down_mine, *down_others))
        up_grad = up_grad.T
        terms = jnp.sum(terms.astype(F32), 0)
        packed = jnp.concatenate([terms[:, :wp].reshape(-1), terms[0, wp : wp + wf]])
        qkv_grad, proj_grad = finish_attend((a_mine, *a_others))
    else:
        vecs = jnp.concatenate([sums_zero, sums_one, sums_two])
        vecs = vecs.reshape(8, devices, wp).transpose(1, 0, 2).reshape(devices, 8 * wp)
        ubias = jnp.concatenate(ub_parts).reshape(batch_count * 2, wf)
        ubias = lax.dot_general(
            spread, ubias, (((1,), (0,)), ((), ())), precision=lax.Precision.HIGHEST
        )
        packed = jnp.concatenate([vecs, ubias], 1)
        packed = lax.all_to_all(
            packed, ("batch", "head"), split_axis=0, concat_axis=0, tiled=True
        )
        packed = jnp.sum(packed, 0)
        wb = D // batch_count
        a_grads = a_grads[0].reshape(2, batch_count, wb, D)
        a_mine = scatter_any(
            [
                lax.dynamic_index_in_dim(a_grads, x, 0, keepdims=False),
                lax.dynamic_index_in_dim(a_grads, 1 - x, 0, keepdims=False),
            ]
        )
        f_mine = scatter_any(
            [
                jnp.concatenate(
                    [ug.reshape(batch_count, wf, D), dg.reshape(batch_count, wf, D)], 1
                )
                for ug, dg in f_parts
            ]
        )
        qkv_grad = a_mine[:, :576].reshape(wb, 3, 3, HEAD_DIM).transpose(0, 2, 1, 3)
        qkv_grad = qkv_grad.reshape(wb, 576)
        proj_grad = a_mine[:, 576:].T
        up_grad, down_grad = f_mine[:wf].T, f_mine[wf:]
    qb_g, vb_g, pb_g, fg_g, fs_g, db_g, sg_g, ss_g = [
        packed[i * wp : (i + 1) * wp] for i in range(8)
    ]
    return (
        layer_out,
        inputs_grad,
        qkv_grad,
        qb_g,
        vb_g,
        proj_grad,
        pb_g,
        fg_g,
        fs_g,
        up_grad,
        packed[8 * wp :],
        down_grad,
        db_g,
        sg_g,
        ss_g,
    )


def solution(mesh):
    both = ("batch", "head")
    in_specs = (
        P(both, None),
        P("batch"),
        P("batch", None),
        P(None, both),
        P(both),
        P(both),
        P(None, both),
        P(both),
        P(both),
        P(both),
        P(None, both),
        P(both),
        P(both, None),
        P(both),
        P(both),
        P(both),
        P(both, None),
    )
    out_specs = (
        P(both, None),
        P(both, None),
        P("batch", "head"),
        P(both),
        P(both),
        P("head", "batch"),
        P(both),
        P(both),
        P(both),
        P(None, both),
        P(both),
        P(both, None),
        P(both),
        P(both),
        P(both),
    )
    return jax.shard_map(local, mesh=mesh, in_specs=in_specs, out_specs=out_specs, check_vma=False)
```

```python
import functools

import jax
import jax.numpy as jnp
from jax import lax
from jax.experimental import pallas as pl
from jax.experimental.pallas import tpu as pltpu
from jax.sharding import PartitionSpec as P

D = 768
HEADS = 12
HEAD_DIM = 64
FF = 3072
BIG = 512
SMALL = 128
UNITS = 4
NORM_EPS = 1e-12
F32 = jnp.float32
BF16 = jnp.bfloat16

ONE, TWO = 80, 16
FIRST = 104

CORE = [(i, i ^ 1) for i in range(4)]
XPAIR = [(i, i ^ 2) for i in range(4)]
YPAIR = [(i, i ^ 1) for i in range(8)]
ZPAIR = [[(i, i ^ (2 * k)) for i in range(8)] for k in range(4)]


def core_swap(v):
    return lax.ppermute(v, "head", CORE)


def x_swap(v):
    return lax.ppermute(v, "head", XPAIR)


def y_swap(v):
    return lax.ppermute(v, "batch", YPAIR)


def z_swap(v, k):
    return lax.ppermute(v, "batch", ZPAIR[k])


def after(value, other):
    return lax.optimization_barrier((value, other))[0]


def nt(a, b, out=F32):
    return lax.dot_general(a, b, (((1,), (1,)), ((), ())), preferred_element_type=F32).astype(out)


def nn(a, b, out=F32):
    return lax.dot_general(a, b, (((1,), (0,)), ((), ())), preferred_element_type=F32).astype(out)


def tn(a, b, out=F32):
    return lax.dot_general(a, b, (((0,), (0,)), ((), ())), preferred_element_type=F32).astype(out)


def z_line(shard):
    return [shard] + [z_swap(shard, k) for k in (1, 2, 3)]


def gather_four(z):
    x, y = x_swap(z), y_swap(z)
    return [z, x, y, x_swap(y[:2]), y_swap(x[2:])]


def gather_any(shard):
    whole = lax.all_gather(shard, "batch", axis=0)
    return [whole, x_swap(whole)]


def scatter_xy(z, x, y):
    return z, x_swap(x), y_swap(y)


def scatter_z(others):
    return [z_swap(others[k - 1], k) for k in (1, 2, 3)]


def scatter_any(parts):
    total = parts[0].astype(F32) + x_swap(parts[1]).astype(F32)
    return lax.psum_scatter(total, "batch", scatter_dimension=0, tiled=False)


def est(flops, moved, trans=0):
    return pl.CostEstimate(flops=int(flops), bytes_accessed=int(moved), transcendentals=int(trans))


def call(kernel, out_shape, operands, scratch=(), cost=None, limit=16, far_in=(), far_out=(), sems=0):
    vmem = pl.BlockSpec(memory_space=pltpu.VMEM)
    hbm = pl.BlockSpec(memory_space=pltpu.HBM)
    smem = pl.BlockSpec(memory_space=pltpu.SMEM)
    ins = [hbm if i in far_in else vmem for i in range(len(operands))]
    ins = [smem if v.dtype == jnp.int32 else spec for spec, v in zip(ins, operands)]
    outs = [hbm if i in far_out else vmem for i in range(len(out_shape))]
    scratch = list(scratch) + ([pltpu.SemaphoreType.DMA((sems,))] if sems else [])
    operands = [
        pltpu.with_memory_space_constraint(v, pltpu.HBM) if i in far_in else v
        for i, v in enumerate(operands)
    ]
    out_shape = [
        pltpu.HBM(v.shape, v.dtype) if i in far_out else v for i, v in enumerate(out_shape)
    ]
    return pl.pallas_call(
        kernel,
        out_shape=out_shape,
        in_specs=ins,
        out_specs=outs,
        scratch_shapes=scratch,
        compiler_params=pltpu.CompilerParams(vmem_limit_bytes=limit << 20),
        cost_estimate=cost,
    )(*operands)


class Copies:
    def __init__(self, sems):
        self.sems, self.used, self.open = sems, 0, []

    def start(self, src, dst):
        copy = pltpu.make_async_copy(src, dst, self.sems.at[self.used])
        self.used += 1
        copy.start()
        self.open.append(copy)
        return copy

    def wait(self, *copies):
        for copy in copies or list(self.open):
            copy.wait()
            self.open.remove(copy)


def add_low(a, b):
    return (a.astype(F32) + b.astype(F32)).astype(BF16)


def shape(dims, dtype=BF16):
    return jax.ShapeDtypeStruct(dims, dtype)


def add_first_kernel(x_up, x_down, for_x, y_up, y_down, for_y, *outs):
    half = x_up.shape[1]
    for i, (x, y) in enumerate(((x_up, y_up), (x_down, y_down))):
        rows = slice(half * i, half * i + half)
        x_out, y_out = outs[2 * i : 2 * i + 2]
        x_out[0:2] = x[0:2]
        y_out[2:4] = y[2:4]
        for k in range(2):
            x_out[2 + k] = add_low(x[2 + k], for_x[k, rows])
            y_out[k] = add_low(y[k], for_y[k, rows])


def combine_kernel(z, x, y, *refs):
    outs, (mine, low, sems) = refs[:4], refs[4:]
    sum_places(z, x, y, outs, mine, low, Copies(sems)).wait()


def sum_places(z, x, y, outs, mine, low, copies, arrived=None):
    for i, k in enumerate((1, 2, 3, 0)):
        if arrived:
            copies.wait(*arrived[i])
        total = z[k].astype(F32) + x[k].astype(F32) + y[k].astype(F32)
        if k == 0:
            mine[...] = total
            copies.start(mine, outs[0])
        else:
            low[k - 1] = total.astype(BF16)
            copies.start(low.at[k - 1], outs[k])
    return copies


def combine(z, x, y):
    rows = z.shape[1]
    mine, *others = call(
        combine_kernel,
        (shape((rows, D), F32),) + (shape((rows, D)),) * 3,
        (z, x, y),
        scratch=[pltpu.VMEM((rows, D), F32), pltpu.VMEM((3, rows, D), BF16)],
        cost=est(1000, 1000),
        limit=8,
        far_out=range(4),
        sems=4,
    )
    return mine, others


def combine_last_kernel(z, x, y, mine, *refs):
    outs, (low, sems) = refs[:3], refs[3:]
    copies = Copies(sems)
    for k in (1, 2, 3, 0):
        total = z[k].astype(F32) + x[k].astype(F32) + y[k].astype(F32)
        if k == 0:
            mine[...] = total
        else:
            low[k - 1] = total.astype(BF16)
            copies.start(low.at[k - 1], outs[k - 1])
    copies.wait()


def combine_last(z, x, y):
    rows = z.shape[1]
    mine, *others = call(
        combine_last_kernel,
        (shape((rows, D), F32),) + (shape((rows, D)),) * 3,
        (z, x, y),
        scratch=[pltpu.VMEM((3, rows, D), BF16)],
        cost=est(1000, 1000),
        limit=8,
        far_out=range(1, 4),
        sems=3,
    )
    return mine, others


def turn_kernel(x, y, z, by_x_far, by_y_far, x_out, y_out, *refs):
    outs, (by_x, by_y, mine, low, sems) = refs[:4], refs[4:]
    copies = Copies(sems)
    arrived = []
    for k in (1, 2, 3, 0, 4):
        rows = pl.ds(k, 1 if k < 4 else 2)
        arrived.append(
            (
                copies.start(by_x_far.at[rows], by_x.at[rows]),
                copies.start(by_y_far.at[rows], by_y.at[rows]),
            )
        )
    sum_places(z, by_x, by_y, outs, mine, low, copies, arrived)
    copies.wait(*arrived[4])
    y_out[0:2] = add_low(y[0:2], by_x[4:6])
    y_out[2:4] = y[2:4]
    x_out[0:2] = x[0:2]
    x_out[2:4] = add_low(x[2:4], by_y[4:6])
    copies.wait()


def turn(x, y, z, by_x, by_y):
    rows = z.shape[1]
    x, y, mine, *others = call(
        turn_kernel,
        (shape(x.shape), shape(y.shape), shape((rows, D), F32)) + (shape((rows, D)),) * 3,
        (x, y, z, by_x, by_y),
        scratch=[pltpu.VMEM(by_x.shape, BF16)] * 2
        + [pltpu.VMEM((rows, D), F32), pltpu.VMEM((3, rows, D), BF16)],
        cost=est(1000, 1000),
        limit=8,
        far_in=(3, 4),
        far_out=range(2, 6),
        sems=14,
    )
    return (x, y), mine, others


def total_of(refs):
    return refs[0][...] + refs[1][...].astype(F32) + refs[2][...].astype(F32) + refs[3][...].astype(F32)


def finish_attend_kernel(mine, one, two, three, qkv, proj):
    total = total_of((mine, one, two, three))
    for hh in range(3):
        for t in range(3):
            at, to = 192 * t + 64 * hh, 192 * hh + 64 * t
            qkv[:, to : to + 64] = total[:, at : at + 64]
    proj[...] = total[:, 576:].T


def finish_attend(parts):
    rows = parts[0].shape[0]
    return call(
        finish_attend_kernel,
        (shape((rows, 576), F32), shape((192, rows), F32)),
        tuple(parts),
        cost=est(8 * rows * D, 16 * rows * D),
        limit=8,
    )


def finish_ffn_kernel(*refs):
    up, down = refs[8:]
    up[...], down[...] = total_of(refs[0:4]), total_of(refs[4:8])


def finish_ffn(ups, downs):
    dims = ups[0].shape
    return call(
        finish_ffn_kernel,
        (shape(dims, F32), shape(dims, F32)),
        (*ups, *downs),
        cost=est(1000, 1000),
        limit=8,
    )


def exchange_kernel(zero, one, two, *refs):
    ubs, out = refs[:4], refs[4]
    vecs = jnp.concatenate([zero[...], one[...], two[...]])
    width = D // out.shape[0]
    vecs = vecs.astype(BF16)
    out[...] = jnp.zeros(out.shape, BF16)
    for i in range(out.shape[0]):
        out[i, 0:8, 0:width] = vecs[:, width * i : width * i + width]
    for spot in range(4):
        for kz in range(4):
            to, ub = slot_of(spot, kz), ubs[spot][...].astype(BF16)
            out[to, 0:1, 24 : 24 + ONE] = ub[:, ONE * kz : ONE * kz + ONE]
            at = 4 * ONE + TWO * kz
            out[to, 0:1, 24 + ONE : 24 + ONE + TWO] = ub[:, at : at + TWO]


def exchange_terms(zero, one, two, ubs, devices):
    return call(
        exchange_kernel,
        (shape((devices, 8, 128)),),
        (zero, one, two, *ubs),
        cost=est(1000, 1000),
        limit=8,
    )[0]


def flip(a, bit):
    return a + bit - 2 * a * bit


def pack_kernel(qkv_in, proj_in, up_in, down_in, bias_in, *refs):
    vectors_in, (a_out, one_a, one_b, two, a, p, f, bias, vectors, sems) = refs[:8], refs[8:]
    rows_q, rows_p, half = qkv_in.shape[0], proj_in.shape[0], down_in.shape[0]
    copies = Copies(sems)
    copies.start(qkv_in, a.at[pl.ds(0, rows_q)])
    copies.start(proj_in, p)
    copies.start(up_in, f.at[pl.ds(0, half)])
    copies.start(down_in, f.at[pl.ds(half, half)])
    copies.start(bias_in, bias)
    for i, r in enumerate(vectors_in):
        copies.start(r, vectors.at[i])
    width = vectors.shape[2]
    b, h = lax.axis_index("batch"), lax.axis_index("head")
    me = b * lax.axis_size("head") + h
    copies.wait()
    v = jnp.concatenate([vectors[i] for i in range(8)]).astype(F32)
    v = jnp.concatenate([v] * (D // width), 1)
    lane = lax.broadcasted_iota(jnp.int32, (8, D), 1)
    mine = jnp.logical_and(lane >= me * width, lane < me * width + width)
    v = jnp.where(mine, v, 0.0)
    gap = jnp.zeros((1, D // 2 - half), F32)
    none = jnp.zeros((1, D // 2), F32)
    row = bias[...].astype(F32)
    early = jnp.concatenate([none, row, gap], 1)
    late = jnp.concatenate([row, gap, none], 1)
    extra = jnp.where(me < lax.axis_size("batch") * lax.axis_size("head") // 2, early, late)
    v = v + jnp.concatenate([extra, jnp.zeros((7, D), F32)])
    a_out[0:rows_q] = a[0:rows_q]
    q = p[...]
    a_out[rows_q : rows_q + rows_p] = jnp.concatenate(
        [q[:, 192 * i : 192 * i + 192] for i in (0, 2, 1, 3)], 1
    )
    a_out[rows_q + rows_p :] = v.astype(BF16)
    one = jnp.concatenate([f[0:ONE], f[half : half + ONE]])
    one_a[...], one_b[...] = one[0:FIRST], one[FIRST:]
    two[0:TWO], two[TWO:] = f[ONE:half], f[half + ONE :]


def pack(qkv, proj, up, down, bias, vectors):
    rows, half = qkv.shape[0] + proj.shape[0] + 8, down.shape[0]
    return call(
        pack_kernel,
        (
            shape((rows, D)),
            shape((FIRST, D)),
            shape((2 * ONE - FIRST, D)),
            shape((2 * TWO, D)),
        ),
        (qkv, proj, up, down, bias[None], *[v[None] for v in vectors]),
        scratch=[
            pltpu.VMEM((rows, D), BF16),
            pltpu.VMEM(proj.shape, BF16),
            pltpu.VMEM((2 * half, D), BF16),
            pltpu.VMEM((1,) + bias.shape, BF16),
            pltpu.VMEM((8, 1) + vectors[0].shape, BF16),
        ],
        cost=est(1000, 1000),
        limit=8,
        far_in=range(13),
        sems=13,
    )


def place_here():
    b, h = lax.axis_index("batch"), lax.axis_index("head")
    return lax.rem(h, 2), lax.div(b, 2), lax.rem(b, 2), lax.div(h, 2)


def live_units(bucket, lengths):
    x = place_here()[3]
    kind, first = bucket[x], lengths[x, 0]
    units = []
    for u in range(UNITS):
        far = jnp.clip(first - SMALL * u, 0, SMALL)
        units.append(jnp.where(kind == 1, far, lengths[x, u]))
    return kind, units


def place_of(index, c):
    return jnp.bitwise_xor(index, c * (BIG // 2))


def live_of(place, units):
    unit = lax.shift_right_logical(place, 7)
    inner = jnp.bitwise_and(place, SMALL - 1)
    count = jnp.where(
        unit < 2, jnp.where(unit == 0, units[0], units[1]), jnp.where(unit == 2, units[2], units[3])
    )
    return inner < count


def heads_of(row, c):
    parts = []
    for g in range(2):
        lo = row[:, 384 * g : 384 * g + 192]
        hi = row[:, 384 * g + 192 : 384 * g + 384]
        parts.append(jnp.where(c == 0, lo, hi))
    return jnp.concatenate(parts, 1)


def fetch_shards(copies, sources, slots):
    c, z, y, x = place_here()
    zl, zh = lax.rem(z, 2), lax.div(z, 2)
    for swapped in range(2):
        cc = c if swapped == 0 else 1 - c
        zs, xs, ys, xa, xb = sources[5 * swapped : 5 * swapped + 5]
        for kx, ky, pair in ((0, 0, (zs,)), (1, 0, (xs,)), (0, 1, (ys,)), (1, 1, (xa, xb))):
            j = flip(y, ky) * 4 + flip(x, kx) * 2 + cc
            for kz in range(4):
                src = pair[0].at[kz] if len(pair) == 1 else pair[kz // 2].at[kz % 2]
                zi = flip(zl, kz % 2) + 2 * flip(zh, kz // 2)
                copies.start(src, slots.at[zi * 8 + j])


def slot_of(spot, kz):
    c, z, y, x = place_here()
    zi = flip(lax.rem(z, 2), kz % 2) + 2 * flip(lax.div(z, 2), kz // 2)
    return zi * 8 + flip(y, spot // 2) * 4 + flip(x, spot % 2) * 2 + c


def bias_order(slots, row, out):
    for spot in range(4):
        for kz in range(4):
            i = slot_of(spot, kz)
            b = slots[i, row : row + 1].astype(F32)
            b = jnp.where(i < 16, b[:, D // 2 : D // 2 + 96], b[:, 0:96])
            at = 4 * ONE * spot + ONE * kz
            out[:, at : at + ONE] = b[:, 0:ONE]
            at = 16 * ONE + 4 * TWO * spot + TWO * kz
            out[:, at : at + TWO] = b[:, ONE:]


def attend_kernel(rows_q, rows_p, bucket, lengths, x0, x1, *refs):
    sources = 10 if rows_q else 2
    weights, refs = refs[:sources], refs[sources:]
    (ctx0, ctx1, q, k, v, ctx, probs, wr), refs = refs[:8], refs[8:]
    if rows_q:
        (ub_out, wp, small, mask, xs, slots, sems) = refs
    else:
        (mask, xs, w, small, sems) = refs
    copies = Copies(sems)
    c = place_here()[0]
    kind, units = live_units(bucket, lengths)
    half = x0.shape[0]
    copies.start(x0, xs.at[0:half])
    copies.start(x1, xs.at[half : 2 * half])
    if rows_q:
        fetch_shards(copies, weights, slots)
    else:
        copies.start(weights[0], w)
        copies.start(weights[1], small)
    rows = lax.broadcasted_iota(jnp.int32, (BIG, BIG), 0)
    cols = lax.broadcasted_iota(jnp.int32, (BIG, BIG), 1)
    prow, pcol = place_of(rows, c), place_of(cols, c)
    same = jnp.logical_or(
        kind == 1, lax.shift_right_logical(prow, 7) == lax.shift_right_logical(pcol, 7)
    )
    mask[...] = jnp.where(jnp.logical_and(same, live_of(pcol, units)), 0.0, -1e30)
    copies.wait()
    if rows_q:
        for g in range(2):
            cuts = jnp.concatenate([slots[16 * g + 8 * c + j, 0:rows_q] for j in range(8)])
            for t in range(3):
                for hh in range(3):
                    src, dst = (hh * 3 + t) * HEAD_DIM, (t * 6 + g * 3 + hh) * HEAD_DIM
                    wr[dst : dst + HEAD_DIM] = cuts[src : src + HEAD_DIM]
        lane = lax.broadcasted_iota(jnp.int32, (8, D), 1)
        small[...] = sum(
            jnp.where(
                jnp.logical_and(lane >= rows_p * i, lane < rows_p * i + rows_p),
                slots[i, rows_q + rows_p :].astype(F32),
                0.0,
            )
            for i in range(32)
        )
    else:
        for t in range(3):
            for hd in range(6):
                src = ((hd // 3) * 9 + (hd % 3) * 3 + t) * HEAD_DIM
                dst = (t * 6 + hd) * HEAD_DIM
                wr[dst : dst + HEAD_DIM] = w[src : src + HEAD_DIM]
    biases = (heads_of(small[0:1], c), None, heads_of(small[1:2], c))
    for t, ref in enumerate((q, k, v)):
        val = nt(xs[...], wr[384 * t : 384 * t + 384])
        if biases[t] is not None:
            val = val + biases[t]
        ref[...] = val.astype(BF16)
    if rows_q:
        for i in range(32):
            wp[rows_p * i : rows_p * i + rows_p] = slots[i, rows_q : rows_q + rows_p]
        bias_order(slots, rows_q + rows_p, ub_out)
    lane = lax.broadcasted_iota(jnp.int32, (half, 128), 1)
    for pair in range(3):
        lanes = slice(128 * pair, 128 * pair + 128)
        kp, vp = k[:, lanes], v[:, lanes]
        for i, near in enumerate((ctx0, ctx1)):
            rws = slice(half * i, half * i + half)
            qp = q[rws, lanes] * jnp.asarray(HEAD_DIM**-0.5, BF16)
            outs = []
            for e in range(2):
                mine = (lane < HEAD_DIM) if e == 0 else (lane >= HEAD_DIM)
                s = nt(jnp.where(mine, qp, jnp.zeros_like(qp)), kp) + mask[rws]
                ex = jnp.exp(s - jnp.max(s, -1, keepdims=True))
                pr = (ex * (1.0 / jnp.sum(ex, -1, keepdims=True))).astype(BF16)
                probs[2 * pair + e, rws] = pr
                outs.append(nn(pr, vp))
            val = jnp.where(lane < HEAD_DIM, outs[0], outs[1]).astype(BF16)
            ctx[rws, lanes] = val
            near[:, lanes] = val


def attend(bucket, lengths, x0, x1, weights, rows_q=0, rows_p=0, rows_s=16):
    rows_s = 8 if rows_q else rows_s
    half = x0.shape[0]
    n = 2 * half
    direct = rows_q > 0
    outs = [
        shape((half, 384)),
        shape((half, 384)),
        shape((n, 384)),
        shape((n, 384)),
        shape((n, 384)),
        shape((n, 384)),
        shape((6, n, n)),
        shape((1152, D)),
    ]
    scratch = [pltpu.VMEM((n, n), F32), pltpu.VMEM((n, D), BF16)]
    if direct:
        outs += [shape((1, FF // 2), F32), shape((D, D)), shape((rows_s, D), F32)]
        scratch += [pltpu.VMEM((32, rows_q + rows_p + rows_s, D), BF16)]
    else:
        scratch += [pltpu.VMEM((1152, D), BF16), pltpu.VMEM((rows_s, D), F32)]
    operands = (bucket, lengths, x0, x1, *weights)
    return call(
        functools.partial(attend_kernel, rows_q, rows_p),
        outs,
        operands,
        scratch=scratch,
        cost=est(1000, 1000),
        limit=32,
        far_in=range(2, len(operands)),
        sems=50,
    )


def norm(values):
    center = values - jnp.mean(values, -1, keepdims=True)
    spread = jnp.mean(center * center, -1, keepdims=True)
    scale = lax.rsqrt(spread + NORM_EPS)
    return center * scale, scale


def norm_back(cot, normal, scale, gain):
    w = cot * gain
    return scale * (
        w - jnp.mean(w, -1, keepdims=True) - normal * jnp.mean(w * normal, -1, keepdims=True)
    )


def first_kernel(x, ctx_own, ctx_in, wp, small, low, first, normal, scale):
    c = place_here()[0]
    mine = pl.multiple_of(c * 384, 128)
    theirs = pl.multiple_of((1 - c) * 384, 128)
    attn = nt(ctx_own[...], wp[:, pl.ds(mine, 384)]) + nt(ctx_in[...], wp[:, pl.ds(theirs, 384)])
    n, r = norm(x[...].astype(F32) + attn + small[2:3])
    normal[...] = n
    out = n * small[3:4] + small[4:5]
    first[...] = out
    low[...] = out.astype(BF16)
    scale[...] = jnp.broadcast_to(r, scale.shape)


def first_norm(x, ctx_own, ctx_in, wp, small):
    n = x.shape[0]
    return call(
        first_kernel,
        (shape((n, D)), shape((n, D), F32), shape((n, D), F32), shape((n, 128), F32)),
        (x, ctx_own, ctx_in, wp, small),
        cost=est(1000, 1000),
        limit=8,
    )


def ffn_weights(refs):
    if len(refs[0].shape) == 2:
        return refs[0][...], refs[1][...]
    return stacked(ones_of(refs) if refs[0].shape[1] == 2 * ONE else twos_of(refs, range(4)))


def ones_of(refs):
    return [(r, i) for r in refs for i in range(r.shape[0])]


def twos_of(refs, spots):
    along_z = [(r, i) for r in refs for i in range(0, r.shape[0], 4)]
    return [(r, i + spot) for spot in spots for r, i in along_z]


def stacked(blocks):
    up = jnp.concatenate([r[i, 0 : r.shape[1] // 2] for r, i in blocks])
    down = jnp.concatenate([r[i, r.shape[1] // 2 :] for r, i in blocks])
    return up, down


def ffn_kernel(first, count, x0, x1, ub, *refs):
    far, refs = refs[:count], refs[count:]
    if first:
        in0 = in1 = None
    else:
        (in0, in1), refs = refs[:2], refs[2:]
    hid, slope, out0, out1 = refs
    half = x0.shape[0]
    uw, dw = ffn_weights(far)
    for i, (xr, before, out) in enumerate(((x0, in0, out0), (x1, in1, out1))):
        rws = slice(half * i, half * i + half)
        up = nt(xr[...], uw) + ub[...]
        phi = 0.5 + 0.5 * lax.erf(up * (2.0**-0.5))
        hd = (up * phi).astype(BF16)
        hid[rws] = hd
        slope[rws] = (phi + up * jnp.exp(-0.5 * up * up) * 0.3989422804014327).astype(BF16)
        part = nn(hd, dw)
        part = part if before is None else before[...] + part
        out[...] = part.astype(out.dtype)


def ffn(x0, x1, ub, weights, sums, last):
    half, width, count = x0.shape[0], ub.shape[1], len(weights)
    n = 2 * half
    return call(
        functools.partial(ffn_kernel, not sums, count),
        (
            shape((n, width)),
            shape((n, width)),
            shape((half, D), F32),
            shape((half, D), BF16 if last else F32),
        ),
        (x0, x1, ub, *weights, *sums),
        cost=est(4 * n * D * width, 4 * D * width + 5e6, 2 * n * width),
    )


def ffn_half_kernel(x, ub, w0, w1, before, hid, slope, out):
    uw, dw = ffn_weights((w0, w1))
    up = nt(x[...], uw) + ub[...]
    phi = 0.5 + 0.5 * lax.erf(up * (2.0**-0.5))
    hd = (up * phi).astype(BF16)
    hid[...] = hd
    slope[...] = (phi + up * jnp.exp(-0.5 * up * up) * 0.3989422804014327).astype(BF16)
    out[...] = (before[...] + nn(hd, dw)).astype(out.dtype)


def ffn_half(x, ub, weights, before, dtype):
    n, width = x.shape[0], ub.shape[1]
    return call(
        ffn_half_kernel,
        (shape((n, width)), shape((n, width)), shape((n, D), dtype)),
        (x, ub, *weights, before),
        cost=est(1000, 1000),
    )


def second_kernel(bucket, lengths, first, part, got, small, cot, low, sum_two, normal):
    c = place_here()[0]
    _, units = live_units(bucket, lengths)
    n, r = norm(first[...] + (part[...] + got[...].astype(F32) + small[5:6]))
    index = lax.broadcasted_iota(jnp.int32, (first.shape[0], 1), 0)
    live = live_of(place_of(index, c), units)
    oc = jnp.where(live, cot[...].astype(F32), 0.0)
    st = norm_back(oc, n, r, small[6:7])
    low[...] = st.astype(BF16)
    sum_two[...] = st
    normal[...] = n


def second_norm(bucket, lengths, first, part, got, small, cot):
    n = first.shape[0]
    return call(
        second_kernel,
        (shape((n, D)), shape((n, D), F32), shape((n, D), F32)),
        (bucket, lengths, first, part, got, small, cot),
        cost=est(1000, 1000),
        limit=8,
    )


def second_rest_kernel(bucket, lengths, normal, small, cot, low, out, sums):
    c = place_here()[0]
    _, units = live_units(bucket, lengths)
    n = normal[...]
    out[...] = (n * small[6:7] + small[7:8]).astype(BF16)
    index = lax.broadcasted_iota(jnp.int32, (normal.shape[0], 1), 0)
    live = live_of(place_of(index, c), units)
    oc = jnp.where(live, cot[...].astype(F32), 0.0)
    sums[0:1] = jnp.sum(low[...].astype(F32), 0, keepdims=True)
    sums[1:2] = jnp.sum(oc * n, 0, keepdims=True)
    sums[2:3] = jnp.sum(oc, 0, keepdims=True)


def second_rest(bucket, lengths, normal, small, cot, low):
    n = normal.shape[0]
    return call(
        second_rest_kernel,
        (shape((n, D)), shape((3, D), F32)),
        (bucket, lengths, normal, small, cot, low),
        cost=est(1000, 1000),
        limit=8,
    )


def ffn_back_kernel(first, spot, count, d0, d1, x0, x1, *refs):
    weights, refs = refs[:count], refs[count:]
    if spot is None:
        hid, slope = refs[0], refs[1]
        refs = refs[2:]
        uw, dw = ffn_weights(weights)
    else:
        (hid1, slope1, hid2, slope2), refs = refs[:4], refs[4:]
        tail = slice(4 * TWO * spot, 4 * TWO * spot + 4 * TWO)
        hid = jnp.concatenate([hid1[...], hid2[:, tail]], 1)
        slope = jnp.concatenate([slope1[...], slope2[:, tail]], 1)
        uw, dw = stacked(ones_of(weights[:-3]) + twos_of(weights[-3:], [spot]))
    if first:
        in0 = in1 = None
    else:
        (in0, in1), refs = refs[:2], refs[2:]
    *outs, ub, out0, out1 = refs
    half = x0.shape[0]
    cots = []
    for i, (d, before, out) in enumerate(((d0, in0, out0), (d1, in1, out1))):
        rws = slice(half * i, half * i + half)
        uc = (nt(d[...], dw) * slope[rws].astype(F32)).astype(BF16)
        cots.append(uc)
        part = nn(uc, uw)
        part = part if before is None else before[...] + part
        out[...] = part.astype(out.dtype)
    ub[...] = jnp.sum(cots[0].astype(F32), 0, keepdims=True) + jnp.sum(
        cots[1].astype(F32), 0, keepdims=True
    )
    dg = (tn(hid[0:half], d0[...]) + tn(hid[half : 2 * half], d1[...])).astype(BF16)
    ug = (tn(cots[0], x0[...]) + tn(cots[1], x1[...])).astype(BF16)
    if spot is None:
        outs[0][...], outs[1][...] = ug, dg
        return
    rows = ONE + TWO
    for k in range(4):
        for e, g in enumerate((ug, dg)):
            out, i, at = (outs[k // 2], k % 2, rows * e) if spot == 3 else (outs[e], k, 0)
            out[i, at : at + ONE] = g[ONE * k : ONE * k + ONE]
            low = 4 * ONE + TWO * k
            out[i, at + ONE : at + rows] = g[low : low + TWO]


def diagonal_of(refs, rows):
    *weights, hid1, slope1, hid2, slope2 = refs
    tail = slice(12 * TWO, 16 * TWO)
    hid = jnp.concatenate([hid1[...], hid2[rows, tail]], 1)
    slope = jnp.concatenate([slope1[...], slope2[rows, tail]], 1)
    return hid, slope, *stacked(ones_of(weights[:-3]) + twos_of(weights[-3:], [3]))


def diagonal_own_kernel(d, x, *refs):
    *refs, down, up, ub, part = refs
    hid, slope, uw, dw = diagonal_of(refs, slice(0, d.shape[0]))
    cot = (nt(d[...], dw) * slope.astype(F32)).astype(BF16)
    part[...] = nn(cot, uw)
    ub[...] = jnp.sum(cot.astype(F32), 0, keepdims=True)
    down[...], up[...] = tn(hid, d[...]), tn(cot, x[...])


def diagonal_other_kernel(d, x, down, up, ub_own, *refs):
    *refs, lo, hi, ub, part = refs
    half, rows = d.shape[0], ONE + TWO
    hid, slope, uw, dw = diagonal_of(refs, slice(half, 2 * half))
    cot = (nt(d[...], dw) * slope.astype(F32)).astype(BF16)
    part[...] = nn(cot, uw)
    ub[...] = ub_own[...] + jnp.sum(cot.astype(F32), 0, keepdims=True)
    dg = (down[...] + tn(hid, d[...])).astype(BF16)
    ug = (up[...] + tn(cot, x[...])).astype(BF16)
    for k in range(4):
        out, i = (lo, hi)[k // 2], k % 2
        for at, g in ((0, ug), (rows, dg)):
            out[i, at : at + ONE] = g[ONE * k : ONE * k + ONE]
            low = 4 * ONE + TWO * k
            out[i, at + ONE : at + rows] = g[low : low + TWO]


def ffn_back_diagonal(d0, d1, x0, x1, weights, own_kept, other_kept):
    half, width = x0.shape[0], 4 * (ONE + TWO)
    down, up, ub, own = call(
        diagonal_own_kernel,
        (shape((width, D), F32),) * 2 + (shape((1, width), F32), shape((half, D), F32)),
        (d0, x0, *weights, *own_kept),
        cost=est(1000, 1000),
    )
    lo, hi, ub, other = call(
        diagonal_other_kernel,
        (shape((2, width // 2, D)),) * 2 + (shape((1, width), F32), shape((half, D), F32)),
        (d1, x1, down, up, ub, *weights, *other_kept),
        cost=est(1000, 1000),
    )
    return [lo, hi], ub, (own, other)


def ffn_back(d0, d1, x0, x1, spot, weights, kept, sums, last):
    half, count = x0.shape[0], len(weights)
    if spot is None:
        outs, width = [shape(w.shape) for w in weights], weights[0].shape[0]
    else:
        width = 4 * (ONE + TWO)
        rows = ONE + TWO
        outs = [shape((2, 2 * rows, D)) if spot == 3 else shape((4, rows, D))] * 2
    *grads, ub, s0, s1 = call(
        functools.partial(ffn_back_kernel, not sums, spot, count),
        (
            *outs,
            shape((1, width), F32),
            shape((half, D), F32),
            shape((half, D), BF16 if last else F32),
        ),
        (d0, d1, x0, x1, *weights, *kept, *sums),
        cost=est(1000, 1000),
    )
    return grads, ub, (s0, s1)


def first_back_kernel(
    sum_two, part, got, normal, scale, small, *refs
):
    *refs, sum_one, low, sums = refs
    fc = sum_two[...] + part[...] + got[...].astype(F32)
    n = normal[...]
    so = norm_back(fc, n, scale[:, 0:1], small[3:4])
    sum_one[...] = so
    lo = so.astype(BF16)
    low[...] = lo
    sums[0:1] = jnp.sum(lo.astype(F32), 0, keepdims=True)
    sums[1:2] = jnp.sum(fc * n, 0, keepdims=True)
    sums[2:3] = jnp.sum(fc, 0, keepdims=True)
    if refs:
        add_first_kernel(*refs)


def first_back(sum_two, part, got, normal, scale, small, moved=()):
    n = sum_two.shape[0]
    outs = [shape(moved[i].shape) for i in (0, 3, 1, 4)] if moved else []
    *added, sum_one, low, sums = call(
        first_back_kernel,
        (*outs, shape((n, D), F32), shape((n, D)), shape((3, D), F32)),
        (sum_two, part, got, normal, scale, small, *moved),
        cost=est(1000, 1000),
        limit=8,
    )
    return added, sum_one, low, sums


def attend_back_kernel(sets, a0, a1, *refs):
    downs, refs = ((), refs) if sets == 1 else (refs[:2], refs[2:])
    far, outs, (in0, in1, sums), refs = refs[:9], refs[9 : 9 + sets], refs[9 + sets : 12 + sets], refs[12 + sets :]
    wp, v, probs, k, q, wr, x0, x1, ctx = far
    dctx, cots, grads, sems = refs
    copies = Copies(sems)
    for down, out in zip(downs, outs[3:]):
        copies.start(down, out.at[pl.ds(0, 4)])
    c, z, y, x = place_here()
    half = a0.shape[0]
    n = 2 * half
    wpo = wp[:, pl.ds(pl.multiple_of(c * 384, 128), 384)]
    dctx[0:half] = nn(a0[...], wpo).astype(BF16)
    dctx[half:n] = nn(a1[...], wpo).astype(BF16)
    lane = lax.broadcasted_iota(jnp.int32, (n, 128), 1)
    zero = jnp.zeros((n, 128), BF16)
    scale = HEAD_DIM**-0.5
    heads = [[], [], []]
    for pair in range(3):
        lanes = slice(128 * pair, 128 * pair + 128)
        qp, kp, vp, dp = q[:, lanes], k[:, lanes], v[:, lanes], dctx[:, lanes]
        dq = dk = dv = 0.0
        for e in range(2):
            mine = (lane < HEAD_DIM) if e == 0 else (lane >= HEAD_DIM)
            dh, kh, qh = jnp.where(mine, dp, zero), jnp.where(mine, kp, zero), jnp.where(mine, qp, zero)
            pr = probs[2 * pair + e]
            dv = dv + tn(pr, dh)
            pf = pr.astype(F32)
            t = pf * nt(dh, vp)
            ds = (t - pf * jnp.sum(t, -1, keepdims=True)).astype(BF16)
            dq = dq + nn(ds, kh)
            dk = dk + tn(ds, qh)
        for t, val in enumerate((dq * scale, dk * scale, dv)):
            val = val.astype(BF16)
            for e in range(2):
                hd = 2 * pair + e
                g, hh = hd // 3, hd % 3
                at = 640 * g + 192 * t + 64 * hh
                cots[:, at : at + 64] = val[:, 64 * e : 64 * e + 64]
            heads[t].append(val)
    for g in range(2):
        cots[:, 640 * g + 576 : 640 * g + 640] = jnp.zeros((n, 64), BF16)
    parts = [jnp.concatenate(heads[t], 1) for t in range(3)]
    for i, out in enumerate((in0, in1)):
        rws = slice(half * i, half * i + half)
        total = 0.0
        for t in range(3):
            total = total + nn(parts[t][rws], wr[384 * t : 384 * t + 384])
        out[...] = total.astype(out.dtype)
    for row, t in ((0, 0), (1, 2)):
        s = jnp.sum(parts[t].astype(F32), 0, keepdims=True)
        for g in range(2):
            sg = s[:, 192 * g : 192 * g + 192]
            sums[row : row + 1, 384 * g : 384 * g + 192] = jnp.where(c == 0, sg, 0.0)
            sums[row : row + 1, 384 * g + 192 : 384 * g + 384] = jnp.where(c == 1, sg, 0.0)
    for d in range(3):
        at = slice(256 * d, 256 * d + 256)
        full = tn(x0[:, at], cots[0:half]) + tn(x1[:, at], cots[half:n])
        pg = tn(a0[:, at], ctx[0:half]) + tn(a1[:, at], ctx[half:n])
        for g in range(2):
            grads[g, at, 0:576] = full[:, 640 * g : 640 * g + 576].astype(BF16)
            grads[g, at, 576:768] = pg[:, 192 * g : 192 * g + 192].astype(BF16)
    if sets == 1:
        copies.start(grads, outs[0])
    else:
        rows = outs[0].shape[1]
        for spot in (3, 2, 1, 0):
            g, yi = flip(x, spot % 2), flip(y, spot // 2)
            for kz in range(4):
                zi = flip(lax.rem(z, 2), kz % 2) + 2 * flip(lax.div(z, 2), kz // 2)
                at = pl.multiple_of((2 * zi + yi) * rows, rows)
                dst = outs[spot].at[kz] if spot < 3 else outs[3 + kz // 2].at[4 + kz % 2]
                copies.start(grads.at[g, pl.ds(at, rows)], dst)
    copies.wait()


def attend_back(downs, a0, a1, x0, x1, wp, wr, q, k, v, ctx, probs):
    half = a0.shape[0]
    n = 2 * half
    sets = (shape((2, D, D)),)
    if downs:
        sets = (shape((4, 96, D)),) * 3 + (shape((6, 96, D)),) * 2
    far = (wp, v, probs, k, q, wr, x0, x1, ctx)
    return call(
        functools.partial(attend_back_kernel, len(sets)),
        (*sets, shape((half, D), F32), shape((half, D)), shape((2, D), F32)),
        (a0, a1, *downs, *far),
        scratch=[
            pltpu.VMEM((n, 384), BF16),
            pltpu.VMEM((n, 1280), BF16),
            pltpu.VMEM((2, D, D), BF16),
        ],
        cost=est(8e9, 14e6),
        limit=16,
        far_out=range(len(sets)),
        sems=20,
    )


def local(
    inputs,
    bucket,
    lengths,
    qkv_weight,
    query_bias,
    value_bias,
    proj_weight,
    proj_bias,
    first_gain,
    first_shift,
    up_weight,
    up_bias,
    down_weight,
    down_bias,
    second_gain,
    second_shift,
    cotangent,
):
    head_count = lax.axis_size("head")
    batch_count = lax.axis_size("batch")
    devices = head_count * batch_count
    direct = batch_count == 8
    b = lax.axis_index("batch")
    h = lax.axis_index("head")
    me = b * head_count + h
    x, c = h // 2, h % 2
    z, y = b // 2, b % 2
    wq, wp, wf = 3 * D // devices, D // devices, FF // devices

    vectors = [
        query_bias,
        value_bias,
        proj_bias,
        first_gain,
        first_shift,
        down_bias,
        second_gain,
        second_shift,
    ]
    if direct:
        a_shard, one_a, one_b, two = pack(
            qkv_weight.T, proj_weight.T, up_weight.T, down_weight, up_bias, vectors
        )
    else:
        small = lax.dynamic_update_slice(
            jnp.zeros((16, D), BF16), jnp.stack(vectors), (0, me * wp)
        )
        per_row = D // wf
        small = lax.dynamic_update_slice(
            small, up_bias[None, :], (8 + me // per_row, (me % per_row) * wf)
        )
        proj_t = proj_weight.T.reshape(wp, 2, 2, 192).transpose(0, 2, 1, 3).reshape(wp, D)
        a_shard = jnp.concatenate([qkv_weight.T, proj_t, small])
    other_in = core_swap(inputs)
    k = jnp.arange(batch_count * 2)
    if direct:
        a_z = z_line(a_shard)
        two = after(two, a_z[1])
        two_x, two_y = x_swap(two), y_swap(two)
        two_d = jnp.concatenate([x_swap(two_y[:TWO]), y_swap(two_x[TWO:])])
        two_lo = jnp.stack([two, two_x, two_y, two_d])
        a_z, two_lo, other_in = lax.optimization_barrier((jnp.stack(a_z), two_lo, other_in))
        one_a = after(one_a, a_z)
        near = z_swap(jnp.concatenate([one_a, two_lo.reshape(8 * TWO, D)]), 1)
        one_a = [one_a, None, z_swap(one_a, 2), z_swap(one_a, 3)]
        a_x, a_y = x_swap(a_z), y_swap(a_z)
        a_x, a_y, near, one_a[2], one_a[3] = lax.optimization_barrier(
            (a_x, a_y, near, one_a[2], one_a[3])
        )
        one_a[1], two_hi = near[:FIRST], near[FIRST:].reshape(two_lo.shape)
        one_b = z_line(after(one_b, near))
        a_d = [x_swap(a_y[:2]), y_swap(a_x[2:])]
        one_b, a_d = lax.optimization_barrier((one_b, a_d))
        a_own = [a_z, a_x, a_y, *a_d]
        one_z = jnp.stack([jnp.concatenate(pair) for pair in zip(one_a, one_b)])
        one_z, a_own = lax.optimization_barrier((one_z, a_own))
        one_x, one_y = x_swap(one_z), y_swap(one_z)
        a_swapped = [core_swap(v) for v in a_own]
        two_far = z_swap(jnp.concatenate([two_lo, two_hi]), 2)
        one_x, one_y, two_far = lax.optimization_barrier((one_x, one_y, two_far))
        one_d = [x_swap(one_y[:2]), y_swap(one_x[2:])]
        twos = [two_lo, two_hi, two_far]
        ctx_own, ctx_other, q, kk, v, ctx, probs, wr, ub_all, proj_w, small_all = attend(
            bucket, lengths, inputs, other_in, (*a_own, *a_swapped), wq, wp
        )
        f_all = [[one_z], [one_x], [one_y], twos, one_d]
    else:
        a_all = lax.all_gather(a_shard, ("batch", "head"), axis=0)
        qkv_all = a_all[:, :wq].reshape(2, 2, 576, D)
        qkv_w = lax.dynamic_index_in_dim(qkv_all, c, 1, keepdims=False).reshape(2 * 576, D)
        proj_w = a_all[:, wq : wq + wp].reshape(D, D)
        small_all = jnp.sum(a_all[:, wq + wp :].astype(F32), 0)
        ctx_own, ctx_other, q, kk, v, ctx, probs, wr = attend(
            bucket, lengths, inputs, other_in, (qkv_w, small_all)
        )
        f_shard = jnp.concatenate([up_weight.T, down_weight])
        f_all = [
            (v[:, :wf].reshape(-1, D), v[:, wf:].reshape(-1, D)) for v in gather_any(f_shard)
        ]
        owner = (k % batch_count) * 4 + (x ^ (k // batch_count)) * 2 + c
    if not direct:
        spread = (owner[None, :] == jnp.arange(devices)[:, None]).astype(F32)
        ub_all = tn(spread, small_all[8:12].reshape(devices, wf)).reshape(1, FF // 2)

    ctx_in = core_swap(ctx_other)
    first_low, first, first_n, first_r = first_norm(inputs, ctx_own, ctx_in, proj_w, small_all)
    first_in = core_swap(first_low)
    sums = ()
    kept = []
    starts = (0, FF // 4)
    if direct:
        starts = (0, 4 * ONE, 8 * ONE, 16 * ONE, 12 * ONE)
    for weights, at in zip(f_all, starts):
        width = FF // 4
        if direct:
            width = 16 * TWO if len(kept) == 3 else 4 * ONE
        if direct and len(kept) == 4:
            ub = ub_all[:, at : at + width]
            hid1, slope1, part1 = ffn_half(first_in, ub, weights, sums[1], BF16)
            hid0, slope0, part0 = ffn_half(first_low, ub, weights, sums[0], F32)
            kept.append(((hid0, slope0), (hid1, slope1)))
            sums = (part0, part1)
            continue
        hid, slope, *sums = ffn(
            first_low,
            first_in,
            ub_all[:, at : at + width],
            weights,
            sums,
            len(kept) == len(f_all) - 1,
        )
        kept.append((hid, slope))
    down_low, sum_two, second_n = second_norm(
        bucket, lengths, first, sums[0], core_swap(sums[1]), small_all, cotangent
    )
    down_in = core_swap(down_low)

    sums = ()
    f_parts, ub_parts = [], []
    if direct:
        for spot, i in ((3, 4), (2, 2), (1, 1), (0, 0)):
            weights = (*f_all[i], *twos)
            rows = (down_low, down_in, first_low, first_in)
            if spot == 3:
                own, other = [(*half, *kept[3]) for half in kept[i]]
                grads, ub, sums = ffn_back_diagonal(*rows, weights, own, other)
            else:
                grads, ub, sums = ffn_back(
                    *rows, spot, weights, (*kept[i], *kept[3]), sums, spot == 0
                )
            f_parts.append(grads)
            ub_parts.insert(0, ub)
    else:
        for weights, pair in zip(f_all, kept):
            grads, ub, sums = ffn_back(
                down_low,
                down_in,
                first_low,
                first_in,
                None,
                weights,
                pair,
                sums,
                len(f_parts) == len(f_all) - 1,
            )
            f_parts.append(grads)
            ub_parts.append(ub)
    part_own, part_other = sums
    layer_out, sums_two = second_rest(
        bucket, lengths, after(second_n, part_other), small_all, cotangent, down_low
    )
    sum_two = after(sum_two, sums_two)
    moved = ()
    if direct:
        (d_lo, d_hi), y_sets, x_sets, z_sets = f_parts
        moved = (*x_sets, y_swap(d_hi), *y_sets, x_swap(d_lo))
    added, sum_one, attn_low, sums_one = first_back(
        sum_two, part_own, core_swap(part_other), first_n, first_r, small_all, moved
    )
    attn_in = core_swap(attn_low)
    *a_grads, in_own, in_other, sums_zero = attend_back(
        added[2:],
        attn_low,
        attn_in,
        inputs,
        other_in,
        proj_w,
        wr,
        q,
        kk,
        v,
        ctx,
        probs,
    )
    in_got = core_swap(in_other)
    inputs_grad = (sum_one + in_own + in_got).astype(BF16)

    if direct:
        up_sets = scatter_xy(z_sets[0], *added[:2])
        a_zz, a_xx, a_yy, by_x, by_y = a_grads
        by_x, by_y, up_sets, in_got = lax.optimization_barrier((by_x, by_y, up_sets, in_got))
        by_x, by_y = x_swap(by_x), y_swap(by_y)
        up_mine, up_others = combine(*up_sets)
        sums_zero = after(sums_zero, up_others)
        terms = exchange_terms(sums_zero, sums_one, sums_two, ub_parts, devices)
        terms = lax.all_to_all(terms, ("batch", "head"), split_axis=0, concat_axis=0, tiled=True)
        up_others = scatter_z(up_others)
        by_x, by_y, up_others, terms, _ = lax.optimization_barrier(
            (by_x, by_y, up_others, terms, inputs_grad)
        )
        a_xy, down_mine, down_others = turn(a_xx, a_yy, z_sets[1], by_x, by_y)
        a_sets = scatter_xy(a_zz, *a_xy)
        down_others = scatter_z(down_others)
        a_sets, down_others = lax.optimization_barrier((a_sets, down_others))
        a_mine, a_others = combine_last(*a_sets)
        a_others = scatter_z(a_others)
        up_grad, down_grad = finish_ffn((up_mine, *up_others), (down_mine, *down_others))
        up_grad = up_grad.T
        terms = jnp.sum(terms.astype(F32), 0)
        packed = jnp.concatenate([terms[:, :wp].reshape(-1), terms[0, wp : wp + wf]])
        qkv_grad, proj_grad = finish_attend((a_mine, *a_others))
    else:
        vecs = jnp.concatenate([sums_zero, sums_one, sums_two])
        vecs = vecs.reshape(8, devices, wp).transpose(1, 0, 2).reshape(devices, 8 * wp)
        ubias = jnp.concatenate(ub_parts).reshape(batch_count * 2, wf)
        ubias = lax.dot_general(
            spread, ubias, (((1,), (0,)), ((), ())), precision=lax.Precision.HIGHEST
        )
        packed = jnp.concatenate([vecs, ubias], 1)
        packed = lax.all_to_all(
            packed, ("batch", "head"), split_axis=0, concat_axis=0, tiled=True
        )
        packed = jnp.sum(packed, 0)
        wb = D // batch_count
        a_grads = a_grads[0].reshape(2, batch_count, wb, D)
        a_mine = scatter_any(
            [
                lax.dynamic_index_in_dim(a_grads, x, 0, keepdims=False),
                lax.dynamic_index_in_dim(a_grads, 1 - x, 0, keepdims=False),
            ]
        )
        f_mine = scatter_any(
            [
                jnp.concatenate(
                    [ug.reshape(batch_count, wf, D), dg.reshape(batch_count, wf, D)], 1
                )
                for ug, dg in f_parts
            ]
        )
        qkv_grad = a_mine[:, :576].reshape(wb, 3, 3, HEAD_DIM).transpose(0, 2, 1, 3)
        qkv_grad = qkv_grad.reshape(wb, 576)
        proj_grad = a_mine[:, 576:].T
        up_grad, down_grad = f_mine[:wf].T, f_mine[wf:]
    qb_g, vb_g, pb_g, fg_g, fs_g, db_g, sg_g, ss_g = [
        packed[i * wp : (i + 1) * wp] for i in range(8)
    ]
    return (
        layer_out,
        inputs_grad,
        qkv_grad,
        qb_g,
        vb_g,
        proj_grad,
        pb_g,
        fg_g,
        fs_g,
        up_grad,
        packed[8 * wp :],
        down_grad,
        db_g,
        sg_g,
        ss_g,
    )


def solution(mesh):
    both = ("batch", "head")
    in_specs = (
        P(both, None),
        P("batch"),
        P("batch", None),
        P(None, both),
        P(both),
        P(both),
        P(None, both),
        P(both),
        P(both),
        P(both),
        P(None, both),
        P(both),
        P(both, None),
        P(both),
        P(both),
        P(both),
        P(both, None),
    )
    out_specs = (
        P(both, None),
        P(both, None),
        P("batch", "head"),
        P(both),
        P(both),
        P("head", "batch"),
        P(both),
        P(both),
        P(both),
        P(None, both),
        P(both),
        P(both, None),
        P(both),
        P(both),
        P(both),
    )
    return jax.shard_map(local, mesh=mesh, in_specs=in_specs, out_specs=out_specs, check_vma=False)
```

```python
import functools

import jax
import jax.numpy as jnp
from jax import lax
from jax.experimental import pallas as pl
from jax.experimental.pallas import tpu as pltpu
from jax.sharding import PartitionSpec as P

D = 768
HEADS = 12
HEAD_DIM = 64
FF = 3072
BIG = 512
SMALL = 128
UNITS = 4
NORM_EPS = 1e-12
F32 = jnp.float32
BF16 = jnp.bfloat16

ONE, TWO = 80, 16
FIRST = 104

CORE = [(i, i ^ 1) for i in range(4)]
XPAIR = [(i, i ^ 2) for i in range(4)]
YPAIR = [(i, i ^ 1) for i in range(8)]
ZPAIR = [[(i, i ^ (2 * k)) for i in range(8)] for k in range(4)]


def core_swap(v):
    return lax.ppermute(v, "head", CORE)


def x_swap(v):
    return lax.ppermute(v, "head", XPAIR)


def y_swap(v):
    return lax.ppermute(v, "batch", YPAIR)


def z_swap(v, k):
    return lax.ppermute(v, "batch", ZPAIR[k])


def after(value, other):
    return lax.optimization_barrier((value, other))[0]


def nt(a, b, out=F32):
    return lax.dot_general(a, b, (((1,), (1,)), ((), ())), preferred_element_type=F32).astype(out)


def nn(a, b, out=F32):
    return lax.dot_general(a, b, (((1,), (0,)), ((), ())), preferred_element_type=F32).astype(out)


def tn(a, b, out=F32):
    return lax.dot_general(a, b, (((0,), (0,)), ((), ())), preferred_element_type=F32).astype(out)


def z_line(shard):
    return [shard] + [z_swap(shard, k) for k in (1, 2, 3)]


def gather_four(z):
    x, y = x_swap(z), y_swap(z)
    return [z, x, y, x_swap(y[:2]), y_swap(x[2:])]


def gather_any(shard):
    whole = lax.all_gather(shard, "batch", axis=0)
    return [whole, x_swap(whole)]


def scatter_xy(z, x, y):
    return z, x_swap(x), y_swap(y)


def scatter_z(others):
    return [z_swap(others[k - 1], k) for k in (1, 2, 3)]


def scatter_any(parts):
    total = parts[0].astype(F32) + x_swap(parts[1]).astype(F32)
    return lax.psum_scatter(total, "batch", scatter_dimension=0, tiled=False)


def est(flops, moved, trans=0):
    return pl.CostEstimate(flops=int(flops), bytes_accessed=int(moved), transcendentals=int(trans))


def call(kernel, out_shape, operands, scratch=(), cost=None, limit=16, far_in=(), far_out=(), sems=0):
    vmem = pl.BlockSpec(memory_space=pltpu.VMEM)
    hbm = pl.BlockSpec(memory_space=pltpu.HBM)
    smem = pl.BlockSpec(memory_space=pltpu.SMEM)
    ins = [hbm if i in far_in else vmem for i in range(len(operands))]
    ins = [smem if v.dtype == jnp.int32 else spec for spec, v in zip(ins, operands)]
    outs = [hbm if i in far_out else vmem for i in range(len(out_shape))]
    scratch = list(scratch) + ([pltpu.SemaphoreType.DMA((sems,))] if sems else [])
    operands = [
        pltpu.with_memory_space_constraint(v, pltpu.HBM) if i in far_in else v
        for i, v in enumerate(operands)
    ]
    out_shape = [
        pltpu.HBM(v.shape, v.dtype) if i in far_out else v for i, v in enumerate(out_shape)
    ]
    return pl.pallas_call(
        kernel,
        out_shape=out_shape,
        in_specs=ins,
        out_specs=outs,
        scratch_shapes=scratch,
        compiler_params=pltpu.CompilerParams(vmem_limit_bytes=limit << 20),
        cost_estimate=cost,
    )(*operands)


class Copies:
    def __init__(self, sems):
        self.sems, self.used, self.open = sems, 0, []

    def start(self, src, dst):
        copy = pltpu.make_async_copy(src, dst, self.sems.at[self.used])
        self.used += 1
        copy.start()
        self.open.append(copy)
        return copy

    def wait(self, *copies):
        for copy in copies or list(self.open):
            copy.wait()
            self.open.remove(copy)


def add_low(a, b):
    return (a.astype(F32) + b.astype(F32)).astype(BF16)


def shape(dims, dtype=BF16):
    return jax.ShapeDtypeStruct(dims, dtype)


def add_first_kernel(x_up, x_down, for_x, y_up, y_down, for_y, *outs):
    half = x_up.shape[1]
    for i, (x, y) in enumerate(((x_up, y_up), (x_down, y_down))):
        rows = slice(half * i, half * i + half)
        x_out, y_out = outs[2 * i : 2 * i + 2]
        x_out[0:2] = x[0:2]
        y_out[2:4] = y[2:4]
        for k in range(2):
            x_out[2 + k] = add_low(x[2 + k], for_x[k, rows])
            y_out[k] = add_low(y[k], for_y[k, rows])


def combine_kernel(z, x, y, *refs):
    outs, (mine, low, sems) = refs[:4], refs[4:]
    sum_places(z, x, y, outs, mine, low, Copies(sems)).wait()


def sum_places(z, x, y, outs, mine, low, copies, arrived=None):
    for i, k in enumerate((1, 2, 3, 0)):
        if arrived:
            copies.wait(*arrived[i])
        total = z[k].astype(F32) + x[k].astype(F32) + y[k].astype(F32)
        if k == 0:
            mine[...] = total
            copies.start(mine, outs[0])
        else:
            low[k - 1] = total.astype(BF16)
            copies.start(low.at[k - 1], outs[k])
    return copies


def combine(z, x, y):
    rows = z.shape[1]
    mine, *others = call(
        combine_kernel,
        (shape((rows, D), F32),) + (shape((rows, D)),) * 3,
        (z, x, y),
        scratch=[pltpu.VMEM((rows, D), F32), pltpu.VMEM((3, rows, D), BF16)],
        cost=est(1000, 1000),
        limit=8,
        far_out=range(4),
        sems=4,
    )
    return mine, others


def combine_last_kernel(z, x, y, *outs):
    for k, out in enumerate(outs):
        total = z[k].astype(F32) + x[k].astype(F32) + y[k].astype(F32)
        out[...] = total.astype(out.dtype)


def combine_last(z, x, y):
    rows = z.shape[1]
    mine, *others = call(
        combine_last_kernel,
        (shape((rows, D), F32),) + (shape((rows, D)),) * 3,
        (z, x, y),
        cost=est(1000, 1000),
        limit=8,
    )
    return mine, others


def turn_kernel(x, y, z, by_x_far, by_y_far, x_out, y_out, *refs):
    outs, (by_x, by_y, mine, low, sems) = refs[:4], refs[4:]
    copies = Copies(sems)
    arrived = []
    for k in (1, 2, 3, 0, 4):
        rows = pl.ds(k, 1 if k < 4 else 2)
        arrived.append(
            (
                copies.start(by_x_far.at[rows], by_x.at[rows]),
                copies.start(by_y_far.at[rows], by_y.at[rows]),
            )
        )
    sum_places(z, by_x, by_y, outs, mine, low, copies, arrived)
    copies.wait(*arrived[4])
    y_out[0:2] = add_low(y[0:2], by_x[4:6])
    y_out[2:4] = y[2:4]
    x_out[0:2] = x[0:2]
    x_out[2:4] = add_low(x[2:4], by_y[4:6])
    copies.wait()


def turn(x, y, z, by_x, by_y):
    rows = z.shape[1]
    x, y, mine, *others = call(
        turn_kernel,
        (shape(x.shape), shape(y.shape), shape((rows, D), F32)) + (shape((rows, D)),) * 3,
        (x, y, z, by_x, by_y),
        scratch=[pltpu.VMEM(by_x.shape, BF16)] * 2
        + [pltpu.VMEM((rows, D), F32), pltpu.VMEM((3, rows, D), BF16)],
        cost=est(1000, 1000),
        limit=8,
        far_in=(3, 4),
        far_out=range(2, 6),
        sems=14,
    )
    return (x, y), mine, others


def total_of(refs):
    return refs[0][...] + refs[1][...].astype(F32) + refs[2][...].astype(F32) + refs[3][...].astype(F32)


def finish_attend_kernel(mine, one, two, three, qkv, proj):
    total = total_of((mine, one, two, three))
    for hh in range(3):
        for t in range(3):
            at, to = 192 * t + 64 * hh, 192 * hh + 64 * t
            qkv[:, to : to + 64] = total[:, at : at + 64]
    proj[...] = total[:, 576:].T


def finish_attend(parts):
    rows = parts[0].shape[0]
    return call(
        finish_attend_kernel,
        (shape((rows, 576), F32), shape((192, rows), F32)),
        tuple(parts),
        cost=est(8 * rows * D, 16 * rows * D),
        limit=8,
    )


def finish_ffn_kernel(*refs):
    up, down = refs[8:]
    up[...], down[...] = total_of(refs[0:4]), total_of(refs[4:8])


def finish_ffn(ups, downs):
    dims = ups[0].shape
    return call(
        finish_ffn_kernel,
        (shape(dims, F32), shape(dims, F32)),
        (*ups, *downs),
        cost=est(1000, 1000),
        limit=8,
    )


def exchange_kernel(zero, one, two, *refs):
    ubs, out = refs[:4], refs[4]
    vecs = jnp.concatenate([zero[...], one[...], two[...]])
    width = D // out.shape[0]
    vecs = vecs.astype(BF16)
    out[...] = jnp.zeros(out.shape, BF16)
    for i in range(out.shape[0]):
        out[i, 0:8, 0:width] = vecs[:, width * i : width * i + width]
    for spot in range(4):
        for kz in range(4):
            to, ub = slot_of(spot, kz), ubs[spot][...].astype(BF16)
            out[to, 0:1, 24 : 24 + ONE] = ub[:, ONE * kz : ONE * kz + ONE]
            at = 4 * ONE + TWO * kz
            out[to, 0:1, 24 + ONE : 24 + ONE + TWO] = ub[:, at : at + TWO]


def exchange_terms(zero, one, two, ubs, devices):
    return call(
        exchange_kernel,
        (shape((devices, 8, 128)),),
        (zero, one, two, *ubs),
        cost=est(1000, 1000),
        limit=8,
    )[0]


def flip(a, bit):
    return a + bit - 2 * a * bit


def pack_kernel(qkv_in, proj_in, up_in, down_in, bias_in, *refs):
    vectors_in, (a_out, one_a, one_b, two, a, p, f, bias, vectors, sems) = refs[:8], refs[8:]
    rows_q, rows_p, half = qkv_in.shape[0], proj_in.shape[0], down_in.shape[0]
    copies = Copies(sems)
    copies.start(qkv_in, a.at[pl.ds(0, rows_q)])
    copies.start(proj_in, p)
    copies.start(up_in, f.at[pl.ds(0, half)])
    copies.start(down_in, f.at[pl.ds(half, half)])
    copies.start(bias_in, bias)
    for i, r in enumerate(vectors_in):
        copies.start(r, vectors.at[i])
    width = vectors.shape[2]
    b, h = lax.axis_index("batch"), lax.axis_index("head")
    me = b * lax.axis_size("head") + h
    copies.wait()
    v = jnp.concatenate([vectors[i] for i in range(8)]).astype(F32)
    v = jnp.concatenate([v] * (D // width), 1)
    lane = lax.broadcasted_iota(jnp.int32, (8, D), 1)
    mine = jnp.logical_and(lane >= me * width, lane < me * width + width)
    v = jnp.where(mine, v, 0.0)
    gap = jnp.zeros((1, D // 2 - half), F32)
    none = jnp.zeros((1, D // 2), F32)
    row = bias[...].astype(F32)
    early = jnp.concatenate([none, row, gap], 1)
    late = jnp.concatenate([row, gap, none], 1)
    extra = jnp.where(me < lax.axis_size("batch") * lax.axis_size("head") // 2, early, late)
    v = v + jnp.concatenate([extra, jnp.zeros((7, D), F32)])
    a_out[0:rows_q] = a[0:rows_q]
    q = p[...]
    a_out[rows_q : rows_q + rows_p] = jnp.concatenate(
        [q[:, 192 * i : 192 * i + 192] for i in (0, 2, 1, 3)], 1
    )
    a_out[rows_q + rows_p :] = v.astype(BF16)
    one = jnp.concatenate([f[0:ONE], f[half : half + ONE]])
    one_a[...], one_b[...] = one[0:FIRST], one[FIRST:]
    two[0:TWO], two[TWO:] = f[ONE:half], f[half + ONE :]


def pack(qkv, proj, up, down, bias, vectors):
    rows, half = qkv.shape[0] + proj.shape[0] + 8, down.shape[0]
    return call(
        pack_kernel,
        (
            shape((rows, D)),
            shape((FIRST, D)),
            shape((2 * ONE - FIRST, D)),
            shape((2 * TWO, D)),
        ),
        (qkv, proj, up, down, bias[None], *[v[None] for v in vectors]),
        scratch=[
            pltpu.VMEM((rows, D), BF16),
            pltpu.VMEM(proj.shape, BF16),
            pltpu.VMEM((2 * half, D), BF16),
            pltpu.VMEM((1,) + bias.shape, BF16),
            pltpu.VMEM((8, 1) + vectors[0].shape, BF16),
        ],
        cost=est(1000, 1000),
        limit=8,
        far_in=range(13),
        sems=13,
    )


def place_here():
    b, h = lax.axis_index("batch"), lax.axis_index("head")
    return lax.rem(h, 2), lax.div(b, 2), lax.rem(b, 2), lax.div(h, 2)


def live_units(bucket, lengths):
    x = place_here()[3]
    kind, first = bucket[x], lengths[x, 0]
    units = []
    for u in range(UNITS):
        far = jnp.clip(first - SMALL * u, 0, SMALL)
        units.append(jnp.where(kind == 1, far, lengths[x, u]))
    return kind, units


def place_of(index, c):
    return jnp.bitwise_xor(index, c * (BIG // 2))


def live_of(place, units):
    unit = lax.shift_right_logical(place, 7)
    inner = jnp.bitwise_and(place, SMALL - 1)
    count = jnp.where(
        unit < 2, jnp.where(unit == 0, units[0], units[1]), jnp.where(unit == 2, units[2], units[3])
    )
    return inner < count


def heads_of(row, c):
    parts = []
    for g in range(2):
        lo = row[:, 384 * g : 384 * g + 192]
        hi = row[:, 384 * g + 192 : 384 * g + 384]
        parts.append(jnp.where(c == 0, lo, hi))
    return jnp.concatenate(parts, 1)


def fetch_shards(copies, sources, slots):
    c, z, y, x = place_here()
    zl, zh = lax.rem(z, 2), lax.div(z, 2)
    for swapped in range(2):
        cc = c if swapped == 0 else 1 - c
        zs, xs, ys, xa, xb = sources[5 * swapped : 5 * swapped + 5]
        for kx, ky, pair in ((0, 0, (zs,)), (1, 0, (xs,)), (0, 1, (ys,)), (1, 1, (xa, xb))):
            j = flip(y, ky) * 4 + flip(x, kx) * 2 + cc
            for kz in range(4):
                src = pair[0].at[kz] if len(pair) == 1 else pair[kz // 2].at[kz % 2]
                zi = flip(zl, kz % 2) + 2 * flip(zh, kz // 2)
                copies.start(src, slots.at[zi * 8 + j])


def slot_of(spot, kz):
    c, z, y, x = place_here()
    zi = flip(lax.rem(z, 2), kz % 2) + 2 * flip(lax.div(z, 2), kz // 2)
    return zi * 8 + flip(y, spot // 2) * 4 + flip(x, spot % 2) * 2 + c


def bias_order(slots, row, out):
    for spot in range(4):
        for kz in range(4):
            i = slot_of(spot, kz)
            b = slots[i, row : row + 1].astype(F32)
            b = jnp.where(i < 16, b[:, D // 2 : D // 2 + 96], b[:, 0:96])
            at = 4 * ONE * spot + ONE * kz
            out[:, at : at + ONE] = b[:, 0:ONE]
            at = 16 * ONE + 4 * TWO * spot + TWO * kz
            out[:, at : at + TWO] = b[:, ONE:]


def attend_kernel(rows_q, rows_p, bucket, lengths, x0, x1, *refs):
    sources = 10 if rows_q else 2
    weights, refs = refs[:sources], refs[sources:]
    (ctx0, ctx1, q, k, v, ctx, probs, wr), refs = refs[:8], refs[8:]
    if rows_q:
        (ub_out, wp, small, mask, xs, slots, sems) = refs
    else:
        (mask, xs, w, small, sems) = refs
    copies = Copies(sems)
    c = place_here()[0]
    kind, units = live_units(bucket, lengths)
    half = x0.shape[0]
    copies.start(x0, xs.at[0:half])
    copies.start(x1, xs.at[half : 2 * half])
    if rows_q:
        fetch_shards(copies, weights, slots)
    else:
        copies.start(weights[0], w)
        copies.start(weights[1], small)
    rows = lax.broadcasted_iota(jnp.int32, (BIG, BIG), 0)
    cols = lax.broadcasted_iota(jnp.int32, (BIG, BIG), 1)
    prow, pcol = place_of(rows, c), place_of(cols, c)
    same = jnp.logical_or(
        kind == 1, lax.shift_right_logical(prow, 7) == lax.shift_right_logical(pcol, 7)
    )
    mask[...] = jnp.where(jnp.logical_and(same, live_of(pcol, units)), 0.0, -1e30)
    copies.wait()
    if rows_q:
        for g in range(2):
            cuts = jnp.concatenate([slots[16 * g + 8 * c + j, 0:rows_q] for j in range(8)])
            for t in range(3):
                for hh in range(3):
                    src, dst = (hh * 3 + t) * HEAD_DIM, (t * 6 + g * 3 + hh) * HEAD_DIM
                    wr[dst : dst + HEAD_DIM] = cuts[src : src + HEAD_DIM]
        lane = lax.broadcasted_iota(jnp.int32, (8, D), 1)
        small[...] = sum(
            jnp.where(
                jnp.logical_and(lane >= rows_p * i, lane < rows_p * i + rows_p),
                slots[i, rows_q + rows_p :].astype(F32),
                0.0,
            )
            for i in range(32)
        )
    else:
        for t in range(3):
            for hd in range(6):
                src = ((hd // 3) * 9 + (hd % 3) * 3 + t) * HEAD_DIM
                dst = (t * 6 + hd) * HEAD_DIM
                wr[dst : dst + HEAD_DIM] = w[src : src + HEAD_DIM]
    biases = (heads_of(small[0:1], c), None, heads_of(small[1:2], c))
    for t, ref in enumerate((q, k, v)):
        val = nt(xs[...], wr[384 * t : 384 * t + 384])
        if biases[t] is not None:
            val = val + biases[t]
        ref[...] = val.astype(BF16)
    if rows_q:
        for i in range(32):
            wp[rows_p * i : rows_p * i + rows_p] = slots[i, rows_q : rows_q + rows_p]
        bias_order(slots, rows_q + rows_p, ub_out)
    lane = lax.broadcasted_iota(jnp.int32, (half, 128), 1)
    for pair in range(3):
        lanes = slice(128 * pair, 128 * pair + 128)
        kp, vp = k[:, lanes], v[:, lanes]
        for i, near in enumerate((ctx0, ctx1)):
            rws = slice(half * i, half * i + half)
            qp = q[rws, lanes] * jnp.asarray(HEAD_DIM**-0.5, BF16)
            outs = []
            for e in range(2):
                mine = (lane < HEAD_DIM) if e == 0 else (lane >= HEAD_DIM)
                s = nt(jnp.where(mine, qp, jnp.zeros_like(qp)), kp) + mask[rws]
                ex = jnp.exp(s - jnp.max(s, -1, keepdims=True))
                pr = (ex * (1.0 / jnp.sum(ex, -1, keepdims=True))).astype(BF16)
                probs[2 * pair + e, rws] = pr
                outs.append(nn(pr, vp))
            val = jnp.where(lane < HEAD_DIM, outs[0], outs[1]).astype(BF16)
            ctx[rws, lanes] = val
            near[:, lanes] = val


def attend(bucket, lengths, x0, x1, weights, rows_q=0, rows_p=0, rows_s=16):
    rows_s = 8 if rows_q else rows_s
    half = x0.shape[0]
    n = 2 * half
    direct = rows_q > 0
    outs = [
        shape((half, 384)),
        shape((half, 384)),
        shape((n, 384)),
        shape((n, 384)),
        shape((n, 384)),
        shape((n, 384)),
        shape((6, n, n)),
        shape((1152, D)),
    ]
    scratch = [pltpu.VMEM((n, n), F32), pltpu.VMEM((n, D), BF16)]
    if direct:
        outs += [shape((1, FF // 2), F32), shape((D, D)), shape((rows_s, D), F32)]
        scratch += [pltpu.VMEM((32, rows_q + rows_p + rows_s, D), BF16)]
    else:
        scratch += [pltpu.VMEM((1152, D), BF16), pltpu.VMEM((rows_s, D), F32)]
    operands = (bucket, lengths, x0, x1, *weights)
    return call(
        functools.partial(attend_kernel, rows_q, rows_p),
        outs,
        operands,
        scratch=scratch,
        cost=est(1000, 1000),
        limit=32,
        far_in=range(2, len(operands)),
        sems=50,
    )


def norm(values):
    center = values - jnp.mean(values, -1, keepdims=True)
    spread = jnp.mean(center * center, -1, keepdims=True)
    scale = lax.rsqrt(spread + NORM_EPS)
    return center * scale, scale


def norm_back(cot, normal, scale, gain):
    w = cot * gain
    return scale * (
        w - jnp.mean(w, -1, keepdims=True) - normal * jnp.mean(w * normal, -1, keepdims=True)
    )


def first_kernel(x, ctx_own, ctx_in, wp, small, low, first, normal, scale):
    c = place_here()[0]
    mine = pl.multiple_of(c * 384, 128)
    theirs = pl.multiple_of((1 - c) * 384, 128)
    attn = nt(ctx_own[...], wp[:, pl.ds(mine, 384)]) + nt(ctx_in[...], wp[:, pl.ds(theirs, 384)])
    n, r = norm(x[...].astype(F32) + attn + small[2:3])
    normal[...] = n
    out = n * small[3:4] + small[4:5]
    first[...] = out
    low[...] = out.astype(BF16)
    scale[...] = jnp.broadcast_to(r, scale.shape)


def first_norm(x, ctx_own, ctx_in, wp, small):
    n = x.shape[0]
    return call(
        first_kernel,
        (shape((n, D)), shape((n, D), F32), shape((n, D), F32), shape((n, 128), F32)),
        (x, ctx_own, ctx_in, wp, small),
        cost=est(1000, 1000),
        limit=8,
    )


def ffn_weights(refs):
    if len(refs[0].shape) == 2:
        return refs[0][...], refs[1][...]
    return stacked(ones_of(refs) if refs[0].shape[1] == 2 * ONE else twos_of(refs, range(4)))


def ones_of(refs):
    return [(r, i) for r in refs for i in range(r.shape[0])]


def twos_of(refs, spots):
    along_z = [(r, i) for r in refs for i in range(0, r.shape[0], 4)]
    return [(r, i + spot) for spot in spots for r, i in along_z]


def stacked(blocks):
    up = jnp.concatenate([r[i, 0 : r.shape[1] // 2] for r, i in blocks])
    down = jnp.concatenate([r[i, r.shape[1] // 2 :] for r, i in blocks])
    return up, down


def ffn_kernel(first, count, x0, x1, ub, *refs):
    far, refs = refs[:count], refs[count:]
    if first:
        in0 = in1 = None
    else:
        (in0, in1), refs = refs[:2], refs[2:]
    hid, slope, out0, out1 = refs
    half = x0.shape[0]
    uw, dw = ffn_weights(far)
    for i, (xr, before, out) in enumerate(((x0, in0, out0), (x1, in1, out1))):
        rws = slice(half * i, half * i + half)
        up = nt(xr[...], uw) + ub[...]
        phi = 0.5 + 0.5 * lax.erf(up * (2.0**-0.5))
        hd = (up * phi).astype(BF16)
        hid[rws] = hd
        slope[rws] = (phi + up * jnp.exp(-0.5 * up * up) * 0.3989422804014327).astype(BF16)
        part = nn(hd, dw)
        part = part if before is None else before[...] + part
        out[...] = part.astype(out.dtype)


def ffn(x0, x1, ub, weights, sums, last):
    half, width, count = x0.shape[0], ub.shape[1], len(weights)
    n = 2 * half
    return call(
        functools.partial(ffn_kernel, not sums, count),
        (
            shape((n, width)),
            shape((n, width)),
            shape((half, D), F32),
            shape((half, D), BF16 if last else F32),
        ),
        (x0, x1, ub, *weights, *sums),
        cost=est(4 * n * D * width, 4 * D * width + 5e6, 2 * n * width),
    )


def ffn_half_kernel(x, ub, w0, w1, before, hid, slope, out):
    uw, dw = ffn_weights((w0, w1))
    up = nt(x[...], uw) + ub[...]
    phi = 0.5 + 0.5 * lax.erf(up * (2.0**-0.5))
    hd = (up * phi).astype(BF16)
    hid[...] = hd
    slope[...] = (phi + up * jnp.exp(-0.5 * up * up) * 0.3989422804014327).astype(BF16)
    out[...] = (before[...] + nn(hd, dw)).astype(out.dtype)


def ffn_half(x, ub, weights, before, dtype):
    n, width = x.shape[0], ub.shape[1]
    return call(
        ffn_half_kernel,
        (shape((n, width)), shape((n, width)), shape((n, D), dtype)),
        (x, ub, *weights, before),
        cost=est(1000, 1000),
    )


def second_kernel(bucket, lengths, first, part, got, small, cot, low, sum_two, normal):
    c = place_here()[0]
    _, units = live_units(bucket, lengths)
    n, r = norm(first[...] + (part[...] + got[...].astype(F32) + small[5:6]))
    index = lax.broadcasted_iota(jnp.int32, (first.shape[0], 1), 0)
    live = live_of(place_of(index, c), units)
    oc = jnp.where(live, cot[...].astype(F32), 0.0)
    st = norm_back(oc, n, r, small[6:7])
    low[...] = st.astype(BF16)
    sum_two[...] = st
    normal[...] = n


def second_norm(bucket, lengths, first, part, got, small, cot):
    n = first.shape[0]
    return call(
        second_kernel,
        (shape((n, D)), shape((n, D), F32), shape((n, D), F32)),
        (bucket, lengths, first, part, got, small, cot),
        cost=est(1000, 1000),
        limit=8,
    )


def second_rest_kernel(bucket, lengths, normal, small, cot, low, out, sums):
    c = place_here()[0]
    _, units = live_units(bucket, lengths)
    n = normal[...]
    out[...] = (n * small[6:7] + small[7:8]).astype(BF16)
    index = lax.broadcasted_iota(jnp.int32, (normal.shape[0], 1), 0)
    live = live_of(place_of(index, c), units)
    oc = jnp.where(live, cot[...].astype(F32), 0.0)
    sums[0:1] = jnp.sum(low[...].astype(F32), 0, keepdims=True)
    sums[1:2] = jnp.sum(oc * n, 0, keepdims=True)
    sums[2:3] = jnp.sum(oc, 0, keepdims=True)


def second_rest(bucket, lengths, normal, small, cot, low):
    n = normal.shape[0]
    return call(
        second_rest_kernel,
        (shape((n, D)), shape((3, D), F32)),
        (bucket, lengths, normal, small, cot, low),
        cost=est(1000, 1000),
        limit=8,
    )


def ffn_back_kernel(first, spot, count, d0, d1, x0, x1, *refs):
    weights, refs = refs[:count], refs[count:]
    if spot is None:
        hid, slope = refs[0], refs[1]
        refs = refs[2:]
        uw, dw = ffn_weights(weights)
    else:
        (hid1, slope1, hid2, slope2), refs = refs[:4], refs[4:]
        tail = slice(4 * TWO * spot, 4 * TWO * spot + 4 * TWO)
        hid = jnp.concatenate([hid1[...], hid2[:, tail]], 1)
        slope = jnp.concatenate([slope1[...], slope2[:, tail]], 1)
        uw, dw = stacked(ones_of(weights[:-3]) + twos_of(weights[-3:], [spot]))
    if first:
        in0 = in1 = None
    else:
        (in0, in1), refs = refs[:2], refs[2:]
    *outs, ub, out0, out1 = refs
    half = x0.shape[0]
    cots = []
    for i, (d, before, out) in enumerate(((d0, in0, out0), (d1, in1, out1))):
        rws = slice(half * i, half * i + half)
        uc = (nt(d[...], dw) * slope[rws].astype(F32)).astype(BF16)
        cots.append(uc)
        part = nn(uc, uw)
        part = part if before is None else before[...] + part
        out[...] = part.astype(out.dtype)
    ub[...] = jnp.sum(cots[0].astype(F32), 0, keepdims=True) + jnp.sum(
        cots[1].astype(F32), 0, keepdims=True
    )
    dg = (tn(hid[0:half], d0[...]) + tn(hid[half : 2 * half], d1[...])).astype(BF16)
    ug = (tn(cots[0], x0[...]) + tn(cots[1], x1[...])).astype(BF16)
    if spot is None:
        outs[0][...], outs[1][...] = ug, dg
        return
    rows = ONE + TWO
    for k in range(4):
        for e, g in enumerate((ug, dg)):
            out, i, at = (outs[k // 2], k % 2, rows * e) if spot == 3 else (outs[e], k, 0)
            out[i, at : at + ONE] = g[ONE * k : ONE * k + ONE]
            low = 4 * ONE + TWO * k
            out[i, at + ONE : at + rows] = g[low : low + TWO]


def diagonal_of(refs, rows):
    *weights, hid1, slope1, hid2, slope2 = refs
    tail = slice(12 * TWO, 16 * TWO)
    hid = jnp.concatenate([hid1[...], hid2[rows, tail]], 1)
    slope = jnp.concatenate([slope1[...], slope2[rows, tail]], 1)
    return hid, slope, *stacked(ones_of(weights[:-3]) + twos_of(weights[-3:], [3]))


def diagonal_own_kernel(d, x, *refs):
    *refs, down, up, ub, part = refs
    hid, slope, uw, dw = diagonal_of(refs, slice(0, d.shape[0]))
    cot = (nt(d[...], dw) * slope.astype(F32)).astype(BF16)
    part[...] = nn(cot, uw)
    ub[...] = jnp.sum(cot.astype(F32), 0, keepdims=True)
    down[...], up[...] = tn(hid, d[...]), tn(cot, x[...])


def diagonal_other_kernel(d, x, down, up, ub_own, *refs):
    *refs, lo, hi, ub, part = refs
    half, rows = d.shape[0], ONE + TWO
    hid, slope, uw, dw = diagonal_of(refs, slice(half, 2 * half))
    cot = (nt(d[...], dw) * slope.astype(F32)).astype(BF16)
    part[...] = nn(cot, uw)
    ub[...] = ub_own[...] + jnp.sum(cot.astype(F32), 0, keepdims=True)
    dg = (down[...] + tn(hid, d[...])).astype(BF16)
    ug = (up[...] + tn(cot, x[...])).astype(BF16)
    for k in range(4):
        out, i = (lo, hi)[k // 2], k % 2
        for at, g in ((0, ug), (rows, dg)):
            out[i, at : at + ONE] = g[ONE * k : ONE * k + ONE]
            low = 4 * ONE + TWO * k
            out[i, at + ONE : at + rows] = g[low : low + TWO]


def ffn_back_diagonal(d0, d1, x0, x1, weights, own_kept, other_kept):
    half, width = x0.shape[0], 4 * (ONE + TWO)
    down, up, ub, own = call(
        diagonal_own_kernel,
        (shape((width, D), F32),) * 2 + (shape((1, width), F32), shape((half, D), F32)),
        (d0, x0, *weights, *own_kept),
        cost=est(1000, 1000),
    )
    lo, hi, ub, other = call(
        diagonal_other_kernel,
        (shape((2, width // 2, D)),) * 2 + (shape((1, width), F32), shape((half, D), F32)),
        (d1, x1, down, up, ub, *weights, *other_kept),
        cost=est(1000, 1000),
    )
    return [lo, hi], ub, (own, other)


def ffn_back(d0, d1, x0, x1, spot, weights, kept, sums, last):
    half, count = x0.shape[0], len(weights)
    if spot is None:
        outs, width = [shape(w.shape) for w in weights], weights[0].shape[0]
    else:
        width = 4 * (ONE + TWO)
        rows = ONE + TWO
        outs = [shape((2, 2 * rows, D)) if spot == 3 else shape((4, rows, D))] * 2
    *grads, ub, s0, s1 = call(
        functools.partial(ffn_back_kernel, not sums, spot, count),
        (
            *outs,
            shape((1, width), F32),
            shape((half, D), F32),
            shape((half, D), BF16 if last else F32),
        ),
        (d0, d1, x0, x1, *weights, *kept, *sums),
        cost=est(1000, 1000),
    )
    return grads, ub, (s0, s1)


def first_back_kernel(
    sum_two, part, got, normal, scale, small, *refs
):
    *refs, sum_one, low, sums = refs
    fc = sum_two[...] + part[...] + got[...].astype(F32)
    n = normal[...]
    so = norm_back(fc, n, scale[:, 0:1], small[3:4])
    sum_one[...] = so
    lo = so.astype(BF16)
    low[...] = lo
    sums[0:1] = jnp.sum(lo.astype(F32), 0, keepdims=True)
    sums[1:2] = jnp.sum(fc * n, 0, keepdims=True)
    sums[2:3] = jnp.sum(fc, 0, keepdims=True)
    if refs:
        add_first_kernel(*refs)


def first_back(sum_two, part, got, normal, scale, small, moved=()):
    n = sum_two.shape[0]
    outs = [shape(moved[i].shape) for i in (0, 3, 1, 4)] if moved else []
    *added, sum_one, low, sums = call(
        first_back_kernel,
        (*outs, shape((n, D), F32), shape((n, D)), shape((3, D), F32)),
        (sum_two, part, got, normal, scale, small, *moved),
        cost=est(1000, 1000),
        limit=8,
    )
    return added, sum_one, low, sums


def attend_back_kernel(sets, a0, a1, *refs):
    downs, refs = ((), refs) if sets == 1 else (refs[:2], refs[2:])
    far, outs, (in0, in1, sums), refs = refs[:9], refs[9 : 9 + sets], refs[9 + sets : 12 + sets], refs[12 + sets :]
    wp, v, probs, k, q, wr, x0, x1, ctx = far
    dctx, cots, grads, sems = refs
    copies = Copies(sems)
    for down, out in zip(downs, outs[3:]):
        copies.start(down, out.at[pl.ds(0, 4)])
    c, z, y, x = place_here()
    half = a0.shape[0]
    n = 2 * half
    wpo = wp[:, pl.ds(pl.multiple_of(c * 384, 128), 384)]
    dctx[0:half] = nn(a0[...], wpo).astype(BF16)
    dctx[half:n] = nn(a1[...], wpo).astype(BF16)
    lane = lax.broadcasted_iota(jnp.int32, (n, 128), 1)
    zero = jnp.zeros((n, 128), BF16)
    scale = HEAD_DIM**-0.5
    heads = [[], [], []]
    for pair in range(3):
        lanes = slice(128 * pair, 128 * pair + 128)
        qp, kp, vp, dp = q[:, lanes], k[:, lanes], v[:, lanes], dctx[:, lanes]
        dq = dk = dv = 0.0
        for e in range(2):
            mine = (lane < HEAD_DIM) if e == 0 else (lane >= HEAD_DIM)
            dh, kh, qh = jnp.where(mine, dp, zero), jnp.where(mine, kp, zero), jnp.where(mine, qp, zero)
            pr = probs[2 * pair + e]
            dv = dv + tn(pr, dh)
            pf = pr.astype(F32)
            t = pf * nt(dh, vp)
            ds = (t - pf * jnp.sum(t, -1, keepdims=True)).astype(BF16)
            dq = dq + nn(ds, kh)
            dk = dk + tn(ds, qh)
        for t, val in enumerate((dq * scale, dk * scale, dv)):
            val = val.astype(BF16)
            for e in range(2):
                hd = 2 * pair + e
                g, hh = hd // 3, hd % 3
                at = 640 * g + 192 * t + 64 * hh
                cots[:, at : at + 64] = val[:, 64 * e : 64 * e + 64]
            heads[t].append(val)
    for g in range(2):
        cots[:, 640 * g + 576 : 640 * g + 640] = jnp.zeros((n, 64), BF16)
    parts = [jnp.concatenate(heads[t], 1) for t in range(3)]
    for i, out in enumerate((in0, in1)):
        rws = slice(half * i, half * i + half)
        total = 0.0
        for t in range(3):
            total = total + nn(parts[t][rws], wr[384 * t : 384 * t + 384])
        out[...] = total.astype(out.dtype)
    for row, t in ((0, 0), (1, 2)):
        s = jnp.sum(parts[t].astype(F32), 0, keepdims=True)
        for g in range(2):
            sg = s[:, 192 * g : 192 * g + 192]
            sums[row : row + 1, 384 * g : 384 * g + 192] = jnp.where(c == 0, sg, 0.0)
            sums[row : row + 1, 384 * g + 192 : 384 * g + 384] = jnp.where(c == 1, sg, 0.0)
    for d in range(3):
        at = slice(256 * d, 256 * d + 256)
        full = tn(x0[:, at], cots[0:half]) + tn(x1[:, at], cots[half:n])
        pg = tn(a0[:, at], ctx[0:half]) + tn(a1[:, at], ctx[half:n])
        for g in range(2):
            grads[g, at, 0:576] = full[:, 640 * g : 640 * g + 576].astype(BF16)
            grads[g, at, 576:768] = pg[:, 192 * g : 192 * g + 192].astype(BF16)
    if sets == 1:
        copies.start(grads, outs[0])
    else:
        rows = outs[0].shape[1]
        for spot in (3, 2, 1, 0):
            g, yi = flip(x, spot % 2), flip(y, spot // 2)
            for kz in range(4):
                zi = flip(lax.rem(z, 2), kz % 2) + 2 * flip(lax.div(z, 2), kz // 2)
                at = pl.multiple_of((2 * zi + yi) * rows, rows)
                dst = outs[spot].at[kz] if spot < 3 else outs[3 + kz // 2].at[4 + kz % 2]
                copies.start(grads.at[g, pl.ds(at, rows)], dst)
    copies.wait()


def attend_back(downs, a0, a1, x0, x1, wp, wr, q, k, v, ctx, probs):
    half = a0.shape[0]
    n = 2 * half
    sets = (shape((2, D, D)),)
    if downs:
        sets = (shape((4, 96, D)),) * 3 + (shape((6, 96, D)),) * 2
    far = (wp, v, probs, k, q, wr, x0, x1, ctx)
    return call(
        functools.partial(attend_back_kernel, len(sets)),
        (*sets, shape((half, D), F32), shape((half, D)), shape((2, D), F32)),
        (a0, a1, *downs, *far),
        scratch=[
            pltpu.VMEM((n, 384), BF16),
            pltpu.VMEM((n, 1280), BF16),
            pltpu.VMEM((2, D, D), BF16),
        ],
        cost=est(8e9, 14e6),
        limit=16,
        far_out=range(len(sets)),
        sems=20,
    )


def local(
    inputs,
    bucket,
    lengths,
    qkv_weight,
    query_bias,
    value_bias,
    proj_weight,
    proj_bias,
    first_gain,
    first_shift,
    up_weight,
    up_bias,
    down_weight,
    down_bias,
    second_gain,
    second_shift,
    cotangent,
):
    head_count = lax.axis_size("head")
    batch_count = lax.axis_size("batch")
    devices = head_count * batch_count
    direct = batch_count == 8
    b = lax.axis_index("batch")
    h = lax.axis_index("head")
    me = b * head_count + h
    x, c = h // 2, h % 2
    z, y = b // 2, b % 2
    wq, wp, wf = 3 * D // devices, D // devices, FF // devices

    vectors = [
        query_bias,
        value_bias,
        proj_bias,
        first_gain,
        first_shift,
        down_bias,
        second_gain,
        second_shift,
    ]
    if direct:
        a_shard, one_a, one_b, two = pack(
            qkv_weight.T, proj_weight.T, up_weight.T, down_weight, up_bias, vectors
        )
    else:
        small = lax.dynamic_update_slice(
            jnp.zeros((16, D), BF16), jnp.stack(vectors), (0, me * wp)
        )
        per_row = D // wf
        small = lax.dynamic_update_slice(
            small, up_bias[None, :], (8 + me // per_row, (me % per_row) * wf)
        )
        proj_t = proj_weight.T.reshape(wp, 2, 2, 192).transpose(0, 2, 1, 3).reshape(wp, D)
        a_shard = jnp.concatenate([qkv_weight.T, proj_t, small])
    other_in = core_swap(inputs)
    k = jnp.arange(batch_count * 2)
    if direct:
        a_z = z_line(a_shard)
        two = after(two, a_z[1])
        two_x, two_y = x_swap(two), y_swap(two)
        two_d = jnp.concatenate([x_swap(two_y[:TWO]), y_swap(two_x[TWO:])])
        two_lo = jnp.stack([two, two_x, two_y, two_d])
        a_z, two_lo, other_in = lax.optimization_barrier((jnp.stack(a_z), two_lo, other_in))
        one_a = after(one_a, a_z)
        near = z_swap(jnp.concatenate([one_a, two_lo.reshape(8 * TWO, D)]), 1)
        one_a = [one_a, None, z_swap(one_a, 2), z_swap(one_a, 3)]
        a_x, a_y = x_swap(a_z), y_swap(a_z)
        a_x, a_y, near, one_a[2], one_a[3] = lax.optimization_barrier(
            (a_x, a_y, near, one_a[2], one_a[3])
        )
        one_a[1], two_hi = near[:FIRST], near[FIRST:].reshape(two_lo.shape)
        one_b = z_line(after(one_b, near))
        a_d = [x_swap(a_y[:2]), y_swap(a_x[2:])]
        one_b, a_d = lax.optimization_barrier((one_b, a_d))
        a_own = [a_z, a_x, a_y, *a_d]
        one_z = jnp.stack([jnp.concatenate(pair) for pair in zip(one_a, one_b)])
        one_z, a_own = lax.optimization_barrier((one_z, a_own))
        one_x, one_y = x_swap(one_z), y_swap(one_z)
        a_swapped = [core_swap(v) for v in a_own]
        two_far = z_swap(jnp.concatenate([two_lo, two_hi]), 2)
        one_x, one_y, two_far = lax.optimization_barrier((one_x, one_y, two_far))
        one_d = [x_swap(one_y[:2]), y_swap(one_x[2:])]
        twos = [two_lo, two_hi, two_far]
        ctx_own, ctx_other, q, kk, v, ctx, probs, wr, ub_all, proj_w, small_all = attend(
            bucket, lengths, inputs, other_in, (*a_own, *a_swapped), wq, wp
        )
        f_all = [[one_z], [one_x], [one_y], twos, one_d]
    else:
        a_all = lax.all_gather(a_shard, ("batch", "head"), axis=0)
        qkv_all = a_all[:, :wq].reshape(2, 2, 576, D)
        qkv_w = lax.dynamic_index_in_dim(qkv_all, c, 1, keepdims=False).reshape(2 * 576, D)
        proj_w = a_all[:, wq : wq + wp].reshape(D, D)
        small_all = jnp.sum(a_all[:, wq + wp :].astype(F32), 0)
        ctx_own, ctx_other, q, kk, v, ctx, probs, wr = attend(
            bucket, lengths, inputs, other_in, (qkv_w, small_all)
        )
        f_shard = jnp.concatenate([up_weight.T, down_weight])
        f_all = [
            (v[:, :wf].reshape(-1, D), v[:, wf:].reshape(-1, D)) for v in gather_any(f_shard)
        ]
        owner = (k % batch_count) * 4 + (x ^ (k // batch_count)) * 2 + c
    if not direct:
        spread = (owner[None, :] == jnp.arange(devices)[:, None]).astype(F32)
        ub_all = tn(spread, small_all[8:12].reshape(devices, wf)).reshape(1, FF // 2)

    ctx_in = core_swap(ctx_other)
    first_low, first, first_n, first_r = first_norm(inputs, ctx_own, ctx_in, proj_w, small_all)
    first_in = core_swap(first_low)
    sums = ()
    kept = []
    starts = (0, FF // 4)
    if direct:
        starts = (0, 4 * ONE, 8 * ONE, 16 * ONE, 12 * ONE)
    for weights, at in zip(f_all, starts):
        width = FF // 4
        if direct:
            width = 16 * TWO if len(kept) == 3 else 4 * ONE
        if direct and len(kept) == 4:
            ub = ub_all[:, at : at + width]
            hid1, slope1, part1 = ffn_half(first_in, ub, weights, sums[1], BF16)
            hid0, slope0, part0 = ffn_half(first_low, ub, weights, sums[0], F32)
            kept.append(((hid0, slope0), (hid1, slope1)))
            sums = (part0, part1)
            continue
        hid, slope, *sums = ffn(
            first_low,
            first_in,
            ub_all[:, at : at + width],
            weights,
            sums,
            len(kept) == len(f_all) - 1,
        )
        kept.append((hid, slope))
    down_low, sum_two, second_n = second_norm(
        bucket, lengths, first, sums[0], core_swap(sums[1]), small_all, cotangent
    )
    down_in = core_swap(down_low)

    sums = ()
    f_parts, ub_parts = [], []
    if direct:
        for spot, i in ((3, 4), (2, 2), (1, 1), (0, 0)):
            weights = (*f_all[i], *twos)
            rows = (down_low, down_in, first_low, first_in)
            if spot == 3:
                own, other = [(*half, *kept[3]) for half in kept[i]]
                grads, ub, sums = ffn_back_diagonal(*rows, weights, own, other)
            else:
                grads, ub, sums = ffn_back(
                    *rows, spot, weights, (*kept[i], *kept[3]), sums, spot == 0
                )
            f_parts.append(grads)
            ub_parts.insert(0, ub)
    else:
        for weights, pair in zip(f_all, kept):
            grads, ub, sums = ffn_back(
                down_low,
                down_in,
                first_low,
                first_in,
                None,
                weights,
                pair,
                sums,
                len(f_parts) == len(f_all) - 1,
            )
            f_parts.append(grads)
            ub_parts.append(ub)
    part_own, part_other = sums
    layer_out, sums_two = second_rest(
        bucket, lengths, after(second_n, part_other), small_all, cotangent, down_low
    )
    sum_two = after(sum_two, sums_two)
    moved = ()
    if direct:
        (d_lo, d_hi), y_sets, x_sets, z_sets = f_parts
        moved = (*x_sets, y_swap(d_hi), *y_sets, x_swap(d_lo))
    added, sum_one, attn_low, sums_one = first_back(
        sum_two, part_own, core_swap(part_other), first_n, first_r, small_all, moved
    )
    attn_in = core_swap(attn_low)
    *a_grads, in_own, in_other, sums_zero = attend_back(
        added[2:],
        attn_low,
        attn_in,
        inputs,
        other_in,
        proj_w,
        wr,
        q,
        kk,
        v,
        ctx,
        probs,
    )
    in_got = core_swap(in_other)
    inputs_grad = (sum_one + in_own + in_got).astype(BF16)

    if direct:
        up_sets = scatter_xy(z_sets[0], *added[:2])
        a_zz, a_xx, a_yy, by_x, by_y = a_grads
        by_x, by_y, up_sets, in_got = lax.optimization_barrier((by_x, by_y, up_sets, in_got))
        by_x, by_y = x_swap(by_x), y_swap(by_y)
        up_mine, up_others = combine(*up_sets)
        sums_zero = after(sums_zero, up_others)
        terms = exchange_terms(sums_zero, sums_one, sums_two, ub_parts, devices)
        terms = lax.all_to_all(terms, ("batch", "head"), split_axis=0, concat_axis=0, tiled=True)
        up_others = scatter_z(up_others)
        by_x, by_y, up_others, terms, _ = lax.optimization_barrier(
            (by_x, by_y, up_others, terms, inputs_grad)
        )
        a_xy, down_mine, down_others = turn(a_xx, a_yy, z_sets[1], by_x, by_y)
        a_sets = scatter_xy(a_zz, *a_xy)
        down_others = scatter_z(down_others)
        a_sets, down_others = lax.optimization_barrier((a_sets, down_others))
        a_mine, a_others = combine_last(*a_sets)
        a_others = scatter_z(a_others)
        up_grad, down_grad = finish_ffn((up_mine, *up_others), (down_mine, *down_others))
        up_grad = up_grad.T
        terms = jnp.sum(terms.astype(F32), 0)
        packed = jnp.concatenate([terms[:, :wp].reshape(-1), terms[0, wp : wp + wf]])
        qkv_grad, proj_grad = finish_attend((a_mine, *a_others))
    else:
        vecs = jnp.concatenate([sums_zero, sums_one, sums_two])
        vecs = vecs.reshape(8, devices, wp).transpose(1, 0, 2).reshape(devices, 8 * wp)
        ubias = jnp.concatenate(ub_parts).reshape(batch_count * 2, wf)
        ubias = lax.dot_general(
            spread, ubias, (((1,), (0,)), ((), ())), precision=lax.Precision.HIGHEST
        )
        packed = jnp.concatenate([vecs, ubias], 1)
        packed = lax.all_to_all(
            packed, ("batch", "head"), split_axis=0, concat_axis=0, tiled=True
        )
        packed = jnp.sum(packed, 0)
        wb = D // batch_count
        a_grads = a_grads[0].reshape(2, batch_count, wb, D)
        a_mine = scatter_any(
            [
                lax.dynamic_index_in_dim(a_grads, x, 0, keepdims=False),
                lax.dynamic_index_in_dim(a_grads, 1 - x, 0, keepdims=False),
            ]
        )
        f_mine = scatter_any(
            [
                jnp.concatenate(
                    [ug.reshape(batch_count, wf, D), dg.reshape(batch_count, wf, D)], 1
                )
                for ug, dg in f_parts
            ]
        )
        qkv_grad = a_mine[:, :576].reshape(wb, 3, 3, HEAD_DIM).transpose(0, 2, 1, 3)
        qkv_grad = qkv_grad.reshape(wb, 576)
        proj_grad = a_mine[:, 576:].T
        up_grad, down_grad = f_mine[:wf].T, f_mine[wf:]
    qb_g, vb_g, pb_g, fg_g, fs_g, db_g, sg_g, ss_g = [
        packed[i * wp : (i + 1) * wp] for i in range(8)
    ]
    return (
        layer_out,
        inputs_grad,
        qkv_grad,
        qb_g,
        vb_g,
        proj_grad,
        pb_g,
        fg_g,
        fs_g,
        up_grad,
        packed[8 * wp :],
        down_grad,
        db_g,
        sg_g,
        ss_g,
    )


def solution(mesh):
    both = ("batch", "head")
    in_specs = (
        P(both, None),
        P("batch"),
        P("batch", None),
        P(None, both),
        P(both),
        P(both),
        P(None, both),
        P(both),
        P(both),
        P(both),
        P(None, both),
        P(both),
        P(both, None),
        P(both),
        P(both),
        P(both),
        P(both, None),
    )
    out_specs = (
        P(both, None),
        P(both, None),
        P("batch", "head"),
        P(both),
        P(both),
        P("head", "batch"),
        P(both),
        P(both),
        P(both),
        P(None, both),
        P(both),
        P(both, None),
        P(both),
        P(both),
        P(both),
    )
    return jax.shard_map(local, mesh=mesh, in_specs=in_specs, out_specs=out_specs, check_vma=False)
```
